32 devices in a mesh: fsdp: 4 (over z), ctx: 4 (over x, core), tp: 2 (over y).
Axes of the slice: x: 2, y: 2, z: 4, core: 2. Of those that a mesh axis runs over, the one named last changes fastest.
Arguments:
- tokens: bfloat16 [4, 2560, 512], P('fsdp', ('ctx', 'tp')), may hold values from -6 to 6
- encoder_states: bfloat16 [4, 512, 512], P('fsdp', 'ctx'), may hold values from -6 to 6
- timesteps: int32 [4], P('fsdp'), may hold values from 0 to 999
- parents: int32 [4, 20], P('fsdp'), may hold values from -1 to 11, as said below
- w_mod: bfloat16 [512, 3072], P('fsdp'), may hold values from -0.25 to 0.25
- w_self_qkv: bfloat16 [3, 512, 512], P(None, 'fsdp', 'tp'), may hold values from -0.25 to 0.25
- w_self_out: bfloat16 [512, 512], P('fsdp', 'tp'), may hold values from -1.5 to 1.5
- w_cross_qkv: bfloat16 [3, 512, 512], P(None, 'fsdp', 'tp'), may hold values from -0.25 to 0.25
- w_cross_out: bfloat16 [512, 512], P('fsdp', 'tp'), may hold values from -1.5 to 1.5
- w_up: bfloat16 [512, 2048], P('fsdp', 'tp'), may hold values from -0.25 to 0.25
- w_down: bfloat16 [512, 2048], P('fsdp', 'tp'), may hold values from -0.125 to 0.125
- cotangent: bfloat16 [4, 2560, 512], P('fsdp', ('ctx', 'tp')), may hold values from -6 to 6
Outputs:
- output: bfloat16 [4, 2560, 512], P('fsdp', ('ctx', 'tp'))
- input_grad: float32 [4, 2560, 512], P('fsdp', ('ctx', 'tp'))
- encoder_grad: float32 [4, 512, 512], P('fsdp', 'ctx')
- modulation_weight_gradient: float32 [512, 3072], P('fsdp')
- grad_w_self_qkv: float32 [3, 512, 512], P(None, 'fsdp', 'tp')
- grad_w_self_out: float32 [512, 512], P('fsdp', 'tp')
- grad_w_cross_qkv: float32 [3, 512, 512], P(None, 'fsdp', 'tp')
- grad_w_cross_out: float32 [512, 512], P('fsdp', 'tp')
- grad_w_up: float32 [512, 2048], P('fsdp', 'tp')
- grad_w_down: float32 [512, 2048], P('fsdp', 'tp')
The draws below stay inside these ranges and needn't reach their ends.
Inputs may be any that keep to these rules, and one draw needn't show every extreme that they name: `parents`: in every tree block 0 has parent -1, block b for 1 <= b < 8 has parent b - 1, blocks 8 to 11 have parent 8 - 1, and each of the last 8 blocks has one of those branch blocks as parent, each branch block being the parent of exactly 2 of them.
All inputs are finite; a program needn't handle non-finite values.
Results may differ from the reference program's by a relative error of at most 0.025.
Values may be sent and summed in bfloat16 or wider, within the bound.
A program may use at most 128 MiB of HBM per device.

```python
import math
import jax
import jax.numpy as jnp
from jax import lax

D = 512
DH = 64
FF = 2048
ENC = 512
TRUNK = 8
BRANCHES = 4
LEAVES = 2
TREE_LEN = 2560
TREES = 4


def draw_parents(key, part):
    leaf_total = BRANCHES * LEAVES

    def one_tree(tree_key):
        shuffled = jax.random.permutation(tree_key, leaf_total).astype(jnp.int32)
        trunk_part = jnp.arange(TRUNK, dtype=jnp.int32) - 1
        branch_part = jnp.full((BRANCHES,), TRUNK - 1, dtype=jnp.int32)
        leaf_part = TRUNK + shuffled // LEAVES
        return jnp.concatenate([trunk_part, branch_part, leaf_part])
    return jax.vmap(one_tree)(jax.random.split(jax.random.fold_in(key, 7), TREES))


def touch_ends(entries, rng, least, top_value):
    place = [jax.random.randint(jax.random.fold_in(rng, axis), (), 0, length) for axis, length in enumerate(entries.shape)]
    main_axis = entries.shape.index(max(entries.shape))
    neighbour = place[:main_axis] + [(place[main_axis] + 1) % entries.shape[main_axis]] + place[main_axis + 1:]
    return entries.at[tuple(place)].set(least).at[tuple(neighbour)].set(top_value)


def strengthened(entries, stream_key, source, target, blocks, factor):
    owner, partner = [(jnp.arange(entries.shape[position]) // (entries.shape[position] // blocks)).reshape([-1 if axis == position else 1 for axis in range(entries.ndim)]) for position in (source, target)]
    chosen = jax.random.permutation(stream_key, blocks)[partner]
    strong = (owner == chosen) | (owner == (partner + blocks // 2) % blocks)
    return jnp.where(strong, factor * entries, entries)


def shard_levels(stream_key, dims, cuts, least, top_value):
    def one(axis_at, shards_of):
        steps = jax.random.uniform(jax.random.fold_in(jax.random.fold_in(stream_key, 6), axis_at), (shards_of,), jnp.float32, least / len(cuts), top_value / len(cuts))
        return jnp.repeat(jnp.exp(steps), dims[axis_at] // shards_of).reshape((-1,) + (1,) * (len(dims) - axis_at - 1))

    factor_of = one(*cuts[0])
    for cut in cuts[1:]:
        factor_of = factor_of * one(*cut)
    return factor_of


def scatter_about(stream_key, extent, deviation, limit, shards=(), kind=jnp.bfloat16):
    entries = jax.random.normal(stream_key, extent, jnp.float32) * deviation
    if len(shards) > 0:
        entries = shard_levels(stream_key, extent, shards, -0.22, 0.18) * entries
    return jnp.clip(entries, min=-limit, max=limit).astype(kind)


def noise_with(rng, shape, deviation, limit, pieces, heavy, kind=jnp.bfloat16):
    array = deviation * jax.random.normal(rng, shape, jnp.float32)
    if pieces:
        array = array * shard_levels(rng, shape, pieces, -0.22, 0.18)
    return jnp.clip(strengthened(array, jax.random.fold_in(rng, 3), *heavy), -limit, limit).astype(kind)


def setup_inputs(seed: int = 0) -> dict:
    keys = jax.random.split(jax.random.key(seed), 13)
    tokens = scatter_about(keys[0], (TREES, TREE_LEN, D), 1.0, 6.0, ((0, 4), (1, 8)))
    encoder_states = scatter_about(keys[1], (TREES, ENC, D), 1.0, 6.0, ((0, 4), (1, 4)))
    timesteps = touch_ends(jax.random.randint(keys[2], (TREES,), 0, 1000), jax.random.fold_in(keys[2], 1), 0, 999).astype(jnp.int32)
    parents = draw_parents(jax.random.fold_in(keys[12], 71), 0)
    w_mod = scatter_about(keys[4], (D, 6 * D), D ** -0.5, 0.25, ((0, 4),))
    w_self_qkv = scatter_about(keys[5], (3, D, D), D ** -0.5, 0.25, ((1, 4), (2, 2)))
    w_self_out = scatter_about(keys[6], (D, D), 16 ** -0.5, 1.5, ((0, 4), (1, 2)))
    w_cross_qkv = scatter_about(keys[7], (3, D, D), D ** -0.5, 0.25, ((1, 4), (2, 2)))
    w_cross_out = scatter_about(keys[8], (D, D), 16 ** -0.5, 1.5, ((0, 4), (1, 2)))
    w_up = scatter_about(keys[9], (D, FF), D ** -0.5, 0.25, ((0, 4), (1, 2)))
    w_down = scatter_about(keys[10], (D, FF), FF ** -0.5, 0.125, ((0, 4), (1, 2)))
    cotangent = noise_with(keys[11], (TREES, TREE_LEN, D), 1.0, 6.0, ((0, 4), (1, 8)), (0, 2, 4, 2.0))
    return dict(tokens=tokens, encoder_states=encoder_states, timesteps=timesteps, parents=parents, w_mod=w_mod, w_self_qkv=w_self_qkv, w_self_out=w_self_out, w_cross_qkv=w_cross_qkv, w_cross_out=w_cross_out, w_up=w_up, w_down=w_down, cotangent=cotangent)


epsilon = 1e-05
masked_score = -1e+30

@jax.custom_vjp
def low(v):
    return lax.optimization_barrier(v.astype(jnp.bfloat16)).astype(jnp.float32)

@jax.custom_vjp
def low_back(v):
    return v

def low_keep(v):
    return (low(v), None)

def low_pass(kept, grad):
    return (grad,)

def back_keep(v):
    return (v, None)

def back_low(kept, grad):
    return (low(grad),)
low.defvjp(low_keep, low_pass)
low_back.defvjp(back_keep, back_low)

def product(left, right):
    return jnp.dot(left, right, precision=lax.Precision.HIGHEST)

def timestep_code(timesteps, code_width):
    half_width = code_width // 2
    frequency = jnp.exp(-math.log(10000.0) * jnp.arange(half_width, dtype=jnp.float32) / half_width)
    angles = timesteps.astype(jnp.float32)[:, None] * frequency[None, :]
    return jnp.concatenate([jnp.sin(angles), jnp.cos(angles)], axis=-1)

def ancestry(parents):
    block_total = parents.shape[-1]
    block_ids = jnp.arange(block_total, dtype=jnp.int32)
    reachable_flags = jnp.logical_or(parents[:, :, None] == block_ids[None, None, :], (block_ids[:, None] == block_ids[None, :])[None])
    for repeat in range((block_total - 1).bit_length()):
        reachable_flags = jnp.any(jnp.logical_and(reachable_flags[:, :, :, None], reachable_flags[:, None, :, :]), axis=2)
    return reachable_flags

def tree_mask(parents, query_start, query_len, tree_len):
    reachable_flags = ancestry(parents)
    block_total = parents.shape[-1]
    block_len = tree_len // block_total
    query_pos = query_start + jnp.arange(query_len, dtype=jnp.int32)
    key_pos = jnp.arange(tree_len, dtype=jnp.int32)
    query_block = (query_pos // block_len).astype(jnp.int32)
    key_block = (key_pos // block_len).astype(jnp.int32)
    linked = reachable_flags[:, query_block][:, :, key_block]
    same_block = query_block[:, None] == key_block[None, :]
    later = key_pos[None, :] > query_pos[:, None]
    return jnp.logical_and(linked, jnp.logical_not(jnp.logical_and(same_block, later))[None])

def modulate(stream, scale_part, shift_part):
    center = stream - lax.optimization_barrier(jnp.mean(stream, axis=-1, keepdims=True))
    normed = center * lax.rsqrt(lax.optimization_barrier(jnp.mean(center * center, axis=-1, keepdims=True)) + epsilon)
    return normed * (1.0 + scale_part) + shift_part

def head_attend(queries, key_rows, value_rows, allowed):
    head_scale_factor = 1.0 / math.sqrt(queries.shape[-1])
    scores = low_back(product(queries, key_rows.T) * head_scale_factor)
    if allowed is not None:
        scores = jnp.where(allowed, scores, masked_score)
    highest = lax.optimization_barrier(jnp.max(scores, axis=-1, keepdims=True))
    log_total = highest + jnp.log(lax.optimization_barrier(jnp.sum(jnp.exp(scores - highest), axis=-1, keepdims=True)))
    shares = jnp.exp(scores - log_total)
    return product(low(shares), value_rows)

def attend_all(queries, key_rows, value_rows, allowed):
    head_count = queries.shape[-1] // DH

    def heads_leading_layout(row_block):
        return row_block.reshape(row_block.shape[0], head_count, DH).transpose(1, 0, 2)

    def one_head(triple):
        return head_attend(triple[0], triple[1], triple[2], allowed)
    mixed_rows = lax.map(jax.checkpoint(one_head), (heads_leading_layout(queries), heads_leading_layout(key_rows), heads_leading_layout(value_rows)))
    return mixed_rows.transpose(1, 0, 2).reshape(queries.shape[0], head_count * DH)

def layer_tree(stream_a, encoder_rows, w_mod, w_self_qkv, w_self_out, w_cross_qkv, w_cross_out, w_up, w_down, condition, allowed):
    modulation = product(low(condition), w_mod).reshape(6, -1)
    hidden_a = low(modulate(stream_a, modulation[0], modulation[1]))
    query_a = low_back(low(product(hidden_a, w_self_qkv[0])))
    key_a = low_back(low(product(hidden_a, w_self_qkv[1])))
    value_a = low_back(low(product(hidden_a, w_self_qkv[2])))
    mixed_a = low_back(low(attend_all(query_a, key_a, value_a, allowed)))
    stream_b = stream_a + low_back(product(mixed_a, w_self_out.T))
    hidden_b = low(modulate(stream_b, modulation[2], modulation[3]))
    query_b = low_back(low(product(hidden_b, w_cross_qkv[0])))
    key_b = low_back(low(product(encoder_rows, w_cross_qkv[1])))
    value_b = low_back(low(product(encoder_rows, w_cross_qkv[2])))
    mixed_b = low_back(low(attend_all(query_b, key_b, value_b, None)))
    stream_c = stream_b + low_back(product(mixed_b, w_cross_out.T))
    hidden_c = low(modulate(stream_c, modulation[4], modulation[5]))
    upper = low_back(product(hidden_c, w_up))
    activated = low(jax.nn.gelu(upper, approximate=False))
    return stream_c + low_back(product(activated, w_down.T))

def reference(tokens, encoder_states, timesteps, parents, w_mod, w_self_qkv, w_self_out, w_cross_qkv, w_cross_out, w_up, w_down, cotangent):
    matrices = tuple((matrix.astype(jnp.float32) for matrix in (w_mod, w_self_qkv, w_self_out, w_cross_qkv, w_cross_out, w_up, w_down)))

    def per_tree(carried, packed):
        tree_tokens, tree_enc, tree_step, tree_parents, tree_cot = packed
        condition = jax.nn.silu(timestep_code(tree_step[None], D)[0])
        allowed = tree_mask(tree_parents[None], 0, TREE_LEN, TREE_LEN)[0]

        def forward(stream_a, encoder_rows, m_mod, m_sqkv, m_sout, m_cqkv, m_cout, m_up, m_down):
            return layer_tree(stream_a, encoder_rows, m_mod, m_sqkv, m_sout, m_cqkv, m_cout, m_up, m_down, condition, allowed)
        result, pullback = jax.vjp(forward, tree_tokens.astype(jnp.float32), tree_enc.astype(jnp.float32), matrices[0], matrices[1], matrices[2], matrices[3], matrices[4], matrices[5], matrices[6])
        grads = pullback(tree_cot.astype(jnp.float32))
        updated = tuple((total + piece for total, piece in zip(carried, grads[2:])))
        return (updated, (result.astype(jnp.bfloat16), grads[0], grads[1]))
    initial = tuple((jnp.zeros_like(matrix) for matrix in matrices))
    totals, stacked = lax.scan(per_tree, initial, (tokens, encoder_states, timesteps, parents, cotangent))
    return (stacked[0], stacked[1], stacked[2], totals[0], totals[1], totals[2], totals[3], totals[4], totals[5], totals[6])
```

```python
import math

import jax
import jax.numpy as jnp
from jax import lax
from jax.experimental import pallas as pl
from jax.experimental.pallas import tpu as pltpu
from jax.sharding import PartitionSpec as P

BF = jnp.bfloat16
F = jnp.float32
D = 512
FF = 2048
HD = 64
ROWS = 320
LOC = 384
BLK = 128
TRUNK = 8
BRANCHES = 4
TRK = TRUNK * BLK
SHARED = (TRUNK + BRANCHES) * BLK
SPEC = 2 * LOC
KV = TRK + SPEC
ENC = 512
EPS = 1e-05
NEG = -1e30
VMEM_LIMIT = 67043328


def nn(a, b):
    return lax.dot_general(a, b, (((1,), (0,)), ((), ())), preferred_element_type=F)


def nt(a, b):
    return lax.dot_general(a, b, (((1,), (1,)), ((), ())), preferred_element_type=F)


def tn(a, b):
    return lax.dot_general(a, b, (((0,), (0,)), ((), ())), preferred_element_type=F)


def normed(v):
    center = v - jnp.mean(v, axis=-1, keepdims=True)
    rstd = lax.rsqrt(jnp.mean(center * center, axis=-1, keepdims=True) + EPS)
    return center * rstd, rstd


def norm_back(grad, stream, scale):
    n, rstd = normed(stream)
    gn = grad * (1.0 + scale)
    back = rstd * (
        gn
        - jnp.mean(gn, axis=-1, keepdims=True)
        - n * jnp.mean(gn * n, axis=-1, keepdims=True)
    )
    return back, jnp.sum(grad * n, axis=0, keepdims=True), jnp.sum(grad, axis=0, keepdims=True)


def row_loop(total, step, body):
    @pl.loop(0, total // step)
    def _(i):
        body(pl.ds(pl.multiple_of(i * step, step), step))


def half_lanes(shape, half):
    lane = lax.broadcasted_iota(jnp.int32, shape, len(shape) - 1)
    return (lane // HD) == half


def keep(value, half):
    return jnp.where(half_lanes(value.shape, half), value, jnp.zeros_like(value))


def layer_kernel(
    parents_ref,
    tok_tb,
    tok_loc,
    enc,
    cot,
    mod,
    wqkv,
    wso,
    wcqkv,
    wco,
    wup,
    wdn,
    out_ref,
    gstream,
    gpart,
    gown,
    egrad,
    mgrad,
    g_qkv,
    g_so,
    g_cqkv,
    g_co,
    g_up,
    g_dn,
    hid,
    hloc,
    kbuf,
    vbuf,
    qbuf,
    pt,
    ps,
    bias_t,
    bias_s,
    st,
    ss,
    spec_o,
    mixa,
    stream_b,
    stream_c,
    hid_b,
    hid_c,
    kenc,
    venc,
    qb,
    pe,
    mixb,
    t0,
    t1,
    b0,
    b1,
    acc0,
    acc1,
    gbf,
    mgr,
    dq,
    dkb,
    dvb,
    gkv,
    wk_acc,
    wv_acc,
):
    ci = lax.axis_index("ctx") * 2 + lax.axis_index("tp")
    odd = lax.rem(ci, 2)
    off = pl.multiple_of(odd * 64, 64)
    own = pl.ds(off, ROWS)
    base = (ci * 5) // 2
    sa, ba = mod[0:1, :], mod[1:2, :]
    sb, bb = mod[2:3, :], mod[3:4, :]
    sf, bf_ = mod[4:5, :], mod[5:6, :]

    def parent_of(lb):
        return jnp.clip(parents_ref[0, base + lb] - TRUNK, 0, BRANCHES - 1)

    def mask_trunk(rs):
        row = lax.broadcasted_iota(jnp.int32, (32, TRK), 0) + rs.start + ci * ROWS
        col = lax.broadcasted_iota(jnp.int32, (32, TRK), 1)
        bias_t[rs, :] = jnp.where(col <= row, 0.0, NEG)

    row_loop(ROWS, 32, mask_trunk)
    for lb in range(3):
        blk = base + lb
        row = lax.broadcasted_iota(jnp.int32, (BLK, 2 * BLK), 0)
        col = lax.broadcasted_iota(jnp.int32, (BLK, 2 * BLK), 1)
        par_ok = jnp.logical_and(col < BLK, blk >= TRUNK + BRANCHES)
        self_ok = jnp.logical_and(
            jnp.logical_and(col >= BLK, col - BLK <= row), blk >= TRUNK
        )
        bias_s[lb * BLK : (lb + 1) * BLK, :] = jnp.where(
            jnp.logical_or(par_ok, self_ok), 0.0, NEG
        )

    def hidden(x):
        n, _ = normed(x.astype(F))
        return (n * (1.0 + sa) + ba).astype(BF)

    def hid_trunk(rs):
        hid[rs, :] = hidden(tok_tb[rs, :])

    row_loop(TRK, 32, hid_trunk)

    def hid_loc(rs):
        hloc[rs, :] = hidden(tok_loc[rs, :])

    row_loop(LOC, 32, hid_loc)
    for lb in range(3):
        at = pl.multiple_of(TRK + parent_of(lb) * BLK, BLK)
        for piece in range(4):
            hid[TRK + lb * 256 + piece * 32 : TRK + lb * 256 + piece * 32 + 32, :] = hidden(
                tok_tb[pl.ds(at + piece * 32, 32), :]
            )
        hid[TRK + lb * 256 + BLK : TRK + lb * 256 + 2 * BLK, :] = hloc[
            lb * BLK : (lb + 1) * BLK, :
        ]

    def project(rs):
        kbuf[rs, :] = nn(hid[rs, :], wqkv[1]).astype(BF)
        vbuf[rs, :] = nn(hid[rs, :], wqkv[2]).astype(BF)

    row_loop(KV, 256, project)
    qbuf[...] = (nn(hloc[...], wqkv[0]) * 0.125).astype(BF)

    @pl.loop(0, 4)
    def _(hp):
        lanes = pl.ds(pl.multiple_of(hp * 128, 128), 128)
        kt = kbuf[0:TRK, lanes]
        for half in range(2):
            h = hp * 2 + half
            st[...] = nt(keep(qbuf[own, lanes], half), kt)
            for lb in range(3):
                r = slice(lb * BLK, (lb + 1) * BLK)
                ks = kbuf[TRK + lb * 256 : TRK + (lb + 1) * 256, lanes]
                ss[r, :] = nt(keep(qbuf[r, lanes], half), ks)

            @pl.loop(0, ROWS // 32)
            def _(i):
                rs = pl.ds(pl.multiple_of(i * 32, 32), 32)
                ro = pl.ds(pl.multiple_of(i * 32 + off, 32), 32)
                a = st[rs, :] + bias_t[rs, :]
                b = ss[ro, :] + bias_s[ro, :]
                top = jnp.maximum(
                    jnp.max(a, axis=-1, keepdims=True), jnp.max(b, axis=-1, keepdims=True)
                )
                a = jnp.exp(a - top)
                b = jnp.exp(b - top)
                inv = 1.0 / (
                    jnp.sum(a, axis=-1, keepdims=True) + jnp.sum(b, axis=-1, keepdims=True)
                )
                pt[h, rs, :] = (a * inv).astype(BF)
                ps[h, ro, :] = (b * inv).astype(BF)

            for lb in range(3):
                r = slice(lb * BLK, (lb + 1) * BLK)
                vs = vbuf[TRK + lb * 256 : TRK + (lb + 1) * 256, lanes]
                spec_o[half, r, :] = nn(ps[h, r, :], vs)
        vt = vbuf[0:TRK, lanes]
        o0 = nn(pt[hp * 2], vt) + spec_o[0, own, :]
        o1 = nn(pt[hp * 2 + 1], vt) + spec_o[1, own, :]
        mixa[:, lanes] = jnp.where(half_lanes(o0.shape, 0), o0, o1).astype(BF)

    t0[...] = nt(mixa[...], wso[...])

    def after_self(rs):
        ro = pl.ds(pl.multiple_of(rs.start + off, 32), 32)
        sbv = tok_loc[ro, :].astype(F) + t0[rs, :]
        stream_b[rs, :] = sbv
        n, _ = normed(sbv)
        hid_b[rs, :] = (n * (1.0 + sb) + bb).astype(BF)

    row_loop(ROWS, 32, after_self)

    kenc[...] = nn(enc[...], wcqkv[1]).astype(BF)
    venc[...] = nn(enc[...], wcqkv[2]).astype(BF)
    qb[...] = (nn(hid_b[...], wcqkv[0]) * 0.125).astype(BF)

    @pl.loop(0, 4)
    def _(hp):
        lanes = pl.ds(pl.multiple_of(hp * 128, 128), 128)
        kt = kenc[:, lanes]
        for half in range(2):
            h = hp * 2 + half
            t0[...] = nt(keep(qb[:, lanes], half), kt)

            @pl.loop(0, ROWS // 32)
            def _(i):
                rs = pl.ds(pl.multiple_of(i * 32, 32), 32)
                a = t0[rs, :]
                a = jnp.exp(a - jnp.max(a, axis=-1, keepdims=True))
                inv = 1.0 / jnp.sum(a, axis=-1, keepdims=True)
                pe[h, rs, :] = (a * inv).astype(BF)

        vt = venc[:, lanes]
        o0 = nn(pe[hp * 2], vt)
        o1 = nn(pe[hp * 2 + 1], vt)
        mixb[:, lanes] = jnp.where(half_lanes(o0.shape, 0), o0, o1).astype(BF)

    t0[...] = nt(mixb[...], wco[...])

    def after_cross(rs):
        scv = stream_b[rs, :] + t0[rs, :]
        stream_c[rs, :] = scv
        n, _ = normed(scv)
        hid_c[rs, :] = (n * (1.0 + sf) + bf_).astype(BF)

    row_loop(ROWS, 32, after_cross)

    acc0[...] = jnp.zeros_like(acc0)
    acc1[...] = jnp.zeros_like(acc1)

    @pl.loop(0, 4)
    def _(ft):
        cols = pl.ds(pl.multiple_of(ft * 512, 512), 512)
        t0[...] = nn(hid_c[...], wup[:, cols])
        t1[...] = nn(cot[...], wdn[:, cols])

        def gelu(rs):
            u = t0[rs, :]
            phi = 0.5 * (1.0 + lax.erf(u * (2.0**-0.5)))
            b0[rs, :] = (u * phi).astype(BF)
            slope = phi + u * (jnp.exp(-0.5 * u * u) * (1.0 / math.sqrt(2.0 * math.pi)))
            b1[rs, :] = (t1[rs, :] * slope).astype(BF)

        row_loop(ROWS, 32, gelu)
        acc0[...] += nt(b0[...], wdn[:, cols])
        acc1[...] += nt(b1[...], wup[:, cols])
        g_dn[:, cols] = tn(cot[...], b0[...]).astype(BF)
        g_up[:, cols] = tn(hid_c[...], b1[...]).astype(BF)

    def fold_mod(at, sums):
        mgrad[at : at + 1, :] = sums[0]
        mgrad[at + 1 : at + 2, :] = sums[1]

    def back_norm(at, scale, grad_src, stream_src, base_src, want_out):
        mgrad[at : at + 2, :] = jnp.zeros((2, D), F)

        def body(rs):
            back, ds, db = norm_back(grad_src[rs, :], stream_src[rs, :], scale)
            total = base_src[rs, :].astype(F) + back
            gstream[rs, :] = total
            gbf[rs, :] = total.astype(BF)
            mgrad[at : at + 1, :] += ds
            mgrad[at + 1 : at + 2, :] += db
            if want_out:
                out_ref[rs, :] = (stream_c[rs, :] + acc0[rs, :]).astype(BF)

        row_loop(ROWS, 32, body)

    back_norm(4, sf, acc1, stream_c, cot, True)

    g_co[...] = tn(gbf[...], mixb[...]).astype(BF)
    mgr[...] = nn(gbf[...], wco[...]).astype(BF)

    @pl.loop(0, 4)
    def _(hp):
        lanes = pl.ds(pl.multiple_of(hp * 128, 128), 128)
        prod = mgr[:, lanes].astype(F) * mixb[:, lanes].astype(F)
        dqs, dks, dvs = [], [], []
        for half in range(2):
            h = hp * 2 + half
            inner = jnp.sum(keep(prod, half), axis=-1, keepdims=True)
            mg = keep(mgr[:, lanes], half)
            dp = nt(mg, venc[:, lanes])
            b0[...] = (pe[h].astype(F) * (dp - inner)).astype(BF)
            dqs.append(nn(b0[...], kenc[:, lanes]))
            dks.append(tn(b0[...], keep(qb[:, lanes], half)))
            dvs.append(tn(pe[h], mg))
        dq[:, lanes] = (jnp.where(half_lanes(dqs[0].shape, 0), dqs[0], dqs[1]) * 0.125).astype(BF)
        dkb[0:ENC, lanes] = (dks[0] + dks[1]).astype(BF)
        dvb[0:ENC, lanes] = (dvs[0] + dvs[1]).astype(BF)

    g_cqkv[0] = tn(hid_b[...], dq[...]).astype(BF)
    g_cqkv[1] = tn(enc[...], dkb[0:ENC, :]).astype(BF)
    g_cqkv[2] = tn(enc[...], dvb[0:ENC, :]).astype(BF)
    egrad[...] = (nt(dkb[0:ENC, :], wcqkv[1]) + nt(dvb[0:ENC, :], wcqkv[2])).astype(BF)
    acc1[...] = nt(dq[...], wcqkv[0])
    back_norm(2, sb, acc1, stream_b, gstream, False)

    g_so[...] = tn(gbf[...], mixa[...]).astype(BF)
    mgr[...] = nn(gbf[...], wso[...]).astype(BF)

    @pl.when(odd == 0)
    def _():
        for h in range(8):
            ps[h, ROWS:LOC, :] = jnp.zeros((LOC - ROWS, 256), BF)
        spec_o[:, ROWS:LOC, :] = jnp.zeros((2, LOC - ROWS, 128), F)

    @pl.when(odd == 1)
    def _():
        for h in range(8):
            ps[h, 0:64, :] = jnp.zeros((64, 256), BF)
        spec_o[:, 0:64, :] = jnp.zeros((2, 64, 128), F)

    @pl.loop(0, 4)
    def _(hp):
        lanes = pl.ds(pl.multiple_of(hp * 128, 128), 128)
        prod = mgr[:, lanes].astype(F) * mixa[:, lanes].astype(F)
        dqs, dks, dvs = [], [], []
        dks_s = [[], [], []]
        dvs_s = [[], [], []]
        for half in range(2):
            h = hp * 2 + half
            inner = jnp.sum(keep(prod, half), axis=-1, keepdims=True)
            mg = keep(mgr[:, lanes], half)
            qm = keep(qbuf[own, lanes], half)
            dp = nt(mg, vbuf[0:TRK, lanes])
            ds = (pt[h].astype(F) * (dp - inner)).astype(BF)
            spec_o[0, own, :] = mg.astype(F)
            spec_o[1, own, :] = jnp.broadcast_to(inner, (ROWS, 128))
            dq_s = []
            for lb in range(3):
                r = slice(lb * BLK, (lb + 1) * BLK)
                k_rows = slice(TRK + lb * 256, TRK + (lb + 1) * 256)
                mgl = spec_o[0, r, :].astype(BF)
                dpl = nt(mgl, vbuf[k_rows, lanes])
                inner_l = spec_o[1, r, 0:1]
                dsl = (ps[h, r, :].astype(F) * (dpl - inner_l)).astype(BF)
                ss[r, 0:128] = nn(dsl, kbuf[k_rows, lanes])
                dks_s[lb].append(tn(dsl, keep(qbuf[r, lanes], half)))
                dvs_s[lb].append(tn(ps[h, r, :], mgl))
            dqs.append(nn(ds, kbuf[0:TRK, lanes]) + ss[own, 0:128])
            dks.append(tn(ds, qm))
            dvs.append(tn(pt[h], mg))
        dq[:, lanes] = (jnp.where(half_lanes(dqs[0].shape, 0), dqs[0], dqs[1]) * 0.125).astype(BF)
        dkb[0:TRK, lanes] = (dks[0] + dks[1]).astype(BF)
        dvb[0:TRK, lanes] = (dvs[0] + dvs[1]).astype(BF)
        for lb in range(3):
            k_rows = slice(TRK + lb * 256, TRK + (lb + 1) * 256)
            dkb[k_rows, lanes] = (dks_s[lb][0] + dks_s[lb][1]).astype(BF)
            dvb[k_rows, lanes] = (dvs_s[lb][0] + dvs_s[lb][1]).astype(BF)

    wk_acc[...] = jnp.zeros_like(wk_acc)
    wv_acc[...] = jnp.zeros_like(wv_acc)

    def key_side(rs):
        gkv[rs, :] = nt(dkb[rs, :], wqkv[1]) + nt(dvb[rs, :], wqkv[2])
        wk_acc[...] += tn(hid[rs, :], dkb[rs, :])
        wv_acc[...] += tn(hid[rs, :], dvb[rs, :])

    row_loop(KV, 256, key_side)
    g_qkv[0] = tn(hloc[own, :], dq[...]).astype(BF)
    g_qkv[1] = wk_acc[...].astype(BF)
    g_qkv[2] = wv_acc[...].astype(BF)
    gown[...] = nt(dq[...], wqkv[0])

    def put_trunk(rs):
        gpart[rs, :] = gkv[rs, :].astype(BF)

    row_loop(TRK, 32, put_trunk)
    for b in range(BRANCHES):
        for piece in range(4):
            total = jnp.zeros((32, D), F)
            for lb in range(3):
                hit = jnp.logical_and(
                    base + lb >= TRUNK + BRANCHES, parents_ref[0, base + lb] == TRUNK + b
                )
                part = gkv[TRK + lb * 256 + piece * 32 : TRK + lb * 256 + piece * 32 + 32, :]
                total += jnp.where(hit, part, 0.0)
            at = TRK + b * BLK + piece * 32
            gpart[at : at + 32, :] = total.astype(BF)
    for lb in range(3):
        gpart[SHARED + lb * BLK : SHARED + (lb + 1) * BLK, :] = gkv[
            TRK + lb * 256 + BLK : TRK + (lb + 1) * 256, :
        ].astype(BF)


def layer_call(parents, tok_tb, tok_loc, enc, cot, mod, weights):
    vm = pl.BlockSpec(memory_space=pltpu.VMEM)
    sds = jax.ShapeDtypeStruct
    return pl.pallas_call(
        layer_kernel,
        out_shape=(
            sds((ROWS, D), BF),
            sds((ROWS, D), F),
            sds((SHARED + LOC, D), BF),
            sds((ROWS, D), F),
            sds((ENC, D), BF),
            sds((8, D), F),
            sds((3, D, D), BF),
            sds((D, D), BF),
            sds((3, D, D), BF),
            sds((D, D), BF),
            sds((D, FF), BF),
            sds((D, FF), BF),
        ),
        in_specs=[pl.BlockSpec(memory_space=pltpu.SMEM)] + [vm] * 11,
        out_specs=(vm,) * 12,
        scratch_shapes=[
            pltpu.VMEM((KV, D), BF),
            pltpu.VMEM((LOC, D), BF),
            pltpu.VMEM((KV, D), BF),
            pltpu.VMEM((KV, D), BF),
            pltpu.VMEM((LOC, D), BF),
            pltpu.VMEM((8, ROWS, TRK), BF),
            pltpu.VMEM((8, LOC, 256), BF),
            pltpu.VMEM((ROWS, TRK), F),
            pltpu.VMEM((LOC, 256), F),
            pltpu.VMEM((ROWS, TRK), F),
            pltpu.VMEM((LOC, 256), F),
            pltpu.VMEM((2, LOC, 128), F),
            pltpu.VMEM((ROWS, D), BF),
            pltpu.VMEM((ROWS, D), F),
            pltpu.VMEM((ROWS, D), F),
            pltpu.VMEM((ROWS, D), BF),
            pltpu.VMEM((ROWS, D), BF),
            pltpu.VMEM((ENC, D), BF),
            pltpu.VMEM((ENC, D), BF),
            pltpu.VMEM((ROWS, D), BF),
            pltpu.VMEM((8, ROWS, ENC), BF),
            pltpu.VMEM((ROWS, D), BF),
            pltpu.VMEM((ROWS, D), F),
            pltpu.VMEM((ROWS, D), F),
            pltpu.VMEM((ROWS, D), BF),
            pltpu.VMEM((ROWS, D), BF),
            pltpu.VMEM((ROWS, D), F),
            pltpu.VMEM((ROWS, D), F),
            pltpu.VMEM((ROWS, D), BF),
            pltpu.VMEM((ROWS, D), BF),
            pltpu.VMEM((ROWS, D), BF),
            pltpu.VMEM((KV, D), BF),
            pltpu.VMEM((KV, D), BF),
            pltpu.VMEM((KV, D), F),
            pltpu.VMEM((D, D), F),
            pltpu.VMEM((D, D), F),
        ],
        compiler_params=pltpu.CompilerParams(vmem_limit_bytes=VMEM_LIMIT),
        name="layer",
    )(parents, tok_tb, tok_loc, enc, cot, mod, *weights)


def timestep_code(timesteps, width):
    half = width // 2
    frequency = jnp.exp(-math.log(10000.0) * jnp.arange(half, dtype=F) / half)
    angles = timesteps.astype(F)[:, None] * frequency[None, :]
    return jnp.concatenate([jnp.sin(angles), jnp.cos(angles)], axis=-1)


def per_device(
    tokens,
    encoder_states,
    timesteps,
    parents,
    w_mod,
    w_self_qkv,
    w_self_out,
    w_cross_qkv,
    w_cross_out,
    w_up,
    w_down,
    cotangent,
):
    fs = lax.axis_index("fsdp")
    rows = w_mod.shape[0]
    ci = lax.axis_index("ctx") * 2 + lax.axis_index("tp")
    condition = jax.nn.silu(timestep_code(timesteps, D)).astype(BF)
    cond_all = lax.all_gather(condition, "fsdp", axis=0, tiled=True)
    part = jnp.dot(
        lax.dynamic_slice(cond_all, (0, fs * rows), (cond_all.shape[0], rows)),
        w_mod,
        preferred_element_type=F,
    )
    mod = lax.psum_scatter(part, "fsdp", scatter_dimension=0, tiled=True).reshape(6, D)
    mod = jnp.concatenate([mod, jnp.zeros((2, D), F)])

    def whole(w, axis):
        return lax.all_gather(
            lax.all_gather(w, "fsdp", axis=axis, tiled=True), "tp", axis=axis + 1, tiled=True
        )

    weights = (
        whole(w_self_qkv, 1),
        whole(w_self_out, 0),
        whole(w_cross_qkv, 1),
        whole(w_cross_out, 0),
        whole(w_up, 0),
        whole(w_down, 0),
    )
    every = lax.all_gather(tokens[0], ("ctx", "tp"), axis=0, tiled=True)
    enc = lax.all_gather(encoder_states[0], "ctx", axis=0, tiled=True)
    off = lax.rem(ci, 2) * 64
    padded = jnp.concatenate([every, jnp.zeros((64, D), BF)])
    tok_loc = lax.dynamic_slice(padded, (ci * ROWS - off, 0), (LOC, D))
    (out, gstream, gpart, gown, egrad, mgrad, g_qkv, g_so, g_cqkv, g_co, g_up, g_dn) = layer_call(
        parents, every[:SHARED], tok_loc, enc, cotangent[0], mod, weights
    )
    total = jnp.zeros(padded.shape, F)
    total = total.at[:SHARED].set(gpart[:SHARED].astype(F))
    window = lax.dynamic_slice(total, (ci * ROWS - off, 0), (LOC, D)) + gpart[SHARED:].astype(F)
    total = lax.dynamic_update_slice(total, window, (ci * ROWS - off, 0))
    mine = lax.psum_scatter(
        total[: every.shape[0]].astype(BF), ("ctx", "tp"), scatter_dimension=0, tiled=True
    )
    hidden_grad = mine.astype(F) + gown
    stream_grad, ds, db = norm_back(hidden_grad, tokens[0].astype(F), mod[0:1])
    input_grad = gstream + stream_grad
    mod_terms = jnp.concatenate([ds, db, mgrad[2:6]]).reshape(1, 6 * D)
    mod_total = lax.psum(mod_terms, ("ctx", "tp"))
    mod_all = lax.all_gather(mod_total, "fsdp", axis=0, tiled=True)
    cond_mine = lax.dynamic_slice(cond_all, (0, fs * rows), (cond_all.shape[0], rows)).astype(F)
    grad_mod = jnp.dot(cond_mine.T, mod_all, precision=lax.Precision.HIGHEST)
    enc_grad = lax.psum(egrad.astype(F), "tp")
    enc_grad = lax.psum_scatter(enc_grad, "ctx", scatter_dimension=0, tiled=True)

    def owned(g, axis):
        g = lax.psum_scatter(g, "tp", scatter_dimension=axis + 1, tiled=True)
        g = lax.psum(g, "ctx")
        return lax.psum_scatter(g, "fsdp", scatter_dimension=axis, tiled=True).astype(F)

    return (
        out[None],
        input_grad[None],
        enc_grad[None],
        grad_mod,
        owned(g_qkv, 1),
        owned(g_so, 0),
        owned(g_cqkv, 1),
        owned(g_co, 0),
        owned(g_up, 0),
        owned(g_dn, 0),
    )


def solution(mesh):
    rows = P("fsdp", ("ctx", "tp"), None)
    return jax.shard_map(
        per_device,
        mesh=mesh,
        in_specs=(
            rows,
            P("fsdp", "ctx", None),
            P("fsdp"),
            P("fsdp", None),
            P("fsdp", None),
            P(None, "fsdp", "tp"),
            P("fsdp", "tp"),
            P(None, "fsdp", "tp"),
            P("fsdp", "tp"),
            P("fsdp", "tp"),
            P("fsdp", "tp"),
            rows,
        ),
        out_specs=(
            rows,
            rows,
            P("fsdp", "ctx", None),
            P("fsdp", None),
            P(None, "fsdp", "tp"),
            P("fsdp", "tp"),
            P(None, "fsdp", "tp"),
            P("fsdp", "tp"),
            P("fsdp", "tp"),
            P("fsdp", "tp"),
        ),
        check_vma=False,
    )
```

```python
import functools
import math

import jax
import jax.numpy as jnp
from jax import lax
from jax.experimental import pallas as pl
from jax.experimental.pallas import tpu as pltpu
from jax.sharding import PartitionSpec as P

BF = jnp.bfloat16
F = jnp.float32
D = 512
FF = 2048
HD = 64
ROWS = 320
LOC = 384
BLK = 128
TRUNK = 8
BRANCHES = 4
TRK = TRUNK * BLK
SHARED = (TRUNK + BRANCHES) * BLK
SPEC = 2 * LOC
KV = TRK + SPEC
ENC = 512
EPS = 1e-05
NEG = -1e30
VMEM_LIMIT = 67043328


def nn(a, b):
    return lax.dot_general(a, b, (((1,), (0,)), ((), ())), preferred_element_type=F)


def nt(a, b):
    return lax.dot_general(a, b, (((1,), (1,)), ((), ())), preferred_element_type=F)


def tn(a, b):
    return lax.dot_general(a, b, (((0,), (0,)), ((), ())), preferred_element_type=F)


def normed(v):
    center = v - jnp.mean(v, axis=-1, keepdims=True)
    rstd = lax.rsqrt(jnp.mean(center * center, axis=-1, keepdims=True) + EPS)
    return center * rstd, rstd


def norm_back(grad, stream, scale):
    n, rstd = normed(stream)
    gn = grad * (1.0 + scale)
    back = rstd * (
        gn
        - jnp.mean(gn, axis=-1, keepdims=True)
        - n * jnp.mean(gn * n, axis=-1, keepdims=True)
    )
    return back, jnp.sum(grad * n, axis=0, keepdims=True), jnp.sum(grad, axis=0, keepdims=True)


def row_loop(total, step, body):
    @pl.loop(0, total // step)
    def _(i):
        body(pl.ds(pl.multiple_of(i * step, step), step))


def half_lanes(shape, half):
    lane = lax.broadcasted_iota(jnp.int32, shape, len(shape) - 1)
    return (lane // HD) == half


def keep(value, half):
    return jnp.where(half_lanes(value.shape, half), value, jnp.zeros_like(value))


MESH = pl.DeviceIdType.MESH


class Wire:
    def __init__(self, send, recv):
        self.send, self.recv, self.used, self.sent = send, recv, 0, []

    def slot(self, count=1):
        self.used += count
        return self.used - count

    def copy(self, src, dst, at, to):
        return pltpu.make_async_remote_copy(
            src_ref=src,
            dst_ref=dst,
            send_sem=self.send.at[at],
            recv_sem=self.recv.at[at],
            device_id=to,
            device_id_type=MESH,
        )

    def push(self, dst, at, to, when=None, src=None):
        src = src or dst
        if when is None:
            self.copy(src(), dst(), at, to).start()
        else:

            @pl.when(when)
            def _():
                self.copy(src(), dst(), at, to).start()

        self.sent.append((src, dst, at, to, when))

    def arrived(self, dst, at, to, when=None):
        if when is None:
            self.copy(dst, dst, at, to).wait_recv()
        else:

            @pl.when(when)
            def _():
                self.copy(dst, dst, at, to).wait_recv()

    def drain(self):
        for src, dst, at, to, when in self.sent:
            if when is None:
                self.copy(src(), dst(), at, to).wait_send()
            else:

                @pl.when(when)
                def _(src=src, dst=dst, at=at, to=to):
                    self.copy(src(), dst(), at, to).wait_send()

        self.sent = []


def layer_kernel(
    n,
    parents_ref,
    cond_parts,
    w_mod,
    tok_in,
    enc_in,
    cot,
    w_sqkv,
    w_so,
    w_cqkv,
    w_co,
    w_up,
    w_dn,
    out_ref,
    gstream,
    gpart,
    gown,
    egrad,
    mgrad,
    mod,
    cond_all,
    g_qkv,
    g_so,
    g_cqkv,
    g_co,
    g_up,
    g_dn,
    watt,
    wup,
    wdn,
    tok,
    enc,
    part_out,
    part_in,
    hid,
    hloc,
    kbuf,
    vbuf,
    qbuf,
    pt,
    ps,
    bias_t,
    bias_s,
    st,
    ss,
    spec_o,
    mixa,
    stream_b,
    stream_c,
    hid_b,
    hid_c,
    kenc,
    venc,
    qb,
    pe,
    mixb,
    t0,
    t1,
    b0,
    b1,
    acc0,
    acc1,
    gbf,
    mgr,
    dq,
    dkb,
    dvb,
    gkv,
    wk_acc,
    wv_acc,
    send,
    recv,
    local,
):
    fs = lax.axis_index("fsdp")
    cx = lax.axis_index("ctx")
    y = lax.axis_index("tp")
    x, c = cx // 2, lax.rem(cx, 2)
    ci = cx * 2 + y
    odd = y
    off = pl.multiple_of(odd * 64, 64)
    own = pl.ds(off, ROWS)
    base = (ci * 5) // 2
    rows = w_mod.shape[0]
    to_y = {"tp": 1 - y}
    to_c = {"ctx": 2 * x + 1 - c}
    to_x = {"ctx": 2 * (1 - x) + c}
    wire = Wire(send, recv)

    my_rows = pl.ds(pl.multiple_of(fs * rows, rows), rows)

    def att_cols(yy, cc):
        return pl.ds(pl.multiple_of(yy * 256 + cc * 128, 128), 128)

    def ffn_cols(yy, xx, cc):
        return pl.ds(pl.multiple_of(yy * 1024 + xx * 512 + cc * 256, 256), 256)

    half = pl.ds(pl.multiple_of(c * 128, 128), 128)
    quarter = pl.ds(pl.multiple_of(cx * 256, 256), 256)
    groups = (
        (w_sqkv.at[:, :, half], watt, slice(0, 3), 0),
        (w_so.at[:, half], watt, 3, 0),
        (w_cqkv.at[:, :, half], watt, slice(4, 7), 0),
        (w_co.at[:, half], watt, 7, 0),
        (w_up.at[:, quarter], wup, None, 1),
        (w_dn.at[:, quarter], wdn, None, 1),
    )

    def place(g, row_at, yy, xx, cc):
        _, buf, index, wide = groups[g]
        if wide:
            return buf.at[row_at, ffn_cols(yy, xx, cc)]
        return buf.at[index, row_at, att_cols(yy, cc)]

    def chunk(i):
        return tok.at[pl.ds(pl.multiple_of(i * ROWS, ROWS), ROWS), :]

    def enc_part(i):
        return enc.at[pl.ds(pl.multiple_of(i * 128, 128), 128), :]

    all_rows = pl.ds(0, D)

    local_copies = [
        pltpu.make_async_copy(tok_in.at[0], chunk(ci), local.at[0]),
        pltpu.make_async_copy(enc_in.at[0], enc_part(cx), local.at[1]),
    ] + [
        pltpu.make_async_copy(groups[g][0], place(g, my_rows, y, x, c), local.at[2 + g])
        for g in range(6)
    ]
    for copy in local_copies:
        copy.start()

    barrier = pltpu.get_barrier_semaphore()

    @pl.loop(1, n)
    def _(k):
        pl.semaphore_signal(
            barrier, inc=1, device_id={"fsdp": lax.rem(fs + k, n)}, device_id_type=MESH
        )

    @pl.loop(1, 8)
    def _(k):
        other = lax.rem(ci + k, 8)
        pl.semaphore_signal(
            barrier,
            inc=1,
            device_id={"ctx": other // 2, "tp": lax.rem(other, 2)},
            device_id_type=MESH,
        )

    pl.semaphore_wait(barrier, n - 1 + 7)

    def peers(make):
        @pl.loop(1, n)
        def _(k):
            make(k, lax.rem(fs + k, n), lax.rem(fs + n - k, n))

    s_cond = wire.slot(n)
    s_part = wire.slot(n)
    s_z = [wire.slot(n) for _ in range(6)]
    s_y = [wire.slot() for _ in range(6)]
    s_c0 = [wire.slot() for _ in range(6)]
    s_c1 = [wire.slot() for _ in range(6)]
    s_x0 = [wire.slot() for _ in range(6)]
    s_x1 = [wire.slot() for _ in range(6)]
    s_c2 = [wire.slot() for _ in range(6)]
    s_c3 = [wire.slot() for _ in range(6)]
    s_ty, s_tx, s_txy, s_tc0, s_tc1, s_tc2, s_tc3 = (wire.slot() for _ in range(7))
    s_ex, s_ec0, s_ec1 = (wire.slot() for _ in range(3))

    peers(
        lambda k, to, _: wire.copy(
            cond_parts.at[to], cond_all.at[fs], s_cond + k, {"fsdp": to}
        ).start()
    )
    wire.push(lambda: chunk(ci), s_ty, to_y, None, lambda: tok_in.at[0])
    wire.push(lambda: chunk(ci), s_tx, to_x, x == 0, lambda: tok_in.at[0])
    wire.push(lambda: chunk(ci), s_tc0, to_c, None, lambda: tok_in.at[0])
    for g in range(6):
        peers(
            lambda k, to, _, g=g: wire.copy(
                groups[g][0], place(g, my_rows, y, x, c), s_z[g] + k, {"fsdp": to}
            ).start()
        )
    wire.push(lambda: enc_part(cx), s_ex, to_x, None, lambda: enc_in.at[0])
    wire.push(lambda: enc_part(cx), s_ec0, to_c, None, lambda: enc_in.at[0])

    cond_all[fs] = cond_parts[fs]
    peers(lambda k, _, src: wire.arrived(cond_all.at[src], s_cond + k, {"fsdp": src}))
    for v in range(6):
        part_out[:, v, :] = nn(
            cond_all[:, 0, 0:rows].astype(BF), w_mod[:, v * D : (v + 1) * D]
        )
    part_out[:, 6:8, :] = jnp.zeros((n, 2, D), F)
    peers(
        lambda k, to, _: wire.copy(
            part_out.at[to], part_in.at[fs], s_part + k, {"fsdp": to}
        ).start()
    )
    part_in[fs] = part_out[fs]

    def z_done(g):
        local_copies[2 + g].wait()
        peers(
            lambda k, _, src: wire.arrived(
                place(g, pl.ds(pl.multiple_of(src * rows, rows), rows), y, x, c),
                s_z[g] + k,
                {"fsdp": src},
            )
        )
        slab = lambda: place(g, all_rows, y, x, c)
        wire.push(slab, s_y[g], to_y)
        if groups[g][3]:
            wire.push(slab, s_x0[g], to_x)
        wire.push(slab, s_c0[g], to_c)

    def y_done(g):
        slab = lambda: place(g, all_rows, 1 - y, x, c)
        wire.arrived(slab(), s_y[g], to_y)
        if groups[g][3]:
            wire.push(slab, s_x1[g], to_x)
        wire.push(slab, s_c1[g], to_c)

    def x_done(g):
        for yy, s_in, s_out in ((y, s_x0[g], s_c2[g]), (1 - y, s_x1[g], s_c3[g])):
            slab = lambda yy=yy: place(g, all_rows, yy, 1 - x, c)
            wire.arrived(slab(), s_in, to_x)
            wire.push(slab, s_out, to_c)

    def c_done(g):
        wire.arrived(place(g, all_rows, y, x, 1 - c), s_c0[g], to_c)
        wire.arrived(place(g, all_rows, 1 - y, x, 1 - c), s_c1[g], to_c)
        if groups[g][3]:
            wire.arrived(place(g, all_rows, y, 1 - x, 1 - c), s_c2[g], to_c)
            wire.arrived(place(g, all_rows, 1 - y, 1 - x, 1 - c), s_c3[g], to_c)

    local_copies[0].wait()
    local_copies[1].wait()
    ciy = 4 * x + 2 * c + 1 - y
    cic = 4 * x + 2 * (1 - c) + y
    ciyc = 4 * x + 2 * (1 - c) + 1 - y
    low, lowy, lowc, lowyc = 2 * c + y, 2 * c + 1 - y, 2 * (1 - c) + y, 2 * (1 - c) + 1 - y
    right = x == 1
    wire.arrived(chunk(ciy), s_ty, to_y)
    wire.push(lambda: chunk(ciy), s_txy, to_x, x == 0)
    wire.push(lambda: chunk(ciy), s_tc1, to_c)
    wire.arrived(chunk(low), s_tx, to_x, right)
    wire.push(lambda: chunk(low), s_tc2, to_c, right)
    z_done(0)
    wire.arrived(enc_part(2 * (1 - x) + c), s_ex, to_x)
    wire.push(lambda: enc_part(2 * (1 - x) + c), s_ec1, to_c)
    wire.arrived(chunk(lowy), s_txy, to_x, right)
    wire.push(lambda: chunk(lowy), s_tc3, to_c, right)
    y_done(0)

    peers(lambda k, _, src: wire.arrived(part_in.at[src], s_part + k, {"fsdp": src}))
    mod[...] = jnp.sum(part_in[...], axis=0)
    sa, ba = mod[0:1, :], mod[1:2, :]
    sb, bb = mod[2:3, :], mod[3:4, :]
    sf, bf_ = mod[4:5, :], mod[5:6, :]

    wire.arrived(chunk(cic), s_tc0, to_c)
    wire.arrived(chunk(ciyc), s_tc1, to_c)
    wire.arrived(chunk(lowc), s_tc2, to_c, right)
    wire.arrived(chunk(lowyc), s_tc3, to_c, right)
    wire.arrived(enc_part(2 * x + 1 - c), s_ec0, to_c)
    wire.arrived(enc_part(2 * (1 - x) + 1 - c), s_ec1, to_c)
    tok_tb = tok
    tok_loc = tok.at[pl.ds(pl.multiple_of(ci * ROWS - off, 64), LOC), :]

    def relay(step):
        if step == 0:
            z_done(1)
            z_done(2)
            z_done(3)
        if step == 1:
            for g in (1, 2, 3):
                y_done(g)
            z_done(4)
        if step == 2:
            z_done(5)
            for g in (1, 2, 3):
                c_done(g)
        if step == 3:
            y_done(4)
            x_done(4)
        if step == 4:
            y_done(5)
            x_done(5)
        if step == 5:
            c_done(4)
            c_done(5)

    def is_parent(lb, branch):
        parent = jnp.full((32, D), parents_ref[0, base + lb], jnp.int32)
        leaf = jnp.full((32, D), base + lb, jnp.int32) >= TRUNK + BRANCHES
        return jnp.logical_and(leaf, parent == TRUNK + branch)

    def mask_trunk(rs):
        row = lax.broadcasted_iota(jnp.int32, (32, TRK), 0) + rs.start + ci * ROWS
        col = lax.broadcasted_iota(jnp.int32, (32, TRK), 1)
        bias_t[rs, :] = jnp.where(col <= row, 0.0, NEG)

    row_loop(ROWS, 32, mask_trunk)
    for lb in range(3):
        blk = base + lb
        row = lax.broadcasted_iota(jnp.int32, (BLK, 2 * BLK), 0)
        col = lax.broadcasted_iota(jnp.int32, (BLK, 2 * BLK), 1)
        par_ok = jnp.logical_and(col < BLK, blk >= TRUNK + BRANCHES)
        self_ok = jnp.logical_and(
            jnp.logical_and(col >= BLK, col - BLK <= row), blk >= TRUNK
        )
        bias_s[lb * BLK : (lb + 1) * BLK, :] = jnp.where(
            jnp.logical_or(par_ok, self_ok), 0.0, NEG
        )

    def hidden(x):
        n, _ = normed(x.astype(F))
        return (n * (1.0 + sa) + ba).astype(BF)

    def hid_trunk(rs):
        hid[rs, :] = hidden(tok_tb[rs, :])

    row_loop(TRK, 32, hid_trunk)

    def hid_loc(rs):
        hloc[rs, :] = hidden(tok_loc[rs, :])

    row_loop(LOC, 32, hid_loc)
    for lb in range(3):
        picks = [is_parent(lb, b) for b in range(1, BRANCHES)]
        for piece in range(4):
            r = piece * 32
            picked = tok_tb[TRK + r : TRK + r + 32, :].astype(F)
            for b in range(1, BRANCHES):
                at = TRK + b * BLK + r
                picked = jnp.where(picks[b - 1], tok_tb[at : at + 32, :].astype(F), picked)
            at = TRK + lb * 256 + r
            hid[at : at + 32, :] = hidden(picked)
        hid[TRK + lb * 256 + BLK : TRK + lb * 256 + 2 * BLK, :] = hloc[
            lb * BLK : (lb + 1) * BLK, :
        ]

    def project(rs):
        kbuf[rs, :] = nn(hid[rs, :], watt[1]).astype(BF)
        vbuf[rs, :] = nn(hid[rs, :], watt[2]).astype(BF)

    c_done(0)
    row_loop(KV, 256, project)
    relay(0)
    qbuf[...] = (nn(hloc[...], watt[0]) * 0.125).astype(BF)

    @pl.loop(0, 4)
    def _(hp):
        @pl.when(hp == 2)
        def _():
            relay(1)

        lanes = pl.ds(pl.multiple_of(hp * 128, 128), 128)
        kt = kbuf[0:TRK, lanes]
        for half in range(2):
            h = hp * 2 + half
            st[...] = nt(keep(qbuf[own, lanes], half), kt)
            for lb in range(3):
                r = slice(lb * BLK, (lb + 1) * BLK)
                ks = kbuf[TRK + lb * 256 : TRK + (lb + 1) * 256, lanes]
                ss[r, :] = nt(keep(qbuf[r, lanes], half), ks)

            @pl.loop(0, ROWS // 32)
            def _(i):
                rs = pl.ds(pl.multiple_of(i * 32, 32), 32)
                ro = pl.ds(pl.multiple_of(i * 32 + off, 32), 32)
                a = st[rs, :] + bias_t[rs, :]
                b = ss[ro, :] + bias_s[ro, :]
                top = jnp.maximum(
                    jnp.max(a, axis=-1, keepdims=True), jnp.max(b, axis=-1, keepdims=True)
                )
                a = jnp.exp(a - top)
                b = jnp.exp(b - top)
                inv = 1.0 / (
                    jnp.sum(a, axis=-1, keepdims=True) + jnp.sum(b, axis=-1, keepdims=True)
                )
                pt[h, rs, :] = (a * inv).astype(BF)
                ps[h, ro, :] = (b * inv).astype(BF)

            for lb in range(3):
                r = slice(lb * BLK, (lb + 1) * BLK)
                vs = vbuf[TRK + lb * 256 : TRK + (lb + 1) * 256, lanes]
                spec_o[half, r, :] = nn(ps[h, r, :], vs)
        vt = vbuf[0:TRK, lanes]
        o0 = nn(pt[hp * 2], vt) + spec_o[0, own, :]
        o1 = nn(pt[hp * 2 + 1], vt) + spec_o[1, own, :]
        mixa[:, lanes] = jnp.where(half_lanes(o0.shape, 0), o0, o1).astype(BF)

    relay(2)
    t0[...] = nt(mixa[...], watt[3])

    def after_self(rs):
        ro = pl.ds(pl.multiple_of(rs.start + off, 32), 32)
        sbv = tok_loc[ro, :].astype(F) + t0[rs, :]
        stream_b[rs, :] = sbv
        n, _ = normed(sbv)
        hid_b[rs, :] = (n * (1.0 + sb) + bb).astype(BF)

    row_loop(ROWS, 32, after_self)

    relay(3)
    kenc[...] = nn(enc[...], watt[5]).astype(BF)
    venc[...] = nn(enc[...], watt[6]).astype(BF)
    qb[...] = (nn(hid_b[...], watt[4]) * 0.125).astype(BF)

    @pl.loop(0, 4)
    def _(hp):
        lanes = pl.ds(pl.multiple_of(hp * 128, 128), 128)
        kt = kenc[:, lanes]
        for half in range(2):
            h = hp * 2 + half
            t0[...] = nt(keep(qb[:, lanes], half), kt)

            @pl.loop(0, ROWS // 32)
            def _(i):
                rs = pl.ds(pl.multiple_of(i * 32, 32), 32)
                a = t0[rs, :]
                a = jnp.exp(a - jnp.max(a, axis=-1, keepdims=True))
                inv = 1.0 / jnp.sum(a, axis=-1, keepdims=True)
                pe[h, rs, :] = (a * inv).astype(BF)

        vt = venc[:, lanes]
        o0 = nn(pe[hp * 2], vt)
        o1 = nn(pe[hp * 2 + 1], vt)
        mixb[:, lanes] = jnp.where(half_lanes(o0.shape, 0), o0, o1).astype(BF)

    relay(4)
    t0[...] = nt(mixb[...], watt[7])

    def after_cross(rs):
        scv = stream_b[rs, :] + t0[rs, :]
        stream_c[rs, :] = scv
        n, _ = normed(scv)
        hid_c[rs, :] = (n * (1.0 + sf) + bf_).astype(BF)

    row_loop(ROWS, 32, after_cross)

    relay(5)
    acc0[...] = jnp.zeros_like(acc0)
    acc1[...] = jnp.zeros_like(acc1)

    @pl.loop(0, 4)
    def _(ft):
        cols = pl.ds(pl.multiple_of(ft * 512, 512), 512)
        t0[...] = nn(hid_c[...], wup[:, cols])
        t1[...] = nn(cot[...], wdn[:, cols])

        def gelu(rs):
            u = t0[rs, :]
            phi = 0.5 * (1.0 + lax.erf(u * (2.0**-0.5)))
            b0[rs, :] = (u * phi).astype(BF)
            slope = phi + u * (jnp.exp(-0.5 * u * u) * (1.0 / math.sqrt(2.0 * math.pi)))
            b1[rs, :] = (t1[rs, :] * slope).astype(BF)

        row_loop(ROWS, 32, gelu)
        acc0[...] += nt(b0[...], wdn[:, cols])
        acc1[...] += nt(b1[...], wup[:, cols])
        g_dn[:, cols] = tn(cot[...], b0[...]).astype(BF)
        g_up[:, cols] = tn(hid_c[...], b1[...]).astype(BF)

    def fold_mod(at, sums):
        mgrad[at : at + 1, :] = sums[0]
        mgrad[at + 1 : at + 2, :] = sums[1]

    def back_norm(at, scale, grad_src, stream_src, base_src, want_out):
        mgrad[at : at + 2, :] = jnp.zeros((2, D), F)

        def body(rs):
            back, ds, db = norm_back(grad_src[rs, :], stream_src[rs, :], scale)
            total = base_src[rs, :].astype(F) + back
            gstream[rs, :] = total
            gbf[rs, :] = total.astype(BF)
            mgrad[at : at + 1, :] += ds
            mgrad[at + 1 : at + 2, :] += db
            if want_out:
                out_ref[rs, :] = (stream_c[rs, :] + acc0[rs, :]).astype(BF)

        row_loop(ROWS, 32, body)

    back_norm(4, sf, acc1, stream_c, cot, True)

    g_co[...] = tn(gbf[...], mixb[...]).astype(BF)
    mgr[...] = nn(gbf[...], watt[7]).astype(BF)

    @pl.loop(0, 4)
    def _(hp):
        lanes = pl.ds(pl.multiple_of(hp * 128, 128), 128)
        prod = mgr[:, lanes].astype(F) * mixb[:, lanes].astype(F)
        dqs, dks, dvs = [], [], []
        for half in range(2):
            h = hp * 2 + half
            inner = jnp.sum(keep(prod, half), axis=-1, keepdims=True)
            mg = keep(mgr[:, lanes], half)
            dp = nt(mg, venc[:, lanes])
            b0[...] = (pe[h].astype(F) * (dp - inner)).astype(BF)
            dqs.append(nn(b0[...], kenc[:, lanes]))
            dks.append(tn(b0[...], keep(qb[:, lanes], half)))
            dvs.append(tn(pe[h], mg))
        dq[:, lanes] = (jnp.where(half_lanes(dqs[0].shape, 0), dqs[0], dqs[1]) * 0.125).astype(BF)
        dkb[0:ENC, lanes] = (dks[0] + dks[1]).astype(BF)
        dvb[0:ENC, lanes] = (dvs[0] + dvs[1]).astype(BF)

    g_cqkv[0] = tn(hid_b[...], dq[...]).astype(BF)
    g_cqkv[1] = tn(enc[...], dkb[0:ENC, :]).astype(BF)
    g_cqkv[2] = tn(enc[...], dvb[0:ENC, :]).astype(BF)
    egrad[...] = (nt(dkb[0:ENC, :], watt[5]) + nt(dvb[0:ENC, :], watt[6])).astype(BF)
    acc1[...] = nt(dq[...], watt[4])
    back_norm(2, sb, acc1, stream_b, gstream, False)

    g_so[...] = tn(gbf[...], mixa[...]).astype(BF)
    mgr[...] = nn(gbf[...], watt[3]).astype(BF)

    @pl.when(odd == 0)
    def _():
        for h in range(8):
            ps[h, ROWS:LOC, :] = jnp.zeros((LOC - ROWS, 256), BF)
        spec_o[:, ROWS:LOC, :] = jnp.zeros((2, LOC - ROWS, 128), F)

    @pl.when(odd == 1)
    def _():
        for h in range(8):
            ps[h, 0:64, :] = jnp.zeros((64, 256), BF)
        spec_o[:, 0:64, :] = jnp.zeros((2, 64, 128), F)

    @pl.loop(0, 4)
    def _(hp):
        lanes = pl.ds(pl.multiple_of(hp * 128, 128), 128)
        prod = mgr[:, lanes].astype(F) * mixa[:, lanes].astype(F)
        dqs, dks, dvs = [], [], []
        dks_s = [[], [], []]
        dvs_s = [[], [], []]
        for half in range(2):
            h = hp * 2 + half
            inner = jnp.sum(keep(prod, half), axis=-1, keepdims=True)
            mg = keep(mgr[:, lanes], half)
            qm = keep(qbuf[own, lanes], half)
            dp = nt(mg, vbuf[0:TRK, lanes])
            ds = (pt[h].astype(F) * (dp - inner)).astype(BF)
            spec_o[0, own, :] = mg.astype(F)
            spec_o[1, own, :] = jnp.broadcast_to(inner, (ROWS, 128))
            dq_s = []
            for lb in range(3):
                r = slice(lb * BLK, (lb + 1) * BLK)
                k_rows = slice(TRK + lb * 256, TRK + (lb + 1) * 256)
                mgl = spec_o[0, r, :].astype(BF)
                dpl = nt(mgl, vbuf[k_rows, lanes])
                inner_l = spec_o[1, r, 0:1]
                dsl = (ps[h, r, :].astype(F) * (dpl - inner_l)).astype(BF)
                ss[r, 0:128] = nn(dsl, kbuf[k_rows, lanes])
                dks_s[lb].append(tn(dsl, keep(qbuf[r, lanes], half)))
                dvs_s[lb].append(tn(ps[h, r, :], mgl))
            dqs.append(nn(ds, kbuf[0:TRK, lanes]) + ss[own, 0:128])
            dks.append(tn(ds, qm))
            dvs.append(tn(pt[h], mg))
        dq[:, lanes] = (jnp.where(half_lanes(dqs[0].shape, 0), dqs[0], dqs[1]) * 0.125).astype(BF)
        dkb[0:TRK, lanes] = (dks[0] + dks[1]).astype(BF)
        dvb[0:TRK, lanes] = (dvs[0] + dvs[1]).astype(BF)
        for lb in range(3):
            k_rows = slice(TRK + lb * 256, TRK + (lb + 1) * 256)
            dkb[k_rows, lanes] = (dks_s[lb][0] + dks_s[lb][1]).astype(BF)
            dvb[k_rows, lanes] = (dvs_s[lb][0] + dvs_s[lb][1]).astype(BF)

    wk_acc[...] = jnp.zeros_like(wk_acc)
    wv_acc[...] = jnp.zeros_like(wv_acc)

    def key_side(rs):
        gkv[rs, :] = nt(dkb[rs, :], watt[1]) + nt(dvb[rs, :], watt[2])
        wk_acc[...] += tn(hid[rs, :], dkb[rs, :])
        wv_acc[...] += tn(hid[rs, :], dvb[rs, :])

    row_loop(KV, 256, key_side)
    g_qkv[0] = tn(hloc[own, :], dq[...]).astype(BF)
    g_qkv[1] = wk_acc[...].astype(BF)
    g_qkv[2] = wv_acc[...].astype(BF)
    gown[...] = nt(dq[...], watt[0])

    def put_trunk(rs):
        gpart[rs, :] = gkv[rs, :].astype(BF)

    row_loop(TRK, 32, put_trunk)
    for b in range(BRANCHES):
        for piece in range(4):
            total = jnp.zeros((32, D), F)
            for lb in range(3):
                hit = is_parent(lb, b)
                part = gkv[TRK + lb * 256 + piece * 32 : TRK + lb * 256 + piece * 32 + 32, :]
                total += jnp.where(hit, part, 0.0)
            at = TRK + b * BLK + piece * 32
            gpart[at : at + 32, :] = total.astype(BF)
    for lb in range(3):
        gpart[SHARED + lb * BLK : SHARED + (lb + 1) * BLK, :] = gkv[
            TRK + lb * 256 + BLK : TRK + (lb + 1) * 256, :
        ].astype(BF)

    wire.drain()
    peers(
        lambda k, to, _: wire.copy(
            cond_parts.at[to], cond_all.at[fs], s_cond + k, {"fsdp": to}
        ).wait_send()
    )
    peers(
        lambda k, to, _: wire.copy(
            part_out.at[to], part_in.at[fs], s_part + k, {"fsdp": to}
        ).wait_send()
    )
    for g in range(6):
        peers(
            lambda k, to, _, g=g: wire.copy(
                groups[g][0], place(g, my_rows, y, x, c), s_z[g] + k, {"fsdp": to}
            ).wait_send()
        )


def layer_call(n, parents, cond_parts, w_mod, tokens, enc, cot, weights):
    vm = pl.BlockSpec(memory_space=pltpu.VMEM)
    hbm = pl.BlockSpec(memory_space=pl.ANY)
    sds = jax.ShapeDtypeStruct
    return pl.pallas_call(
        functools.partial(layer_kernel, n),
        out_shape=(
            sds((ROWS, D), BF),
            sds((ROWS, D), F),
            sds((SHARED + LOC, D), BF),
            sds((ROWS, D), F),
            sds((ENC, D), BF),
            sds((8, D), F),
            sds((8, D), F),
            sds(cond_parts.shape, F),
            sds((3, D, D), BF),
            sds((D, D), BF),
            sds((3, D, D), BF),
            sds((D, D), BF),
            sds((D, FF), BF),
            sds((D, FF), BF),
        ),
        in_specs=[pl.BlockSpec(memory_space=pltpu.SMEM), vm, vm, hbm, hbm, vm] + [hbm] * 6,
        out_specs=(vm,) * 14,
        scratch_shapes=[
            pltpu.VMEM((8, D, D), BF),
            pltpu.VMEM((D, FF), BF),
            pltpu.VMEM((D, FF), BF),
            pltpu.VMEM((8 * ROWS + 64, D), BF),
            pltpu.VMEM((ENC, D), BF),
            pltpu.VMEM((n, 8, D), F),
            pltpu.VMEM((n, 8, D), F),
            pltpu.VMEM((KV, D), BF),
            pltpu.VMEM((LOC, D), BF),
            pltpu.VMEM((KV, D), BF),
            pltpu.VMEM((KV, D), BF),
            pltpu.VMEM((LOC, D), BF),
            pltpu.VMEM((8, ROWS, TRK), BF),
            pltpu.VMEM((8, LOC, 256), BF),
            pltpu.VMEM((ROWS, TRK), F),
            pltpu.VMEM((LOC, 256), F),
            pltpu.VMEM((ROWS, TRK), F),
            pltpu.VMEM((LOC, 256), F),
            pltpu.VMEM((2, LOC, 128), F),
            pltpu.VMEM((ROWS, D), BF),
            pltpu.VMEM((ROWS, D), F),
            pltpu.VMEM((ROWS, D), F),
            pltpu.VMEM((ROWS, D), BF),
            pltpu.VMEM((ROWS, D), BF),
            pltpu.VMEM((ENC, D), BF),
            pltpu.VMEM((ENC, D), BF),
            pltpu.VMEM((ROWS, D), BF),
            pltpu.VMEM((8, ROWS, ENC), BF),
            pltpu.VMEM((ROWS, D), BF),
            pltpu.VMEM((ROWS, D), F),
            pltpu.VMEM((ROWS, D), F),
            pltpu.VMEM((ROWS, D), BF),
            pltpu.VMEM((ROWS, D), BF),
            pltpu.VMEM((ROWS, D), F),
            pltpu.VMEM((ROWS, D), F),
            pltpu.VMEM((ROWS, D), BF),
            pltpu.VMEM((ROWS, D), BF),
            pltpu.VMEM((ROWS, D), BF),
            pltpu.VMEM((KV, D), BF),
            pltpu.VMEM((KV, D), BF),
            pltpu.VMEM((KV, D), F),
            pltpu.VMEM((D, D), F),
            pltpu.VMEM((D, D), F),
            pltpu.SemaphoreType.DMA((8 * n + 66,)),
            pltpu.SemaphoreType.DMA((8 * n + 66,)),
            pltpu.SemaphoreType.DMA((8,)),
        ],
        compiler_params=pltpu.CompilerParams(
            vmem_limit_bytes=VMEM_LIMIT, collective_id=0, has_side_effects=True
        ),
        name="layer",
    )(parents, cond_parts, w_mod, tokens, enc, cot, *weights)


def timestep_code(timesteps, width):
    half = width // 2
    frequency = jnp.exp(-math.log(10000.0) * jnp.arange(half, dtype=F) / half)
    angles = timesteps.astype(F)[:, None] * frequency[None, :]
    return jnp.concatenate([jnp.sin(angles), jnp.cos(angles)], axis=-1)


def per_device(
    tokens,
    encoder_states,
    timesteps,
    parents,
    w_mod,
    w_self_qkv,
    w_self_out,
    w_cross_qkv,
    w_cross_out,
    w_up,
    w_down,
    cotangent,
):
    rows = w_mod.shape[0]
    ci = lax.axis_index("ctx") * 2 + lax.axis_index("tp")
    condition = jax.nn.silu(timestep_code(timesteps, D)).astype(BF)
    n = lax.axis_size("fsdp")
    padded_cond = jnp.pad(condition.astype(F).reshape(n, 1, rows), ((0, 0), (0, 7), (0, max(128 - rows, 0))))
    (out, gstream, gpart, gown, egrad, mgrad, mod, cond_all, g_qkv, g_so, g_cqkv, g_co, g_up, g_dn) = layer_call(
        n,
        parents,
        padded_cond,
        w_mod,
        tokens,
        encoder_states,
        cotangent[0],
        (w_self_qkv, w_self_out, w_cross_qkv, w_cross_out, w_up, w_down),
    )
    cond_mine = cond_all[:, 0, :rows]
    off = lax.rem(ci, 2) * 64
    total = jnp.zeros((8 * ROWS + 64, D), F)
    total = total.at[:SHARED].set(gpart[:SHARED].astype(F))
    window = lax.dynamic_slice(total, (ci * ROWS - off, 0), (LOC, D)) + gpart[SHARED:].astype(F)
    total = lax.dynamic_update_slice(total, window, (ci * ROWS - off, 0))
    mine = lax.psum_scatter(
        total[: 8 * ROWS].astype(BF), ("ctx", "tp"), scatter_dimension=0, tiled=True
    )
    hidden_grad = mine.astype(F) + gown
    stream_grad, ds, db = norm_back(hidden_grad, tokens[0].astype(F), mod[0:1])
    input_grad = gstream + stream_grad
    mod_terms = jnp.concatenate([ds, db, mgrad[2:6]]).reshape(1, 6 * D)
    mod_total = lax.psum(mod_terms, ("ctx", "tp"))
    mod_all = lax.all_gather(mod_total, "fsdp", axis=0, tiled=True)
    grad_mod = jnp.dot(cond_mine.T, mod_all, precision=lax.Precision.HIGHEST)
    enc_grad = lax.psum(egrad.astype(F), "tp")
    enc_grad = lax.psum_scatter(enc_grad, "ctx", scatter_dimension=0, tiled=True)

    def owned(g, axis):
        g = lax.psum_scatter(g, "tp", scatter_dimension=axis + 1, tiled=True)
        g = lax.psum(g, "ctx")
        return lax.psum_scatter(g, "fsdp", scatter_dimension=axis, tiled=True).astype(F)

    return (
        out[None],
        input_grad[None],
        enc_grad[None],
        grad_mod,
        owned(g_qkv, 1),
        owned(g_so, 0),
        owned(g_cqkv, 1),
        owned(g_co, 0),
        owned(g_up, 0),
        owned(g_dn, 0),
    )


def solution(mesh):
    rows = P("fsdp", ("ctx", "tp"), None)
    return jax.shard_map(
        per_device,
        mesh=mesh,
        in_specs=(
            rows,
            P("fsdp", "ctx", None),
            P("fsdp"),
            P("fsdp", None),
            P("fsdp", None),
            P(None, "fsdp", "tp"),
            P("fsdp", "tp"),
            P(None, "fsdp", "tp"),
            P("fsdp", "tp"),
            P("fsdp", "tp"),
            P("fsdp", "tp"),
            rows,
        ),
        out_specs=(
            rows,
            rows,
            P("fsdp", "ctx", None),
            P("fsdp", None),
            P(None, "fsdp", "tp"),
            P("fsdp", "tp"),
            P(None, "fsdp", "tp"),
            P("fsdp", "tp"),
            P("fsdp", "tp"),
            P("fsdp", "tp"),
        ),
        check_vma=False,
    )
```

```python
import functools
import math

import jax
import jax.numpy as jnp
from jax import lax
from jax.experimental import pallas as pl
from jax.experimental.pallas import tpu as pltpu
from jax.sharding import PartitionSpec as P

BF = jnp.bfloat16
F = jnp.float32
D = 512
FF = 2048
HD = 64
ROWS = 320
LOC = 384
BLK = 128
TRUNK = 8
BRANCHES = 4
TRK = TRUNK * BLK
SHARED = (TRUNK + BRANCHES) * BLK
SPEC = 2 * LOC
KV = TRK + SPEC
ENC = 512
EPS = 1e-05
NEG = -1e30
VMEM_LIMIT = 67043328


def nn(a, b):
    return lax.dot_general(a, b, (((1,), (0,)), ((), ())), preferred_element_type=F)


def nt(a, b):
    return lax.dot_general(a, b, (((1,), (1,)), ((), ())), preferred_element_type=F)


def tn(a, b):
    return lax.dot_general(a, b, (((0,), (0,)), ((), ())), preferred_element_type=F)


def normed(v):
    center = v - jnp.mean(v, axis=-1, keepdims=True)
    rstd = lax.rsqrt(jnp.mean(center * center, axis=-1, keepdims=True) + EPS)
    return center * rstd, rstd


def norm_back(grad, stream, scale):
    n, rstd = normed(stream)
    gn = grad * (1.0 + scale)
    back = rstd * (
        gn
        - jnp.mean(gn, axis=-1, keepdims=True)
        - n * jnp.mean(gn * n, axis=-1, keepdims=True)
    )
    return back, jnp.sum(grad * n, axis=0, keepdims=True), jnp.sum(grad, axis=0, keepdims=True)


def row_loop(total, step, body):
    @pl.loop(0, total // step)
    def _(i):
        body(pl.ds(pl.multiple_of(i * step, step), step))


def half_lanes(shape, half):
    lane = lax.broadcasted_iota(jnp.int32, shape, len(shape) - 1)
    return (lane // HD) == half


def keep(value, half):
    return jnp.where(half_lanes(value.shape, half), value, jnp.zeros_like(value))


MESH = pl.DeviceIdType.MESH


class Wire:
    def __init__(self, send, recv):
        self.send, self.recv, self.used, self.sent = send, recv, 0, []

    def slot(self, count=1):
        self.used += count
        return self.used - count

    def copy(self, src, dst, at, to):
        return pltpu.make_async_remote_copy(
            src_ref=src,
            dst_ref=dst,
            send_sem=self.send.at[at],
            recv_sem=self.recv.at[at],
            device_id=to,
            device_id_type=MESH,
        )

    def push(self, dst, at, to, when=None, src=None):
        src = src or dst
        if when is None:
            self.copy(src(), dst(), at, to).start()
        else:

            @pl.when(when)
            def _():
                self.copy(src(), dst(), at, to).start()

        self.sent.append((src, dst, at, to, when))

    def arrived(self, dst, at, to, when=None):
        if when is None:
            self.copy(dst, dst, at, to).wait_recv()
        else:

            @pl.when(when)
            def _():
                self.copy(dst, dst, at, to).wait_recv()

    def drain(self):
        for src, dst, at, to, when in self.sent:
            if when is None:
                self.copy(src(), dst(), at, to).wait_send()
            else:

                @pl.when(when)
                def _(src=src, dst=dst, at=at, to=to):
                    self.copy(src(), dst(), at, to).wait_send()

        self.sent = []


def layer_kernel(
    n,
    parents_ref,
    cond_parts,
    w_mod,
    tok_in,
    enc_in,
    cot,
    w_sqkv,
    w_so,
    w_cqkv,
    w_co,
    w_up,
    w_dn,
    out_ref,
    in_grad,
    enc_out,
    mod_out,
    att_out,
    ffn_out,
    watt,
    wup,
    wdn,
    tok,
    enc,
    part_out,
    part_in,
    mod,
    cond_all,
    tok_own,
    mgrad,
    hid,
    hloc,
    kbuf,
    vbuf,
    qbuf,
    pt,
    ps,
    bias_t,
    bias_s,
    st,
    ss,
    spec_o,
    mixa,
    stream_b,
    stream_c,
    hid_b,
    hid_c,
    kenc,
    venc,
    qb,
    pe,
    mixb,
    b0,
    b1,
    acc0,
    acc1,
    gbf,
    mgr,
    dq,
    wk_acc,
    wv_acc,
    gatt,
    gffn,
    egrad,
    rc_att,
    rx_att,
    zr_att,
    rg_att,
    zr_ffn,
    rg_ffn,
    rc_g,
    rx_g,
    halo,
    rc_e,
    rx_e,
    mod1,
    mod2,
    send,
    recv,
    local,
    ready,
):
    t0, t1 = st.at[:, 0:D], st.at[:, D : 2 * D]
    fs = lax.axis_index("fsdp")
    cx = lax.axis_index("ctx")
    y = lax.axis_index("tp")
    x, c = cx // 2, lax.rem(cx, 2)
    ci = cx * 2 + y
    odd = y
    off = pl.multiple_of(odd * 64, 64)
    own = pl.ds(off, ROWS)
    base = (ci * 5) // 2
    rows = w_mod.shape[0]
    to_y = {"tp": 1 - y}
    to_c = {"ctx": 2 * x + 1 - c}
    to_x = {"ctx": 2 * (1 - x) + c}
    wire = Wire(send, recv)

    my_rows = pl.ds(pl.multiple_of(fs * rows, rows), rows)

    def att_cols(yy, cc):
        return pl.ds(pl.multiple_of(yy * 256 + cc * 128, 128), 128)

    def ffn_cols(yy, xx, cc):
        return pl.ds(pl.multiple_of(yy * 1024 + xx * 512 + cc * 256, 256), 256)

    half = pl.ds(pl.multiple_of(c * 128, 128), 128)
    quarter = pl.ds(pl.multiple_of(cx * 256, 256), 256)
    groups = (
        (w_sqkv.at[:, :, half], watt, slice(0, 3), 0),
        (w_so.at[:, half], watt, 3, 0),
        (w_cqkv.at[:, :, half], watt, slice(4, 7), 0),
        (w_co.at[:, half], watt, 7, 0),
        (w_up.at[:, quarter], wup, None, 1),
        (w_dn.at[:, quarter], wdn, None, 1),
    )

    def place(g, row_at, yy, xx, cc):
        _, buf, index, wide = groups[g]
        if wide:
            return buf.at[row_at, ffn_cols(yy, xx, cc)]
        return buf.at[index, row_at, att_cols(yy, cc)]

    def chunk(i):
        return tok.at[pl.ds(pl.multiple_of(i * ROWS, ROWS), ROWS), :]

    def enc_part(i):
        return enc.at[pl.ds(pl.multiple_of(i * 128, 128), 128), :]

    all_rows = pl.ds(0, D)

    local_copies = [
        pltpu.make_async_copy(tok_in.at[0], chunk(ci), local.at[0]),
        pltpu.make_async_copy(enc_in.at[0], enc_part(cx), local.at[1]),
    ] + [
        pltpu.make_async_copy(groups[g][0], place(g, my_rows, y, x, c), local.at[2 + g])
        for g in range(6)
    ]
    local_copies.append(pltpu.make_async_copy(tok_in.at[0], tok_own, local.at[8]))
    for copy in local_copies:
        copy.start()

    barrier = pltpu.get_barrier_semaphore()

    @pl.loop(1, n)
    def _(k):
        pl.semaphore_signal(
            barrier, inc=1, device_id={"fsdp": lax.rem(fs + k, n)}, device_id_type=MESH
        )

    @pl.loop(1, 8)
    def _(k):
        other = lax.rem(ci + k, 8)
        pl.semaphore_signal(
            barrier,
            inc=1,
            device_id={"ctx": other // 2, "tp": lax.rem(other, 2)},
            device_id_type=MESH,
        )

    pl.semaphore_wait(barrier, n - 1 + 7)

    def peers(make):
        @pl.loop(1, n)
        def _(k):
            make(k, lax.rem(fs + k, n), lax.rem(fs + n - k, n))

    s_cond = wire.slot(n)
    s_part = wire.slot(n)
    s_z = [wire.slot(n) for _ in range(6)]
    s_y = [wire.slot() for _ in range(6)]
    s_c0 = [wire.slot() for _ in range(6)]
    s_c1 = [wire.slot() for _ in range(6)]
    s_x0 = [wire.slot() for _ in range(6)]
    s_x1 = [wire.slot() for _ in range(6)]
    s_c2 = [wire.slot() for _ in range(6)]
    s_c3 = [wire.slot() for _ in range(6)]
    s_ty, s_tx, s_txy, s_tc0, s_tc1, s_tc2, s_tc3 = (wire.slot() for _ in range(7))
    s_ex, s_ec0, s_ec1 = (wire.slot() for _ in range(3))

    peers(
        lambda k, to, _: wire.copy(
            cond_parts.at[to], cond_all.at[fs], s_cond + k, {"fsdp": to}
        ).start()
    )
    wire.push(lambda: chunk(ci), s_ty, to_y, None, lambda: tok_in.at[0])
    wire.push(lambda: chunk(ci), s_tx, to_x, x == 0, lambda: tok_in.at[0])
    wire.push(lambda: chunk(ci), s_tc0, to_c, None, lambda: tok_in.at[0])
    for g in range(6):
        peers(
            lambda k, to, _, g=g: wire.copy(
                groups[g][0], place(g, my_rows, y, x, c), s_z[g] + k, {"fsdp": to}
            ).start()
        )
    wire.push(lambda: enc_part(cx), s_ex, to_x, None, lambda: enc_in.at[0])
    wire.push(lambda: enc_part(cx), s_ec0, to_c, None, lambda: enc_in.at[0])

    cond_all[fs] = cond_parts[fs]
    peers(lambda k, _, src: wire.arrived(cond_all.at[src], s_cond + k, {"fsdp": src}))
    for v in range(6):
        part_out[:, v, :] = nn(
            cond_all[:, 0, 0:rows].astype(BF), w_mod[:, v * D : (v + 1) * D]
        )
    part_out[:, 6:8, :] = jnp.zeros((n, 2, D), F)
    peers(
        lambda k, to, _: wire.copy(
            part_out.at[to], part_in.at[fs], s_part + k, {"fsdp": to}
        ).start()
    )
    part_in[fs] = part_out[fs]

    def z_done(g):
        local_copies[2 + g].wait()
        peers(
            lambda k, _, src: wire.arrived(
                place(g, pl.ds(pl.multiple_of(src * rows, rows), rows), y, x, c),
                s_z[g] + k,
                {"fsdp": src},
            )
        )
        slab = lambda: place(g, all_rows, y, x, c)
        wire.push(slab, s_y[g], to_y)
        if groups[g][3]:
            wire.push(slab, s_x0[g], to_x)
        wire.push(slab, s_c0[g], to_c)

    def y_done(g):
        slab = lambda: place(g, all_rows, 1 - y, x, c)
        wire.arrived(slab(), s_y[g], to_y)
        if groups[g][3]:
            wire.push(slab, s_x1[g], to_x)
        wire.push(slab, s_c1[g], to_c)

    def x_done(g):
        for yy, s_in, s_out in ((y, s_x0[g], s_c2[g]), (1 - y, s_x1[g], s_c3[g])):
            slab = lambda yy=yy: place(g, all_rows, yy, 1 - x, c)
            wire.arrived(slab(), s_in, to_x)
            wire.push(slab, s_out, to_c)

    def c_done(g):
        wire.arrived(place(g, all_rows, y, x, 1 - c), s_c0[g], to_c)
        wire.arrived(place(g, all_rows, 1 - y, x, 1 - c), s_c1[g], to_c)
        if groups[g][3]:
            wire.arrived(place(g, all_rows, y, 1 - x, 1 - c), s_c2[g], to_c)
            wire.arrived(place(g, all_rows, 1 - y, 1 - x, 1 - c), s_c3[g], to_c)

    local_copies[0].wait()
    local_copies[1].wait()
    ciy = 4 * x + 2 * c + 1 - y
    cic = 4 * x + 2 * (1 - c) + y
    ciyc = 4 * x + 2 * (1 - c) + 1 - y
    low, lowy, lowc, lowyc = 2 * c + y, 2 * c + 1 - y, 2 * (1 - c) + y, 2 * (1 - c) + 1 - y
    right = x == 1
    local_copies[8].wait()
    wire.arrived(chunk(ciy), s_ty, to_y)
    wire.push(lambda: chunk(ciy), s_txy, to_x, x == 0)
    wire.push(lambda: chunk(ciy), s_tc1, to_c)
    wire.arrived(chunk(low), s_tx, to_x, right)
    wire.push(lambda: chunk(low), s_tc2, to_c, right)
    z_done(0)
    wire.arrived(enc_part(2 * (1 - x) + c), s_ex, to_x)
    wire.push(lambda: enc_part(2 * (1 - x) + c), s_ec1, to_c)
    wire.arrived(chunk(lowy), s_txy, to_x, right)
    wire.push(lambda: chunk(lowy), s_tc3, to_c, right)
    y_done(0)

    peers(lambda k, _, src: wire.arrived(part_in.at[src], s_part + k, {"fsdp": src}))
    mod[...] = jnp.sum(part_in[...], axis=0)
    sa, ba = mod[0:1, :], mod[1:2, :]
    sb, bb = mod[2:3, :], mod[3:4, :]
    sf, bf_ = mod[4:5, :], mod[5:6, :]

    wire.arrived(chunk(cic), s_tc0, to_c)
    wire.arrived(chunk(ciyc), s_tc1, to_c)
    wire.arrived(chunk(lowc), s_tc2, to_c, right)
    wire.arrived(chunk(lowyc), s_tc3, to_c, right)
    wire.arrived(enc_part(2 * x + 1 - c), s_ec0, to_c)
    wire.arrived(enc_part(2 * (1 - x) + 1 - c), s_ec1, to_c)
    tok_tb = tok
    tok_loc = tok.at[pl.ds(pl.multiple_of(ci * ROWS - off, 64), LOC), :]

    def relay(step):
        if step == 0:
            z_done(1)
            z_done(2)
            z_done(3)
        if step == 1:
            for g in (1, 2, 3):
                y_done(g)
            z_done(4)
        if step == 2:
            z_done(5)
            for g in (1, 2, 3):
                c_done(g)
        if step == 3:
            y_done(4)
            x_done(4)
        if step == 4:
            y_done(5)
            x_done(5)
        if step == 5:
            c_done(4)
            c_done(5)

    spec_g = qbuf

    def is_parent(lb, branch):
        parent = jnp.full((32, D), parents_ref[0, base + lb], jnp.int32)
        leaf = jnp.full((32, D), base + lb, jnp.int32) >= TRUNK + BRANCHES
        return jnp.logical_and(leaf, parent == TRUNK + branch)

    to_xy = {"ctx": 2 * (1 - x) + c, "tp": 1 - y}
    s_rcf = [wire.slot() for _ in range(8)]
    s_rxf = [wire.slot() for _ in range(6)]
    s_zf = wire.slot(n)
    s_gf = wire.slot(4)
    s_rca = [[wire.slot(), wire.slot()] for _ in range(2)]
    s_rxa = [[wire.slot() for _ in range(3)] for _ in range(2)]
    s_za = [wire.slot(n) for _ in range(2)]
    s_ga = [wire.slot(4) for _ in range(2)]
    s_rcg, s_rcg4, s_rcg5, s_halo = (wire.slot() for _ in range(4))
    s_rxg = [wire.slot() for _ in range(3)]
    s_rce = [wire.slot(), wire.slot()]
    s_rxe = [wire.slot() for _ in range(3)]
    s_m1 = wire.slot(8)
    s_m2 = wire.slot(n)
    quad = ((to_y, x, 1 - y), (to_x, 1 - x, y), (to_xy, 1 - x, 1 - y))

    def add_rows(target, terms, total, step=64):
        def body(rs):
            value = terms[0][rs, :].astype(F)
            for term in terms[1:]:
                value += term[rs, :].astype(F)
            target[rs, :] = value.astype(BF)

        row_loop(total, step, body)

    def ctx_peers(make):
        @pl.loop(1, 4)
        def _(k):
            make(k, lax.rem(cx + k, 4), lax.rem(cx + 4 - k, 4))

    def strip(buf, at):
        return buf.at[:, at * 256 : (at + 1) * 256]

    def ffn_core_send():
        wire.drain()
        for target in (to_c, to_y, to_x, to_xy):
            pl.semaphore_signal(ready, inc=1, device_id=target, device_id_type=MESH)
        pl.semaphore_wait(ready, 4)
        for t in range(4):
            for m in range(2):
                wire.push(
                    lambda t=t, m=m: strip(wup, t * 2 + m),
                    s_rcf[t * 2 + m],
                    to_c,
                    None,
                    lambda t=t, m=m: gffn.at[m, :, ffn_cols(t // 2, t % 2, 1 - c)],
                )

    def ffn_chip_send():
        for t in range(4):
            for m in range(2):
                wire.arrived(strip(wup, t * 2 + m), s_rcf[t * 2 + m], to_c)
                own_slab = gffn.at[m, :, ffn_cols(t // 2, t % 2, c)]
                add_rows(own_slab, (own_slab, strip(wup, t * 2 + m)), D)
        for r, (target, xx, yy) in enumerate(quad):
            for m in range(2):
                wire.push(
                    lambda r=r, m=m: strip(wdn, r * 2 + m),
                    s_rxf[r * 2 + m],
                    target,
                    None,
                    lambda m=m, xx=xx, yy=yy: gffn.at[m, :, ffn_cols(yy, xx, c)],
                )

    def ffn_tree_send():
        for r, (target, _, _) in enumerate(quad):
            for m in range(2):
                wire.arrived(strip(wdn, r * 2 + m), s_rxf[r * 2 + m], target)
        for m in range(2):
            mine = gffn.at[m, :, ffn_cols(y, x, c)]
            add_rows(mine, [mine] + [strip(wdn, r * 2 + m) for r in range(3)], D)
        peers(lambda k, to, _: ffn_z(k, to).start())
        zr_ffn[fs] = gffn[:, my_rows, ffn_cols(y, x, c)]

    def ffn_z(k, to):
        part = pl.ds(pl.multiple_of(to * rows, rows), rows)
        return wire.copy(gffn.at[:, part, ffn_cols(y, x, c)], zr_ffn.at[fs], s_zf + k, {"fsdp": to})

    def ffn_copy_send():
        peers(lambda k, _, src: wire.arrived(zr_ffn.at[src], s_zf + k, {"fsdp": src}))
        rg_ffn[cx] = jnp.sum(zr_ffn[...].astype(F), axis=0).astype(BF)
        ctx_peers(lambda k, to, _: ffn_g(k, to).start())

    def ffn_g(k, to):
        return wire.copy(rg_ffn.at[cx], rg_ffn.at[cx], s_gf + k, {"ctx": to})

    def ffn_finish():
        ctx_peers(lambda k, _, src: wire.arrived(rg_ffn.at[src], s_gf + k, {"ctx": src}))
        for q in range(4):
            ffn_out[:, :, q * 256 : (q + 1) * 256] = rg_ffn[q].astype(F)

    def att_core_send(a):
        for yy in range(2):
            wire.push(
                lambda yy=yy: rc_att.at[a, yy],
                s_rca[a][yy],
                to_c,
                None,
                lambda yy=yy: gatt.at[4 * a : 4 * a + 4, :, att_cols(yy, 1 - c)],
            )

    def att_chip_send(a):
        for yy in range(2):
            wire.arrived(rc_att.at[a, yy], s_rca[a][yy], to_c)
            for m in range(4):
                mine = gatt.at[4 * a + m, :, att_cols(yy, c)]
                add_rows(mine, (mine, rc_att.at[a, yy, m]), D)
        for r, (target, xx, yy) in enumerate(quad):
            wire.push(
                lambda r=r: rx_att.at[a, r],
                s_rxa[a][r],
                target,
                None,
                lambda xx=xx, yy=yy: gatt.at[pl.ds(4 * a + 2 * xx, 2), :, att_cols(yy, c)],
            )

    def att_tree_send(a):
        for r, (target, _, _) in enumerate(quad):
            wire.arrived(rx_att.at[a, r], s_rxa[a][r], target)
        for m in range(2):
            mine = gatt.at[4 * a + 2 * x + m, :, att_cols(y, c)]
            add_rows(mine, [mine] + [rx_att.at[a, r, m] for r in range(3)], D)
        peers(lambda k, to, _: att_z(a, k, to).start())
        zr_att[a, fs] = gatt[pl.ds(4 * a + 2 * x, 2), my_rows, att_cols(y, c)]

    def att_z(a, k, to):
        part = pl.ds(pl.multiple_of(to * rows, rows), rows)
        return wire.copy(
            gatt.at[pl.ds(4 * a + 2 * x, 2), part, att_cols(y, c)],
            zr_att.at[a, fs],
            s_za[a] + k,
            {"fsdp": to},
        )

    def att_copy_send(a):
        peers(lambda k, _, src: wire.arrived(zr_att.at[a, src], s_za[a] + k, {"fsdp": src}))
        rg_att[a, cx] = jnp.sum(zr_att[a].astype(F), axis=0).astype(BF)
        ctx_peers(lambda k, to, _: att_g(a, k, to).start())

    def att_g(a, k, to):
        return wire.copy(rg_att.at[a, cx], rg_att.at[a, cx], s_ga[a] + k, {"ctx": to})

    def att_finish(a):
        ctx_peers(lambda k, _, src: wire.arrived(rg_att.at[a, src], s_ga[a] + k, {"ctx": src}))
        for q in range(4):
            for m in range(2):
                at = 4 * a + 2 * (q // 2) + m
                att_out[at, :, (q % 2) * 128 : (q % 2) * 128 + 128] = rg_att[a, q, m].astype(F)

    def enc_core_send():
        for xx in range(2):
            wire.push(
                lambda xx=xx: rc_e.at[xx],
                s_rce[xx],
                to_c,
                None,
                lambda xx=xx: egrad.at[pl.ds(pl.multiple_of((2 * xx + 1 - c) * 128, 128), 128), :],
            )

    def enc_rows(xx):
        return egrad.at[pl.ds(pl.multiple_of((2 * xx + c) * 128, 128), 128), :]

    def enc_chip_send():
        for xx in range(2):
            wire.arrived(rc_e.at[xx], s_rce[xx], to_c)
            add_rows(enc_rows(xx), (enc_rows(xx), rc_e.at[xx]), 128)
        for r, (target, xx, _) in enumerate(quad):
            wire.push(
                lambda: rx_e.at[2 * x + y], s_rxe[r], target, None, lambda xx=xx: enc_rows(xx)
            )
        rx_e[2 * x + y] = enc_rows(x)[...]

    def enc_finish():
        for r, (target, xx, yy) in enumerate(quad):
            wire.arrived(rx_e.at[2 * xx + yy], s_rxe[r], target)
        enc_out[...] = jnp.sum(rx_e[...].astype(F), axis=0)

    def shared_core_send():
        to_core = pl.ds(pl.multiple_of(640 * (1 - c), 640), 640)
        wire.push(lambda: rc_g.at[0:640], s_rcg, to_c, None, lambda: tok.at[to_core, :])
        wire.push(
            lambda: rc_g.at[640:896],
            s_rcg4,
            to_c,
            jnp.logical_and(x == 1, c == 1),
            lambda: tok.at[1280:1536, :],
        )
        wire.push(lambda: halo, s_halo, to_y, y == 1, lambda: spec_g.at[0:64, :])

    def shared_chip_send():
        wire.arrived(rc_g.at[0:640], s_rcg, to_c)
        mine = tok.at[pl.ds(pl.multiple_of(640 * c, 640), 640), :]
        add_rows(mine, (mine, rc_g.at[0:640]), 640)
        last = jnp.logical_and(x == 1, c == 0)

        @pl.when(last)
        def _():
            wire.arrived(rc_g.at[640:896], s_rcg4, to_c)
            four = tok.at[1280:1536, :]
            add_rows(four, (four, rc_g.at[640:896]), 256)

        def rows_of(yy):
            return lambda: chunk(2 * c + yy)

        wire.push(lambda: rx_g.at[0], s_rxg[0], to_y, x == 0, rows_of(1 - y))
        wire.push(lambda: rx_g.at[1], s_rxg[1], to_x, x == 1, rows_of(y))
        wire.push(lambda: rx_g.at[2], s_rxg[2], to_xy, x == 1, rows_of(1 - y))
        wire.push(
            lambda: rx_g.at[0, 0:256],
            s_rcg5,
            to_y,
            jnp.logical_and(last, y == 1),
            lambda: tok.at[1280:1536, :],
        )

    def shared_arrived():
        wire.arrived(rx_g.at[0], s_rxg[0], to_y, x == 0)
        wire.arrived(rx_g.at[1], s_rxg[1], to_x, x == 0)
        wire.arrived(rx_g.at[2], s_rxg[2], to_xy, x == 0)
        wire.arrived(rx_g.at[0, 0:256], s_rcg5, to_y, ci == 4)

    def tree_peers(make):
        @pl.loop(1, 8)
        def _(k):
            make(k, lax.rem(ci + k, 8), lax.rem(ci + 8 - k, 8))

    def device_of(i):
        return {"ctx": i // 2, "tp": lax.rem(i, 2)}

    def mod_1(k, to):
        return wire.copy(mgrad, mod1.at[ci], s_m1 + k, device_of(to))

    def mod_2(k, to):
        return wire.copy(mod2.at[fs], mod2.at[fs], s_m2 + k, {"fsdp": to})

    def mod_tree_send():
        tree_peers(lambda k, to, _: mod_1(k, to).start())
        mod1[ci] = mgrad[...]

    def mod_all_send():
        tree_peers(lambda k, _, src: wire.arrived(mod1.at[src], s_m1 + k, device_of(src)))
        mod2[fs] = jnp.sum(mod1[...], axis=0)
        peers(lambda k, to, _: mod_2(k, to).start())

    def mod_finish():
        peers(lambda k, _, src: wire.arrived(mod2.at[src], s_m2 + k, {"fsdp": src}))
        cond = cond_all[:, 0, 0:rows]
        for v in range(6):
            held = (wk_acc, wv_acc)[v // 4]
            at = (v % 4) * rows
            held[at : at + rows, :] = lax.dot_general(
                cond,
                mod2[:, v, :],
                (((0,), (0,)), ((), ())),
                precision=lax.Precision.HIGHEST,
                preferred_element_type=F,
            )
        copies = [
            pltpu.make_async_copy(
                (wk_acc, wv_acc)[v // 4].at[(v % 4) * rows : (v % 4 + 1) * rows, :],
                mod_out.at[:, v * D : (v + 1) * D],
                local.at[v],
            )
            for v in range(6)
        ]
        for copy in copies:
            copy.start()
        for copy in copies:
            copy.wait()

    def leave(step):
        if step == 0:
            ffn_core_send()
        if step == 1:
            att_core_send(1)
            enc_core_send()
            ffn_chip_send()
        if step == 2:
            att_chip_send(1)
            enc_chip_send()
            ffn_tree_send()
        if step == 3:
            ffn_copy_send()
            att_tree_send(1)
        if step == 4:
            shared_core_send()
        if step == 5:
            att_core_send(0)
        if step == 6:
            shared_chip_send()
            att_chip_send(0)
            att_copy_send(1)
            enc_finish()
            ffn_finish()
            shared_arrived()
        if step == 7:
            mod_tree_send()
            att_tree_send(0)
            mod_all_send()
            att_copy_send(0)
            att_finish(1)
            mod_finish()
            att_finish(0)

    def mask_trunk(rs):
        row = lax.broadcasted_iota(jnp.int32, (32, TRK), 0) + rs.start + ci * ROWS
        col = lax.broadcasted_iota(jnp.int32, (32, TRK), 1)
        bias_t[rs, :] = jnp.where(col <= row, 0.0, NEG).astype(BF)

    row_loop(ROWS, 32, mask_trunk)
    for lb in range(3):
        blk = base + lb
        row = lax.broadcasted_iota(jnp.int32, (BLK, 2 * BLK), 0)
        col = lax.broadcasted_iota(jnp.int32, (BLK, 2 * BLK), 1)
        par_ok = jnp.logical_and(col < BLK, blk >= TRUNK + BRANCHES)
        self_ok = jnp.logical_and(
            jnp.logical_and(col >= BLK, col - BLK <= row), blk >= TRUNK
        )
        bias_s[lb * BLK : (lb + 1) * BLK, :] = jnp.where(
            jnp.logical_or(par_ok, self_ok), 0.0, NEG
        ).astype(BF)

    def hidden(x):
        n, _ = normed(x.astype(F))
        return (n * (1.0 + sa) + ba).astype(BF)

    def hid_trunk(rs):
        hid[rs, :] = hidden(tok_tb[rs, :])

    row_loop(TRK, 32, hid_trunk)

    def hid_loc(rs):
        hloc[rs, :] = hidden(tok_loc[rs, :])

    row_loop(LOC, 32, hid_loc)
    for lb in range(3):
        picks = [is_parent(lb, b) for b in range(1, BRANCHES)]
        for piece in range(4):
            r = piece * 32
            picked = tok_tb[TRK + r : TRK + r + 32, :].astype(F)
            for b in range(1, BRANCHES):
                at = TRK + b * BLK + r
                picked = jnp.where(picks[b - 1], tok_tb[at : at + 32, :].astype(F), picked)
            at = TRK + lb * 256 + r
            hid[at : at + 32, :] = hidden(picked)
        hid[TRK + lb * 256 + BLK : TRK + lb * 256 + 2 * BLK, :] = hloc[
            lb * BLK : (lb + 1) * BLK, :
        ]

    def project(rs):
        kbuf[rs, :] = nn(hid[rs, :], watt[1]).astype(BF)
        vbuf[rs, :] = nn(hid[rs, :], watt[2]).astype(BF)

    c_done(0)
    row_loop(KV, 256, project)
    relay(0)
    qbuf[...] = (nn(hloc[...], watt[0]) * 0.125).astype(BF)

    @pl.loop(0, 4)
    def _(hp):
        @pl.when(hp == 2)
        def _():
            relay(1)

        lanes = pl.ds(pl.multiple_of(hp * 128, 128), 128)
        kt = kbuf[0:TRK, lanes]
        for half in range(2):
            h = hp * 2 + half
            st[...] = nt(keep(qbuf[own, lanes], half), kt)
            for lb in range(3):
                r = slice(lb * BLK, (lb + 1) * BLK)
                ks = kbuf[TRK + lb * 256 : TRK + (lb + 1) * 256, lanes]
                ss[r, :] = nt(keep(qbuf[r, lanes], half), ks)

            @pl.loop(0, ROWS // 32)
            def _(i):
                rs = pl.ds(pl.multiple_of(i * 32, 32), 32)
                ro = pl.ds(pl.multiple_of(i * 32 + off, 32), 32)
                a = st[rs, :] + bias_t[rs, :].astype(F)
                b = ss[ro, :] + bias_s[ro, :].astype(F)
                top = jnp.maximum(
                    jnp.max(a, axis=-1, keepdims=True), jnp.max(b, axis=-1, keepdims=True)
                )
                a = jnp.exp(a - top)
                b = jnp.exp(b - top)
                inv = 1.0 / (
                    jnp.sum(a, axis=-1, keepdims=True) + jnp.sum(b, axis=-1, keepdims=True)
                )
                pt[h, rs, :] = (a * inv).astype(BF)
                ps[h, ro, :] = (b * inv).astype(BF)

            for lb in range(3):
                r = slice(lb * BLK, (lb + 1) * BLK)
                vs = vbuf[TRK + lb * 256 : TRK + (lb + 1) * 256, lanes]
                spec_o[half, r, :] = nn(ps[h, r, :], vs)
        vt = vbuf[0:TRK, lanes]
        o0 = nn(pt[hp * 2], vt) + spec_o[0, own, :]
        o1 = nn(pt[hp * 2 + 1], vt) + spec_o[1, own, :]
        mixa[:, lanes] = jnp.where(half_lanes(o0.shape, 0), o0, o1).astype(BF)

    relay(2)
    t0[...] = nt(mixa[...], watt[3])

    def after_self(rs):
        sbv = tok_own[rs, :].astype(F) + t0[rs, :]
        stream_b[rs, :] = sbv
        n, _ = normed(sbv)
        hid_b[rs, :] = (n * (1.0 + sb) + bb).astype(BF)

    row_loop(ROWS, 32, after_self)

    relay(3)
    kenc[...] = nn(enc[...], watt[5]).astype(BF)
    venc[...] = nn(enc[...], watt[6]).astype(BF)
    qb[...] = (nn(hid_b[...], watt[4]) * 0.125).astype(BF)

    @pl.loop(0, 4)
    def _(hp):
        lanes = pl.ds(pl.multiple_of(hp * 128, 128), 128)
        kt = kenc[:, lanes]
        for half in range(2):
            h = hp * 2 + half
            t0[...] = nt(keep(qb[:, lanes], half), kt)

            @pl.loop(0, ROWS // 32)
            def _(i):
                rs = pl.ds(pl.multiple_of(i * 32, 32), 32)
                a = t0[rs, :]
                a = jnp.exp(a - jnp.max(a, axis=-1, keepdims=True))
                inv = 1.0 / jnp.sum(a, axis=-1, keepdims=True)
                pe[h, rs, :] = (a * inv).astype(BF)

        vt = venc[:, lanes]
        o0 = nn(pe[hp * 2], vt)
        o1 = nn(pe[hp * 2 + 1], vt)
        mixb[:, lanes] = jnp.where(half_lanes(o0.shape, 0), o0, o1).astype(BF)

    relay(4)
    t0[...] = nt(mixb[...], watt[7])

    def after_cross(rs):
        scv = stream_b[rs, :] + t0[rs, :]
        stream_c[rs, :] = scv
        n, _ = normed(scv)
        hid_c[rs, :] = (n * (1.0 + sf) + bf_).astype(BF)

    row_loop(ROWS, 32, after_cross)

    relay(5)
    acc0[...] = jnp.zeros_like(acc0)
    acc1[...] = jnp.zeros_like(acc1)

    @pl.loop(0, 4)
    def _(ft):
        cols = pl.ds(pl.multiple_of(ft * 512, 512), 512)
        t0[...] = nn(hid_c[...], wup[:, cols])
        t1[...] = nn(cot[...], wdn[:, cols])

        def gelu(rs):
            u = t0[rs, :]
            phi = 0.5 * (1.0 + lax.erf(u * (2.0**-0.5)))
            b0[rs, :] = (u * phi).astype(BF)
            slope = phi + u * (jnp.exp(-0.5 * u * u) * (1.0 / math.sqrt(2.0 * math.pi)))
            b1[rs, :] = (t1[rs, :] * slope).astype(BF)

        row_loop(ROWS, 32, gelu)
        acc0[...] += nt(b0[...], wdn[:, cols])
        acc1[...] += nt(b1[...], wup[:, cols])
        gffn[1, :, cols] = tn(cot[...], b0[...]).astype(BF)
        gffn[0, :, cols] = tn(hid_c[...], b1[...]).astype(BF)

    def back_norm(at, scale, grad_src, stream_src, base_src, want_out):
        mgrad[at : at + 2, :] = jnp.zeros((2, D), F)

        def body(rs):
            back, ds, db = norm_back(grad_src[rs, :], stream_src[rs, :], scale)
            total = base_src[rs, :].astype(F) + back
            in_grad[rs, :] = total
            gbf[rs, :] = total.astype(BF)
            mgrad[at : at + 1, :] += ds
            mgrad[at + 1 : at + 2, :] += db
            if want_out:
                out_ref[rs, :] = (stream_c[rs, :] + acc0[rs, :]).astype(BF)

        row_loop(ROWS, 32, body)

    leave(0)
    back_norm(4, sf, acc1, stream_c, cot, True)

    gatt[7] = tn(gbf[...], mixb[...]).astype(BF)
    mgr[...] = nn(gbf[...], watt[7]).astype(BF)

    @pl.loop(0, 4)
    def _(hp):
        lanes = pl.ds(pl.multiple_of(hp * 128, 128), 128)
        prod = mgr[:, lanes].astype(F) * mixb[:, lanes].astype(F)
        dqs, dks, dvs = [], [], []
        for half in range(2):
            h = hp * 2 + half
            inner = jnp.sum(keep(prod, half), axis=-1, keepdims=True)
            mg = keep(mgr[:, lanes], half)
            dp = nt(mg, venc[:, lanes])
            b0[...] = (pe[h].astype(F) * (dp - inner)).astype(BF)
            dqs.append(nn(b0[...], kenc[:, lanes]))
            dks.append(tn(b0[...], keep(qb[:, lanes], half)))
            dvs.append(tn(pe[h], mg))
        dq[:, lanes] = (jnp.where(half_lanes(dqs[0].shape, 0), dqs[0], dqs[1]) * 0.125).astype(BF)
        kenc[:, lanes] = (dks[0] + dks[1]).astype(BF)
        venc[:, lanes] = (dvs[0] + dvs[1]).astype(BF)

    gatt[4] = tn(hid_b[...], dq[...]).astype(BF)
    gatt[5] = tn(enc[...], kenc[...]).astype(BF)
    gatt[6] = tn(enc[...], venc[...]).astype(BF)
    egrad[...] = (nt(kenc[...], watt[5]) + nt(venc[...], watt[6])).astype(BF)
    leave(1)
    acc1[...] = nt(dq[...], watt[4])
    back_norm(2, sb, acc1, stream_b, in_grad, False)

    gatt[3] = tn(gbf[...], mixa[...]).astype(BF)
    mgr[...] = nn(gbf[...], watt[3]).astype(BF)

    @pl.when(odd == 0)
    def _():
        for h in range(8):
            ps[h, ROWS:LOC, :] = jnp.zeros((LOC - ROWS, 256), BF)
        spec_o[:, ROWS:LOC, :] = jnp.zeros((2, LOC - ROWS, 128), F)

    @pl.when(odd == 1)
    def _():
        for h in range(8):
            ps[h, 0:64, :] = jnp.zeros((64, 256), BF)
        spec_o[:, 0:64, :] = jnp.zeros((2, 64, 128), F)

    @pl.loop(0, 4)
    def _(hp):
        lanes = pl.ds(pl.multiple_of(hp * 128, 128), 128)
        prod = mgr[:, lanes].astype(F) * mixa[:, lanes].astype(F)
        dqs, dks, dvs = [], [], []
        dks_s = [[], [], []]
        dvs_s = [[], [], []]
        for half in range(2):
            h = hp * 2 + half
            inner = jnp.sum(keep(prod, half), axis=-1, keepdims=True)
            mg = keep(mgr[:, lanes], half)
            qm = keep(qbuf[own, lanes], half)
            dp = nt(mg, vbuf[0:TRK, lanes])
            ds = (pt[h].astype(F) * (dp - inner)).astype(BF)
            spec_o[0, own, :] = mg.astype(F)
            spec_o[1, own, :] = jnp.broadcast_to(inner, (ROWS, 128))
            dq_s = []
            for lb in range(3):
                r = slice(lb * BLK, (lb + 1) * BLK)
                k_rows = slice(TRK + lb * 256, TRK + (lb + 1) * 256)
                mgl = spec_o[0, r, :].astype(BF)
                dpl = nt(mgl, vbuf[k_rows, lanes])
                inner_l = spec_o[1, r, 0:1]
                dsl = (ps[h, r, :].astype(F) * (dpl - inner_l)).astype(BF)
                ss[r, 0:128] = nn(dsl, kbuf[k_rows, lanes])
                dks_s[lb].append(tn(dsl, keep(qbuf[r, lanes], half)))
                dvs_s[lb].append(tn(ps[h, r, :], mgl))
            dqs.append(nn(ds, kbuf[0:TRK, lanes]) + ss[own, 0:128])
            dks.append(tn(ds, qm))
            dvs.append(tn(pt[h], mg))
        dq[:, lanes] = (jnp.where(half_lanes(dqs[0].shape, 0), dqs[0], dqs[1]) * 0.125).astype(BF)
        kbuf[0:TRK, lanes] = (dks[0] + dks[1]).astype(BF)
        vbuf[0:TRK, lanes] = (dvs[0] + dvs[1]).astype(BF)
        for lb in range(3):
            k_rows = slice(TRK + lb * 256, TRK + (lb + 1) * 256)
            kbuf[k_rows, lanes] = (dks_s[lb][0] + dks_s[lb][1]).astype(BF)
            vbuf[k_rows, lanes] = (dvs_s[lb][0] + dvs_s[lb][1]).astype(BF)

        @pl.when(hp == 1)
        def _():
            leave(2)

        @pl.when(hp == 3)
        def _():
            leave(3)

    wk_acc[...] = jnp.zeros_like(wk_acc)
    wv_acc[...] = jnp.zeros_like(wv_acc)

    def key_side(rs):
        wk_acc[...] += tn(hid[rs, :], kbuf[rs, :])
        wv_acc[...] += tn(hid[rs, :], vbuf[rs, :])
        hid[rs, :] = (nt(kbuf[rs, :], watt[1]) + nt(vbuf[rs, :], watt[2])).astype(BF)

    row_loop(KV, 256, key_side)

    def put_trunk(rs):
        tok[rs, :] = hid[rs, :]

    row_loop(TRK, 64, put_trunk)
    for b in range(BRANCHES):
        hits = [is_parent(lb, b) for lb in range(3)]
        for piece in range(4):
            total = jnp.zeros((32, D), F)
            for lb in range(3):
                at = TRK + lb * 256 + piece * 32
                total += jnp.where(hits[lb], hid[at : at + 32, :].astype(F), 0.0)
            at = TRK + b * BLK + piece * 32
            tok[at : at + 32, :] = total.astype(BF)
    for lb in range(3):
        spec_g[lb * BLK : (lb + 1) * BLK, :] = hid[TRK + lb * 256 + BLK : TRK + (lb + 1) * 256, :]

    leave(4)
    gatt[0] = tn(hloc[own, :], dq[...]).astype(BF)
    gatt[1] = wk_acc[...].astype(BF)
    gatt[2] = wv_acc[...].astype(BF)
    leave(5)
    acc1[...] = nt(dq[...], watt[0])
    leave(6)

    wire.arrived(halo, s_halo, to_y, y == 0)

    def own_sum(rs):
        extra = spec_g[pl.ds(pl.multiple_of(rs.start + off, 32), 32), :].astype(F)
        acc1[rs, :] += extra

    row_loop(ROWS, 32, own_sum)

    @pl.when(y == 0)
    def _():
        acc1[ROWS - 64 : ROWS, :] += halo[...].astype(F)

    @pl.when(x == 0)
    def _():
        def body(rs):
            mine = tok[pl.ds(pl.multiple_of(ci * ROWS + rs.start, 32), 32), :].astype(F)
            for r in range(3):
                mine += rx_g[r, rs, :].astype(F)
            acc1[rs, :] += mine

        row_loop(ROWS, 32, body)

    @pl.when(ci == 4)
    def _():
        def body(rs):
            mine = tok[pl.ds(pl.multiple_of(4 * ROWS + rs.start, 32), 32), :].astype(F)
            acc1[rs, :] += mine + rx_g[0, rs, :].astype(F)

        row_loop(256, 32, body)

    mgrad[0:2, :] = jnp.zeros((2, D), F)
    mgrad[6:8, :] = jnp.zeros((2, D), F)

    def first_norm(rs):
        back, ds, db = norm_back(acc1[rs, :], tok_own[rs, :].astype(F), sa)
        in_grad[rs, :] += back
        mgrad[0:1, :] += ds
        mgrad[1:2, :] += db

    row_loop(ROWS, 32, first_norm)
    leave(7)

    wire.drain()
    peers(lambda k, to, _: ffn_z(k, to).wait_send())
    ctx_peers(lambda k, to, _: ffn_g(k, to).wait_send())
    for a in range(2):
        peers(lambda k, to, _, a=a: att_z(a, k, to).wait_send())
        ctx_peers(lambda k, to, _, a=a: att_g(a, k, to).wait_send())
    tree_peers(lambda k, to, _: mod_1(k, to).wait_send())
    peers(lambda k, to, _: mod_2(k, to).wait_send())
    peers(
        lambda k, to, _: wire.copy(
            cond_parts.at[to], cond_all.at[fs], s_cond + k, {"fsdp": to}
        ).wait_send()
    )
    peers(
        lambda k, to, _: wire.copy(
            part_out.at[to], part_in.at[fs], s_part + k, {"fsdp": to}
        ).wait_send()
    )
    for g in range(6):
        peers(
            lambda k, to, _, g=g: wire.copy(
                groups[g][0], place(g, my_rows, y, x, c), s_z[g] + k, {"fsdp": to}
            ).wait_send()
        )


def layer_call(n, parents, cond_parts, w_mod, tokens, enc, cot, weights):
    vm = pl.BlockSpec(memory_space=pltpu.VMEM)
    hbm = pl.BlockSpec(memory_space=pl.ANY)
    sds = jax.ShapeDtypeStruct
    rows = w_mod.shape[0]
    return pl.pallas_call(
        functools.partial(layer_kernel, n),
        out_shape=(
            sds((ROWS, D), BF),
            sds((ROWS, D), F),
            sds((ENC // 4, D), F),
            sds((rows, 6 * D), F),
            sds((8, rows, 256), F),
            sds((2, rows, 1024), F),
        ),
        in_specs=[pl.BlockSpec(memory_space=pltpu.SMEM), vm, vm, hbm, hbm, vm] + [hbm] * 6,
        out_specs=(vm, vm, vm, hbm, vm, vm),
        scratch_shapes=[
            pltpu.VMEM((8, D, D), BF),
            pltpu.VMEM((D, FF), BF),
            pltpu.VMEM((D, FF), BF),
            pltpu.VMEM((8 * ROWS + 64, D), BF),
            pltpu.VMEM((ENC, D), BF),
            pltpu.VMEM((n, 8, D), F),
            pltpu.VMEM((n, 8, D), F),
            pltpu.VMEM((8, D), F),
            pltpu.VMEM((*cond_parts.shape,), F),
            pltpu.VMEM((ROWS, D), BF),
            pltpu.VMEM((8, D), F),
            pltpu.VMEM((KV, D), BF),
            pltpu.VMEM((LOC, D), BF),
            pltpu.VMEM((KV, D), BF),
            pltpu.VMEM((KV, D), BF),
            pltpu.VMEM((LOC, D), BF),
            pltpu.VMEM((8, ROWS, TRK), BF),
            pltpu.VMEM((8, LOC, 256), BF),
            pltpu.VMEM((ROWS, TRK), BF),
            pltpu.VMEM((LOC, 256), BF),
            pltpu.VMEM((ROWS, TRK), F),
            pltpu.VMEM((LOC, 256), F),
            pltpu.VMEM((2, LOC, 128), F),
            pltpu.VMEM((ROWS, D), BF),
            pltpu.VMEM((ROWS, D), F),
            pltpu.VMEM((ROWS, D), F),
            pltpu.VMEM((ROWS, D), BF),
            pltpu.VMEM((ROWS, D), BF),
            pltpu.VMEM((ENC, D), BF),
            pltpu.VMEM((ENC, D), BF),
            pltpu.VMEM((ROWS, D), BF),
            pltpu.VMEM((8, ROWS, ENC), BF),
            pltpu.VMEM((ROWS, D), BF),
            pltpu.VMEM((ROWS, D), BF),
            pltpu.VMEM((ROWS, D), BF),
            pltpu.VMEM((ROWS, D), F),
            pltpu.VMEM((ROWS, D), F),
            pltpu.VMEM((ROWS, D), BF),
            pltpu.VMEM((ROWS, D), BF),
            pltpu.VMEM((ROWS, D), BF),
            pltpu.VMEM((D, D), F),
            pltpu.VMEM((D, D), F),
            pltpu.VMEM((8, D, D), BF),
            pltpu.VMEM((2, D, FF), BF),
            pltpu.VMEM((ENC, D), BF),
            pltpu.VMEM((2, 2, 4, D, 128), BF),
            pltpu.VMEM((2, 3, 2, D, 128), BF),
            pltpu.VMEM((2, n, 2, rows, 128), BF),
            pltpu.VMEM((2, 4, 2, rows, 128), BF),
            pltpu.VMEM((n, 2, rows, 256), BF),
            pltpu.VMEM((4, 2, rows, 256), BF),
            pltpu.VMEM((896, D), BF),
            pltpu.VMEM((3, ROWS, D), BF),
            pltpu.VMEM((64, D), BF),
            pltpu.VMEM((2, 128, D), BF),
            pltpu.VMEM((4, 128, D), BF),
            pltpu.VMEM((8, 8, D), F),
            pltpu.VMEM((n, 8, D), F),
            pltpu.SemaphoreType.DMA((12 * n + 124,)),
            pltpu.SemaphoreType.DMA((12 * n + 124,)),
            pltpu.SemaphoreType.DMA((9,)),
            pltpu.SemaphoreType.REGULAR,
        ],
        compiler_params=pltpu.CompilerParams(
            vmem_limit_bytes=VMEM_LIMIT, collective_id=0, has_side_effects=True
        ),
        name="layer",
    )(parents, cond_parts, w_mod, tokens, enc, cot, *weights)


def timestep_code(timesteps, width):
    half = width // 2
    frequency = jnp.exp(-math.log(10000.0) * jnp.arange(half, dtype=F) / half)
    angles = timesteps.astype(F)[:, None] * frequency[None, :]
    return jnp.concatenate([jnp.sin(angles), jnp.cos(angles)], axis=-1)


def per_device(
    tokens,
    encoder_states,
    timesteps,
    parents,
    w_mod,
    w_self_qkv,
    w_self_out,
    w_cross_qkv,
    w_cross_out,
    w_up,
    w_down,
    cotangent,
):
    rows = w_mod.shape[0]
    condition = jax.nn.silu(timestep_code(timesteps, D)).astype(BF)
    n = lax.axis_size("fsdp")
    padded_cond = jnp.pad(condition.astype(F).reshape(n, 1, rows), ((0, 0), (0, 7), (0, max(128 - rows, 0))))
    out, in_grad, enc_grad, grad_mod, att, ffn = layer_call(
        n,
        parents,
        padded_cond,
        w_mod,
        tokens,
        encoder_states,
        cotangent[0],
        (w_self_qkv, w_self_out, w_cross_qkv, w_cross_out, w_up, w_down),
    )
    return (
        out[None],
        in_grad[None],
        enc_grad[None],
        grad_mod,
        att[0:3],
        att[3],
        att[4:7],
        att[7],
        ffn[0],
        ffn[1],
    )


def solution(mesh):
    rows = P("fsdp", ("ctx", "tp"), None)
    return jax.shard_map(
        per_device,
        mesh=mesh,
        in_specs=(
            rows,
            P("fsdp", "ctx", None),
            P("fsdp"),
            P("fsdp", None),
            P("fsdp", None),
            P(None, "fsdp", "tp"),
            P("fsdp", "tp"),
            P(None, "fsdp", "tp"),
            P("fsdp", "tp"),
            P("fsdp", "tp"),
            P("fsdp", "tp"),
            rows,
        ),
        out_specs=(
            rows,
            rows,
            P("fsdp", "ctx", None),
            P("fsdp", None),
            P(None, "fsdp", "tp"),
            P("fsdp", "tp"),
            P(None, "fsdp", "tp"),
            P("fsdp", "tp"),
            P("fsdp", "tp"),
            P("fsdp", "tp"),
        ),
        check_vma=False,
    )
```

```python
import functools
import math

import jax
import jax.numpy as jnp
from jax import lax
from jax.experimental import pallas as pl
from jax.experimental.pallas import tpu as pltpu
from jax.sharding import PartitionSpec as P

BF = jnp.bfloat16
F = jnp.float32
D = 512
FF = 2048
HD = 64
ROWS = 320
LOC = 384
BLK = 128
TRUNK = 8
BRANCHES = 4
TRK = TRUNK * BLK
SHARED = (TRUNK + BRANCHES) * BLK
SPEC = 2 * LOC
KV = TRK + SPEC
ENC = 512
EPS = 1e-05
NEG = -1e30
VMEM_LIMIT = 67043328


def nn(a, b):
    return lax.dot_general(a, b, (((1,), (0,)), ((), ())), preferred_element_type=F)


def nt(a, b):
    return lax.dot_general(a, b, (((1,), (1,)), ((), ())), preferred_element_type=F)


def tn(a, b):
    return lax.dot_general(a, b, (((0,), (0,)), ((), ())), preferred_element_type=F)


def normed(v):
    center = v - jnp.mean(v, axis=-1, keepdims=True)
    rstd = lax.rsqrt(jnp.mean(center * center, axis=-1, keepdims=True) + EPS)
    return center * rstd, rstd


def norm_back(grad, stream, scale):
    n, rstd = normed(stream)
    gn = grad * (1.0 + scale)
    back = rstd * (
        gn
        - jnp.mean(gn, axis=-1, keepdims=True)
        - n * jnp.mean(gn * n, axis=-1, keepdims=True)
    )
    return back, jnp.sum(grad * n, axis=0, keepdims=True), jnp.sum(grad, axis=0, keepdims=True)


def row_loop(total, step, body, unroll=1):
    if unroll == 0:
        for i in range(total // step):
            body(pl.ds(i * step, step))
        return

    @pl.loop(0, total // (step * unroll))
    def _(i):
        for j in range(unroll):
            body(pl.ds(pl.multiple_of((i * unroll + j) * step, step), step))


def half_lanes(shape, half):
    lane = lax.broadcasted_iota(jnp.int32, shape, len(shape) - 1)
    return (lane // HD) == half


def keep(value, half):
    return jnp.where(half_lanes(value.shape, half), value, jnp.zeros_like(value))


MESH = pl.DeviceIdType.MESH


class Wire:
    def __init__(self, send, recv):
        self.send, self.recv, self.used, self.sent = send, recv, 0, []

    def slot(self, count=1):
        self.used += count
        return self.used - count

    def copy(self, src, dst, at, to):
        return pltpu.make_async_remote_copy(
            src_ref=src,
            dst_ref=dst,
            send_sem=self.send.at[at],
            recv_sem=self.recv.at[at],
            device_id=to,
            device_id_type=MESH,
        )

    def push(self, dst, at, to, when=None, src=None):
        src = src or dst
        if when is None:
            self.copy(src(), dst(), at, to).start()
        else:

            @pl.when(when)
            def _():
                self.copy(src(), dst(), at, to).start()

        self.sent.append((src, dst, at, to, when))

    def arrived(self, dst, at, to, when=None):
        if when is None:
            self.copy(dst, dst, at, to).wait_recv()
        else:

            @pl.when(when)
            def _():
                self.copy(dst, dst, at, to).wait_recv()

    def drain(self):
        for src, dst, at, to, when in self.sent:
            if when is None:
                self.copy(src(), dst(), at, to).wait_send()
            else:

                @pl.when(when)
                def _(src=src, dst=dst, at=at, to=to):
                    self.copy(src(), dst(), at, to).wait_send()

        self.sent = []


def layer_kernel(
    n,
    parents_ref,
    cond_parts,
    w_mod,
    tok_in,
    enc_in,
    cot,
    w_sqkv,
    w_so,
    w_cqkv,
    w_co,
    w_up,
    w_dn,
    out_ref,
    in_grad,
    enc_out,
    mod_out,
    att_out,
    ffn_out,
    watt,
    wup,
    wdn,
    tok,
    enc,
    part_out,
    part_in,
    mod,
    cond_all,
    tok_own,
    mgrad,
    hid,
    hloc,
    kbuf,
    vbuf,
    qbuf,
    pt,
    ps,
    bias_t,
    bias_s,
    st,
    ss,
    spec_o,
    mixa,
    stream_b,
    stream_c,
    hid_b,
    hid_c,
    kenc,
    venc,
    qb,
    pe,
    mixb,
    b0,
    b1,
    acc0,
    acc1,
    gbf,
    mgr,
    dq,
    wk_acc,
    wv_acc,
    gatt,
    gffn,
    egrad,
    rc_att,
    rx_att,
    zr_att,
    rg_att,
    zr_ffn,
    rg_ffn,
    rc_g,
    rx_g,
    halo,
    rc_e,
    rx_e,
    mod1,
    mod2,
    send,
    recv,
    local,
    ready,
):
    t0, t1 = st.at[:, 0:D], st.at[:, D : 2 * D]
    fs = lax.axis_index("fsdp")
    cx = lax.axis_index("ctx")
    y = lax.axis_index("tp")
    x, c = cx // 2, lax.rem(cx, 2)
    ci = cx * 2 + y
    odd = y
    off = pl.multiple_of(odd * 64, 64)
    own = pl.ds(off, ROWS)
    base = (ci * 5) // 2
    rows = w_mod.shape[0]
    to_y = {"tp": 1 - y}
    to_c = {"ctx": 2 * x + 1 - c}
    to_x = {"ctx": 2 * (1 - x) + c}
    wire = Wire(send, recv)

    my_rows = pl.ds(pl.multiple_of(fs * rows, rows), rows)

    def att_cols(yy, cc):
        return pl.ds(pl.multiple_of(yy * 256 + cc * 128, 128), 128)

    def ffn_cols(yy, xx, cc):
        return pl.ds(pl.multiple_of(yy * 1024 + xx * 512 + cc * 256, 256), 256)

    half = pl.ds(pl.multiple_of(c * 128, 128), 128)
    quarter = pl.ds(pl.multiple_of(cx * 256, 256), 256)
    groups = (
        (w_sqkv.at[:, :, half], watt, slice(0, 3), 0),
        (w_so.at[:, half], watt, 3, 0),
        (w_cqkv.at[:, :, half], watt, slice(4, 7), 0),
        (w_co.at[:, half], watt, 7, 0),
        (w_up.at[:, quarter], wup, None, 1),
        (w_dn.at[:, quarter], wdn, None, 1),
    )

    def place(g, row_at, yy, xx, cc):
        _, buf, index, wide = groups[g]
        if wide:
            return buf.at[row_at, ffn_cols(yy, xx, cc)]
        return buf.at[index, row_at, att_cols(yy, cc)]

    def chunk(i):
        return tok.at[pl.ds(pl.multiple_of(i * ROWS, ROWS), ROWS), :]

    def enc_part(i):
        return enc.at[pl.ds(pl.multiple_of(i * 128, 128), 128), :]

    all_rows = pl.ds(0, D)

    local_copies = [
        pltpu.make_async_copy(tok_in.at[0], chunk(ci), local.at[0]),
        pltpu.make_async_copy(enc_in.at[0], enc_part(cx), local.at[1]),
    ] + [
        pltpu.make_async_copy(groups[g][0], place(g, my_rows, y, x, c), local.at[2 + g])
        for g in range(6)
    ]
    local_copies.append(pltpu.make_async_copy(tok_in.at[0], tok_own, local.at[8]))
    for copy in local_copies:
        copy.start()

    barrier = pltpu.get_barrier_semaphore()

    @pl.loop(1, n)
    def _(k):
        pl.semaphore_signal(
            barrier, inc=1, device_id={"fsdp": lax.rem(fs + k, n)}, device_id_type=MESH
        )

    @pl.loop(1, 8)
    def _(k):
        other = lax.rem(ci + k, 8)
        pl.semaphore_signal(
            barrier,
            inc=1,
            device_id={"ctx": other // 2, "tp": lax.rem(other, 2)},
            device_id_type=MESH,
        )

    pl.semaphore_wait(barrier, n - 1 + 7)

    def peers(make):
        @pl.loop(1, n)
        def _(k):
            make(k, lax.rem(fs + k, n), lax.rem(fs + n - k, n))

    s_cond = wire.slot(n)
    s_part = wire.slot(n)
    s_z = [wire.slot(n) for _ in range(6)]
    s_y = [wire.slot() for _ in range(6)]
    s_c0 = [wire.slot() for _ in range(6)]
    s_c1 = [wire.slot() for _ in range(6)]
    s_x0 = [wire.slot() for _ in range(6)]
    s_x1 = [wire.slot() for _ in range(6)]
    s_c2 = [wire.slot() for _ in range(6)]
    s_c3 = [wire.slot() for _ in range(6)]
    s_ty, s_tx, s_txy, s_tc0, s_tc1, s_tc2, s_tc3 = (wire.slot() for _ in range(7))
    s_ex, s_ec0, s_ec1 = (wire.slot() for _ in range(3))

    peers(
        lambda k, to, _: wire.copy(
            cond_parts.at[to], cond_all.at[fs], s_cond + k, {"fsdp": to}
        ).start()
    )
    wire.push(lambda: chunk(ci), s_ty, to_y, None, lambda: tok_in.at[0])
    wire.push(lambda: chunk(ci), s_tx, to_x, x == 0, lambda: tok_in.at[0])
    wire.push(lambda: chunk(ci), s_tc0, to_c, None, lambda: tok_in.at[0])

    def z_start(g):
        peers(
            lambda k, to, _: wire.copy(
                groups[g][0], place(g, my_rows, y, x, c), s_z[g] + k, {"fsdp": to}
            ).start()
        )

    z_start(0)
    wire.push(lambda: enc_part(cx), s_ex, to_x, None, lambda: enc_in.at[0])
    wire.push(lambda: enc_part(cx), s_ec0, to_c, None, lambda: enc_in.at[0])

    def mask_trunk(rs):
        row = lax.broadcasted_iota(jnp.int32, (32, TRK), 0) + rs.start + ci * ROWS
        col = lax.broadcasted_iota(jnp.int32, (32, TRK), 1)
        bias_t[rs, :] = jnp.where(col <= row, 0.0, NEG).astype(BF)

    row_loop(ROWS, 32, mask_trunk)
    for lb in range(3):
        blk = base + lb
        row = lax.broadcasted_iota(jnp.int32, (BLK, 2 * BLK), 0)
        col = lax.broadcasted_iota(jnp.int32, (BLK, 2 * BLK), 1)
        par_ok = jnp.logical_and(col < BLK, blk >= TRUNK + BRANCHES)
        self_ok = jnp.logical_and(
            jnp.logical_and(col >= BLK, col - BLK <= row), blk >= TRUNK
        )
        bias_s[lb * BLK : (lb + 1) * BLK, :] = jnp.where(
            jnp.logical_or(par_ok, self_ok), 0.0, NEG
        ).astype(BF)

    cond_all[fs] = cond_parts[fs]
    peers(lambda k, _, src: wire.arrived(cond_all.at[src], s_cond + k, {"fsdp": src}))
    for v in range(6):
        part_out[:, v, :] = nn(
            cond_all[:, 0, 0:rows].astype(BF), w_mod[:, v * D : (v + 1) * D]
        )
    part_out[:, 6:8, :] = jnp.zeros((n, 2, D), F)
    peers(
        lambda k, to, _: wire.copy(
            part_out.at[to], part_in.at[fs], s_part + k, {"fsdp": to}
        ).start()
    )
    part_in[fs] = part_out[fs]

    def z_done(g):
        local_copies[2 + g].wait()
        peers(
            lambda k, _, src: wire.arrived(
                place(g, pl.ds(pl.multiple_of(src * rows, rows), rows), y, x, c),
                s_z[g] + k,
                {"fsdp": src},
            )
        )
        slab = lambda: place(g, all_rows, y, x, c)
        wire.push(slab, s_y[g], to_y)
        if groups[g][3]:
            wire.push(slab, s_x0[g], to_x)
        wire.push(slab, s_c0[g], to_c)

    def y_done(g):
        slab = lambda: place(g, all_rows, 1 - y, x, c)
        wire.arrived(slab(), s_y[g], to_y)
        if groups[g][3]:
            wire.push(slab, s_x1[g], to_x)
        wire.push(slab, s_c1[g], to_c)

    def x_done(g):
        for yy, s_in, s_out in ((y, s_x0[g], s_c2[g]), (1 - y, s_x1[g], s_c3[g])):
            slab = lambda yy=yy: place(g, all_rows, yy, 1 - x, c)
            wire.arrived(slab(), s_in, to_x)
            wire.push(slab, s_out, to_c)

    def c_done(g):
        wire.arrived(place(g, all_rows, y, x, 1 - c), s_c0[g], to_c)
        wire.arrived(place(g, all_rows, 1 - y, x, 1 - c), s_c1[g], to_c)
        if groups[g][3]:
            wire.arrived(place(g, all_rows, y, 1 - x, 1 - c), s_c2[g], to_c)
            wire.arrived(place(g, all_rows, 1 - y, 1 - x, 1 - c), s_c3[g], to_c)

    local_copies[0].wait()
    local_copies[1].wait()
    ciy = 4 * x + 2 * c + 1 - y
    cic = 4 * x + 2 * (1 - c) + y
    ciyc = 4 * x + 2 * (1 - c) + 1 - y
    low, lowy, lowc, lowyc = 2 * c + y, 2 * c + 1 - y, 2 * (1 - c) + y, 2 * (1 - c) + 1 - y
    right = x == 1
    local_copies[8].wait()
    wire.arrived(chunk(ciy), s_ty, to_y)
    wire.push(lambda: chunk(ciy), s_txy, to_x, x == 0)
    wire.push(lambda: chunk(ciy), s_tc1, to_c)
    wire.arrived(chunk(low), s_tx, to_x, right)
    wire.push(lambda: chunk(low), s_tc2, to_c, right)
    z_done(0)
    for g in (1, 2, 3):
        z_start(g)
    wire.arrived(enc_part(2 * (1 - x) + c), s_ex, to_x)
    wire.push(lambda: enc_part(2 * (1 - x) + c), s_ec1, to_c)
    wire.arrived(chunk(lowy), s_txy, to_x, right)
    wire.push(lambda: chunk(lowy), s_tc3, to_c, right)
    y_done(0)

    peers(lambda k, _, src: wire.arrived(part_in.at[src], s_part + k, {"fsdp": src}))
    mod[...] = jnp.sum(part_in[...], axis=0)
    sa, ba = mod[0:1, :], mod[1:2, :]
    sb, bb = mod[2:3, :], mod[3:4, :]
    sf, bf_ = mod[4:5, :], mod[5:6, :]

    wire.arrived(chunk(cic), s_tc0, to_c)
    wire.arrived(chunk(ciyc), s_tc1, to_c)
    wire.arrived(chunk(lowc), s_tc2, to_c, right)
    wire.arrived(chunk(lowyc), s_tc3, to_c, right)
    wire.arrived(enc_part(2 * x + 1 - c), s_ec0, to_c)
    wire.arrived(enc_part(2 * (1 - x) + 1 - c), s_ec1, to_c)
    tok_tb = tok
    tok_loc = tok.at[pl.ds(pl.multiple_of(ci * ROWS - off, 64), LOC), :]

    def relay(step):
        if step == 0:
            for g in (1, 2, 3):
                z_done(g)
            z_start(4)
            z_start(5)
        if step == 1:
            z_done(4)
        if step == 2:
            z_done(5)
            for g in (1, 2, 3):
                y_done(g)
        if step == 3:
            y_done(4)
        if step == 4:
            for g in (1, 2, 3):
                c_done(g)
            y_done(5)
            x_done(4)
        if step == 5:
            x_done(5)
        if step == 6:
            c_done(4)
            c_done(5)

    spec_g = qbuf

    def is_parent(lb, branch):
        parent = jnp.full((32, D), parents_ref[0, base + lb], jnp.int32)
        leaf = jnp.full((32, D), base + lb, jnp.int32) >= TRUNK + BRANCHES
        return jnp.logical_and(leaf, parent == TRUNK + branch)

    to_xy = {"ctx": 2 * (1 - x) + c, "tp": 1 - y}
    s_rcg, s_rcg4, s_rcg5, s_halo = (wire.slot() for _ in range(4))
    s_rxg = [wire.slot() for _ in range(3)]
    s_rce = [wire.slot(), wire.slot()]
    s_rxe = [wire.slot() for _ in range(3)]
    s_m1 = wire.slot(8)
    s_m2 = wire.slot(n)
    quad = ((to_y, x, 1 - y), (to_x, 1 - x, y), (to_xy, 1 - x, 1 - y))

    def add_rows(target, terms, total, step=64):
        def body(rs):
            value = terms[0][rs, :].astype(F)
            for term in terms[1:]:
                value += term[rs, :].astype(F)
            target[rs, :] = value.astype(BF)

        row_loop(total, step, body)

    def ctx_peers(make):
        @pl.loop(1, 4)
        def _(k):
            make(k, lax.rem(cx + k, 4), lax.rem(cx + 4 - k, 4))

    def strip(buf, at):
        return buf.at[:, at * 256 : (at + 1) * 256]

    class Family:
        def __init__(self, unit, core_box, box, landing, held, shape_rows):
            self.unit, self.core_box, self.box = unit, core_box, box
            self.landing, self.held = landing, held
            self.s_core = [[wire.slot() for _ in range(4)] for _ in range(2)]
            self.s_one = [[wire.slot() for _ in range(2)] for _ in range(2)]
            self.s_two = [wire.slot() for _ in range(2)]
            self.s_z = [wire.slot(n) for _ in range(2)]
            self.s_g = wire.slot(4)

        def core_send(self):
            for m in range(2):
                for t in range(4):
                    wire.push(
                        lambda m=m, t=t: self.core_box(m, t),
                        self.s_core[m][t],
                        to_c,
                        None,
                        lambda m=m, t=t: self.unit(m, t // 2, t % 2, 1 - c),
                    )

        def first_send(self):
            for m in range(2):
                for t in range(4):
                    wire.arrived(self.core_box(m, t), self.s_core[m][t], to_c)
                    mine = self.unit(m, t // 2, t % 2, c)
                    add_rows(mine, (mine, self.core_box(m, t)), D)
            for j in range(2):
                wire.push(
                    lambda j=j: self.box(j),
                    self.s_one[0][j],
                    to_x,
                    None,
                    lambda j=j: self.unit(0, j, 1 - x, c),
                )
                wire.push(
                    lambda j=j: self.box(2 + j),
                    self.s_one[1][j],
                    to_y,
                    None,
                    lambda j=j: self.unit(1, 1 - y, j, c),
                )

        def second_send(self):
            for j in range(2):
                wire.arrived(self.box(j), self.s_one[0][j], to_x)
                mine = self.unit(0, j, x, c)
                add_rows(mine, (mine, self.box(j)), D)
            wire.push(
                lambda: self.box(4),
                self.s_two[0],
                to_y,
                None,
                lambda: self.unit(0, 1 - y, x, c),
            )
            for j in range(2):
                wire.arrived(self.box(2 + j), self.s_one[1][j], to_y)
                mine = self.unit(1, y, j, c)
                add_rows(mine, (mine, self.box(2 + j)), D)
            wire.push(
                lambda: self.box(5),
                self.s_two[1],
                to_x,
                None,
                lambda: self.unit(1, y, 1 - x, c),
            )

        def z_copy(self, m, k, to):
            part = pl.ds(pl.multiple_of(to * rows, rows), rows)
            return wire.copy(
                self.unit(m, y, x, c).at[part, :],
                self.landing.at[fs, m],
                self.s_z[m] + k,
                {"fsdp": to},
            )

        def tree_send(self):
            for m, target in ((0, to_y), (1, to_x)):
                wire.arrived(self.box(4 + m), self.s_two[m], target)
                mine = self.unit(m, y, x, c)
                add_rows(mine, (mine, self.box(4 + m)), D)
                peers(lambda k, to, _, m=m: self.z_copy(m, k, to).start())
                self.landing[fs, m] = self.unit(m, y, x, c)[my_rows, :]

        def g_copy(self, k, to):
            return wire.copy(self.held.at[cx], self.held.at[cx], self.s_g + k, {"ctx": to})

        def copy_send(self):
            for m in range(2):
                peers(
                    lambda k, _, src, m=m: wire.arrived(
                        self.landing.at[src, m], self.s_z[m] + k, {"fsdp": src}
                    )
                )
            self.held[cx] = jnp.sum(self.landing[...].astype(F), axis=0).astype(BF)
            ctx_peers(lambda k, to, _: self.g_copy(k, to).start())

        def collect(self):
            ctx_peers(
                lambda k, _, src: wire.arrived(self.held.at[src], self.s_g + k, {"ctx": src})
            )

        def drain(self):
            for m in range(2):
                peers(lambda k, to, _, m=m: self.z_copy(m, k, to).wait_send())
            ctx_peers(lambda k, to, _: self.g_copy(k, to).wait_send())

    ffn = Family(
        lambda m, yy, xx, cc: gffn.at[m, :, ffn_cols(yy, xx, cc)],
        lambda m, t: strip(wup, m * 4 + t),
        lambda i: strip(wdn, i),
        zr_ffn,
        rg_ffn,
        rows,
    )

    def attention_family(a):
        return Family(
            lambda m, yy, xx, cc: gatt.at[4 * a + 2 * xx + m, :, att_cols(yy, cc)],
            lambda m, t: rc_att.at[a, m, t],
            lambda i: rx_att.at[a, i],
            zr_att.at[a],
            rg_att.at[a],
            rows,
        )

    att = (attention_family(0), attention_family(1))

    def ffn_core_send():
        wire.drain()
        for target in (to_c, to_y, to_x):
            pl.semaphore_signal(ready, inc=1, device_id=target, device_id_type=MESH)
        pl.semaphore_wait(ready, 3)
        ffn.core_send()

    def ffn_finish():
        ffn.collect()
        for q in range(4):
            ffn_out[:, :, q * 256 : (q + 1) * 256] = rg_ffn[q].astype(F)

    def att_finish(a):
        att[a].collect()
        for q in range(4):
            for m in range(2):
                at = 4 * a + 2 * (q // 2) + m
                att_out[at, :, (q % 2) * 128 : (q % 2) * 128 + 128] = rg_att[a, q, m].astype(F)

    def enc_core_send():
        for xx in range(2):
            wire.push(
                lambda xx=xx: rc_e.at[xx],
                s_rce[xx],
                to_c,
                None,
                lambda xx=xx: egrad.at[pl.ds(pl.multiple_of((2 * xx + 1 - c) * 128, 128), 128), :],
            )

    def enc_rows(xx):
        return egrad.at[pl.ds(pl.multiple_of((2 * xx + c) * 128, 128), 128), :]

    def enc_chip_send():
        for xx in range(2):
            wire.arrived(rc_e.at[xx], s_rce[xx], to_c)
            add_rows(enc_rows(xx), (enc_rows(xx), rc_e.at[xx]), 128)
        for r, (target, xx, _) in enumerate(quad):
            wire.push(
                lambda: rx_e.at[2 * x + y], s_rxe[r], target, None, lambda xx=xx: enc_rows(xx)
            )
        rx_e[2 * x + y] = enc_rows(x)[...]

    def enc_finish():
        for r, (target, xx, yy) in enumerate(quad):
            wire.arrived(rx_e.at[2 * xx + yy], s_rxe[r], target)
        enc_out[...] = jnp.sum(rx_e[...].astype(F), axis=0)

    def shared_core_send():
        to_core = pl.ds(pl.multiple_of(640 * (1 - c), 640), 640)
        wire.push(lambda: rc_g.at[0:640], s_rcg, to_c, None, lambda: tok.at[to_core, :])
        wire.push(
            lambda: rc_g.at[640:896],
            s_rcg4,
            to_c,
            jnp.logical_and(x == 1, c == 1),
            lambda: tok.at[1280:1536, :],
        )
        wire.push(lambda: halo, s_halo, to_y, y == 1, lambda: spec_g.at[0:64, :])

    def shared_y_send():
        wire.arrived(rc_g.at[0:640], s_rcg, to_c)
        mine = tok.at[pl.ds(pl.multiple_of(640 * c, 640), 640), :]
        add_rows(mine, (mine, rc_g.at[0:640]), 640)
        last = jnp.logical_and(x == 1, c == 0)

        @pl.when(last)
        def _():
            wire.arrived(rc_g.at[640:896], s_rcg4, to_c)
            four = tok.at[1280:1536, :]
            add_rows(four, (four, rc_g.at[640:896]), 256)

        def rows_of(yy):
            return lambda: chunk(2 * c + yy)

        wire.push(lambda: rx_g.at[0], s_rxg[0], to_y, None, rows_of(1 - y))
        wire.push(
            lambda: rx_g.at[1, 0:256],
            s_rcg5,
            to_y,
            jnp.logical_and(last, y == 1),
            lambda: tok.at[1280:1536, :],
        )

    def shared_x_send():
        wire.arrived(rx_g.at[0], s_rxg[0], to_y)
        mine = chunk(2 * c + y)
        add_rows(mine, (mine, rx_g.at[0]), ROWS)
        wire.push(lambda: rx_g.at[1], s_rxg[1], to_x, x == 1, lambda: chunk(2 * c + y))

    def shared_arrived():
        wire.arrived(rx_g.at[1], s_rxg[1], to_x, x == 0)
        wire.arrived(rx_g.at[1, 0:256], s_rcg5, to_y, ci == 4)

    def tree_peers(make):
        @pl.loop(1, 8)
        def _(k):
            make(k, lax.rem(ci + k, 8), lax.rem(ci + 8 - k, 8))

    def device_of(i):
        return {"ctx": i // 2, "tp": lax.rem(i, 2)}

    def mod_1(k, to):
        return wire.copy(mgrad, mod1.at[ci], s_m1 + k, device_of(to))

    def mod_2(k, to):
        return wire.copy(mod2.at[fs], mod2.at[fs], s_m2 + k, {"fsdp": to})

    def mod_tree_send():
        tree_peers(lambda k, to, _: mod_1(k, to).start())
        mod1[ci] = mgrad[...]

    def mod_all_send():
        tree_peers(lambda k, _, src: wire.arrived(mod1.at[src], s_m1 + k, device_of(src)))
        mod2[fs] = jnp.sum(mod1[...], axis=0)
        peers(lambda k, to, _: mod_2(k, to).start())

    def mod_finish():
        peers(lambda k, _, src: wire.arrived(mod2.at[src], s_m2 + k, {"fsdp": src}))
        cond = cond_all[:, 0, 0:rows]
        for v in range(6):
            held = (wk_acc, wv_acc)[v // 4]
            at = (v % 4) * rows
            held[at : at + rows, :] = lax.dot_general(
                cond,
                mod2[:, v, :],
                (((0,), (0,)), ((), ())),
                precision=lax.Precision.HIGHEST,
                preferred_element_type=F,
            )
        copies = [
            pltpu.make_async_copy(
                (wk_acc, wv_acc)[v // 4].at[(v % 4) * rows : (v % 4 + 1) * rows, :],
                mod_out.at[:, v * D : (v + 1) * D],
                local.at[v],
            )
            for v in range(6)
        ]
        for copy in copies:
            copy.start()
        for copy in copies:
            copy.wait()

    def leave(step):
        if step == 0:
            ffn_core_send()
        if step == 1:
            ffn.first_send()
        if step == 2:
            att[1].core_send()
            enc_core_send()
        if step == 3:
            att[1].first_send()
            enc_chip_send()
        if step == 4:
            ffn.second_send()
        if step == 5:
            att[1].second_send()
            ffn.tree_send()
        if step == 6:
            shared_core_send()
        if step == 7:
            att[0].core_send()
            shared_y_send()
        if step == 8:
            att[0].first_send()
            att[1].tree_send()
            ffn.copy_send()
            shared_x_send()
            enc_finish()
            att[0].second_send()
            att[1].copy_send()
            ffn_finish()
            shared_arrived()
        if step == 9:
            mod_tree_send()
            att[0].tree_send()
            att_finish(1)
            mod_all_send()
            att[0].copy_send()
            mod_finish()
            att_finish(0)

    def hidden(x):
        n, _ = normed(x.astype(F))
        return (n * (1.0 + sa) + ba).astype(BF)

    def hid_trunk(rs):
        hid[rs, :] = hidden(tok_tb[rs, :])

    row_loop(TRK, 32, hid_trunk, 8)

    def hid_loc(rs):
        hloc[rs, :] = hidden(tok_loc[rs, :])

    row_loop(LOC, 32, hid_loc, 6)
    for lb in range(3):
        picks = [is_parent(lb, b) for b in range(1, BRANCHES)]
        for piece in range(4):
            r = piece * 32
            picked = tok_tb[TRK + r : TRK + r + 32, :].astype(F)
            for b in range(1, BRANCHES):
                at = TRK + b * BLK + r
                picked = jnp.where(picks[b - 1], tok_tb[at : at + 32, :].astype(F), picked)
            at = TRK + lb * 256 + r
            hid[at : at + 32, :] = hidden(picked)
        hid[TRK + lb * 256 + BLK : TRK + lb * 256 + 2 * BLK, :] = hloc[
            lb * BLK : (lb + 1) * BLK, :
        ]

    def project(rs):
        kbuf[rs, :] = nn(hid[rs, :], watt[1]).astype(BF)
        vbuf[rs, :] = nn(hid[rs, :], watt[2]).astype(BF)

    c_done(0)
    row_loop(KV, 256, project)
    qbuf[...] = (nn(hloc[...], watt[0]) * 0.125).astype(BF)

    linv_a, linv_b = wk_acc.at[0:ROWS, :], wv_acc.at[0:ROWS, :]

    def with_ones(values, half):
        return jnp.where(half_lanes(values.shape, half), values, jnp.ones_like(values))

    def finish_heads(o0, o1, mixed, linv, lanes):
        inv0, inv1 = 1.0 / pltpu.roll(o0, HD, 1), 1.0 / pltpu.roll(o1, HD, 1)
        first = half_lanes(o0.shape, 0)
        mixed[:, lanes] = jnp.where(first, o0 * inv0, o1 * inv1).astype(BF)
        linv[:, lanes] = jnp.where(first, inv0, inv1)

    @pl.loop(0, 4)
    def _(hp):
        for step in range(4):

            @pl.when(hp == step)
            def _(step=step):
                relay(step)

        lanes = pl.ds(pl.multiple_of(hp * 128, 128), 128)
        kt = kbuf[0:TRK, lanes]
        vt = vbuf[0:TRK, lanes]
        outs = []
        for half in range(2):
            h = hp * 2 + half
            st[...] = nt(keep(qbuf[own, lanes], half), kt) + bias_t[...].astype(F)
            for lb in range(3):
                r = slice(lb * BLK, (lb + 1) * BLK)
                ks = kbuf[TRK + lb * 256 : TRK + (lb + 1) * 256, lanes]
                ss[r, :] = nt(keep(qbuf[r, lanes], half), ks) + bias_s[r, :].astype(F)
            for i in range(ROWS // 32):
                rs = slice(i * 32, i * 32 + 32)
                ro = pl.ds(pl.multiple_of(i * 32 + off, 32), 32)
                a, b = st[rs, :], ss[ro, :]
                top = jnp.maximum(
                    jnp.max(a, axis=-1, keepdims=True), jnp.max(b, axis=-1, keepdims=True)
                )
                pt[h, rs, :] = jnp.exp(a - top).astype(BF)
                ps[h, ro, :] = jnp.exp(b - top).astype(BF)
            for lb in range(3):
                r = slice(lb * BLK, (lb + 1) * BLK)
                vs = vbuf[TRK + lb * 256 : TRK + (lb + 1) * 256, lanes]
                spec_o[half, r, :] = nn(ps[h, r, :], with_ones(vs, half))
            outs.append(nn(pt[h], with_ones(vt, half)) + spec_o[half, own, :])
        finish_heads(outs[0], outs[1], mixa, linv_a, lanes)

    relay(4)
    t0[...] = nt(mixa[...], watt[3])

    def after_self(rs):
        sbv = tok_own[rs, :].astype(F) + t0[rs, :]
        stream_b[rs, :] = sbv
        n, _ = normed(sbv)
        hid_b[rs, :] = (n * (1.0 + sb) + bb).astype(BF)

    row_loop(ROWS, 32, after_self, 0)

    kenc[...] = nn(enc[...], watt[5]).astype(BF)
    venc[...] = nn(enc[...], watt[6]).astype(BF)
    qb[...] = (nn(hid_b[...], watt[4]) * 0.125).astype(BF)

    @pl.loop(0, 4)
    def _(hp):
        lanes = pl.ds(pl.multiple_of(hp * 128, 128), 128)
        kt = kenc[:, lanes]
        vt = venc[:, lanes]
        outs = []
        for half in range(2):
            h = hp * 2 + half
            t0[...] = nt(keep(qb[:, lanes], half), kt)
            for i in range(ROWS // 32):
                rs = slice(i * 32, i * 32 + 32)
                a = t0[rs, :]
                pe[h, rs, :] = jnp.exp(a - jnp.max(a, axis=-1, keepdims=True)).astype(BF)
            outs.append(nn(pe[h], with_ones(vt, half)))
        finish_heads(outs[0], outs[1], mixb, linv_b, lanes)

    relay(5)
    t0[...] = nt(mixb[...], watt[7])

    def after_cross(rs):
        scv = stream_b[rs, :] + t0[rs, :]
        stream_c[rs, :] = scv
        n, _ = normed(scv)
        hid_c[rs, :] = (n * (1.0 + sf) + bf_).astype(BF)

    row_loop(ROWS, 32, after_cross, 0)

    relay(6)
    acc0[...] = jnp.zeros_like(acc0)
    acc1[...] = jnp.zeros_like(acc1)

    @pl.loop(0, 4)
    def _(ft):
        cols = pl.ds(pl.multiple_of(ft * 512, 512), 512)
        t0[...] = nn(hid_c[...], wup[:, cols])
        t1[...] = nn(cot[...], wdn[:, cols])

        def gelu(rs):
            u = t0[rs, :]
            phi = 0.5 * (1.0 + lax.erf(u * (2.0**-0.5)))
            b0[rs, :] = (u * phi).astype(BF)
            slope = phi + u * (jnp.exp(-0.5 * u * u) * (1.0 / math.sqrt(2.0 * math.pi)))
            b1[rs, :] = (t1[rs, :] * slope).astype(BF)

        row_loop(ROWS, 32, gelu)
        acc0[...] += nt(b0[...], wdn[:, cols])
        acc1[...] += nt(b1[...], wup[:, cols])
        gffn[1, :, cols] = tn(cot[...], b0[...]).astype(BF)
        gffn[0, :, cols] = tn(hid_c[...], b1[...]).astype(BF)

    def back_norm(at, scale, grad_src, stream_src, base_src, want_out):
        sums = [jnp.zeros((1, D), F), jnp.zeros((1, D), F)]
        for i in range(ROWS // 32):
            rs = slice(i * 32, i * 32 + 32)
            back, ds, db = norm_back(grad_src[rs, :], stream_src[rs, :], scale)
            total = base_src[rs, :].astype(F) + back
            in_grad[rs, :] = total
            gbf[rs, :] = total.astype(BF)
            sums = [sums[0] + ds, sums[1] + db]
            if want_out:
                out_ref[rs, :] = (stream_c[rs, :] + acc0[rs, :]).astype(BF)
        mgrad[at : at + 1, :] = sums[0]
        mgrad[at + 1 : at + 2, :] = sums[1]

    leave(0)
    back_norm(4, sf, acc1, stream_c, cot, True)

    gatt[7] = tn(gbf[...], mixb[...]).astype(BF)
    mgr[...] = (nn(gbf[...], watt[7]) * linv_b[...]).astype(BF)

    @pl.loop(0, 4)
    def _(hp):
        lanes = pl.ds(pl.multiple_of(hp * 128, 128), 128)
        prod = mgr[:, lanes].astype(F) * mixb[:, lanes].astype(F)
        dqs, dks, dvs = [], [], []
        for half in range(2):
            h = hp * 2 + half
            inner = jnp.sum(keep(prod, half), axis=-1, keepdims=True)
            mg = keep(mgr[:, lanes], half)
            dp = nt(mg, venc[:, lanes])
            b0[...] = (pe[h].astype(F) * (dp - inner)).astype(BF)
            dqs.append(nn(b0[...], kenc[:, lanes]))
            dks.append(tn(b0[...], keep(qb[:, lanes], half)))
            dvs.append(tn(pe[h], mg))
        dq[:, lanes] = (jnp.where(half_lanes(dqs[0].shape, 0), dqs[0], dqs[1]) * 0.125).astype(BF)
        kenc[:, lanes] = (dks[0] + dks[1]).astype(BF)
        venc[:, lanes] = (dvs[0] + dvs[1]).astype(BF)

    leave(1)
    gatt[4] = tn(hid_b[...], dq[...]).astype(BF)
    gatt[5] = tn(enc[...], kenc[...]).astype(BF)
    gatt[6] = tn(enc[...], venc[...]).astype(BF)
    egrad[...] = (nt(kenc[...], watt[5]) + nt(venc[...], watt[6])).astype(BF)
    leave(2)
    acc1[...] = nt(dq[...], watt[4])
    back_norm(2, sb, acc1, stream_b, in_grad, False)

    gatt[3] = tn(gbf[...], mixa[...]).astype(BF)
    mgr[...] = (nn(gbf[...], watt[3]) * linv_a[...]).astype(BF)

    @pl.when(odd == 0)
    def _():
        for h in range(8):
            ps[h, ROWS:LOC, :] = jnp.zeros((LOC - ROWS, 256), BF)
        spec_o[:, ROWS:LOC, :] = jnp.zeros((2, LOC - ROWS, 128), F)

    @pl.when(odd == 1)
    def _():
        for h in range(8):
            ps[h, 0:64, :] = jnp.zeros((64, 256), BF)
        spec_o[:, 0:64, :] = jnp.zeros((2, 64, 128), F)

    @pl.loop(0, 4)
    def _(hp):
        lanes = pl.ds(pl.multiple_of(hp * 128, 128), 128)
        prod = mgr[:, lanes].astype(F) * mixa[:, lanes].astype(F)
        dqs, dks, dvs = [], [], []
        dks_s = [[], [], []]
        dvs_s = [[], [], []]
        for half in range(2):
            h = hp * 2 + half
            inner = jnp.sum(keep(prod, half), axis=-1, keepdims=True)
            mg = keep(mgr[:, lanes], half)
            qm = keep(qbuf[own, lanes], half)
            dp = nt(mg, vbuf[0:TRK, lanes])
            ds = (pt[h].astype(F) * (dp - inner)).astype(BF)
            spec_o[0, own, :] = mg.astype(F)
            spec_o[1, own, :] = jnp.broadcast_to(inner, (ROWS, 128))
            dq_s = []
            for lb in range(3):
                r = slice(lb * BLK, (lb + 1) * BLK)
                k_rows = slice(TRK + lb * 256, TRK + (lb + 1) * 256)
                mgl = spec_o[0, r, :].astype(BF)
                dpl = nt(mgl, vbuf[k_rows, lanes])
                inner_l = spec_o[1, r, 0:1]
                dsl = (ps[h, r, :].astype(F) * (dpl - inner_l)).astype(BF)
                ss[r, 0:128] = nn(dsl, kbuf[k_rows, lanes])
                dks_s[lb].append(tn(dsl, keep(qbuf[r, lanes], half)))
                dvs_s[lb].append(tn(ps[h, r, :], mgl))
            dqs.append(nn(ds, kbuf[0:TRK, lanes]) + ss[own, 0:128])
            dks.append(tn(ds, qm))
            dvs.append(tn(pt[h], mg))
        dq[:, lanes] = (jnp.where(half_lanes(dqs[0].shape, 0), dqs[0], dqs[1]) * 0.125).astype(BF)
        kbuf[0:TRK, lanes] = (dks[0] + dks[1]).astype(BF)
        vbuf[0:TRK, lanes] = (dvs[0] + dvs[1]).astype(BF)
        for lb in range(3):
            k_rows = slice(TRK + lb * 256, TRK + (lb + 1) * 256)
            kbuf[k_rows, lanes] = (dks_s[lb][0] + dks_s[lb][1]).astype(BF)
            vbuf[k_rows, lanes] = (dvs_s[lb][0] + dvs_s[lb][1]).astype(BF)

        for step in range(3):

            @pl.when(hp == step)
            def _(step=step):
                leave(3 + step)

    wk_acc[...] = jnp.zeros_like(wk_acc)
    wv_acc[...] = jnp.zeros_like(wv_acc)

    def key_side(rs):
        wk_acc[...] += tn(hid[rs, :], kbuf[rs, :])
        wv_acc[...] += tn(hid[rs, :], vbuf[rs, :])
        hid[rs, :] = (nt(kbuf[rs, :], watt[1]) + nt(vbuf[rs, :], watt[2])).astype(BF)

    row_loop(KV, 256, key_side)

    def put_trunk(rs):
        tok[rs, :] = hid[rs, :]

    row_loop(TRK, 64, put_trunk)
    for b in range(BRANCHES):
        hits = [is_parent(lb, b) for lb in range(3)]
        for piece in range(4):
            total = jnp.zeros((32, D), F)
            for lb in range(3):
                at = TRK + lb * 256 + piece * 32
                total += jnp.where(hits[lb], hid[at : at + 32, :].astype(F), 0.0)
            at = TRK + b * BLK + piece * 32
            tok[at : at + 32, :] = total.astype(BF)
    for lb in range(3):
        spec_g[lb * BLK : (lb + 1) * BLK, :] = hid[TRK + lb * 256 + BLK : TRK + (lb + 1) * 256, :]

    leave(6)
    gatt[0] = tn(hloc[own, :], dq[...]).astype(BF)
    gatt[1] = wk_acc[...].astype(BF)
    gatt[2] = wv_acc[...].astype(BF)
    leave(7)
    acc1[...] = nt(dq[...], watt[0])
    leave(8)

    wire.arrived(halo, s_halo, to_y, y == 0)

    def own_sum(rs):
        extra = spec_g[pl.ds(pl.multiple_of(rs.start + off, 32), 32), :].astype(F)
        acc1[rs, :] += extra

    row_loop(ROWS, 32, own_sum, 5)

    @pl.when(y == 0)
    def _():
        acc1[ROWS - 64 : ROWS, :] += halo[...].astype(F)

    @pl.when(x == 0)
    def _():
        def body(rs):
            mine = tok[pl.ds(pl.multiple_of(ci * ROWS + rs.start, 32), 32), :].astype(F)
            acc1[rs, :] += mine + rx_g[1, rs, :].astype(F)

        row_loop(ROWS, 32, body)

    @pl.when(ci == 4)
    def _():
        def body(rs):
            mine = tok[pl.ds(pl.multiple_of(4 * ROWS + rs.start, 32), 32), :].astype(F)
            acc1[rs, :] += mine + rx_g[1, rs, :].astype(F)

        row_loop(256, 32, body)

    mgrad[6:8, :] = jnp.zeros((2, D), F)
    sums = [jnp.zeros((1, D), F), jnp.zeros((1, D), F)]
    for i in range(ROWS // 32):
        rs = slice(i * 32, i * 32 + 32)
        back, ds, db = norm_back(acc1[rs, :], tok_own[rs, :].astype(F), sa)
        in_grad[rs, :] += back
        sums = [sums[0] + ds, sums[1] + db]
    mgrad[0:1, :] = sums[0]
    mgrad[1:2, :] = sums[1]
    leave(9)

    wire.drain()
    for family in (ffn, *att):
        family.drain()
    tree_peers(lambda k, to, _: mod_1(k, to).wait_send())
    peers(lambda k, to, _: mod_2(k, to).wait_send())
    peers(
        lambda k, to, _: wire.copy(
            cond_parts.at[to], cond_all.at[fs], s_cond + k, {"fsdp": to}
        ).wait_send()
    )
    peers(
        lambda k, to, _: wire.copy(
            part_out.at[to], part_in.at[fs], s_part + k, {"fsdp": to}
        ).wait_send()
    )
    for g in range(6):
        peers(
            lambda k, to, _, g=g: wire.copy(
                groups[g][0], place(g, my_rows, y, x, c), s_z[g] + k, {"fsdp": to}
            ).wait_send()
        )


def layer_call(n, parents, cond_parts, w_mod, tokens, enc, cot, weights):
    vm = pl.BlockSpec(memory_space=pltpu.VMEM)
    hbm = pl.BlockSpec(memory_space=pl.ANY)
    sds = jax.ShapeDtypeStruct
    rows = w_mod.shape[0]
    return pl.pallas_call(
        functools.partial(layer_kernel, n),
        out_shape=(
            sds((ROWS, D), BF),
            sds((ROWS, D), F),
            sds((ENC // 4, D), F),
            sds((rows, 6 * D), F),
            sds((8, rows, 256), F),
            sds((2, rows, 1024), F),
        ),
        in_specs=[pl.BlockSpec(memory_space=pltpu.SMEM), vm, vm, hbm, hbm, vm] + [hbm] * 6,
        out_specs=(vm, vm, vm, hbm, vm, vm),
        scratch_shapes=[
            pltpu.VMEM((8, D, D), BF),
            pltpu.VMEM((D, FF), BF),
            pltpu.VMEM((D, FF), BF),
            pltpu.VMEM((8 * ROWS + 64, D), BF),
            pltpu.VMEM((ENC, D), BF),
            pltpu.VMEM((n, 8, D), F),
            pltpu.VMEM((n, 8, D), F),
            pltpu.VMEM((8, D), F),
            pltpu.VMEM((*cond_parts.shape,), F),
            pltpu.VMEM((ROWS, D), BF),
            pltpu.VMEM((8, D), F),
            pltpu.VMEM((KV, D), BF),
            pltpu.VMEM((LOC, D), BF),
            pltpu.VMEM((KV, D), BF),
            pltpu.VMEM((KV, D), BF),
            pltpu.VMEM((LOC, D), BF),
            pltpu.VMEM((8, ROWS, TRK), BF),
            pltpu.VMEM((8, LOC, 256), BF),
            pltpu.VMEM((ROWS, TRK), BF),
            pltpu.VMEM((LOC, 256), BF),
            pltpu.VMEM((ROWS, TRK), F),
            pltpu.VMEM((LOC, 256), F),
            pltpu.VMEM((2, LOC, 128), F),
            pltpu.VMEM((ROWS, D), BF),
            pltpu.VMEM((ROWS, D), F),
            pltpu.VMEM((ROWS, D), F),
            pltpu.VMEM((ROWS, D), BF),
            pltpu.VMEM((ROWS, D), BF),
            pltpu.VMEM((ENC, D), BF),
            pltpu.VMEM((ENC, D), BF),
            pltpu.VMEM((ROWS, D), BF),
            pltpu.VMEM((8, ROWS, ENC), BF),
            pltpu.VMEM((ROWS, D), BF),
            pltpu.VMEM((ROWS, D), BF),
            pltpu.VMEM((ROWS, D), BF),
            pltpu.VMEM((ROWS, D), F),
            pltpu.VMEM((ROWS, D), F),
            pltpu.VMEM((ROWS, D), BF),
            pltpu.VMEM((ROWS, D), BF),
            pltpu.VMEM((ROWS, D), BF),
            pltpu.VMEM((D, D), F),
            pltpu.VMEM((D, D), F),
            pltpu.VMEM((8, D, D), BF),
            pltpu.VMEM((2, D, FF), BF),
            pltpu.VMEM((ENC, D), BF),
            pltpu.VMEM((2, 2, 4, D, 128), BF),
            pltpu.VMEM((2, 6, D, 128), BF),
            pltpu.VMEM((2, n, 2, rows, 128), BF),
            pltpu.VMEM((2, 4, 2, rows, 128), BF),
            pltpu.VMEM((n, 2, rows, 256), BF),
            pltpu.VMEM((4, 2, rows, 256), BF),
            pltpu.VMEM((896, D), BF),
            pltpu.VMEM((2, ROWS, D), BF),
            pltpu.VMEM((64, D), BF),
            pltpu.VMEM((2, 128, D), BF),
            pltpu.VMEM((4, 128, D), BF),
            pltpu.VMEM((8, 8, D), F),
            pltpu.VMEM((n, 8, D), F),
            pltpu.SemaphoreType.DMA((16 * n + 160,)),
            pltpu.SemaphoreType.DMA((16 * n + 160,)),
            pltpu.SemaphoreType.DMA((9,)),
            pltpu.SemaphoreType.REGULAR,
        ],
        compiler_params=pltpu.CompilerParams(
            vmem_limit_bytes=VMEM_LIMIT, collective_id=0, has_side_effects=True
        ),
        name="layer",
    )(parents, cond_parts, w_mod, tokens, enc, cot, *weights)


def timestep_code(timesteps, width):
    half = width // 2
    frequency = jnp.exp(-math.log(10000.0) * jnp.arange(half, dtype=F) / half)
    angles = timesteps.astype(F)[:, None] * frequency[None, :]
    return jnp.concatenate([jnp.sin(angles), jnp.cos(angles)], axis=-1)


def per_device(
    tokens,
    encoder_states,
    timesteps,
    parents,
    w_mod,
    w_self_qkv,
    w_self_out,
    w_cross_qkv,
    w_cross_out,
    w_up,
    w_down,
    cotangent,
):
    rows = w_mod.shape[0]
    condition = jax.nn.silu(timestep_code(timesteps, D)).astype(BF)
    n = lax.axis_size("fsdp")
    padded_cond = jnp.pad(condition.astype(F).reshape(n, 1, rows), ((0, 0), (0, 7), (0, max(128 - rows, 0))))
    out, in_grad, enc_grad, grad_mod, att, ffn = layer_call(
        n,
        parents,
        padded_cond,
        w_mod,
        tokens,
        encoder_states,
        cotangent[0],
        (w_self_qkv, w_self_out, w_cross_qkv, w_cross_out, w_up, w_down),
    )
    return (
        out[None],
        in_grad[None],
        enc_grad[None],
        grad_mod,
        att[0:3],
        att[3],
        att[4:7],
        att[7],
        ffn[0],
        ffn[1],
    )


def solution(mesh):
    rows = P("fsdp", ("ctx", "tp"), None)
    return jax.shard_map(
        per_device,
        mesh=mesh,
        in_specs=(
            rows,
            P("fsdp", "ctx", None),
            P("fsdp"),
            P("fsdp", None),
            P("fsdp", None),
            P(None, "fsdp", "tp"),
            P("fsdp", "tp"),
            P(None, "fsdp", "tp"),
            P("fsdp", "tp"),
            P("fsdp", "tp"),
            P("fsdp", "tp"),
            rows,
        ),
        out_specs=(
            rows,
            rows,
            P("fsdp", "ctx", None),
            P("fsdp", None),
            P(None, "fsdp", "tp"),
            P("fsdp", "tp"),
            P(None, "fsdp", "tp"),
            P("fsdp", "tp"),
            P("fsdp", "tp"),
            P("fsdp", "tp"),
        ),
        check_vma=False,
    )
```

```python
import functools
import math

import jax
import jax.numpy as jnp
from jax import lax
from jax.experimental import pallas as pl
from jax.experimental.pallas import tpu as pltpu
from jax.sharding import PartitionSpec as P

BF = jnp.bfloat16
F = jnp.float32
D = 512
FF = 2048
HD = 64
ROWS = 320
LOC = 384
BLK = 128
TRUNK = 8
BRANCHES = 4
TRK = TRUNK * BLK
SHARED = (TRUNK + BRANCHES) * BLK
SPEC = 2 * LOC
KV = TRK + SPEC
ENC = 512
EPS = 1e-05
NEG = -1e30
VMEM_LIMIT = 67043328


def nn(a, b):
    return lax.dot_general(a, b, (((1,), (0,)), ((), ())), preferred_element_type=F)


def nt(a, b):
    return lax.dot_general(a, b, (((1,), (1,)), ((), ())), preferred_element_type=F)


def tn(a, b):
    return lax.dot_general(a, b, (((0,), (0,)), ((), ())), preferred_element_type=F)


def normed(v):
    center = v - jnp.mean(v, axis=-1, keepdims=True)
    rstd = lax.rsqrt(jnp.mean(center * center, axis=-1, keepdims=True) + EPS)
    return center * rstd, rstd


def norm_back(grad, stream, scale):
    n, rstd = normed(stream)
    gn = grad * (1.0 + scale)
    back = rstd * (
        gn
        - jnp.mean(gn, axis=-1, keepdims=True)
        - n * jnp.mean(gn * n, axis=-1, keepdims=True)
    )
    return back, jnp.sum(grad * n, axis=0, keepdims=True), jnp.sum(grad, axis=0, keepdims=True)


def row_loop(total, step, body, unroll=1):
    if unroll == 0:
        for i in range(total // step):
            body(pl.ds(i * step, step))
        return

    @pl.loop(0, total // (step * unroll))
    def _(i):
        for j in range(unroll):
            body(pl.ds(pl.multiple_of((i * unroll + j) * step, step), step))


def half_lanes(shape, half):
    lane = lax.broadcasted_iota(jnp.int32, shape, len(shape) - 1)
    return (lane // HD) == half


def keep(value, half):
    return jnp.where(half_lanes(value.shape, half), value, jnp.zeros_like(value))


MESH = pl.DeviceIdType.MESH


class Wire:
    def __init__(self, send, recv):
        self.send, self.recv, self.used, self.sent = send, recv, 0, []

    def slot(self, count=1):
        self.used += count
        return self.used - count

    def copy(self, src, dst, at, to):
        return pltpu.make_async_remote_copy(
            src_ref=src,
            dst_ref=dst,
            send_sem=self.send.at[at],
            recv_sem=self.recv.at[at],
            device_id=to,
            device_id_type=MESH,
        )

    def push(self, dst, at, to, when=None, src=None):
        src = src or dst
        if when is None:
            self.copy(src(), dst(), at, to).start()
        else:

            @pl.when(when)
            def _():
                self.copy(src(), dst(), at, to).start()

        self.sent.append((src, dst, at, to, when))

    def arrived(self, dst, at, to, when=None):
        if when is None:
            self.copy(dst, dst, at, to).wait_recv()
        else:

            @pl.when(when)
            def _():
                self.copy(dst, dst, at, to).wait_recv()

    def drain(self):
        for src, dst, at, to, when in self.sent:
            if when is None:
                self.copy(src(), dst(), at, to).wait_send()
            else:

                @pl.when(when)
                def _(src=src, dst=dst, at=at, to=to):
                    self.copy(src(), dst(), at, to).wait_send()

        self.sent = []


def layer_kernel(
    n,
    parents_ref,
    cond_parts,
    w_mod,
    tok_in,
    enc_in,
    cot,
    w_sqkv,
    w_so,
    w_cqkv,
    w_co,
    w_up,
    w_dn,
    out_ref,
    in_grad,
    enc_out,
    mod_out,
    att_out,
    ffn_out,
    watt,
    wup,
    wdn,
    tok,
    enc,
    part_out,
    part_in,
    mod,
    cond_all,
    tok_own,
    mgrad,
    hid,
    hloc,
    kbuf,
    vbuf,
    qbuf,
    pt,
    ps,
    bias_t,
    bias_s,
    st,
    ss,
    spec_o,
    mixa,
    stream_b,
    stream_c,
    hid_b,
    hid_c,
    kenc,
    venc,
    qb,
    pe,
    mixb,
    b0,
    b1,
    acc0,
    acc1,
    gbf,
    mgr,
    dq,
    wk_acc,
    wv_acc,
    gatt,
    gffn,
    rc_att,
    rx_att,
    zr_att,
    rg_att,
    zr_ffn,
    rg_ffn,
    rc_g,
    rx_g,
    halo,
    rc_e,
    rx_e,
    mod1,
    mod2,
    send,
    recv,
    local,
    ready,
):
    t0, t1 = st.at[:, 0:D], st.at[:, D : 2 * D]
    egrad = enc
    fs = lax.axis_index("fsdp")
    cx = lax.axis_index("ctx")
    y = lax.axis_index("tp")
    x, c = cx // 2, lax.rem(cx, 2)
    ci = cx * 2 + y
    odd = y
    off = pl.multiple_of(odd * 64, 64)
    own = pl.ds(off, ROWS)
    base = (ci * 5) // 2
    rows = w_mod.shape[0]
    to_y = {"tp": 1 - y}
    to_c = {"ctx": 2 * x + 1 - c}
    to_x = {"ctx": 2 * (1 - x) + c}
    wire = Wire(send, recv)

    my_rows = pl.ds(pl.multiple_of(fs * rows, rows), rows)

    def att_cols(yy, cc):
        return pl.ds(pl.multiple_of(yy * 256 + cc * 128, 128), 128)

    def ffn_cols(yy, xx, cc):
        return pl.ds(pl.multiple_of(yy * 1024 + xx * 512 + cc * 256, 256), 256)

    half = pl.ds(pl.multiple_of(c * 128, 128), 128)
    quarter = pl.ds(pl.multiple_of(cx * 256, 256), 256)
    groups = (
        (w_sqkv.at[:, :, half], watt, slice(0, 3), 0),
        (w_so.at[:, half], watt, 3, 0),
        (w_cqkv.at[:, :, half], watt, slice(4, 7), 0),
        (w_co.at[:, half], watt, 7, 0),
        (w_up.at[:, quarter], wup, None, 1),
        (w_dn.at[:, quarter], wdn, None, 1),
    )

    def place(g, row_at, yy, xx, cc):
        _, buf, index, wide = groups[g]
        if wide:
            return buf.at[row_at, ffn_cols(yy, xx, cc)]
        return buf.at[index, row_at, att_cols(yy, cc)]

    def chunk(i):
        return tok.at[pl.ds(pl.multiple_of(i * ROWS, ROWS), ROWS), :]

    def enc_part(i):
        return enc.at[pl.ds(pl.multiple_of(i * 128, 128), 128), :]

    all_rows = pl.ds(0, D)

    local_copies = [
        pltpu.make_async_copy(tok_in.at[0], chunk(ci), local.at[0]),
        pltpu.make_async_copy(enc_in.at[0], enc_part(cx), local.at[1]),
    ] + [
        pltpu.make_async_copy(groups[g][0], place(g, my_rows, y, x, c), local.at[2 + g])
        for g in range(6)
    ]
    local_copies.append(pltpu.make_async_copy(tok_in.at[0], tok_own, local.at[8]))
    for copy in local_copies:
        copy.start()

    barrier = pltpu.get_barrier_semaphore()

    @pl.loop(1, n)
    def _(k):
        pl.semaphore_signal(
            barrier, inc=1, device_id={"fsdp": lax.rem(fs + k, n)}, device_id_type=MESH
        )

    @pl.loop(1, 8)
    def _(k):
        other = lax.rem(ci + k, 8)
        pl.semaphore_signal(
            barrier,
            inc=1,
            device_id={"ctx": other // 2, "tp": lax.rem(other, 2)},
            device_id_type=MESH,
        )

    pl.semaphore_wait(barrier, n - 1 + 7)

    def peers(make):
        @pl.loop(1, n)
        def _(k):
            make(k, lax.rem(fs + k, n), lax.rem(fs + n - k, n))

    s_cond = wire.slot(n)
    s_part = wire.slot(n)
    s_z = [wire.slot(n) for _ in range(6)]
    s_y = [wire.slot() for _ in range(6)]
    s_c0 = [wire.slot() for _ in range(6)]
    s_c1 = [wire.slot() for _ in range(6)]
    s_x0 = [wire.slot() for _ in range(6)]
    s_x1 = [wire.slot() for _ in range(6)]
    s_c2 = [wire.slot() for _ in range(6)]
    s_c3 = [wire.slot() for _ in range(6)]
    s_ty, s_tx, s_txy, s_tc0, s_tc1, s_tc2, s_tc3, s_ty2 = (
        wire.slot() for _ in range(8)
    )
    s_ex, s_ec0, s_ec1 = (wire.slot() for _ in range(3))

    peers(
        lambda k, to, _: wire.copy(
            cond_parts.at[to], cond_all.at[fs], s_cond + k, {"fsdp": to}
        ).start()
    )
    left = x == 0

    def tail_rows(i):
        return tok.at[pl.ds(pl.multiple_of(i * ROWS + ROWS - 64, 64), 64), :]

    wire.push(
        lambda: chunk(ci), s_ty, to_y, jnp.logical_or(left, ci == 4), lambda: tok_in.at[0]
    )
    wire.push(
        lambda: tail_rows(ci), s_ty2, to_y, ci == 6, lambda: tok_in.at[0, ROWS - 64 : ROWS, :]
    )
    wire.push(lambda: chunk(ci), s_tx, to_x, x == 0, lambda: tok_in.at[0])
    wire.push(
        lambda: chunk(ci), s_tc0, to_c, jnp.logical_or(left, ci == 4), lambda: tok_in.at[0]
    )

    def z_start(g):
        peers(
            lambda k, to, _: wire.copy(
                groups[g][0], place(g, my_rows, y, x, c), s_z[g] + k, {"fsdp": to}
            ).start()
        )

    z_start(0)

    def mask_trunk(rs):
        row = lax.broadcasted_iota(jnp.int32, (32, TRK), 0) + rs.start + ci * ROWS
        col = lax.broadcasted_iota(jnp.int32, (32, TRK), 1)
        bias_t[rs, :] = jnp.where(col <= row, 0.0, NEG).astype(BF)

    row_loop(ROWS, 32, mask_trunk)
    for lb in range(3):
        blk = base + lb
        row = lax.broadcasted_iota(jnp.int32, (BLK, 2 * BLK), 0)
        col = lax.broadcasted_iota(jnp.int32, (BLK, 2 * BLK), 1)
        par_ok = jnp.logical_and(col < BLK, blk >= TRUNK + BRANCHES)
        self_ok = jnp.logical_and(
            jnp.logical_and(col >= BLK, col - BLK <= row), blk >= TRUNK
        )
        bias_s[lb * BLK : (lb + 1) * BLK, :] = jnp.where(
            jnp.logical_or(par_ok, self_ok), 0.0, NEG
        ).astype(BF)

    cond_all[fs] = cond_parts[fs]
    peers(lambda k, _, src: wire.arrived(cond_all.at[src], s_cond + k, {"fsdp": src}))
    for v in range(6):
        part_out[:, v, :] = nn(
            cond_all[:, 0, 0:rows].astype(BF), w_mod[:, v * D : (v + 1) * D]
        )
    part_out[:, 6:8, :] = jnp.zeros((n, 2, D), F)
    peers(
        lambda k, to, _: wire.copy(
            part_out.at[to], part_in.at[fs], s_part + k, {"fsdp": to}
        ).start()
    )
    part_in[fs] = part_out[fs]

    def z_done(g):
        local_copies[2 + g].wait()
        peers(
            lambda k, _, src: wire.arrived(
                place(g, pl.ds(pl.multiple_of(src * rows, rows), rows), y, x, c),
                s_z[g] + k,
                {"fsdp": src},
            )
        )
        slab = lambda: place(g, all_rows, y, x, c)
        wire.push(slab, s_y[g], to_y)
        if groups[g][3]:
            wire.push(slab, s_x0[g], to_x)
        wire.push(slab, s_c0[g], to_c)

    def y_done(g):
        slab = lambda: place(g, all_rows, 1 - y, x, c)
        wire.arrived(slab(), s_y[g], to_y)
        if groups[g][3]:
            wire.push(slab, s_x1[g], to_x)
        wire.push(slab, s_c1[g], to_c)

    def x_done(g, part):
        s_in, s_out = ((s_x0[g], s_c2[g]), (s_x1[g], s_c3[g]))[part]
        slab = lambda: place(g, all_rows, 1 - y if part else y, 1 - x, c)
        wire.arrived(slab(), s_in, to_x)
        wire.push(slab, s_out, to_c)

    def c_part(g, part):
        yy, xx, at = (
            (y, x, s_c0[g]),
            (1 - y, x, s_c1[g]),
            (y, 1 - x, s_c2[g]),
            (1 - y, 1 - x, s_c3[g]),
        )[part]
        wire.arrived(place(g, all_rows, yy, xx, 1 - c), at, to_c)

    def c_done(g):
        wire.arrived(place(g, all_rows, y, x, 1 - c), s_c0[g], to_c)
        wire.arrived(place(g, all_rows, 1 - y, x, 1 - c), s_c1[g], to_c)
    local_copies[0].wait()
    local_copies[1].wait()
    ciy = 4 * x + 2 * c + 1 - y
    cic = 4 * x + 2 * (1 - c) + y
    ciyc = 4 * x + 2 * (1 - c) + 1 - y
    low, lowy, lowc, lowyc = 2 * c + y, 2 * c + 1 - y, 2 * (1 - c) + y, 2 * (1 - c) + 1 - y
    right = x == 1
    local_copies[8].wait()
    wire.arrived(chunk(ciy), s_ty, to_y, jnp.logical_or(left, ci == 5))
    wire.push(lambda: chunk(ciy), s_txy, to_x, left)
    wire.push(lambda: chunk(ciy), s_tc1, to_c, jnp.logical_or(left, ci == 5))
    wire.arrived(tail_rows(ciy), s_ty2, to_y, ci == 7)

    @pl.when(jnp.logical_and(right, y == 0))
    def _():
        tok[pl.ds(pl.multiple_of((ci + 1) * ROWS, 64), 64), :] = jnp.zeros((64, D), BF)

    z_start(1)
    z_start(4)
    wire.arrived(chunk(low), s_tx, to_x, right)
    wire.push(lambda: chunk(low), s_tc2, to_c, right)
    z_done(0)
    z_start(2)
    wire.arrived(chunk(lowy), s_txy, to_x, right)
    wire.push(lambda: chunk(lowy), s_tc3, to_c, right)
    wire.push(lambda: enc_part(cx), s_ex, to_x, None, lambda: enc_in.at[0])
    wire.push(lambda: enc_part(cx), s_ec0, to_c, None, lambda: enc_in.at[0])
    y_done(0)
    z_done(1)
    z_done(4)
    z_start(5)
    z_start(3)

    peers(lambda k, _, src: wire.arrived(part_in.at[src], s_part + k, {"fsdp": src}))
    mod[...] = jnp.sum(part_in[...], axis=0)
    sa, ba = mod[0:1, :], mod[1:2, :]
    sb, bb = mod[2:3, :], mod[3:4, :]
    sf, bf_ = mod[4:5, :], mod[5:6, :]

    wire.arrived(chunk(cic), s_tc0, to_c, jnp.logical_or(left, ci == 6))
    wire.arrived(chunk(ciyc), s_tc1, to_c, jnp.logical_or(left, ci == 7))
    wire.arrived(chunk(lowc), s_tc2, to_c, right)
    wire.arrived(chunk(lowyc), s_tc3, to_c, right)

    def enc_done(step):
        if step == 0:
            wire.arrived(enc_part(2 * (1 - x) + c), s_ex, to_x)
            wire.push(lambda: enc_part(2 * (1 - x) + c), s_ec1, to_c)
        else:
            wire.arrived(enc_part(2 * x + 1 - c), s_ec0, to_c)
            wire.arrived(enc_part(2 * (1 - x) + 1 - c), s_ec1, to_c)

    tok_tb = tok
    tok_loc = tok.at[pl.ds(pl.multiple_of(ci * ROWS - off, 64), LOC), :]

    def relay(step):
        if step == 1:
            y_done(1)
            y_done(4)
            enc_done(0)
        if step == 2:
            z_done(5)
            z_done(3)
        if step == 4:
            c_done(1)
        if step == 5:
            y_done(3)
            c_done(3)
        if step == 6:
            x_done(4, 0)
            x_done(5, 0)
        if step == 7:
            y_done(2)
            y_done(5)
            enc_done(1)
            c_done(2)

    spec_g = qbuf

    def is_parent(lb, branch):
        parent = jnp.full((32, D), parents_ref[0, base + lb], jnp.int32)
        leaf = jnp.full((32, D), base + lb, jnp.int32) >= TRUNK + BRANCHES
        return jnp.logical_and(leaf, parent == TRUNK + branch)

    to_xy = {"ctx": 2 * (1 - x) + c, "tp": 1 - y}
    s_rcg, s_rcg4, s_rcg5, s_halo = (wire.slot() for _ in range(4))
    s_rxy = [wire.slot() for _ in range(2)]
    s_rxx = [wire.slot() for _ in range(2)]
    s_rce = [wire.slot(), wire.slot()]
    s_rxe = [wire.slot() for _ in range(3)]
    s_m1 = wire.slot(8)
    s_m2 = wire.slot(n)
    quad = ((to_y, x, 1 - y), (to_x, 1 - x, y), (to_xy, 1 - x, 1 - y))

    def add_rows(target, terms, total, step=64):
        def body(rs):
            value = terms[0][rs, :].astype(F)
            for term in terms[1:]:
                value += term[rs, :].astype(F)
            target[rs, :] = value.astype(BF)

        row_loop(total, step, body)

    def strip(buf, at):
        return buf.at[:, at * 256 : (at + 1) * 256]

    class Family:
        def __init__(self, unit, core_box, box, landing, held, shape_rows):
            self.unit, self.core_box, self.box = unit, core_box, box
            self.landing, self.held = landing, held
            self.s_core = [wire.slot(4) for _ in range(2)]
            self.s_one = [[wire.slot() for _ in range(2)] for _ in range(2)]
            self.s_two = [wire.slot() for _ in range(2)]
            self.s_z = [wire.slot(n) for _ in range(2)]
            self.s_g = wire.slot(4)

        def core_copy(self, m, t):
            return wire.copy(
                self.unit(m, t // 2, lax.rem(t, 2), 1 - c),
                self.core_box(m, t),
                self.s_core[m] + t,
                to_c,
            )

        def core_send(self):
            for m in range(2):
                for t in range(4):
                    self.core_copy(m, t).start()

        def first_send(self):
            for m in range(2):
                for t in range(4):
                    wire.arrived(self.core_box(m, t), self.s_core[m] + t, to_c)
                    mine = self.unit(m, t // 2, t % 2, c)
                    add_rows(mine, (mine, self.core_box(m, t)), D)
            for j in range(2):
                wire.push(
                    lambda j=j: self.box(j),
                    self.s_one[0][j],
                    to_x,
                    None,
                    lambda j=j: self.unit(0, j, 1 - x, c),
                )
                wire.push(
                    lambda j=j: self.box(2 + j),
                    self.s_one[1][j],
                    to_y,
                    None,
                    lambda j=j: self.unit(1, 1 - y, j, c),
                )

        def second_send(self):
            for j in range(2):
                wire.arrived(self.box(j), self.s_one[0][j], to_x)
                mine = self.unit(0, j, x, c)
                add_rows(mine, (mine, self.box(j)), D)
            wire.push(
                lambda: self.box(4),
                self.s_two[0],
                to_y,
                None,
                lambda: self.unit(0, 1 - y, x, c),
            )
            for j in range(2):
                wire.arrived(self.box(2 + j), self.s_one[1][j], to_y)
                mine = self.unit(1, y, j, c)
                add_rows(mine, (mine, self.box(2 + j)), D)
            wire.push(
                lambda: self.box(5),
                self.s_two[1],
                to_x,
                None,
                lambda: self.unit(1, y, 1 - x, c),
            )

        def z_copy(self, m, k, to):
            part = pl.ds(pl.multiple_of(to * rows, rows), rows)
            return wire.copy(
                self.unit(m, y, x, c).at[part, :],
                self.landing.at[fs, m],
                self.s_z[m] + k,
                {"fsdp": to},
            )

        def tree_send(self):
            for m, target in ((0, to_y), (1, to_x)):
                wire.arrived(self.box(4 + m), self.s_two[m], target)
                mine = self.unit(m, y, x, c)
                add_rows(mine, (mine, self.box(4 + m)), D)
                peers(lambda k, to, _, m=m: self.z_copy(m, k, to).start())
                self.landing[fs, m] = self.unit(m, y, x, c)[my_rows, :]

        def g_copy(self, i):
            target, at = ((to_x, cx), (to_c, cx), (to_c, 2 * (1 - x) + c))[i]
            return wire.copy(self.held.at[at], self.held.at[at], self.s_g + i, target)

        def copy_send(self):
            for m in range(2):
                peers(
                    lambda k, _, src, m=m: wire.arrived(
                        self.landing.at[src, m], self.s_z[m] + k, {"fsdp": src}
                    )
                )
            self.held[cx] = jnp.sum(self.landing[...].astype(F), axis=0).astype(BF)
            self.g_copy(0).start()
            self.g_copy(1).start()

        def relay_copy(self):
            wire.arrived(self.held.at[2 * (1 - x) + c], self.s_g, to_x)
            self.g_copy(2).start()

        def collect(self):
            wire.arrived(self.held.at[2 * x + 1 - c], self.s_g + 1, to_c)
            wire.arrived(self.held.at[2 * (1 - x) + 1 - c], self.s_g + 2, to_c)

        def drain(self):
            for m in range(2):
                for t in range(4):
                    self.core_copy(m, t).wait_send()
                peers(lambda k, to, _, m=m: self.z_copy(m, k, to).wait_send())
            for i in range(3):
                self.g_copy(i).wait_send()

    ffn = Family(
        lambda m, yy, xx, cc: gffn.at[m, :, ffn_cols(yy, xx, cc)],
        lambda m, t: rc_att.at[m * 4 + t],
        lambda i: strip(wdn, i),
        zr_ffn,
        rg_ffn,
        rows,
    )

    def attention_family(a):
        return Family(
            lambda m, yy, xx, cc: gatt.at[4 * a + 2 * xx + m, :, att_cols(yy, cc)],
            lambda m, t: rc_att.at[
                4 * a + 2 * m + t // 2, :, pl.ds(pl.multiple_of(lax.rem(t, 2) * 128, 128), 128)
            ],
            lambda i: rx_att.at[a, i],
            zr_att.at[a],
            rg_att.at[a],
            rows,
        )

    att = (attention_family(0), attention_family(1))

    def ffn_free():
        wire.drain()
        for target in (to_y, to_x):
            pl.semaphore_signal(ready.at[0], inc=1, device_id=target, device_id_type=MESH)

    def ffn_chip_send():
        pl.semaphore_wait(ready.at[0], 2)
        ffn.first_send()
        pl.semaphore_signal(ready.at[1], inc=1, device_id=to_c, device_id_type=MESH)

    def ffn_finish():
        ffn.collect()
        for q in range(4):
            ffn_out[:, :, q * 256 : (q + 1) * 256] = rg_ffn[q].astype(F)

    def att_finish(a):
        att[a].collect()
        for q in range(4):
            for m in range(2):
                at = 4 * a + 2 * (q // 2) + m
                att_out[at, :, (q % 2) * 128 : (q % 2) * 128 + 128] = rg_att[a, q, m].astype(F)

    def enc_core_send():
        for xx in range(2):
            wire.push(
                lambda xx=xx: rc_e.at[xx],
                s_rce[xx],
                to_c,
                None,
                lambda xx=xx: egrad.at[pl.ds(pl.multiple_of((2 * xx + 1 - c) * 128, 128), 128), :],
            )

    def enc_rows(xx):
        return egrad.at[pl.ds(pl.multiple_of((2 * xx + c) * 128, 128), 128), :]

    def enc_chip_send():
        for xx in range(2):
            wire.arrived(rc_e.at[xx], s_rce[xx], to_c)
            add_rows(enc_rows(xx), (enc_rows(xx), rc_e.at[xx]), 128)
        for r, (target, xx, _) in enumerate(quad):
            wire.push(
                lambda: rx_e.at[2 * x + y], s_rxe[r], target, None, lambda xx=xx: enc_rows(xx)
            )
        rx_e[2 * x + y] = enc_rows(x)[...]

    def enc_finish():
        for r, (target, xx, yy) in enumerate(quad):
            wire.arrived(rx_e.at[2 * xx + yy], s_rxe[r], target)
        enc_out[...] = jnp.sum(rx_e[...].astype(F), axis=0)

    def shared_core_send():
        to_core = pl.ds(pl.multiple_of(640 * (1 - c), 640), 640)
        wire.push(lambda: rc_g.at[0:640], s_rcg, to_c, None, lambda: tok.at[to_core, :])
        wire.push(
            lambda: rc_g.at[640:896],
            s_rcg4,
            to_c,
            jnp.logical_and(x == 1, c == 1),
            lambda: tok.at[1280:1536, :],
        )
        wire.push(lambda: halo, s_halo, to_y, y == 1, lambda: spec_g.at[0:64, :])

    def part_rows(yy, p):
        return tok.at[pl.ds(pl.multiple_of((2 * c + yy) * ROWS + p * 160, 32), 160), :]

    def core_rows(yy, p):
        return rc_g.at[pl.ds(pl.multiple_of(yy * ROWS + p * 160, 32), 160), :]

    def shared_y_send():
        wire.arrived(rc_g.at[0:640], s_rcg, to_c)
        for p in range(2):
            mine = part_rows(1 - y, p)
            add_rows(mine, (mine, core_rows(1 - y, p)), 160, 32)
            wire.push(
                lambda p=p: rx_g.at[0, p * 160 : p * 160 + 160],
                s_rxy[p],
                to_y,
                None,
                lambda p=p: part_rows(1 - y, p),
            )
        last = jnp.logical_and(x == 1, c == 0)

        @pl.when(last)
        def _():
            wire.arrived(rc_g.at[640:896], s_rcg4, to_c)
            four = tok.at[1280:1536, :]
            add_rows(four, (four, rc_g.at[640:896]), 256)

        wire.push(
            lambda: rx_g.at[1, 0:256],
            s_rcg5,
            to_y,
            jnp.logical_and(last, y == 1),
            lambda: tok.at[1280:1536, :],
        )
        for p in range(2):
            mine = part_rows(y, p)
            add_rows(mine, (mine, core_rows(y, p)), 160, 32)

    def shared_x_send():
        for p in range(2):
            wire.arrived(rx_g.at[0, p * 160 : p * 160 + 160], s_rxy[p], to_y)
            mine = part_rows(y, p)
            add_rows(mine, (mine, rx_g.at[0, p * 160 : p * 160 + 160]), 160, 32)
            wire.push(
                lambda p=p: rx_g.at[1, p * 160 : p * 160 + 160],
                s_rxx[p],
                to_x,
                x == 1,
                lambda p=p: part_rows(y, p),
            )

    def shared_arrived():
        for p in range(2):
            wire.arrived(rx_g.at[1, p * 160 : p * 160 + 160], s_rxx[p], to_x, x == 0)
        wire.arrived(rx_g.at[1, 0:256], s_rcg5, to_y, ci == 4)

    def tree_peers(make):
        @pl.loop(1, 8)
        def _(k):
            make(k, lax.rem(ci + k, 8), lax.rem(ci + 8 - k, 8))

    def device_of(i):
        return {"ctx": i // 2, "tp": lax.rem(i, 2)}

    def mod_1(k, to):
        return wire.copy(mgrad, mod1.at[ci], s_m1 + k, device_of(to))

    def mod_2(k, to):
        return wire.copy(mod2.at[fs], mod2.at[fs], s_m2 + k, {"fsdp": to})

    def mod_tree_send():
        tree_peers(lambda k, to, _: mod_1(k, to).start())
        mod1[ci] = mgrad[...]

    def mod_all_send():
        tree_peers(lambda k, _, src: wire.arrived(mod1.at[src], s_m1 + k, device_of(src)))
        mod2[fs] = jnp.sum(mod1[...], axis=0)
        peers(lambda k, to, _: mod_2(k, to).start())

    def mod_finish():
        peers(lambda k, _, src: wire.arrived(mod2.at[src], s_m2 + k, {"fsdp": src}))
        cond = cond_all[:, 0, 0:rows]
        for v in range(6):
            held = (wk_acc, wv_acc)[v // 4]
            at = (v % 4) * rows
            held[at : at + rows, :] = lax.dot_general(
                cond,
                mod2[:, v, :],
                (((0,), (0,)), ((), ())),
                precision=lax.Precision.HIGHEST,
                preferred_element_type=F,
            )
        copies = [
            pltpu.make_async_copy(
                (wk_acc, wv_acc)[v // 4].at[(v % 4) * rows : (v % 4 + 1) * rows, :],
                mod_out.at[:, v * D : (v + 1) * D],
                local.at[v],
            )
            for v in range(6)
        ]
        for copy in copies:
            copy.start()
        for copy in copies:
            copy.wait()

    def leave(step):
        if step == 0:
            ffn_free()
        if step == 1:
            ffn_chip_send()
        if step == 2:
            pl.semaphore_wait(ready.at[1], 1)
            att[1].core_send()
            enc_core_send()
        if step == 3:
            att[1].first_send()
            enc_chip_send()
        if step == 4:
            ffn.second_send()
        if step == 5:
            att[1].second_send()
            ffn.tree_send()
        if step == 6:
            shared_core_send()
            att[1].tree_send()
        if step == 7:
            shared_y_send()
            att[0].first_send()
            ffn.copy_send()
            enc_finish()
            shared_x_send()
        if step == 8:
            att[0].second_send()
            att[1].copy_send()
            ffn.relay_copy()
            shared_arrived()
        if step == 9:
            mod_tree_send()
            att[0].tree_send()
            att[1].relay_copy()
            ffn_finish()
            mod_all_send()
            att[0].copy_send()
            att_finish(1)
            mod_finish()
            att[0].relay_copy()
            att_finish(0)

    def hidden(x):
        n, _ = normed(x.astype(F))
        return (n * (1.0 + sa) + ba).astype(BF)

    def hid_trunk(rs):
        hid[rs, :] = hidden(tok_tb[rs, :])

    row_loop(TRK, 32, hid_trunk, 8)

    def hid_loc(rs):
        hloc[rs, :] = hidden(tok_loc[rs, :])

    row_loop(LOC, 32, hid_loc, 6)
    for lb in range(3):
        picks = [is_parent(lb, b) for b in range(1, BRANCHES)]
        for piece in range(4):
            r = piece * 32
            picked = tok_tb[TRK + r : TRK + r + 32, :].astype(F)
            for b in range(1, BRANCHES):
                at = TRK + b * BLK + r
                picked = jnp.where(picks[b - 1], tok_tb[at : at + 32, :].astype(F), picked)
            at = TRK + lb * 256 + r
            hid[at : at + 32, :] = hidden(picked)
        hid[TRK + lb * 256 + BLK : TRK + lb * 256 + 2 * BLK, :] = hloc[
            lb * BLK : (lb + 1) * BLK, :
        ]

    def project(rs):
        kbuf[rs, :] = nn(hid[rs, :], watt[1]).astype(BF)
        vbuf[rs, :] = nn(hid[rs, :], watt[2]).astype(BF)

    z_done(2)
    c_done(0)
    row_loop(KV, 256, project)
    qbuf[...] = (nn(hloc[...], watt[0]) * 0.125).astype(BF)

    linv_a, linv_b = wk_acc.at[0:ROWS, :], wv_acc.at[0:ROWS, :]

    def with_ones(values, half):
        return jnp.where(half_lanes(values.shape, half), values, jnp.ones_like(values))

    def finish_heads(o0, o1, mixed, linv, lanes):
        inv0, inv1 = 1.0 / pltpu.roll(o0, HD, 1), 1.0 / pltpu.roll(o1, HD, 1)
        first = half_lanes(o0.shape, 0)
        mixed[:, lanes] = jnp.where(first, o0 * inv0, o1 * inv1).astype(BF)
        linv[:, lanes] = jnp.where(first, inv0, inv1)

    @pl.loop(0, 4)
    def _(hp):
        for step in (1, 2):

            @pl.when(hp == step)
            def _(step=step):
                relay(step)

        lanes = pl.ds(pl.multiple_of(hp * 128, 128), 128)
        kt = kbuf[0:TRK, lanes]
        vt = vbuf[0:TRK, lanes]
        outs = []
        for half in range(2):
            h = hp * 2 + half
            st[...] = nt(keep(qbuf[own, lanes], half), kt) + bias_t[...].astype(F)
            for lb in range(3):
                r = slice(lb * BLK, (lb + 1) * BLK)
                ks = kbuf[TRK + lb * 256 : TRK + (lb + 1) * 256, lanes]
                ss[r, :] = nt(keep(qbuf[r, lanes], half), ks) + bias_s[r, :].astype(F)
            for i in range(ROWS // 32):
                rs = slice(i * 32, i * 32 + 32)
                ro = pl.ds(pl.multiple_of(i * 32 + off, 32), 32)
                a, b = st[rs, :], ss[ro, :]
                top = jnp.maximum(
                    jnp.max(a, axis=-1, keepdims=True), jnp.max(b, axis=-1, keepdims=True)
                )
                pt[h, rs, :] = jnp.exp(a - top).astype(BF)
                ps[h, ro, :] = jnp.exp(b - top).astype(BF)
            for lb in range(3):
                r = slice(lb * BLK, (lb + 1) * BLK)
                vs = vbuf[TRK + lb * 256 : TRK + (lb + 1) * 256, lanes]
                spec_o[half, r, :] = nn(ps[h, r, :], with_ones(vs, half))
            outs.append(nn(pt[h], with_ones(vt, half)) + spec_o[half, own, :])
        finish_heads(outs[0], outs[1], mixa, linv_a, lanes)

    relay(4)
    t0[...] = nt(mixa[...], watt[3])

    def after_self(rs):
        sbv = tok_own[rs, :].astype(F) + t0[rs, :]
        stream_b[rs, :] = sbv
        n, _ = normed(sbv)
        hid_b[rs, :] = (n * (1.0 + sb) + bb).astype(BF)

    row_loop(ROWS, 32, after_self, 0)

    relay(7)
    kenc[...] = nn(enc[...], watt[5]).astype(BF)
    venc[...] = nn(enc[...], watt[6]).astype(BF)
    qb[...] = (nn(hid_b[...], watt[4]) * 0.125).astype(BF)

    @pl.loop(0, 4)
    def _(hp):
        lanes = pl.ds(pl.multiple_of(hp * 128, 128), 128)
        kt = kenc[:, lanes]
        vt = venc[:, lanes]
        outs = []
        for half in range(2):
            h = hp * 2 + half
            t0[...] = nt(keep(qb[:, lanes], half), kt)
            for i in range(ROWS // 32):
                rs = slice(i * 32, i * 32 + 32)
                a = t0[rs, :]
                pe[h, rs, :] = jnp.exp(a - jnp.max(a, axis=-1, keepdims=True)).astype(BF)
            outs.append(nn(pe[h], with_ones(vt, half)))
        finish_heads(outs[0], outs[1], mixb, linv_b, lanes)

    relay(5)
    t0[...] = nt(mixb[...], watt[7])

    def after_cross(rs):
        scv = stream_b[rs, :] + t0[rs, :]
        stream_c[rs, :] = scv
        n, _ = normed(scv)
        hid_c[rs, :] = (n * (1.0 + sf) + bf_).astype(BF)

    row_loop(ROWS, 32, after_cross, 0)

    relay(6)
    acc0[...] = jnp.zeros_like(acc0)
    acc1[...] = jnp.zeros_like(acc1)

    def flip(v, by):
        return v + by - 2 * v * by

    @pl.loop(0, 4)
    def _(ft):
        @pl.when(ft == 2)
        def _():
            x_done(4, 1)
            x_done(5, 1)

        for part in range(4):

            @pl.when(ft == part)
            def _(part=part):
                c_part(4, part)
                c_part(5, part)

        tile = flip(y, lax.rem(ft, 2)) * 2 + flip(x, ft // 2)
        cols = pl.ds(pl.multiple_of(tile * 512, 512), 512)
        t0[...] = nn(hid_c[...], wup[:, cols])
        t1[...] = nn(cot[...], wdn[:, cols])

        def gelu(rs):
            u = t0[rs, :]
            phi = 0.5 * (1.0 + lax.erf(u * (2.0**-0.5)))
            b0[rs, :] = (u * phi).astype(BF)
            slope = phi + u * (jnp.exp(-0.5 * u * u) * (1.0 / math.sqrt(2.0 * math.pi)))
            b1[rs, :] = (t1[rs, :] * slope).astype(BF)

        row_loop(ROWS, 32, gelu)
        acc0[...] += nt(b0[...], wdn[:, cols])
        acc1[...] += nt(b1[...], wup[:, cols])
        gffn[1, :, cols] = tn(cot[...], b0[...]).astype(BF)
        gffn[0, :, cols] = tn(hid_c[...], b1[...]).astype(BF)
        for m in range(2):
            ffn.core_copy(m, tile).start()

    def back_norm(at, scale, grad_src, stream_src, base_src, want_out):
        sums = [jnp.zeros((1, D), F), jnp.zeros((1, D), F)]
        for i in range(ROWS // 32):
            rs = slice(i * 32, i * 32 + 32)
            back, ds, db = norm_back(grad_src[rs, :], stream_src[rs, :], scale)
            total = base_src[rs, :].astype(F) + back
            in_grad[rs, :] = total
            gbf[rs, :] = total.astype(BF)
            sums = [sums[0] + ds, sums[1] + db]
            if want_out:
                out_ref[rs, :] = (stream_c[rs, :] + acc0[rs, :]).astype(BF)
        mgrad[at : at + 1, :] = sums[0]
        mgrad[at + 1 : at + 2, :] = sums[1]

    leave(0)
    back_norm(4, sf, acc1, stream_c, cot, True)

    gatt[7] = tn(gbf[...], mixb[...]).astype(BF)
    mgr[...] = (nn(gbf[...], watt[7]) * linv_b[...]).astype(BF)
    leave(1)

    @pl.loop(0, 4)
    def _(hp):
        lanes = pl.ds(pl.multiple_of(hp * 128, 128), 128)
        prod = mgr[:, lanes].astype(F) * mixb[:, lanes].astype(F)
        dqs, dks, dvs = [], [], []
        for half in range(2):
            h = hp * 2 + half
            inner = jnp.sum(keep(prod, half), axis=-1, keepdims=True)
            mg = keep(mgr[:, lanes], half)
            dp = nt(mg, venc[:, lanes])
            b0[...] = (pe[h].astype(F) * (dp - inner)).astype(BF)
            dqs.append(nn(b0[...], kenc[:, lanes]))
            dks.append(tn(b0[...], keep(qb[:, lanes], half)))
            dvs.append(tn(pe[h], mg))
        dq[:, lanes] = (jnp.where(half_lanes(dqs[0].shape, 0), dqs[0], dqs[1]) * 0.125).astype(BF)
        kenc[:, lanes] = (dks[0] + dks[1]).astype(BF)
        venc[:, lanes] = (dvs[0] + dvs[1]).astype(BF)

    gatt[4] = tn(hid_b[...], dq[...]).astype(BF)
    gatt[5] = tn(enc[...], kenc[...]).astype(BF)
    gatt[6] = tn(enc[...], venc[...]).astype(BF)
    egrad[...] = (nt(kenc[...], watt[5]) + nt(venc[...], watt[6])).astype(BF)
    leave(2)
    acc1[...] = nt(dq[...], watt[4])
    back_norm(2, sb, acc1, stream_b, in_grad, False)

    gatt[3] = tn(gbf[...], mixa[...]).astype(BF)
    mgr[...] = (nn(gbf[...], watt[3]) * linv_a[...]).astype(BF)
    leave(3)

    @pl.when(odd == 0)
    def _():
        for h in range(8):
            ps[h, ROWS:LOC, :] = jnp.zeros((LOC - ROWS, 256), BF)
        spec_o[:, ROWS:LOC, :] = jnp.zeros((2, LOC - ROWS, 128), F)

    @pl.when(odd == 1)
    def _():
        for h in range(8):
            ps[h, 0:64, :] = jnp.zeros((64, 256), BF)
        spec_o[:, 0:64, :] = jnp.zeros((2, 64, 128), F)

    @pl.loop(0, 4)
    def _(turn):
        side = jnp.where(turn < 2, 1 - c, c)
        band = jnp.where(turn < 2, turn, jnp.where(turn == 2, 1 - y, y))
        hp = band * 2 + side
        lanes = pl.ds(pl.multiple_of(hp * 128, 128), 128)
        prod = mgr[:, lanes].astype(F) * mixa[:, lanes].astype(F)
        dqs, dks, dvs = [], [], []
        dks_s = [[], [], []]
        dvs_s = [[], [], []]
        for half in range(2):
            h = hp * 2 + half
            inner = jnp.sum(keep(prod, half), axis=-1, keepdims=True)
            mg = keep(mgr[:, lanes], half)
            qm = keep(qbuf[own, lanes], half)
            dp = nt(mg, vbuf[0:TRK, lanes])
            ds = (pt[h].astype(F) * (dp - inner)).astype(BF)
            spec_o[0, own, :] = mg.astype(F)
            spec_o[1, own, :] = jnp.broadcast_to(inner, (ROWS, 128))
            dq_s = []
            for lb in range(3):
                r = slice(lb * BLK, (lb + 1) * BLK)
                k_rows = slice(TRK + lb * 256, TRK + (lb + 1) * 256)
                mgl = spec_o[0, r, :].astype(BF)
                dpl = nt(mgl, vbuf[k_rows, lanes])
                inner_l = spec_o[1, r, 0:1]
                dsl = (ps[h, r, :].astype(F) * (dpl - inner_l)).astype(BF)
                ss[r, 0:128] = nn(dsl, kbuf[k_rows, lanes])
                dks_s[lb].append(tn(dsl, keep(qbuf[r, lanes], half)))
                dvs_s[lb].append(tn(ps[h, r, :], mgl))
            dqs.append(nn(ds, kbuf[0:TRK, lanes]) + ss[own, 0:128])
            dks.append(tn(ds, qm))
            dvs.append(tn(pt[h], mg))
        dq[:, lanes] = (jnp.where(half_lanes(dqs[0].shape, 0), dqs[0], dqs[1]) * 0.125).astype(BF)
        kbuf[0:TRK, lanes] = (dks[0] + dks[1]).astype(BF)
        vbuf[0:TRK, lanes] = (dvs[0] + dvs[1]).astype(BF)
        for lb in range(3):
            k_rows = slice(TRK + lb * 256, TRK + (lb + 1) * 256)
            kbuf[k_rows, lanes] = (dks_s[lb][0] + dks_s[lb][1]).astype(BF)
            vbuf[k_rows, lanes] = (dvs_s[lb][0] + dvs_s[lb][1]).astype(BF)

        total = None
        for at in range(0, KV, KV // 2):
            rs = slice(at, at + KV // 2)
            both = jnp.concatenate([kbuf[rs, lanes], vbuf[rs, lanes]], axis=1)
            part = tn(both, hid[rs, :])
            total = part if total is None else total + part
        kv_grad = jnp.transpose(total)
        gatt[1, :, lanes] = kv_grad[:, 0:128].astype(BF)
        gatt[2, :, lanes] = kv_grad[:, 128:256].astype(BF)
        gatt[0, :, lanes] = tn(hloc[own, :], dq[:, lanes]).astype(BF)

        @pl.when(turn < 2)
        def _():
            for m in range(2):
                for xx in range(2):
                    att[0].core_copy(m, band * 2 + xx).start()

        @pl.when(turn == 0)
        def _():
            leave(4)

        @pl.when(turn == 2)
        def _():
            leave(5)

    def key_grad(rs):
        return (nt(kbuf[rs, :], watt[1]) + nt(vbuf[rs, :], watt[2])).astype(BF)

    for lb in range(3):
        pe[lb, 0:256, :] = key_grad(slice(TRK + lb * 256, TRK + (lb + 1) * 256))

    def trunk_grad(rs):
        tok[rs, :] = key_grad(rs)

    row_loop(TRK, 256, trunk_grad)

    for b in range(BRANCHES):
        hits = [is_parent(lb, b) for lb in range(3)]
        for piece in range(4):
            total = jnp.zeros((32, D), F)
            for lb in range(3):
                at = piece * 32
                total += jnp.where(hits[lb], pe[lb, at : at + 32, :].astype(F), 0.0)
            at = TRK + b * BLK + piece * 32
            tok[at : at + 32, :] = total.astype(BF)
    for lb in range(3):
        spec_g[lb * BLK : (lb + 1) * BLK, :] = pe[lb, BLK : 2 * BLK, :]

    leave(6)
    acc1[...] = nt(dq[...], watt[0])

    def own_sum(rs):
        extra = spec_g[pl.ds(pl.multiple_of(rs.start + off, 32), 32), :].astype(F)
        acc1[rs, :] += extra

    row_loop(ROWS, 32, own_sum, 5)
    leave(7)
    leave(8)

    wire.arrived(halo, s_halo, to_y, y == 0)

    @pl.when(y == 0)
    def _():
        acc1[ROWS - 64 : ROWS, :] += halo[...].astype(F)

    @pl.when(x == 0)
    def _():
        def body(rs):
            mine = tok[pl.ds(pl.multiple_of(ci * ROWS + rs.start, 32), 32), :].astype(F)
            acc1[rs, :] += mine + rx_g[1, rs, :].astype(F)

        row_loop(ROWS, 32, body)

    @pl.when(ci == 4)
    def _():
        def body(rs):
            mine = tok[pl.ds(pl.multiple_of(4 * ROWS + rs.start, 32), 32), :].astype(F)
            acc1[rs, :] += mine + rx_g[1, rs, :].astype(F)

        row_loop(256, 32, body)

    mgrad[6:8, :] = jnp.zeros((2, D), F)
    sums = [jnp.zeros((1, D), F), jnp.zeros((1, D), F)]
    for i in range(ROWS // 32):
        rs = slice(i * 32, i * 32 + 32)
        back, ds, db = norm_back(acc1[rs, :], tok_own[rs, :].astype(F), sa)
        in_grad[rs, :] += back
        sums = [sums[0] + ds, sums[1] + db]
    mgrad[0:1, :] = sums[0]
    mgrad[1:2, :] = sums[1]
    leave(9)

    wire.drain()
    for family in (ffn, *att):
        family.drain()
    tree_peers(lambda k, to, _: mod_1(k, to).wait_send())
    peers(lambda k, to, _: mod_2(k, to).wait_send())
    peers(
        lambda k, to, _: wire.copy(
            cond_parts.at[to], cond_all.at[fs], s_cond + k, {"fsdp": to}
        ).wait_send()
    )
    peers(
        lambda k, to, _: wire.copy(
            part_out.at[to], part_in.at[fs], s_part + k, {"fsdp": to}
        ).wait_send()
    )
    for g in range(6):
        peers(
            lambda k, to, _, g=g: wire.copy(
                groups[g][0], place(g, my_rows, y, x, c), s_z[g] + k, {"fsdp": to}
            ).wait_send()
        )


def layer_call(n, parents, cond_parts, w_mod, tokens, enc, cot, weights):
    vm = pl.BlockSpec(memory_space=pltpu.VMEM)
    hbm = pl.BlockSpec(memory_space=pl.ANY)
    sds = jax.ShapeDtypeStruct
    rows = w_mod.shape[0]
    return pl.pallas_call(
        functools.partial(layer_kernel, n),
        out_shape=(
            sds((ROWS, D), BF),
            sds((ROWS, D), F),
            sds((ENC // 4, D), F),
            sds((rows, 6 * D), F),
            sds((8, rows, 256), F),
            sds((2, rows, 1024), F),
        ),
        in_specs=[pl.BlockSpec(memory_space=pltpu.SMEM), vm, vm, hbm, hbm, vm] + [hbm] * 6,
        out_specs=(vm, vm, vm, hbm, vm, vm),
        scratch_shapes=[
            pltpu.VMEM((8, D, D), BF),
            pltpu.VMEM((D, FF), BF),
            pltpu.VMEM((D, FF), BF),
            pltpu.VMEM((8 * ROWS + 64, D), BF),
            pltpu.VMEM((ENC, D), BF),
            pltpu.VMEM((n, 8, D), F),
            pltpu.VMEM((n, 8, D), F),
            pltpu.VMEM((8, D), F),
            pltpu.VMEM((*cond_parts.shape,), F),
            pltpu.VMEM((ROWS, D), BF),
            pltpu.VMEM((8, D), F),
            pltpu.VMEM((KV, D), BF),
            pltpu.VMEM((LOC, D), BF),
            pltpu.VMEM((KV, D), BF),
            pltpu.VMEM((KV, D), BF),
            pltpu.VMEM((LOC, D), BF),
            pltpu.VMEM((8, ROWS, TRK), BF),
            pltpu.VMEM((8, LOC, 256), BF),
            pltpu.VMEM((ROWS, TRK), BF),
            pltpu.VMEM((LOC, 256), BF),
            pltpu.VMEM((ROWS, TRK), F),
            pltpu.VMEM((LOC, 256), F),
            pltpu.VMEM((2, LOC, 128), F),
            pltpu.VMEM((ROWS, D), BF),
            pltpu.VMEM((ROWS, D), F),
            pltpu.VMEM((ROWS, D), F),
            pltpu.VMEM((ROWS, D), BF),
            pltpu.VMEM((ROWS, D), BF),
            pltpu.VMEM((ENC, D), BF),
            pltpu.VMEM((ENC, D), BF),
            pltpu.VMEM((ROWS, D), BF),
            pltpu.VMEM((8, ROWS, ENC), BF),
            pltpu.VMEM((ROWS, D), BF),
            pltpu.VMEM((ROWS, D), BF),
            pltpu.VMEM((ROWS, D), BF),
            pltpu.VMEM((ROWS, D), F),
            pltpu.VMEM((ROWS, D), F),
            pltpu.VMEM((ROWS, D), BF),
            pltpu.VMEM((ROWS, D), BF),
            pltpu.VMEM((ROWS, D), BF),
            pltpu.VMEM((D, D), F),
            pltpu.VMEM((ROWS, D), F),
            pltpu.VMEM((8, D, D), BF),
            pltpu.VMEM((2, D, FF), BF),
            pltpu.VMEM((8, D, 256), BF),
            pltpu.VMEM((2, 6, D, 128), BF),
            pltpu.VMEM((2, n, 2, rows, 128), BF),
            pltpu.VMEM((2, 4, 2, rows, 128), BF),
            pltpu.VMEM((n, 2, rows, 256), BF),
            pltpu.VMEM((4, 2, rows, 256), BF),
            pltpu.VMEM((896, D), BF),
            pltpu.VMEM((2, ROWS, D), BF),
            pltpu.VMEM((64, D), BF),
            pltpu.VMEM((2, 128, D), BF),
            pltpu.VMEM((4, 128, D), BF),
            pltpu.VMEM((8, 8, D), F),
            pltpu.VMEM((n, 8, D), F),
            pltpu.SemaphoreType.DMA((16 * n + 160,)),
            pltpu.SemaphoreType.DMA((16 * n + 160,)),
            pltpu.SemaphoreType.DMA((9,)),
            pltpu.SemaphoreType.REGULAR((2,)),
        ],
        compiler_params=pltpu.CompilerParams(
            vmem_limit_bytes=VMEM_LIMIT, collective_id=0, has_side_effects=True
        ),
        name="layer",
    )(parents, cond_parts, w_mod, tokens, enc, cot, *weights)


def timestep_code(timesteps, width):
    half = width // 2
    frequency = jnp.exp(-math.log(10000.0) * jnp.arange(half, dtype=F) / half)
    angles = timesteps.astype(F)[:, None] * frequency[None, :]
    return jnp.concatenate([jnp.sin(angles), jnp.cos(angles)], axis=-1)


def per_device(
    tokens,
    encoder_states,
    timesteps,
    parents,
    w_mod,
    w_self_qkv,
    w_self_out,
    w_cross_qkv,
    w_cross_out,
    w_up,
    w_down,
    cotangent,
):
    rows = w_mod.shape[0]
    condition = jax.nn.silu(timestep_code(timesteps, D)).astype(BF)
    n = lax.axis_size("fsdp")
    padded_cond = jnp.pad(condition.astype(F).reshape(n, 1, rows), ((0, 0), (0, 7), (0, max(128 - rows, 0))))
    out, in_grad, enc_grad, grad_mod, att, ffn = layer_call(
        n,
        parents,
        padded_cond,
        w_mod,
        tokens,
        encoder_states,
        cotangent[0],
        (w_self_qkv, w_self_out, w_cross_qkv, w_cross_out, w_up, w_down),
    )
    return (
        out[None],
        in_grad[None],
        enc_grad[None],
        grad_mod,
        att[0:3],
        att[3],
        att[4:7],
        att[7],
        ffn[0],
        ffn[1],
    )


def solution(mesh):
    rows = P("fsdp", ("ctx", "tp"), None)
    return jax.shard_map(
        per_device,
        mesh=mesh,
        in_specs=(
            rows,
            P("fsdp", "ctx", None),
            P("fsdp"),
            P("fsdp", None),
            P("fsdp", None),
            P(None, "fsdp", "tp"),
            P("fsdp", "tp"),
            P(None, "fsdp", "tp"),
            P("fsdp", "tp"),
            P("fsdp", "tp"),
            P("fsdp", "tp"),
            rows,
        ),
        out_specs=(
            rows,
            rows,
            P("fsdp", "ctx", None),
            P("fsdp", None),
            P(None, "fsdp", "tp"),
            P("fsdp", "tp"),
            P(None, "fsdp", "tp"),
            P("fsdp", "tp"),
            P("fsdp", "tp"),
            P("fsdp", "tp"),
        ),
        check_vma=False,
    )
```

```python
import functools
import math

import jax
import jax.numpy as jnp
from jax import lax
from jax.experimental import pallas as pl
from jax.experimental.pallas import tpu as pltpu
from jax.sharding import PartitionSpec as P

BF = jnp.bfloat16
F = jnp.float32
D = 512
FF = 2048
HD = 64
ROWS = 320
LOC = 384
BLK = 128
TRUNK = 8
BRANCHES = 4
TRK = TRUNK * BLK
SHARED = (TRUNK + BRANCHES) * BLK
SPEC = 2 * LOC
KV = TRK + SPEC
ENC = 512
EPS = 1e-05
NEG = -1e30
VMEM_LIMIT = 67043328


def nn(a, b):
    return lax.dot_general(a, b, (((1,), (0,)), ((), ())), preferred_element_type=F)


def nt(a, b):
    return lax.dot_general(a, b, (((1,), (1,)), ((), ())), preferred_element_type=F)


def tn(a, b):
    return lax.dot_general(a, b, (((0,), (0,)), ((), ())), preferred_element_type=F)


def normed(v):
    center = v - jnp.mean(v, axis=-1, keepdims=True)
    rstd = lax.rsqrt(jnp.mean(center * center, axis=-1, keepdims=True) + EPS)
    return center * rstd, rstd


def norm_back(grad, stream, scale):
    n, rstd = normed(stream)
    gn = grad * (1.0 + scale)
    back = rstd * (
        gn
        - jnp.mean(gn, axis=-1, keepdims=True)
        - n * jnp.mean(gn * n, axis=-1, keepdims=True)
    )
    return back, jnp.sum(grad * n, axis=0, keepdims=True), jnp.sum(grad, axis=0, keepdims=True)


def row_loop(total, step, body, unroll=1):
    if unroll == 0:
        for i in range(total // step):
            body(pl.ds(i * step, step))
        return

    @pl.loop(0, total // (step * unroll))
    def _(i):
        for j in range(unroll):
            body(pl.ds(pl.multiple_of((i * unroll + j) * step, step), step))


def half_lanes(shape, half):
    lane = lax.broadcasted_iota(jnp.int32, shape, len(shape) - 1)
    return (lane // HD) == half


def keep(value, half):
    return jnp.where(half_lanes(value.shape, half), value, jnp.zeros_like(value))


MESH = pl.DeviceIdType.MESH


class Wire:
    def __init__(self, send, recv):
        self.send, self.recv, self.used, self.sent = send, recv, 0, []

    def slot(self, count=1):
        self.used += count
        return self.used - count

    def copy(self, src, dst, at, to):
        return pltpu.make_async_remote_copy(
            src_ref=src,
            dst_ref=dst,
            send_sem=self.send.at[at],
            recv_sem=self.recv.at[at],
            device_id=to,
            device_id_type=MESH,
        )

    def push(self, dst, at, to, when=None, src=None):
        src = src or dst
        if when is None:
            self.copy(src(), dst(), at, to).start()
        else:

            @pl.when(when)
            def _():
                self.copy(src(), dst(), at, to).start()

        self.sent.append((src, dst, at, to, when))

    def arrived(self, dst, at, to, when=None):
        if when is None:
            self.copy(dst, dst, at, to).wait_recv()
        else:

            @pl.when(when)
            def _():
                self.copy(dst, dst, at, to).wait_recv()

    def drain(self):
        for src, dst, at, to, when in self.sent:
            if when is None:
                self.copy(src(), dst(), at, to).wait_send()
            else:

                @pl.when(when)
                def _(src=src, dst=dst, at=at, to=to):
                    self.copy(src(), dst(), at, to).wait_send()

        self.sent = []


def layer_kernel(
    n,
    parents_ref,
    cond_parts,
    w_mod,
    tok_in,
    enc_in,
    cot,
    w_sqkv,
    w_so,
    w_cqkv,
    w_co,
    w_up,
    w_dn,
    out_ref,
    in_grad,
    enc_out,
    mod_out,
    cond_out,
    att_out,
    ffn_out,
    watt,
    wup,
    wdn,
    tok,
    enc,
    part_out,
    part_in,
    mod,
    cond_all,
    tok_own,
    mgrad,
    hid,
    hloc,
    kbuf,
    vbuf,
    qbuf,
    pt,
    ps,
    bias_t,
    bias_s,
    st,
    ss,
    spec_o,
    mixa,
    stream_b,
    stream_c,
    hid_b,
    hid_c,
    kenc,
    venc,
    qb,
    pe,
    mixb,
    b0,
    b1,
    acc0,
    acc1,
    gbf,
    mgr,
    dq,
    wk_acc,
    wv_acc,
    gatt,
    gffn,
    rc_att,
    rx_att,
    zr_att,
    rg_att,
    zr_ffn,
    rg_ffn,
    rc_g,
    rx_g,
    halo,
    rc_e,
    rx_e,
    mod1,
    mod2,
    send,
    recv,
    local,
    ready,
):
    t0, t1 = st.at[:, 0:D], st.at[:, D : 2 * D]
    egrad = enc
    fs = lax.axis_index("fsdp")
    cx = lax.axis_index("ctx")
    y = lax.axis_index("tp")
    x, c = cx // 2, lax.rem(cx, 2)
    ci = cx * 2 + y
    odd = y
    off = pl.multiple_of(odd * 64, 64)
    own = pl.ds(off, ROWS)
    base = (ci * 5) // 2
    rows = w_mod.shape[0]
    to_y = {"tp": 1 - y}
    to_c = {"ctx": 2 * x + 1 - c}
    to_x = {"ctx": 2 * (1 - x) + c}
    wire = Wire(send, recv)

    my_rows = pl.ds(pl.multiple_of(fs * rows, rows), rows)

    def att_cols(yy, cc):
        return pl.ds(pl.multiple_of(yy * 256 + cc * 128, 128), 128)

    def ffn_cols(yy, xx, cc):
        return pl.ds(pl.multiple_of(yy * 1024 + xx * 512 + cc * 256, 256), 256)

    half = pl.ds(pl.multiple_of(c * 128, 128), 128)
    quarter = pl.ds(pl.multiple_of(cx * 256, 256), 256)
    groups = (
        (w_sqkv.at[:, :, half], watt, slice(0, 3), 0),
        (w_so.at[:, half], watt, 3, 0),
        (w_cqkv.at[:, :, half], watt, slice(4, 7), 0),
        (w_co.at[:, half], watt, 7, 0),
        (w_up.at[:, quarter], wup, None, 1),
        (w_dn.at[:, quarter], wdn, None, 1),
    )

    def place(g, row_at, yy, xx, cc):
        _, buf, index, wide = groups[g]
        if wide:
            return buf.at[row_at, ffn_cols(yy, xx, cc)]
        return buf.at[index, row_at, att_cols(yy, cc)]

    def chunk(i):
        return tok.at[pl.ds(pl.multiple_of(i * ROWS, ROWS), ROWS), :]

    def enc_part(i):
        return enc.at[pl.ds(pl.multiple_of(i * 128, 128), 128), :]

    all_rows = pl.ds(0, D)

    local_copies = [
        pltpu.make_async_copy(tok_in.at[0], chunk(ci), local.at[0]),
        pltpu.make_async_copy(enc_in.at[0], enc_part(cx), local.at[1]),
    ] + [
        pltpu.make_async_copy(groups[g][0], place(g, my_rows, y, x, c), local.at[2 + g])
        for g in range(6)
    ]
    local_copies.append(pltpu.make_async_copy(tok_in.at[0], tok_own, local.at[8]))
    for copy in local_copies:
        copy.start()

    barrier = pltpu.get_barrier_semaphore()

    @pl.loop(1, n)
    def _(k):
        pl.semaphore_signal(
            barrier, inc=1, device_id={"fsdp": lax.rem(fs + k, n)}, device_id_type=MESH
        )

    @pl.loop(1, 8)
    def _(k):
        other = lax.rem(ci + k, 8)
        pl.semaphore_signal(
            barrier,
            inc=1,
            device_id={"ctx": other // 2, "tp": lax.rem(other, 2)},
            device_id_type=MESH,
        )

    pl.semaphore_wait(barrier, n - 1 + 7)

    def peers(make):
        @pl.loop(1, n)
        def _(k):
            make(k, lax.rem(fs + k, n), lax.rem(fs + n - k, n))

    s_cond = wire.slot(n)
    s_part = wire.slot(n)
    s_z = [wire.slot(n) for _ in range(6)]
    s_y = [wire.slot() for _ in range(6)]
    s_c0 = [wire.slot() for _ in range(6)]
    s_c1 = [wire.slot() for _ in range(6)]
    s_x0 = [wire.slot() for _ in range(6)]
    s_x1 = [wire.slot() for _ in range(6)]
    s_c2 = [wire.slot() for _ in range(6)]
    s_c3 = [wire.slot() for _ in range(6)]
    s_ty, s_tx, s_txy, s_tc0, s_tc1, s_tc2, s_tc3, s_ty2 = (
        wire.slot() for _ in range(8)
    )
    s_ex, s_ec0, s_ec1 = (wire.slot() for _ in range(3))

    peers(
        lambda k, to, _: wire.copy(
            cond_parts.at[to], cond_all.at[fs], s_cond + k, {"fsdp": to}
        ).start()
    )
    left = x == 0

    def tail_rows(i):
        return tok.at[pl.ds(pl.multiple_of(i * ROWS + ROWS - 64, 64), 64), :]

    wire.push(
        lambda: chunk(ci), s_ty, to_y, jnp.logical_or(left, ci == 4), lambda: tok_in.at[0]
    )
    wire.push(
        lambda: tail_rows(ci), s_ty2, to_y, ci == 6, lambda: tok_in.at[0, ROWS - 64 : ROWS, :]
    )
    wire.push(lambda: chunk(ci), s_tx, to_x, x == 0, lambda: tok_in.at[0])
    wire.push(
        lambda: chunk(ci), s_tc0, to_c, jnp.logical_or(left, ci == 4), lambda: tok_in.at[0]
    )

    def z_start(g):
        peers(
            lambda k, to, _: wire.copy(
                groups[g][0], place(g, my_rows, y, x, c), s_z[g] + k, {"fsdp": to}
            ).start()
        )

    z_start(0)

    def mask_trunk(rs):
        row = lax.broadcasted_iota(jnp.int32, (32, TRK), 0) + rs.start + ci * ROWS
        col = lax.broadcasted_iota(jnp.int32, (32, TRK), 1)
        bias_t[rs, :] = jnp.where(col <= row, 0.0, NEG).astype(BF)

    row_loop(ROWS, 32, mask_trunk)
    for lb in range(3):
        blk = base + lb
        row = lax.broadcasted_iota(jnp.int32, (BLK, 2 * BLK), 0)
        col = lax.broadcasted_iota(jnp.int32, (BLK, 2 * BLK), 1)
        par_ok = jnp.logical_and(col < BLK, blk >= TRUNK + BRANCHES)
        self_ok = jnp.logical_and(
            jnp.logical_and(col >= BLK, col - BLK <= row), blk >= TRUNK
        )
        bias_s[lb * BLK : (lb + 1) * BLK, :] = jnp.where(
            jnp.logical_or(par_ok, self_ok), 0.0, NEG
        ).astype(BF)

    cond_all[fs] = cond_parts[fs]
    peers(lambda k, _, src: wire.arrived(cond_all.at[src], s_cond + k, {"fsdp": src}))
    for v in range(6):
        part_out[:, v, :] = nn(
            cond_all[:, 0, 0:rows].astype(BF), w_mod[:, v * D : (v + 1) * D]
        )
    part_out[:, 6:8, :] = jnp.zeros((n, 2, D), F)
    peers(
        lambda k, to, _: wire.copy(
            part_out.at[to], part_in.at[fs], s_part + k, {"fsdp": to}
        ).start()
    )
    part_in[fs] = part_out[fs]

    def z_done(g):
        local_copies[2 + g].wait()
        peers(
            lambda k, _, src: wire.arrived(
                place(g, pl.ds(pl.multiple_of(src * rows, rows), rows), y, x, c),
                s_z[g] + k,
                {"fsdp": src},
            )
        )
        slab = lambda: place(g, all_rows, y, x, c)
        wire.push(slab, s_y[g], to_y)
        if groups[g][3]:
            wire.push(slab, s_x0[g], to_x)
        wire.push(slab, s_c0[g], to_c)

    def y_done(g):
        slab = lambda: place(g, all_rows, 1 - y, x, c)
        wire.arrived(slab(), s_y[g], to_y)
        if groups[g][3]:
            wire.push(slab, s_x1[g], to_x)
        wire.push(slab, s_c1[g], to_c)

    def x_done(g, part):
        s_in, s_out = ((s_x0[g], s_c2[g]), (s_x1[g], s_c3[g]))[part]
        slab = lambda: place(g, all_rows, 1 - y if part else y, 1 - x, c)
        wire.arrived(slab(), s_in, to_x)
        wire.push(slab, s_out, to_c)

    def c_part(g, part):
        yy, xx, at = (
            (y, x, s_c0[g]),
            (1 - y, x, s_c1[g]),
            (y, 1 - x, s_c2[g]),
            (1 - y, 1 - x, s_c3[g]),
        )[part]
        wire.arrived(place(g, all_rows, yy, xx, 1 - c), at, to_c)

    def c_done(g):
        wire.arrived(place(g, all_rows, y, x, 1 - c), s_c0[g], to_c)
        wire.arrived(place(g, all_rows, 1 - y, x, 1 - c), s_c1[g], to_c)
    local_copies[0].wait()
    local_copies[1].wait()
    ciy = 4 * x + 2 * c + 1 - y
    cic = 4 * x + 2 * (1 - c) + y
    ciyc = 4 * x + 2 * (1 - c) + 1 - y
    low, lowy, lowc, lowyc = 2 * c + y, 2 * c + 1 - y, 2 * (1 - c) + y, 2 * (1 - c) + 1 - y
    right = x == 1
    local_copies[8].wait()
    wire.arrived(chunk(ciy), s_ty, to_y, jnp.logical_or(left, ci == 5))
    wire.push(lambda: chunk(ciy), s_txy, to_x, left)
    wire.push(lambda: chunk(ciy), s_tc1, to_c, jnp.logical_or(left, ci == 5))
    wire.arrived(tail_rows(ciy), s_ty2, to_y, ci == 7)

    @pl.when(jnp.logical_and(right, y == 0))
    def _():
        tok[pl.ds(pl.multiple_of((ci + 1) * ROWS, 64), 64), :] = jnp.zeros((64, D), BF)

    z_start(1)
    z_start(4)
    wire.arrived(chunk(low), s_tx, to_x, right)
    wire.push(lambda: chunk(low), s_tc2, to_c, right)
    z_done(0)
    z_start(2)
    wire.arrived(chunk(lowy), s_txy, to_x, right)
    wire.push(lambda: chunk(lowy), s_tc3, to_c, right)
    wire.push(lambda: enc_part(cx), s_ex, to_x, None, lambda: enc_in.at[0])
    wire.push(lambda: enc_part(cx), s_ec0, to_c, None, lambda: enc_in.at[0])
    y_done(0)
    z_done(1)
    z_done(4)
    z_start(5)
    z_start(3)

    peers(lambda k, _, src: wire.arrived(part_in.at[src], s_part + k, {"fsdp": src}))
    mod[...] = jnp.sum(part_in[...], axis=0)
    sa, ba = mod[0:1, :], mod[1:2, :]
    sb, bb = mod[2:3, :], mod[3:4, :]
    sf, bf_ = mod[4:5, :], mod[5:6, :]

    wire.arrived(chunk(cic), s_tc0, to_c, jnp.logical_or(left, ci == 6))
    wire.arrived(chunk(ciyc), s_tc1, to_c, jnp.logical_or(left, ci == 7))
    wire.arrived(chunk(lowc), s_tc2, to_c, right)
    wire.arrived(chunk(lowyc), s_tc3, to_c, right)

    def enc_done(step):
        if step == 0:
            wire.arrived(enc_part(2 * (1 - x) + c), s_ex, to_x)
            wire.push(lambda: enc_part(2 * (1 - x) + c), s_ec1, to_c)
        else:
            wire.arrived(enc_part(2 * x + 1 - c), s_ec0, to_c)
            wire.arrived(enc_part(2 * (1 - x) + 1 - c), s_ec1, to_c)

    tok_tb = tok
    tok_loc = tok.at[pl.ds(pl.multiple_of(ci * ROWS - off, 64), LOC), :]

    def relay(step):
        if step == 1:
            y_done(1)
            y_done(4)
            enc_done(0)
        if step == 2:
            z_done(5)
            z_done(3)
        if step == 4:
            c_done(1)
        if step == 5:
            y_done(3)
            c_done(3)
        if step == 6:
            x_done(4, 0)
            x_done(5, 0)
        if step == 7:
            y_done(2)
            y_done(5)
            enc_done(1)
            c_done(2)

    spec_g = qbuf

    def is_parent(lb, branch):
        parent = jnp.full((32, D), parents_ref[0, base + lb], jnp.int32)
        leaf = jnp.full((32, D), base + lb, jnp.int32) >= TRUNK + BRANCHES
        return jnp.logical_and(leaf, parent == TRUNK + branch)

    to_xy = {"ctx": 2 * (1 - x) + c, "tp": 1 - y}
    s_rcg, s_rcg4, s_rcg5, s_halo = (wire.slot() for _ in range(4))
    s_rxy = [wire.slot() for _ in range(2)]
    s_rxx = [wire.slot() for _ in range(2)]
    s_rce = [wire.slot(), wire.slot()]
    s_rxe = [wire.slot() for _ in range(3)]
    s_m1 = wire.slot(8)
    s_m2 = wire.slot(n)
    quad = ((to_y, x, 1 - y), (to_x, 1 - x, y), (to_xy, 1 - x, 1 - y))

    def add_rows(target, terms, total, step=64):
        def body(rs):
            value = terms[0][rs, :].astype(F)
            for term in terms[1:]:
                value += term[rs, :].astype(F)
            target[rs, :] = value.astype(BF)

        row_loop(total, step, body)

    def strip(buf, at):
        return buf.at[:, at * 256 : (at + 1) * 256]

    class Family:
        def __init__(self, unit, core_box, box, landing, held, shape_rows):
            self.unit, self.core_box, self.box = unit, core_box, box
            self.landing, self.held = landing, held
            self.s_core = [wire.slot(4) for _ in range(2)]
            self.s_one = [[wire.slot() for _ in range(2)] for _ in range(2)]
            self.s_two = [wire.slot() for _ in range(2)]
            self.s_z = [wire.slot(n) for _ in range(2)]
            self.s_g = wire.slot(4)

        def core_copy(self, m, t):
            return wire.copy(
                self.unit(m, t // 2, lax.rem(t, 2), 1 - c),
                self.core_box(m, t),
                self.s_core[m] + t,
                to_c,
            )

        def core_send(self):
            for m in range(2):
                for t in range(4):
                    self.core_copy(m, t).start()

        def first_send(self):
            for m in range(2):
                for t in range(4):
                    wire.arrived(self.core_box(m, t), self.s_core[m] + t, to_c)
                    mine = self.unit(m, t // 2, t % 2, c)
                    add_rows(mine, (mine, self.core_box(m, t)), D)
            for j in range(2):
                wire.push(
                    lambda j=j: self.box(j),
                    self.s_one[0][j],
                    to_x,
                    None,
                    lambda j=j: self.unit(0, j, 1 - x, c),
                )
                wire.push(
                    lambda j=j: self.box(2 + j),
                    self.s_one[1][j],
                    to_y,
                    None,
                    lambda j=j: self.unit(1, 1 - y, j, c),
                )

        def second_send(self):
            for j in range(2):
                wire.arrived(self.box(j), self.s_one[0][j], to_x)
                mine = self.unit(0, j, x, c)
                add_rows(mine, (mine, self.box(j)), D)
            wire.push(
                lambda: self.box(4),
                self.s_two[0],
                to_y,
                None,
                lambda: self.unit(0, 1 - y, x, c),
            )
            for j in range(2):
                wire.arrived(self.box(2 + j), self.s_one[1][j], to_y)
                mine = self.unit(1, y, j, c)
                add_rows(mine, (mine, self.box(2 + j)), D)
            wire.push(
                lambda: self.box(5),
                self.s_two[1],
                to_x,
                None,
                lambda: self.unit(1, y, 1 - x, c),
            )

        def z_copy(self, m, k, to):
            part = pl.ds(pl.multiple_of(to * rows, rows), rows)
            return wire.copy(
                self.unit(m, y, x, c).at[part, :],
                self.landing.at[fs, m],
                self.s_z[m] + k,
                {"fsdp": to},
            )

        def tree_send(self):
            for m, target in ((0, to_y), (1, to_x)):
                wire.arrived(self.box(4 + m), self.s_two[m], target)
                mine = self.unit(m, y, x, c)
                add_rows(mine, (mine, self.box(4 + m)), D)
                peers(lambda k, to, _, m=m: self.z_copy(m, k, to).start())
                self.landing[fs, m] = self.unit(m, y, x, c)[my_rows, :]

        def g_copy(self, i):
            target, at = ((to_x, cx), (to_c, cx), (to_c, 2 * (1 - x) + c))[i]
            return wire.copy(self.held.at[at], self.held.at[at], self.s_g + i, target)

        def copy_send(self):
            for m in range(2):
                peers(
                    lambda k, _, src, m=m: wire.arrived(
                        self.landing.at[src, m], self.s_z[m] + k, {"fsdp": src}
                    )
                )
            self.held[cx] = jnp.sum(self.landing[...].astype(F), axis=0).astype(BF)
            self.g_copy(0).start()
            self.g_copy(1).start()

        def relay_copy(self):
            wire.arrived(self.held.at[2 * (1 - x) + c], self.s_g, to_x)
            self.g_copy(2).start()

        def collect(self):
            wire.arrived(self.held.at[2 * x + 1 - c], self.s_g + 1, to_c)
            wire.arrived(self.held.at[2 * (1 - x) + 1 - c], self.s_g + 2, to_c)

        def drain(self):
            for m in range(2):
                for t in range(4):
                    self.core_copy(m, t).wait_send()
                peers(lambda k, to, _, m=m: self.z_copy(m, k, to).wait_send())
            for i in range(3):
                self.g_copy(i).wait_send()

    ffn = Family(
        lambda m, yy, xx, cc: gffn.at[m, :, ffn_cols(yy, xx, cc)],
        lambda m, t: rc_att.at[m * 4 + t],
        lambda i: strip(wdn, i),
        zr_ffn,
        rg_ffn,
        rows,
    )

    def attention_family(a):
        return Family(
            lambda m, yy, xx, cc: gatt.at[4 * a + 2 * xx + m, :, att_cols(yy, cc)],
            lambda m, t: rc_att.at[
                4 * a + 2 * m + t // 2, :, pl.ds(pl.multiple_of(lax.rem(t, 2) * 128, 128), 128)
            ],
            lambda i: rx_att.at[a, i],
            zr_att.at[a],
            rg_att.at[a],
            rows,
        )

    att = (attention_family(0), attention_family(1))

    def ffn_free():
        wire.drain()
        for target in (to_y, to_x):
            pl.semaphore_signal(ready.at[0], inc=1, device_id=target, device_id_type=MESH)

    def ffn_chip_send():
        pl.semaphore_wait(ready.at[0], 2)
        ffn.first_send()
        pl.semaphore_signal(ready.at[1], inc=1, device_id=to_c, device_id_type=MESH)

    results = (
        (rg_ffn, ffn_out),
        (rg_att.at[0], att_out.at[0]),
        (rg_att.at[1], att_out.at[1]),
        (mod2, mod_out),
        (cond_all, cond_out),
    )

    def result(i):
        return pltpu.make_async_copy(results[i][0], results[i][1], local.at[i])

    def ffn_finish():
        ffn.collect()
        result(0).start()

    def att_finish(a):
        att[a].collect()
        result(1 + a).start()

    def enc_core_send():
        for xx in range(2):
            wire.push(
                lambda xx=xx: rc_e.at[xx],
                s_rce[xx],
                to_c,
                None,
                lambda xx=xx: egrad.at[pl.ds(pl.multiple_of((2 * xx + 1 - c) * 128, 128), 128), :],
            )

    def enc_rows(xx):
        return egrad.at[pl.ds(pl.multiple_of((2 * xx + c) * 128, 128), 128), :]

    def enc_chip_send():
        for xx in range(2):
            wire.arrived(rc_e.at[xx], s_rce[xx], to_c)
            add_rows(enc_rows(xx), (enc_rows(xx), rc_e.at[xx]), 128)
        for r, (target, xx, _) in enumerate(quad):
            wire.push(
                lambda: rx_e.at[2 * x + y], s_rxe[r], target, None, lambda xx=xx: enc_rows(xx)
            )
        rx_e[2 * x + y] = enc_rows(x)[...]

    def enc_finish():
        for r, (target, xx, yy) in enumerate(quad):
            wire.arrived(rx_e.at[2 * xx + yy], s_rxe[r], target)
        enc_out[...] = jnp.sum(rx_e[...].astype(F), axis=0)

    def shared_core_send():
        to_core = pl.ds(pl.multiple_of(640 * (1 - c), 640), 640)
        wire.push(lambda: rc_g.at[0:640], s_rcg, to_c, None, lambda: tok.at[to_core, :])
        wire.push(
            lambda: rc_g.at[640:896],
            s_rcg4,
            to_c,
            jnp.logical_and(x == 1, c == 1),
            lambda: tok.at[1280:1536, :],
        )
        wire.push(lambda: halo, s_halo, to_y, y == 1, lambda: spec_g.at[0:64, :])

    def part_rows(yy, p):
        return tok.at[pl.ds(pl.multiple_of((2 * c + yy) * ROWS + p * 160, 32), 160), :]

    def core_rows(yy, p):
        return rc_g.at[pl.ds(pl.multiple_of(yy * ROWS + p * 160, 32), 160), :]

    def shared_y_send():
        wire.arrived(rc_g.at[0:640], s_rcg, to_c)
        for p in range(2):
            mine = part_rows(1 - y, p)
            add_rows(mine, (mine, core_rows(1 - y, p)), 160, 32)
            wire.push(
                lambda p=p: rx_g.at[0, p * 160 : p * 160 + 160],
                s_rxy[p],
                to_y,
                None,
                lambda p=p: part_rows(1 - y, p),
            )
        last = jnp.logical_and(x == 1, c == 0)

        @pl.when(last)
        def _():
            wire.arrived(rc_g.at[640:896], s_rcg4, to_c)
            four = tok.at[1280:1536, :]
            add_rows(four, (four, rc_g.at[640:896]), 256)

        wire.push(
            lambda: rx_g.at[1, 0:256],
            s_rcg5,
            to_y,
            jnp.logical_and(last, y == 1),
            lambda: tok.at[1280:1536, :],
        )
        for p in range(2):
            mine = part_rows(y, p)
            add_rows(mine, (mine, core_rows(y, p)), 160, 32)

    def shared_x_send():
        for p in range(2):
            wire.arrived(rx_g.at[0, p * 160 : p * 160 + 160], s_rxy[p], to_y)
            mine = part_rows(y, p)
            add_rows(mine, (mine, rx_g.at[0, p * 160 : p * 160 + 160]), 160, 32)
            wire.push(
                lambda p=p: rx_g.at[1, p * 160 : p * 160 + 160],
                s_rxx[p],
                to_x,
                x == 1,
                lambda p=p: part_rows(y, p),
            )

    def shared_arrived():
        for p in range(2):
            wire.arrived(rx_g.at[1, p * 160 : p * 160 + 160], s_rxx[p], to_x, x == 0)
        wire.arrived(rx_g.at[1, 0:256], s_rcg5, to_y, ci == 4)

    def tree_peers(make):
        @pl.loop(1, 8)
        def _(k):
            make(k, lax.rem(ci + k, 8), lax.rem(ci + 8 - k, 8))

    def device_of(i):
        return {"ctx": i // 2, "tp": lax.rem(i, 2)}

    def mod_1(k, to):
        return wire.copy(mgrad, mod1.at[ci], s_m1 + k, device_of(to))

    def mod_2(k, to):
        return wire.copy(mod2.at[fs], mod2.at[fs], s_m2 + k, {"fsdp": to})

    def mod_tree_send():
        tree_peers(lambda k, to, _: mod_1(k, to).start())
        mod1[ci] = mgrad[...]

    def mod_all_send():
        tree_peers(lambda k, _, src: wire.arrived(mod1.at[src], s_m1 + k, device_of(src)))
        mod2[fs] = jnp.sum(mod1[...], axis=0)
        peers(lambda k, to, _: mod_2(k, to).start())

    def mod_finish():
        peers(lambda k, _, src: wire.arrived(mod2.at[src], s_m2 + k, {"fsdp": src}))
        result(3).start()
        result(4).start()

    def leave(step):
        if step == 0:
            ffn_free()
        if step == 1:
            ffn_chip_send()
        if step == 2:
            pl.semaphore_wait(ready.at[1], 1)
            att[1].core_send()
            enc_core_send()
        if step == 3:
            att[1].first_send()
            enc_chip_send()
        if step == 4:
            ffn.second_send()
        if step == 5:
            att[1].second_send()
            ffn.tree_send()
        if step == 6:
            shared_core_send()
            att[1].tree_send()
        if step == 7:
            shared_y_send()
            att[0].first_send()
            ffn.copy_send()
            enc_finish()
            shared_x_send()
        if step == 8:
            att[0].second_send()
            att[1].copy_send()
            ffn.relay_copy()
            shared_arrived()
        if step == 9:
            mod_tree_send()
            att[0].tree_send()
            att[1].relay_copy()
            ffn_finish()
            mod_all_send()
            att[0].copy_send()
            att_finish(1)
            mod_finish()
            att[0].relay_copy()
            att_finish(0)

    def hidden(x):
        n, _ = normed(x.astype(F))
        return (n * (1.0 + sa) + ba).astype(BF)

    def hid_trunk(rs):
        hid[rs, :] = hidden(tok_tb[rs, :])

    row_loop(TRK, 32, hid_trunk, 8)

    def hid_loc(rs):
        hloc[rs, :] = hidden(tok_loc[rs, :])

    row_loop(LOC, 32, hid_loc, 6)
    for lb in range(3):
        picks = [is_parent(lb, b) for b in range(1, BRANCHES)]
        for piece in range(4):
            r = piece * 32
            picked = tok_tb[TRK + r : TRK + r + 32, :].astype(F)
            for b in range(1, BRANCHES):
                at = TRK + b * BLK + r
                picked = jnp.where(picks[b - 1], tok_tb[at : at + 32, :].astype(F), picked)
            at = TRK + lb * 256 + r
            hid[at : at + 32, :] = hidden(picked)
        hid[TRK + lb * 256 + BLK : TRK + lb * 256 + 2 * BLK, :] = hloc[
            lb * BLK : (lb + 1) * BLK, :
        ]

    def project(rs):
        kbuf[rs, :] = nn(hid[rs, :], watt[1]).astype(BF)
        vbuf[rs, :] = nn(hid[rs, :], watt[2]).astype(BF)

    z_done(2)
    c_done(0)
    row_loop(KV, 256, project)
    qbuf[...] = (nn(hloc[...], watt[0]) * 0.125).astype(BF)

    linv_a, linv_b = wk_acc.at[0:ROWS, :], wv_acc.at[0:ROWS, :]

    def with_ones(values, half):
        return jnp.where(half_lanes(values.shape, half), values, jnp.ones_like(values))

    def finish_heads(o0, o1, mixed, linv, lanes):
        inv0, inv1 = 1.0 / pltpu.roll(o0, HD, 1), 1.0 / pltpu.roll(o1, HD, 1)
        first = half_lanes(o0.shape, 0)
        mixed[:, lanes] = jnp.where(first, o0 * inv0, o1 * inv1).astype(BF)
        linv[:, lanes] = jnp.where(first, inv0, inv1)

    @pl.loop(0, 4)
    def _(hp):
        for step in (1, 2):

            @pl.when(hp == step)
            def _(step=step):
                relay(step)

        lanes = pl.ds(pl.multiple_of(hp * 128, 128), 128)
        kt = kbuf[0:TRK, lanes]
        vt = vbuf[0:TRK, lanes]
        outs = []
        for half in range(2):
            h = hp * 2 + half
            st[...] = nt(keep(qbuf[own, lanes], half), kt) + bias_t[...].astype(F)
            for lb in range(3):
                r = slice(lb * BLK, (lb + 1) * BLK)
                ks = kbuf[TRK + lb * 256 : TRK + (lb + 1) * 256, lanes]
                ss[r, :] = nt(keep(qbuf[r, lanes], half), ks) + bias_s[r, :].astype(F)
            for i in range(ROWS // 32):
                rs = slice(i * 32, i * 32 + 32)
                ro = pl.ds(pl.multiple_of(i * 32 + off, 32), 32)
                a, b = st[rs, :], ss[ro, :]
                top = jnp.maximum(
                    jnp.max(a, axis=-1, keepdims=True), jnp.max(b, axis=-1, keepdims=True)
                )
                pt[h, rs, :] = jnp.exp(a - top).astype(BF)
                ps[h, ro, :] = jnp.exp(b - top).astype(BF)
            for lb in range(3):
                r = slice(lb * BLK, (lb + 1) * BLK)
                vs = vbuf[TRK + lb * 256 : TRK + (lb + 1) * 256, lanes]
                spec_o[half, r, :] = nn(ps[h, r, :], with_ones(vs, half))
            outs.append(nn(pt[h], with_ones(vt, half)) + spec_o[half, own, :])
        finish_heads(outs[0], outs[1], mixa, linv_a, lanes)

    relay(4)
    t0[...] = nt(mixa[...], watt[3])

    def after_self(rs):
        sbv = tok_own[rs, :].astype(F) + t0[rs, :]
        stream_b[rs, :] = sbv
        n, _ = normed(sbv)
        hid_b[rs, :] = (n * (1.0 + sb) + bb).astype(BF)

    row_loop(ROWS, 32, after_self, 0)

    relay(7)
    kenc[...] = nn(enc[...], watt[5]).astype(BF)
    venc[...] = nn(enc[...], watt[6]).astype(BF)
    qb[...] = (nn(hid_b[...], watt[4]) * 0.125).astype(BF)

    @pl.loop(0, 4)
    def _(hp):
        lanes = pl.ds(pl.multiple_of(hp * 128, 128), 128)
        kt = kenc[:, lanes]
        vt = venc[:, lanes]
        outs = []
        for half in range(2):
            h = hp * 2 + half
            t0[...] = nt(keep(qb[:, lanes], half), kt)
            for i in range(ROWS // 32):
                rs = slice(i * 32, i * 32 + 32)
                a = t0[rs, :]
                pe[h, rs, :] = jnp.exp(a - jnp.max(a, axis=-1, keepdims=True)).astype(BF)
            outs.append(nn(pe[h], with_ones(vt, half)))
        finish_heads(outs[0], outs[1], mixb, linv_b, lanes)

    relay(5)
    t0[...] = nt(mixb[...], watt[7])

    def after_cross(rs):
        scv = stream_b[rs, :] + t0[rs, :]
        stream_c[rs, :] = scv
        n, _ = normed(scv)
        hid_c[rs, :] = (n * (1.0 + sf) + bf_).astype(BF)

    row_loop(ROWS, 32, after_cross, 0)

    relay(6)
    acc0[...] = jnp.zeros_like(acc0)
    acc1[...] = jnp.zeros_like(acc1)

    def flip(v, by):
        return v + by - 2 * v * by

    @pl.loop(0, 4)
    def _(ft):
        @pl.when(ft == 2)
        def _():
            x_done(4, 1)
            x_done(5, 1)

        for part in range(4):

            @pl.when(ft == part)
            def _(part=part):
                c_part(4, part)
                c_part(5, part)

        tile = flip(y, lax.rem(ft, 2)) * 2 + flip(x, ft // 2)
        cols = pl.ds(pl.multiple_of(tile * 512, 512), 512)
        t0[...] = nn(hid_c[...], wup[:, cols])
        t1[...] = nn(cot[...], wdn[:, cols])

        def gelu(rs):
            u = t0[rs, :]
            phi = 0.5 * (1.0 + lax.erf(u * (2.0**-0.5)))
            b0[rs, :] = (u * phi).astype(BF)
            slope = phi + u * (jnp.exp(-0.5 * u * u) * (1.0 / math.sqrt(2.0 * math.pi)))
            b1[rs, :] = (t1[rs, :] * slope).astype(BF)

        row_loop(ROWS, 32, gelu)
        acc0[...] += nt(b0[...], wdn[:, cols])
        acc1[...] += nt(b1[...], wup[:, cols])
        gffn[1, :, cols] = tn(cot[...], b0[...]).astype(BF)
        gffn[0, :, cols] = tn(hid_c[...], b1[...]).astype(BF)
        for m in range(2):
            ffn.core_copy(m, tile).start()

    def back_norm(at, scale, grad_src, stream_src, base_src, want_out):
        sums = [jnp.zeros((1, D), F), jnp.zeros((1, D), F)]
        for i in range(ROWS // 32):
            rs = slice(i * 32, i * 32 + 32)
            back, ds, db = norm_back(grad_src[rs, :], stream_src[rs, :], scale)
            total = base_src[rs, :].astype(F) + back
            in_grad[rs, :] = total
            gbf[rs, :] = total.astype(BF)
            sums = [sums[0] + ds, sums[1] + db]
            if want_out:
                out_ref[rs, :] = (stream_c[rs, :] + acc0[rs, :]).astype(BF)
        mgrad[at : at + 1, :] = sums[0]
        mgrad[at + 1 : at + 2, :] = sums[1]

    leave(0)
    back_norm(4, sf, acc1, stream_c, cot, True)

    gatt[7] = tn(gbf[...], mixb[...]).astype(BF)
    mgr[...] = (nn(gbf[...], watt[7]) * linv_b[...]).astype(BF)
    leave(1)

    @pl.loop(0, 4)
    def _(hp):
        lanes = pl.ds(pl.multiple_of(hp * 128, 128), 128)
        prod = mgr[:, lanes].astype(F) * mixb[:, lanes].astype(F)
        dqs, dks, dvs = [], [], []
        for half in range(2):
            h = hp * 2 + half
            inner = jnp.sum(keep(prod, half), axis=-1, keepdims=True)
            mg = keep(mgr[:, lanes], half)
            dp = nt(mg, venc[:, lanes])
            b0[...] = (pe[h].astype(F) * (dp - inner)).astype(BF)
            dqs.append(nn(b0[...], kenc[:, lanes]))
            dks.append(tn(b0[...], keep(qb[:, lanes], half)))
            dvs.append(tn(pe[h], mg))
        dq[:, lanes] = (jnp.where(half_lanes(dqs[0].shape, 0), dqs[0], dqs[1]) * 0.125).astype(BF)
        kenc[:, lanes] = (dks[0] + dks[1]).astype(BF)
        venc[:, lanes] = (dvs[0] + dvs[1]).astype(BF)

    gatt[4] = tn(hid_b[...], dq[...]).astype(BF)
    gatt[5] = tn(enc[...], kenc[...]).astype(BF)
    gatt[6] = tn(enc[...], venc[...]).astype(BF)
    egrad[...] = (nt(kenc[...], watt[5]) + nt(venc[...], watt[6])).astype(BF)
    leave(2)
    acc1[...] = nt(dq[...], watt[4])
    back_norm(2, sb, acc1, stream_b, in_grad, False)

    gatt[3] = tn(gbf[...], mixa[...]).astype(BF)
    mgr[...] = (nn(gbf[...], watt[3]) * linv_a[...]).astype(BF)
    leave(3)

    @pl.when(odd == 0)
    def _():
        for h in range(8):
            ps[h, ROWS:LOC, :] = jnp.zeros((LOC - ROWS, 256), BF)
        spec_o[:, ROWS:LOC, :] = jnp.zeros((2, LOC - ROWS, 128), F)

    @pl.when(odd == 1)
    def _():
        for h in range(8):
            ps[h, 0:64, :] = jnp.zeros((64, 256), BF)
        spec_o[:, 0:64, :] = jnp.zeros((2, 64, 128), F)

    @pl.loop(0, 4)
    def _(turn):
        side = jnp.where(turn < 2, 1 - c, c)
        band = jnp.where(turn < 2, turn, jnp.where(turn == 2, 1 - y, y))
        hp = band * 2 + side
        lanes = pl.ds(pl.multiple_of(hp * 128, 128), 128)
        prod = mgr[:, lanes].astype(F) * mixa[:, lanes].astype(F)
        dqs, dks, dvs = [], [], []
        dks_s = [[], [], []]
        dvs_s = [[], [], []]
        for half in range(2):
            h = hp * 2 + half
            inner = jnp.sum(keep(prod, half), axis=-1, keepdims=True)
            mg = keep(mgr[:, lanes], half)
            qm = keep(qbuf[own, lanes], half)
            dp = nt(mg, vbuf[0:TRK, lanes])
            ds = (pt[h].astype(F) * (dp - inner)).astype(BF)
            spec_o[0, own, :] = mg.astype(F)
            spec_o[1, own, :] = jnp.broadcast_to(inner, (ROWS, 128))
            dq_s = []
            for lb in range(3):
                r = slice(lb * BLK, (lb + 1) * BLK)
                k_rows = slice(TRK + lb * 256, TRK + (lb + 1) * 256)
                mgl = spec_o[0, r, :].astype(BF)
                dpl = nt(mgl, vbuf[k_rows, lanes])
                inner_l = spec_o[1, r, 0:1]
                dsl = (ps[h, r, :].astype(F) * (dpl - inner_l)).astype(BF)
                ss[r, 0:128] = nn(dsl, kbuf[k_rows, lanes])
                dks_s[lb].append(tn(dsl, keep(qbuf[r, lanes], half)))
                dvs_s[lb].append(tn(ps[h, r, :], mgl))
            dqs.append(nn(ds, kbuf[0:TRK, lanes]) + ss[own, 0:128])
            dks.append(tn(ds, qm))
            dvs.append(tn(pt[h], mg))
        dq[:, lanes] = (jnp.where(half_lanes(dqs[0].shape, 0), dqs[0], dqs[1]) * 0.125).astype(BF)
        kbuf[0:TRK, lanes] = (dks[0] + dks[1]).astype(BF)
        vbuf[0:TRK, lanes] = (dvs[0] + dvs[1]).astype(BF)
        for lb in range(3):
            k_rows = slice(TRK + lb * 256, TRK + (lb + 1) * 256)
            kbuf[k_rows, lanes] = (dks_s[lb][0] + dks_s[lb][1]).astype(BF)
            vbuf[k_rows, lanes] = (dvs_s[lb][0] + dvs_s[lb][1]).astype(BF)

        total = None
        for at in range(0, KV, KV // 2):
            rs = slice(at, at + KV // 2)
            both = jnp.concatenate([kbuf[rs, lanes], vbuf[rs, lanes]], axis=1)
            part = tn(both, hid[rs, :])
            total = part if total is None else total + part
        kv_grad = jnp.transpose(total)
        gatt[1, :, lanes] = kv_grad[:, 0:128].astype(BF)
        gatt[2, :, lanes] = kv_grad[:, 128:256].astype(BF)
        gatt[0, :, lanes] = tn(hloc[own, :], dq[:, lanes]).astype(BF)

        @pl.when(turn < 2)
        def _():
            for m in range(2):
                for xx in range(2):
                    att[0].core_copy(m, band * 2 + xx).start()

        @pl.when(turn == 0)
        def _():
            leave(4)

        @pl.when(turn == 2)
        def _():
            leave(5)

    def key_grad(rs):
        return (nt(kbuf[rs, :], watt[1]) + nt(vbuf[rs, :], watt[2])).astype(BF)

    for lb in range(3):
        pe[lb, 0:256, :] = key_grad(slice(TRK + lb * 256, TRK + (lb + 1) * 256))

    def trunk_grad(rs):
        tok[rs, :] = key_grad(rs)

    row_loop(TRK, 256, trunk_grad)

    for b in range(BRANCHES):
        hits = [is_parent(lb, b) for lb in range(3)]
        for piece in range(4):
            total = jnp.zeros((32, D), F)
            for lb in range(3):
                at = piece * 32
                total += jnp.where(hits[lb], pe[lb, at : at + 32, :].astype(F), 0.0)
            at = TRK + b * BLK + piece * 32
            tok[at : at + 32, :] = total.astype(BF)
    for lb in range(3):
        spec_g[lb * BLK : (lb + 1) * BLK, :] = pe[lb, BLK : 2 * BLK, :]

    leave(6)
    acc1[...] = nt(dq[...], watt[0])

    def own_sum(rs):
        extra = spec_g[pl.ds(pl.multiple_of(rs.start + off, 32), 32), :].astype(F)
        acc1[rs, :] += extra

    row_loop(ROWS, 32, own_sum, 5)
    leave(7)
    leave(8)

    wire.arrived(halo, s_halo, to_y, y == 0)

    @pl.when(y == 0)
    def _():
        acc1[ROWS - 64 : ROWS, :] += halo[...].astype(F)

    @pl.when(x == 0)
    def _():
        def body(rs):
            mine = tok[pl.ds(pl.multiple_of(ci * ROWS + rs.start, 32), 32), :].astype(F)
            acc1[rs, :] += mine + rx_g[1, rs, :].astype(F)

        row_loop(ROWS, 32, body)

    @pl.when(ci == 4)
    def _():
        def body(rs):
            mine = tok[pl.ds(pl.multiple_of(4 * ROWS + rs.start, 32), 32), :].astype(F)
            acc1[rs, :] += mine + rx_g[1, rs, :].astype(F)

        row_loop(256, 32, body)

    mgrad[6:8, :] = jnp.zeros((2, D), F)
    sums = [jnp.zeros((1, D), F), jnp.zeros((1, D), F)]
    for i in range(ROWS // 32):
        rs = slice(i * 32, i * 32 + 32)
        back, ds, db = norm_back(acc1[rs, :], tok_own[rs, :].astype(F), sa)
        in_grad[rs, :] += back
        sums = [sums[0] + ds, sums[1] + db]
    mgrad[0:1, :] = sums[0]
    mgrad[1:2, :] = sums[1]
    leave(9)

    for i in range(5):
        result(i).wait()
    wire.drain()
    for family in (ffn, *att):
        family.drain()
    tree_peers(lambda k, to, _: mod_1(k, to).wait_send())
    peers(lambda k, to, _: mod_2(k, to).wait_send())
    peers(
        lambda k, to, _: wire.copy(
            cond_parts.at[to], cond_all.at[fs], s_cond + k, {"fsdp": to}
        ).wait_send()
    )
    peers(
        lambda k, to, _: wire.copy(
            part_out.at[to], part_in.at[fs], s_part + k, {"fsdp": to}
        ).wait_send()
    )
    for g in range(6):
        peers(
            lambda k, to, _, g=g: wire.copy(
                groups[g][0], place(g, my_rows, y, x, c), s_z[g] + k, {"fsdp": to}
            ).wait_send()
        )


def layer_call(n, parents, cond_parts, w_mod, tokens, enc, cot, weights):
    vm = pl.BlockSpec(memory_space=pltpu.VMEM)
    hbm = pl.BlockSpec(memory_space=pl.ANY)
    sds = jax.ShapeDtypeStruct
    rows = w_mod.shape[0]
    return pl.pallas_call(
        functools.partial(layer_kernel, n),
        out_shape=(
            sds((ROWS, D), BF),
            sds((ROWS, D), F),
            sds((ENC // 4, D), F),
            sds((n, 8, D), F),
            sds(cond_parts.shape, F),
            sds((2, 4, 2, rows, 128), BF),
            sds((4, 2, rows, 256), BF),
        ),
        in_specs=[pl.BlockSpec(memory_space=pltpu.SMEM), vm, vm, hbm, hbm, vm] + [hbm] * 6,
        out_specs=(vm, vm, vm, hbm, hbm, hbm, hbm),
        scratch_shapes=[
            pltpu.VMEM((8, D, D), BF),
            pltpu.VMEM((D, FF), BF),
            pltpu.VMEM((D, FF), BF),
            pltpu.VMEM((8 * ROWS + 64, D), BF),
            pltpu.VMEM((ENC, D), BF),
            pltpu.VMEM((n, 8, D), F),
            pltpu.VMEM((n, 8, D), F),
            pltpu.VMEM((8, D), F),
            pltpu.VMEM((*cond_parts.shape,), F),
            pltpu.VMEM((ROWS, D), BF),
            pltpu.VMEM((8, D), F),
            pltpu.VMEM((KV, D), BF),
            pltpu.VMEM((LOC, D), BF),
            pltpu.VMEM((KV, D), BF),
            pltpu.VMEM((KV, D), BF),
            pltpu.VMEM((LOC, D), BF),
            pltpu.VMEM((8, ROWS, TRK), BF),
            pltpu.VMEM((8, LOC, 256), BF),
            pltpu.VMEM((ROWS, TRK), BF),
            pltpu.VMEM((LOC, 256), BF),
            pltpu.VMEM((ROWS, TRK), F),
            pltpu.VMEM((LOC, 256), F),
            pltpu.VMEM((2, LOC, 128), F),
            pltpu.VMEM((ROWS, D), BF),
            pltpu.VMEM((ROWS, D), F),
            pltpu.VMEM((ROWS, D), F),
            pltpu.VMEM((ROWS, D), BF),
            pltpu.VMEM((ROWS, D), BF),
            pltpu.VMEM((ENC, D), BF),
            pltpu.VMEM((ENC, D), BF),
            pltpu.VMEM((ROWS, D), BF),
            pltpu.VMEM((8, ROWS, ENC), BF),
            pltpu.VMEM((ROWS, D), BF),
            pltpu.VMEM((ROWS, D), BF),
            pltpu.VMEM((ROWS, D), BF),
            pltpu.VMEM((ROWS, D), F),
            pltpu.VMEM((ROWS, D), F),
            pltpu.VMEM((ROWS, D), BF),
            pltpu.VMEM((ROWS, D), BF),
            pltpu.VMEM((ROWS, D), BF),
            pltpu.VMEM((D, D), F),
            pltpu.VMEM((ROWS, D), F),
            pltpu.VMEM((8, D, D), BF),
            pltpu.VMEM((2, D, FF), BF),
            pltpu.VMEM((8, D, 256), BF),
            pltpu.VMEM((2, 6, D, 128), BF),
            pltpu.VMEM((2, n, 2, rows, 128), BF),
            pltpu.VMEM((2, 4, 2, rows, 128), BF),
            pltpu.VMEM((n, 2, rows, 256), BF),
            pltpu.VMEM((4, 2, rows, 256), BF),
            pltpu.VMEM((896, D), BF),
            pltpu.VMEM((2, ROWS, D), BF),
            pltpu.VMEM((64, D), BF),
            pltpu.VMEM((2, 128, D), BF),
            pltpu.VMEM((4, 128, D), BF),
            pltpu.VMEM((8, 8, D), F),
            pltpu.VMEM((n, 8, D), F),
            pltpu.SemaphoreType.DMA((16 * n + 160,)),
            pltpu.SemaphoreType.DMA((16 * n + 160,)),
            pltpu.SemaphoreType.DMA((9,)),
            pltpu.SemaphoreType.REGULAR((2,)),
        ],
        compiler_params=pltpu.CompilerParams(
            vmem_limit_bytes=VMEM_LIMIT, collective_id=0, has_side_effects=True
        ),
        name="layer",
    )(parents, cond_parts, w_mod, tokens, enc, cot, *weights)


def finish_kernel(
    n, rows, out, grad, enc, mod, cond, att, ffn, o_out, o_grad, o_enc, o_mod, qkv, so, cqkv, co, up, dn
):
    o_out[...] = out[...]
    o_grad[...] = grad[...]
    o_enc[...] = enc[...]
    for v in range(6):
        o_mod[:, v * D : (v + 1) * D] = lax.dot_general(
            cond[:, 0, 0:rows],
            mod[:, v, :],
            (((0,), (0,)), ((), ())),
            precision=lax.Precision.HIGHEST,
            preferred_element_type=F,
        )
    for q in range(4):
        up[:, q * 256 : (q + 1) * 256] = ffn[q, 0].astype(F)
        dn[:, q * 256 : (q + 1) * 256] = ffn[q, 1].astype(F)
        cols = slice((q % 2) * 128, (q % 2) * 128 + 128)
        for a, (stack, single) in enumerate(((qkv, so), (cqkv, co))):
            for m in range(2):
                value = att[a, q, m].astype(F)
                at = 2 * (q // 2) + m
                if at < 3:
                    stack[at, :, cols] = value
                else:
                    single[:, cols] = value


def finish_call(n, rows, *parts):
    vm = pl.BlockSpec(memory_space=pltpu.VMEM)
    sds = jax.ShapeDtypeStruct
    return pl.pallas_call(
        functools.partial(finish_kernel, n, rows),
        out_shape=(
            sds((ROWS, D), BF),
            sds((ROWS, D), F),
            sds((ENC // 4, D), F),
            sds((rows, 6 * D), F),
            sds((3, rows, 256), F),
            sds((rows, 256), F),
            sds((3, rows, 256), F),
            sds((rows, 256), F),
            sds((rows, 1024), F),
            sds((rows, 1024), F),
        ),
        in_specs=[vm] * 7,
        out_specs=(vm,) * 10,
        name="finish",
    )(*parts)


def timestep_code(timesteps, width):
    half = width // 2
    frequency = jnp.exp(-math.log(10000.0) * jnp.arange(half, dtype=F) / half)
    angles = timesteps.astype(F)[:, None] * frequency[None, :]
    return jnp.concatenate([jnp.sin(angles), jnp.cos(angles)], axis=-1)


def per_device(
    tokens,
    encoder_states,
    timesteps,
    parents,
    w_mod,
    w_self_qkv,
    w_self_out,
    w_cross_qkv,
    w_cross_out,
    w_up,
    w_down,
    cotangent,
):
    rows = w_mod.shape[0]
    condition = jax.nn.silu(timestep_code(timesteps, D)).astype(BF)
    n = lax.axis_size("fsdp")
    padded_cond = jnp.pad(condition.astype(F).reshape(n, 1, rows), ((0, 0), (0, 7), (0, max(128 - rows, 0))))
    parts = layer_call(
        n,
        parents,
        padded_cond,
        w_mod,
        tokens,
        encoder_states,
        cotangent[0],
        (w_self_qkv, w_self_out, w_cross_qkv, w_cross_out, w_up, w_down),
    )
    out, in_grad, enc_grad, grad_mod, *weights = finish_call(n, rows, *parts)
    return (out[None], in_grad[None], enc_grad[None], grad_mod, *weights)


def solution(mesh):
    rows = P("fsdp", ("ctx", "tp"), None)
    return jax.shard_map(
        per_device,
        mesh=mesh,
        in_specs=(
            rows,
            P("fsdp", "ctx", None),
            P("fsdp"),
            P("fsdp", None),
            P("fsdp", None),
            P(None, "fsdp", "tp"),
            P("fsdp", "tp"),
            P(None, "fsdp", "tp"),
            P("fsdp", "tp"),
            P("fsdp", "tp"),
            P("fsdp", "tp"),
            rows,
        ),
        out_specs=(
            rows,
            rows,
            P("fsdp", "ctx", None),
            P("fsdp", None),
            P(None, "fsdp", "tp"),
            P("fsdp", "tp"),
            P(None, "fsdp", "tp"),
            P("fsdp", "tp"),
            P("fsdp", "tp"),
            P("fsdp", "tp"),
        ),
        check_vma=False,
    )
```

```python
import functools
import math

import jax
import jax.numpy as jnp
from jax import lax
from jax.experimental import pallas as pl
from jax.experimental.pallas import tpu as pltpu
from jax.sharding import PartitionSpec as P

BF = jnp.bfloat16
F = jnp.float32
D = 512
FF = 2048
HD = 64
ROWS = 320
LOC = 384
BLK = 128
TRUNK = 8
BRANCHES = 4
TRK = TRUNK * BLK
SHARED = (TRUNK + BRANCHES) * BLK
SPEC = 2 * LOC
KV = TRK + SPEC
ENC = 512
EPS = 1e-05
NEG = -1e30
VMEM_LIMIT = 67043328


def nn(a, b):
    return lax.dot_general(a, b, (((1,), (0,)), ((), ())), preferred_element_type=F)


def nt(a, b):
    return lax.dot_general(a, b, (((1,), (1,)), ((), ())), preferred_element_type=F)


def tn(a, b):
    return lax.dot_general(a, b, (((0,), (0,)), ((), ())), preferred_element_type=F)


def normed(v):
    center = v - jnp.mean(v, axis=-1, keepdims=True)
    rstd = lax.rsqrt(jnp.mean(center * center, axis=-1, keepdims=True) + EPS)
    return center * rstd, rstd


def norm_back(grad, stream, scale):
    n, rstd = normed(stream)
    gn = grad * (1.0 + scale)
    back = rstd * (
        gn
        - jnp.mean(gn, axis=-1, keepdims=True)
        - n * jnp.mean(gn * n, axis=-1, keepdims=True)
    )
    return back, jnp.sum(grad * n, axis=0, keepdims=True), jnp.sum(grad, axis=0, keepdims=True)


def row_loop(total, step, body, unroll=1):
    if unroll == 0:
        for i in range(total // step):
            body(pl.ds(i * step, step))
        return

    @pl.loop(0, total // (step * unroll))
    def _(i):
        for j in range(unroll):
            body(pl.ds(pl.multiple_of((i * unroll + j) * step, step), step))


def half_lanes(shape, half):
    lane = lax.broadcasted_iota(jnp.int32, shape, len(shape) - 1)
    return (lane // HD) == half


def keep(value, half):
    return jnp.where(half_lanes(value.shape, half), value, jnp.zeros_like(value))


MESH = pl.DeviceIdType.MESH


class Wire:
    def __init__(self, send, recv):
        self.send, self.recv, self.used, self.sent = send, recv, 0, []

    def slot(self, count=1):
        self.used += count
        return self.used - count

    def copy(self, src, dst, at, to):
        return pltpu.make_async_remote_copy(
            src_ref=src,
            dst_ref=dst,
            send_sem=self.send.at[at],
            recv_sem=self.recv.at[at],
            device_id=to,
            device_id_type=MESH,
        )

    def push(self, dst, at, to, when=None, src=None):
        src = src or dst
        if when is None:
            self.copy(src(), dst(), at, to).start()
        else:

            @pl.when(when)
            def _():
                self.copy(src(), dst(), at, to).start()

        self.sent.append((src, dst, at, to, when))

    def arrived(self, dst, at, to, when=None):
        if when is None:
            self.copy(dst, dst, at, to).wait_recv()
        else:

            @pl.when(when)
            def _():
                self.copy(dst, dst, at, to).wait_recv()

    def drain(self):
        for src, dst, at, to, when in self.sent:
            if when is None:
                self.copy(src(), dst(), at, to).wait_send()
            else:

                @pl.when(when)
                def _(src=src, dst=dst, at=at, to=to):
                    self.copy(src(), dst(), at, to).wait_send()

        self.sent = []


def layer_kernel(
    n,
    parents_ref,
    cond_parts,
    w_mod,
    tok_in,
    enc_in,
    cot,
    w_sqkv,
    w_so,
    w_cqkv,
    w_co,
    w_up,
    w_dn,
    out_ref,
    in_grad,
    enc_out,
    mod_out,
    cond_out,
    att_out,
    ffn_out,
    watt,
    wup,
    wdn,
    tok,
    enc,
    part_out,
    part_in,
    mod,
    cond_all,
    tok_own,
    mgrad,
    hid,
    hloc,
    kbuf,
    vbuf,
    qbuf,
    pt,
    ps,
    bias_t,
    bias_s,
    st,
    ss,
    spec_o,
    mixa,
    stream_b,
    stream_c,
    hid_b,
    hid_c,
    kenc,
    venc,
    qb,
    pe,
    mixb,
    b0,
    b1,
    acc0,
    acc1,
    gbf,
    mgr,
    dq,
    wk_acc,
    wv_acc,
    gatt,
    gffn,
    rc_att,
    rx_att,
    zr_att,
    rg_att,
    zl_att,
    zs_att,
    zr_ffn,
    rg_ffn,
    rc_g,
    rx_g,
    halo,
    rc_e,
    rx_e,
    mod1,
    mod2,
    send,
    recv,
    local,
    ready,
):
    t0, t1 = st.at[:, 0:D], st.at[:, D : 2 * D]
    egrad = enc
    fs = lax.axis_index("fsdp")
    cx = lax.axis_index("ctx")
    y = lax.axis_index("tp")
    x, c = cx // 2, lax.rem(cx, 2)
    ci = cx * 2 + y
    odd = y
    off = pl.multiple_of(odd * 64, 64)
    own = pl.ds(off, ROWS)
    base = (ci * 5) // 2
    rows = w_mod.shape[0]
    to_y = {"tp": 1 - y}
    to_c = {"ctx": 2 * x + 1 - c}
    to_x = {"ctx": 2 * (1 - x) + c}
    wire = Wire(send, recv)

    my_rows = pl.ds(pl.multiple_of(fs * rows, rows), rows)

    def att_cols(yy, cc):
        return pl.ds(pl.multiple_of(yy * 256 + cc * 128, 128), 128)

    def ffn_cols(yy, xx, cc):
        return pl.ds(pl.multiple_of(yy * 1024 + xx * 512 + cc * 256, 256), 256)

    half = pl.ds(pl.multiple_of(c * 128, 128), 128)
    quarter = pl.ds(pl.multiple_of(cx * 256, 256), 256)
    groups = (
        (w_sqkv.at[:, :, half], watt, slice(0, 3), 0),
        (w_so.at[:, half], watt, 3, 0),
        (w_cqkv.at[:, :, half], watt, slice(4, 7), 0),
        (w_co.at[:, half], watt, 7, 0),
        (w_up.at[:, quarter], wup, None, 1),
        (w_dn.at[:, quarter], wdn, None, 1),
    )

    def place(g, row_at, yy, xx, cc):
        _, buf, index, wide = groups[g]
        if wide:
            return buf.at[row_at, ffn_cols(yy, xx, cc)]
        return buf.at[index, row_at, att_cols(yy, cc)]

    def chunk(i):
        return tok.at[pl.ds(pl.multiple_of(i * ROWS, ROWS), ROWS), :]

    def enc_part(i):
        return enc.at[pl.ds(pl.multiple_of(i * 128, 128), 128), :]

    all_rows = pl.ds(0, D)

    local_copies = [
        pltpu.make_async_copy(tok_in.at[0], chunk(ci), local.at[0]),
        pltpu.make_async_copy(enc_in.at[0], enc_part(cx), local.at[1]),
    ] + [
        pltpu.make_async_copy(groups[g][0], place(g, my_rows, y, x, c), local.at[2 + g])
        for g in range(6)
    ]
    local_copies.append(pltpu.make_async_copy(tok_in.at[0], tok_own, local.at[8]))
    for copy in local_copies:
        copy.start()

    barrier = pltpu.get_barrier_semaphore()

    @pl.loop(1, n)
    def _(k):
        pl.semaphore_signal(
            barrier, inc=1, device_id={"fsdp": lax.rem(fs + k, n)}, device_id_type=MESH
        )

    @pl.loop(1, 8)
    def _(k):
        other = lax.rem(ci + k, 8)
        pl.semaphore_signal(
            barrier,
            inc=1,
            device_id={"ctx": other // 2, "tp": lax.rem(other, 2)},
            device_id_type=MESH,
        )

    pl.semaphore_wait(barrier, n - 1 + 7)

    def peers(make):
        @pl.loop(1, n)
        def _(k):
            make(k, lax.rem(fs + k, n), lax.rem(fs + n - k, n))

    s_cond = wire.slot(n)
    s_part = wire.slot(n)
    s_z = [wire.slot(n) for _ in range(6)]
    s_y = [wire.slot() for _ in range(6)]
    s_c0 = [wire.slot() for _ in range(6)]
    s_c1 = [wire.slot() for _ in range(6)]
    s_x0 = [wire.slot() for _ in range(6)]
    s_x1 = [wire.slot() for _ in range(6)]
    s_c2 = [wire.slot() for _ in range(6)]
    s_c3 = [wire.slot() for _ in range(6)]
    s_ty, s_tx, s_txy, s_tc0, s_tc1, s_tc2, s_tc3, s_ty2 = (
        wire.slot() for _ in range(8)
    )
    s_ex, s_ec0, s_ec1 = (wire.slot() for _ in range(3))

    peers(
        lambda k, to, _: wire.copy(
            cond_parts.at[to], cond_all.at[fs], s_cond + k, {"fsdp": to}
        ).start()
    )
    left = x == 0

    def tail_rows(i):
        return tok.at[pl.ds(pl.multiple_of(i * ROWS + ROWS - 64, 64), 64), :]

    wire.push(
        lambda: chunk(ci), s_ty, to_y, jnp.logical_or(left, ci == 4), lambda: tok_in.at[0]
    )
    wire.push(
        lambda: tail_rows(ci), s_ty2, to_y, ci == 6, lambda: tok_in.at[0, ROWS - 64 : ROWS, :]
    )
    wire.push(lambda: chunk(ci), s_tx, to_x, x == 0, lambda: tok_in.at[0])
    wire.push(
        lambda: chunk(ci), s_tc0, to_c, jnp.logical_or(left, ci == 4), lambda: tok_in.at[0]
    )

    def z_start(g):
        peers(
            lambda k, to, _: wire.copy(
                groups[g][0], place(g, my_rows, y, x, c), s_z[g] + k, {"fsdp": to}
            ).start()
        )

    z_start(0)

    def mask_trunk(rs):
        row = lax.broadcasted_iota(jnp.int32, (32, TRK), 0) + rs.start + ci * ROWS
        col = lax.broadcasted_iota(jnp.int32, (32, TRK), 1)
        bias_t[rs, :] = jnp.where(col <= row, 0.0, NEG).astype(BF)

    row_loop(ROWS, 32, mask_trunk)
    for lb in range(3):
        blk = base + lb
        row = lax.broadcasted_iota(jnp.int32, (BLK, 2 * BLK), 0)
        col = lax.broadcasted_iota(jnp.int32, (BLK, 2 * BLK), 1)
        par_ok = jnp.logical_and(col < BLK, blk >= TRUNK + BRANCHES)
        self_ok = jnp.logical_and(
            jnp.logical_and(col >= BLK, col - BLK <= row), blk >= TRUNK
        )
        bias_s[lb * BLK : (lb + 1) * BLK, :] = jnp.where(
            jnp.logical_or(par_ok, self_ok), 0.0, NEG
        ).astype(BF)

    cond_all[fs] = cond_parts[fs]
    peers(lambda k, _, src: wire.arrived(cond_all.at[src], s_cond + k, {"fsdp": src}))
    for v in range(6):
        part_out[:, v, :] = nn(
            cond_all[:, 0, 0:rows].astype(BF), w_mod[:, v * D : (v + 1) * D]
        )
    part_out[:, 6:8, :] = jnp.zeros((n, 2, D), F)
    peers(
        lambda k, to, _: wire.copy(
            part_out.at[to], part_in.at[fs], s_part + k, {"fsdp": to}
        ).start()
    )
    part_in[fs] = part_out[fs]

    def z_done(g):
        local_copies[2 + g].wait()
        peers(
            lambda k, _, src: wire.arrived(
                place(g, pl.ds(pl.multiple_of(src * rows, rows), rows), y, x, c),
                s_z[g] + k,
                {"fsdp": src},
            )
        )
        slab = lambda: place(g, all_rows, y, x, c)
        wire.push(slab, s_y[g], to_y)
        if groups[g][3]:
            wire.push(slab, s_x0[g], to_x)
        wire.push(slab, s_c0[g], to_c)

    def y_done(g):
        slab = lambda: place(g, all_rows, 1 - y, x, c)
        wire.arrived(slab(), s_y[g], to_y)
        if groups[g][3]:
            wire.push(slab, s_x1[g], to_x)
        wire.push(slab, s_c1[g], to_c)

    def x_done(g, part):
        s_in, s_out = ((s_x0[g], s_c2[g]), (s_x1[g], s_c3[g]))[part]
        slab = lambda: place(g, all_rows, 1 - y if part else y, 1 - x, c)
        wire.arrived(slab(), s_in, to_x)
        wire.push(slab, s_out, to_c)

    def c_part(g, part):
        yy, xx, at = (
            (y, x, s_c0[g]),
            (1 - y, x, s_c1[g]),
            (y, 1 - x, s_c2[g]),
            (1 - y, 1 - x, s_c3[g]),
        )[part]
        wire.arrived(place(g, all_rows, yy, xx, 1 - c), at, to_c)

    def c_done(g):
        wire.arrived(place(g, all_rows, y, x, 1 - c), s_c0[g], to_c)
        wire.arrived(place(g, all_rows, 1 - y, x, 1 - c), s_c1[g], to_c)
    local_copies[0].wait()
    local_copies[1].wait()
    ciy = 4 * x + 2 * c + 1 - y
    cic = 4 * x + 2 * (1 - c) + y
    ciyc = 4 * x + 2 * (1 - c) + 1 - y
    low, lowy, lowc, lowyc = 2 * c + y, 2 * c + 1 - y, 2 * (1 - c) + y, 2 * (1 - c) + 1 - y
    right = x == 1
    local_copies[8].wait()
    wire.arrived(chunk(ciy), s_ty, to_y, jnp.logical_or(left, ci == 5))
    wire.push(lambda: chunk(ciy), s_txy, to_x, left)
    wire.push(lambda: chunk(ciy), s_tc1, to_c, jnp.logical_or(left, ci == 5))
    wire.arrived(tail_rows(ciy), s_ty2, to_y, ci == 7)

    @pl.when(jnp.logical_and(right, y == 0))
    def _():
        tok[pl.ds(pl.multiple_of((ci + 1) * ROWS, 64), 64), :] = jnp.zeros((64, D), BF)

    z_start(1)
    z_start(4)
    wire.arrived(chunk(low), s_tx, to_x, right)
    wire.push(lambda: chunk(low), s_tc2, to_c, right)
    z_done(0)
    z_start(2)
    wire.arrived(chunk(lowy), s_txy, to_x, right)
    wire.push(lambda: chunk(lowy), s_tc3, to_c, right)
    wire.push(lambda: enc_part(cx), s_ex, to_x, None, lambda: enc_in.at[0])
    wire.push(lambda: enc_part(cx), s_ec0, to_c, None, lambda: enc_in.at[0])
    y_done(0)
    z_done(1)
    z_done(4)
    z_start(5)
    z_start(3)

    peers(lambda k, _, src: wire.arrived(part_in.at[src], s_part + k, {"fsdp": src}))
    mod[...] = jnp.sum(part_in[...], axis=0)
    sa, ba = mod[0:1, :], mod[1:2, :]
    sb, bb = mod[2:3, :], mod[3:4, :]
    sf, bf_ = mod[4:5, :], mod[5:6, :]

    wire.arrived(chunk(cic), s_tc0, to_c, jnp.logical_or(left, ci == 6))
    wire.arrived(chunk(ciyc), s_tc1, to_c, jnp.logical_or(left, ci == 7))
    wire.arrived(chunk(lowc), s_tc2, to_c, right)
    wire.arrived(chunk(lowyc), s_tc3, to_c, right)

    def enc_done(step):
        if step == 0:
            wire.arrived(enc_part(2 * (1 - x) + c), s_ex, to_x)
            wire.push(lambda: enc_part(2 * (1 - x) + c), s_ec1, to_c)
        else:
            wire.arrived(enc_part(2 * x + 1 - c), s_ec0, to_c)
            wire.arrived(enc_part(2 * (1 - x) + 1 - c), s_ec1, to_c)

    tok_tb = tok
    tok_loc = tok.at[pl.ds(pl.multiple_of(ci * ROWS - off, 64), LOC), :]

    def relay(step):
        if step == 1:
            y_done(1)
            y_done(4)
            enc_done(0)
        if step == 2:
            z_done(5)
            z_done(3)
        if step == 4:
            c_done(1)
        if step == 5:
            y_done(5)
            y_done(3)
            c_done(3)
        if step == 6:
            x_done(4, 0)
            x_done(5, 0)
        if step == 7:
            y_done(2)
            enc_done(1)
            c_done(2)

    spec_g = qbuf

    def is_parent(lb, branch):
        parent = jnp.full((32, D), parents_ref[0, base + lb], jnp.int32)
        leaf = jnp.full((32, D), base + lb, jnp.int32) >= TRUNK + BRANCHES
        return jnp.logical_and(leaf, parent == TRUNK + branch)

    to_xy = {"ctx": 2 * (1 - x) + c, "tp": 1 - y}
    s_rcg, s_rcg4, s_rcg5, s_halo = (wire.slot() for _ in range(4))
    s_rxy = [wire.slot() for _ in range(2)]
    s_rxx = [wire.slot() for _ in range(2)]
    s_rce = [wire.slot(), wire.slot()]
    s_rxe = [wire.slot() for _ in range(3)]
    s_m1 = wire.slot(8)
    s_m2 = wire.slot(n)
    quad = ((to_y, x, 1 - y), (to_x, 1 - x, y), (to_xy, 1 - x, 1 - y))

    def add_rows(target, terms, total, step=64):
        def body(rs):
            value = terms[0][rs, :].astype(F)
            for term in terms[1:]:
                value += term[rs, :].astype(F)
            target[rs, :] = value.astype(BF)

        row_loop(total, step, body)

    def strip(buf, at):
        return buf.at[:, at * 256 : (at + 1) * 256]

    class Family:
        def __init__(self, unit, core_box, box, landing, held, shape_rows):
            self.unit, self.core_box, self.box = unit, core_box, box
            self.landing, self.held, self.tall = landing, held, shape_rows
            self.s_core = [wire.slot(4) for _ in range(2)]
            self.s_one = [[wire.slot() for _ in range(2)] for _ in range(2)]
            self.s_two = [wire.slot() for _ in range(2)]
            self.s_z = [wire.slot(n) for _ in range(2)]
            self.s_g = wire.slot(4)

        def core_copy(self, m, t):
            return wire.copy(
                self.unit(m, t // 2, lax.rem(t, 2), 1 - c),
                self.core_box(m, t),
                self.s_core[m] + t,
                to_c,
            )

        def core_send(self):
            for m in range(2):
                for t in range(4):
                    self.core_copy(m, t).start()

        def first_send(self):
            for m in range(2):
                for t in range(4):
                    wire.arrived(self.core_box(m, t), self.s_core[m] + t, to_c)
                    mine = self.unit(m, t // 2, t % 2, c)
                    add_rows(mine, (mine, self.core_box(m, t)), D)
            self.one_send()

        def piece(self, m, yy, xx):
            return self.unit(m, yy, xx, c)

        def one_send(self):
            for j in range(2):
                wire.push(
                    lambda j=j: self.box(j),
                    self.s_one[0][j],
                    to_x,
                    None,
                    lambda j=j: self.piece(0, j, 1 - x),
                )
                wire.push(
                    lambda j=j: self.box(2 + j),
                    self.s_one[1][j],
                    to_y,
                    None,
                    lambda j=j: self.piece(1, 1 - y, j),
                )

        def second_send(self):
            for j in range(2):
                wire.arrived(self.box(j), self.s_one[0][j], to_x)
                mine = self.piece(0, j, x)
                add_rows(mine, (mine, self.box(j)), self.tall, min(64, self.tall))
            wire.push(
                lambda: self.box(4),
                self.s_two[0],
                to_y,
                None,
                lambda: self.piece(0, 1 - y, x),
            )
            for j in range(2):
                wire.arrived(self.box(2 + j), self.s_one[1][j], to_y)
                mine = self.piece(1, y, j)
                add_rows(mine, (mine, self.box(2 + j)), self.tall, min(64, self.tall))
            wire.push(
                lambda: self.box(5),
                self.s_two[1],
                to_x,
                None,
                lambda: self.piece(1, y, 1 - x),
            )

        def z_copy(self, m, k, to):
            part = pl.ds(pl.multiple_of(to * rows, rows), rows)
            return wire.copy(
                self.unit(m, y, x, c).at[part, :],
                self.landing.at[fs, m],
                self.s_z[m] + k,
                {"fsdp": to},
            )

        def tree_send(self):
            for m, target in ((0, to_y), (1, to_x)):
                wire.arrived(self.box(4 + m), self.s_two[m], target)
                mine = self.unit(m, y, x, c)
                add_rows(mine, (mine, self.box(4 + m)), D)
                peers(lambda k, to, _, m=m: self.z_copy(m, k, to).start())
                self.landing[fs, m] = self.unit(m, y, x, c)[my_rows, :]

        def g_copy(self, i):
            target, at = ((to_x, cx), (to_c, cx), (to_c, 2 * (1 - x) + c))[i]
            return wire.copy(self.held.at[at], self.held.at[at], self.s_g + i, target)

        def copy_send(self):
            for m in range(2):
                peers(
                    lambda k, _, src, m=m: wire.arrived(
                        self.landing.at[src, m], self.s_z[m] + k, {"fsdp": src}
                    )
                )
            self.held[cx] = jnp.sum(self.landing[...].astype(F), axis=0).astype(BF)
            self.g_copy(0).start()
            self.g_copy(1).start()

        def relay_copy(self):
            wire.arrived(self.held.at[2 * (1 - x) + c], self.s_g, to_x)
            self.g_copy(2).start()

        def collect(self):
            wire.arrived(self.held.at[2 * x + 1 - c], self.s_g + 1, to_c)
            wire.arrived(self.held.at[2 * (1 - x) + 1 - c], self.s_g + 2, to_c)

        def drain(self):
            for m in range(2):
                for t in range(4):
                    self.core_copy(m, t).wait_send()
                peers(lambda k, to, _, m=m: self.z_copy(m, k, to).wait_send())
            for i in range(3):
                self.g_copy(i).wait_send()

    class TreeFirst(Family):
        def piece(self, m, yy, xx):
            return zs_att.at[yy, 2 * xx + m]

        def row_copy(self, yy, k, to):
            part = pl.ds(pl.multiple_of(to * rows, rows), rows)
            return wire.copy(
                gatt.at[4:8, part, att_cols(yy, c)],
                zl_att.at[fs, yy],
                self.s_z[yy] + k,
                {"fsdp": to},
            )

        def one_send(self):
            for yy in range(2):
                peers(lambda k, to, _, yy=yy: self.row_copy(yy, k, to).start())
                zl_att[fs, yy] = gatt[4:8, my_rows, att_cols(yy, c)]

        def sum_trees(self):
            for yy in range(2):
                peers(
                    lambda k, _, src, yy=yy: wire.arrived(
                        zl_att.at[src, yy], self.s_z[yy] + k, {"fsdp": src}
                    )
                )
            zs_att[...] = jnp.sum(zl_att[...].astype(F), axis=0).astype(BF)
            Family.one_send(self)

        def copy_send(self):
            for m, target in ((0, to_y), (1, to_x)):
                wire.arrived(self.box(4 + m), self.s_two[m], target)
                total = self.piece(m, y, x)[...].astype(F) + self.box(4 + m)[...].astype(F)
                self.held[cx, m] = total.astype(BF)
            self.g_copy(0).start()
            self.g_copy(1).start()

        def drain(self):
            for m in range(2):
                for t in range(4):
                    self.core_copy(m, t).wait_send()
                peers(lambda k, to, _, m=m: self.row_copy(m, k, to).wait_send())
            for i in range(3):
                self.g_copy(i).wait_send()

    ffn = Family(
        lambda m, yy, xx, cc: gffn.at[m, :, ffn_cols(yy, xx, cc)],
        lambda m, t: rc_att.at[m * 4 + t],
        lambda i: strip(wdn, i),
        zr_ffn,
        rg_ffn,
        D,
    )

    def attention_family(a):
        kind = (Family, TreeFirst)[a]
        tall = (D, rows)[a]
        return kind(
            lambda m, yy, xx, cc: gatt.at[4 * a + 2 * xx + m, :, att_cols(yy, cc)],
            lambda m, t: rc_att.at[
                4 * a + 2 * m + t // 2, :, pl.ds(pl.multiple_of(lax.rem(t, 2) * 128, 128), 128)
            ],
            lambda i: rx_att.at[a, i, 0:tall],
            zr_att.at[a],
            rg_att.at[a],
            tall,
        )

    att = (attention_family(0), attention_family(1))

    def ffn_free():
        wire.drain()
        for target in (to_y, to_x):
            pl.semaphore_signal(ready.at[0], inc=1, device_id=target, device_id_type=MESH)

    def ffn_chip_send():
        pl.semaphore_wait(ready.at[0], 2)
        ffn.first_send()
        pl.semaphore_signal(ready.at[1], inc=1, device_id=to_c, device_id_type=MESH)

    results = (
        (rg_ffn, ffn_out),
        (rg_att.at[0], att_out.at[0]),
        (rg_att.at[1], att_out.at[1]),
        (mod2, mod_out),
        (cond_all, cond_out),
    )

    def result(i):
        return pltpu.make_async_copy(results[i][0], results[i][1], local.at[i])

    def ffn_finish():
        ffn.collect()
        result(0).start()

    def att_finish(a):
        att[a].collect()
        result(1 + a).start()

    def enc_core_send():
        for xx in range(2):
            wire.push(
                lambda xx=xx: rc_e.at[xx],
                s_rce[xx],
                to_c,
                None,
                lambda xx=xx: egrad.at[pl.ds(pl.multiple_of((2 * xx + 1 - c) * 128, 128), 128), :],
            )

    def enc_rows(xx):
        return egrad.at[pl.ds(pl.multiple_of((2 * xx + c) * 128, 128), 128), :]

    def enc_chip_send():
        for xx in range(2):
            wire.arrived(rc_e.at[xx], s_rce[xx], to_c)
            add_rows(enc_rows(xx), (enc_rows(xx), rc_e.at[xx]), 128)
        for r, (target, xx, _) in enumerate(quad):
            wire.push(
                lambda: rx_e.at[2 * x + y], s_rxe[r], target, None, lambda xx=xx: enc_rows(xx)
            )
        rx_e[2 * x + y] = enc_rows(x)[...]

    def enc_finish():
        for r, (target, xx, yy) in enumerate(quad):
            wire.arrived(rx_e.at[2 * xx + yy], s_rxe[r], target)
        enc_out[...] = jnp.sum(rx_e[...].astype(F), axis=0)

    def shared_core_send():
        to_core = pl.ds(pl.multiple_of(640 * (1 - c), 640), 640)
        wire.push(lambda: rc_g.at[0:640], s_rcg, to_c, None, lambda: tok.at[to_core, :])
        wire.push(
            lambda: rc_g.at[640:896],
            s_rcg4,
            to_c,
            jnp.logical_and(x == 1, c == 1),
            lambda: tok.at[1280:1536, :],
        )
        wire.push(lambda: halo, s_halo, to_y, y == 1, lambda: spec_g.at[0:64, :])

    def part_rows(yy, p):
        return tok.at[pl.ds(pl.multiple_of((2 * c + yy) * ROWS + p * 160, 32), 160), :]

    def core_rows(yy, p):
        return rc_g.at[pl.ds(pl.multiple_of(yy * ROWS + p * 160, 32), 160), :]

    def shared_y_send():
        wire.arrived(rc_g.at[0:640], s_rcg, to_c)
        for p in range(2):
            mine = part_rows(1 - y, p)
            add_rows(mine, (mine, core_rows(1 - y, p)), 160, 32)
            wire.push(
                lambda p=p: rx_g.at[0, p * 160 : p * 160 + 160],
                s_rxy[p],
                to_y,
                None,
                lambda p=p: part_rows(1 - y, p),
            )
        last = jnp.logical_and(x == 1, c == 0)

        @pl.when(last)
        def _():
            wire.arrived(rc_g.at[640:896], s_rcg4, to_c)
            four = tok.at[1280:1536, :]
            add_rows(four, (four, rc_g.at[640:896]), 256)

        wire.push(
            lambda: rx_g.at[1, 0:256],
            s_rcg5,
            to_y,
            jnp.logical_and(last, y == 1),
            lambda: tok.at[1280:1536, :],
        )
        for p in range(2):
            mine = part_rows(y, p)
            add_rows(mine, (mine, core_rows(y, p)), 160, 32)

    def shared_x_send():
        for p in range(2):
            wire.arrived(rx_g.at[0, p * 160 : p * 160 + 160], s_rxy[p], to_y)
            mine = part_rows(y, p)
            add_rows(mine, (mine, rx_g.at[0, p * 160 : p * 160 + 160]), 160, 32)
            wire.push(
                lambda p=p: rx_g.at[1, p * 160 : p * 160 + 160],
                s_rxx[p],
                to_x,
                x == 1,
                lambda p=p: part_rows(y, p),
            )

    def shared_arrived():
        for p in range(2):
            wire.arrived(rx_g.at[1, p * 160 : p * 160 + 160], s_rxx[p], to_x, x == 0)
        wire.arrived(rx_g.at[1, 0:256], s_rcg5, to_y, ci == 4)

    def tree_peers(make):
        @pl.loop(1, 8)
        def _(k):
            make(k, lax.rem(ci + k, 8), lax.rem(ci + 8 - k, 8))

    def device_of(i):
        return {"ctx": i // 2, "tp": lax.rem(i, 2)}

    def mod_1(k, to):
        return wire.copy(mgrad, mod1.at[ci], s_m1 + k, device_of(to))

    def mod_2(k, to):
        return wire.copy(mod2.at[fs], mod2.at[fs], s_m2 + k, {"fsdp": to})

    def mod_tree_send():
        tree_peers(lambda k, to, _: mod_1(k, to).start())
        mod1[ci] = mgrad[...]

    def mod_all_send():
        tree_peers(lambda k, _, src: wire.arrived(mod1.at[src], s_m1 + k, device_of(src)))
        mod2[fs] = jnp.sum(mod1[...], axis=0)
        peers(lambda k, to, _: mod_2(k, to).start())

    def mod_finish():
        peers(lambda k, _, src: wire.arrived(mod2.at[src], s_m2 + k, {"fsdp": src}))
        result(3).start()
        result(4).start()

    def leave(step):
        if step == 0:
            ffn_free()
        if step == 1:
            ffn_chip_send()
        if step == 2:
            pl.semaphore_wait(ready.at[1], 1)
            att[1].core_send()
            enc_core_send()
        if step == 3:
            att[1].first_send()
            enc_chip_send()
        if step == 4:
            ffn.second_send()
        if step == 5:
            ffn.tree_send()
        if step == 6:
            shared_core_send()
        if step == 7:
            shared_y_send()
            att[0].first_send()
            att[1].sum_trees()
            enc_finish()
            shared_x_send()
        if step == 8:
            att[1].second_send()
            att[0].second_send()
            ffn.copy_send()
            shared_arrived()
        if step == 9:
            mod_tree_send()
            att[0].tree_send()
            att[1].copy_send()
            ffn.relay_copy()
            mod_all_send()
            att[0].copy_send()
            att[1].relay_copy()
            ffn_finish()
            mod_finish()
            att[0].relay_copy()
            att_finish(1)
            att_finish(0)

    def hidden(x):
        n, _ = normed(x.astype(F))
        return (n * (1.0 + sa) + ba).astype(BF)

    def hid_trunk(rs):
        hid[rs, :] = hidden(tok_tb[rs, :])

    row_loop(TRK, 32, hid_trunk, 8)

    def hid_loc(rs):
        hloc[rs, :] = hidden(tok_loc[rs, :])

    row_loop(LOC, 32, hid_loc, 6)
    for lb in range(3):
        picks = [is_parent(lb, b) for b in range(1, BRANCHES)]
        for piece in range(4):
            r = piece * 32
            picked = tok_tb[TRK + r : TRK + r + 32, :].astype(F)
            for b in range(1, BRANCHES):
                at = TRK + b * BLK + r
                picked = jnp.where(picks[b - 1], tok_tb[at : at + 32, :].astype(F), picked)
            at = TRK + lb * 256 + r
            hid[at : at + 32, :] = hidden(picked)
        hid[TRK + lb * 256 + BLK : TRK + lb * 256 + 2 * BLK, :] = hloc[
            lb * BLK : (lb + 1) * BLK, :
        ]

    def project(rs):
        kbuf[rs, :] = nn(hid[rs, :], watt[1]).astype(BF)
        vbuf[rs, :] = nn(hid[rs, :], watt[2]).astype(BF)

    z_done(2)
    c_done(0)
    row_loop(KV, 256, project)
    qbuf[...] = (nn(hloc[...], watt[0]) * 0.125).astype(BF)

    linv_a, linv_b = wk_acc.at[0:ROWS, :], wv_acc.at[0:ROWS, :]

    def with_ones(values, half):
        return jnp.where(half_lanes(values.shape, half), values, jnp.ones_like(values))

    def finish_heads(o0, o1, mixed, linv, lanes):
        inv0, inv1 = 1.0 / pltpu.roll(o0, HD, 1), 1.0 / pltpu.roll(o1, HD, 1)
        first = half_lanes(o0.shape, 0)
        mixed[:, lanes] = jnp.where(first, o0 * inv0, o1 * inv1).astype(BF)
        linv[:, lanes] = jnp.where(first, inv0, inv1)

    @pl.loop(0, 4)
    def _(hp):
        for step in (1, 2):

            @pl.when(hp == step)
            def _(step=step):
                relay(step)

        lanes = pl.ds(pl.multiple_of(hp * 128, 128), 128)
        kt = kbuf[0:TRK, lanes]
        vt = vbuf[0:TRK, lanes]
        outs = []
        for half in range(2):
            h = hp * 2 + half
            st[...] = nt(keep(qbuf[own, lanes], half), kt) + bias_t[...].astype(F)
            for lb in range(3):
                r = slice(lb * BLK, (lb + 1) * BLK)
                ks = kbuf[TRK + lb * 256 : TRK + (lb + 1) * 256, lanes]
                ss[r, :] = nt(keep(qbuf[r, lanes], half), ks) + bias_s[r, :].astype(F)
            for i in range(ROWS // 32):
                rs = slice(i * 32, i * 32 + 32)
                ro = pl.ds(pl.multiple_of(i * 32 + off, 32), 32)
                a, b = st[rs, :], ss[ro, :]
                top = jnp.maximum(
                    jnp.max(a, axis=-1, keepdims=True), jnp.max(b, axis=-1, keepdims=True)
                )
                pt[h, rs, :] = jnp.exp(a - top).astype(BF)
                ps[h, ro, :] = jnp.exp(b - top).astype(BF)
            for lb in range(3):
                r = slice(lb * BLK, (lb + 1) * BLK)
                vs = vbuf[TRK + lb * 256 : TRK + (lb + 1) * 256, lanes]
                spec_o[half, r, :] = nn(ps[h, r, :], with_ones(vs, half))
            outs.append(nn(pt[h], with_ones(vt, half)) + spec_o[half, own, :])
        finish_heads(outs[0], outs[1], mixa, linv_a, lanes)

    relay(4)
    t0[...] = nt(mixa[...], watt[3])

    def after_self(rs):
        sbv = tok_own[rs, :].astype(F) + t0[rs, :]
        stream_b[rs, :] = sbv
        n, _ = normed(sbv)
        hid_b[rs, :] = (n * (1.0 + sb) + bb).astype(BF)

    row_loop(ROWS, 32, after_self, 0)

    relay(7)
    kenc[...] = nn(enc[...], watt[5]).astype(BF)
    venc[...] = nn(enc[...], watt[6]).astype(BF)
    qb[...] = (nn(hid_b[...], watt[4]) * 0.125).astype(BF)

    @pl.loop(0, 4)
    def _(hp):
        lanes = pl.ds(pl.multiple_of(hp * 128, 128), 128)
        kt = kenc[:, lanes]
        vt = venc[:, lanes]
        outs = []
        for half in range(2):
            h = hp * 2 + half
            t0[...] = nt(keep(qb[:, lanes], half), kt)
            for i in range(ROWS // 32):
                rs = slice(i * 32, i * 32 + 32)
                a = t0[rs, :]
                pe[h, rs, :] = jnp.exp(a - jnp.max(a, axis=-1, keepdims=True)).astype(BF)
            outs.append(nn(pe[h], with_ones(vt, half)))
        finish_heads(outs[0], outs[1], mixb, linv_b, lanes)

    relay(5)
    t0[...] = nt(mixb[...], watt[7])

    def after_cross(rs):
        scv = stream_b[rs, :] + t0[rs, :]
        stream_c[rs, :] = scv
        n, _ = normed(scv)
        hid_c[rs, :] = (n * (1.0 + sf) + bf_).astype(BF)

    row_loop(ROWS, 32, after_cross, 0)

    relay(6)
    acc0[...] = jnp.zeros_like(acc0)
    acc1[...] = jnp.zeros_like(acc1)

    def flip(v, by):
        return v + by - 2 * v * by

    @pl.loop(0, 4)
    def _(ft):
        @pl.when(ft == 2)
        def _():
            x_done(4, 1)
            x_done(5, 1)

        for part in range(4):

            @pl.when(ft == part)
            def _(part=part):
                c_part(4, part)
                c_part(5, part)

        tile = flip(y, lax.rem(ft, 2)) * 2 + flip(x, ft // 2)
        cols = pl.ds(pl.multiple_of(tile * 512, 512), 512)
        t0[...] = nn(hid_c[...], wup[:, cols])
        t1[...] = nn(cot[...], wdn[:, cols])

        def gelu(rs):
            u = t0[rs, :]
            phi = 0.5 * (1.0 + lax.erf(u * (2.0**-0.5)))
            b0[rs, :] = (u * phi).astype(BF)
            slope = phi + u * (jnp.exp(-0.5 * u * u) * (1.0 / math.sqrt(2.0 * math.pi)))
            b1[rs, :] = (t1[rs, :] * slope).astype(BF)

        row_loop(ROWS, 32, gelu)
        acc0[...] += nt(b0[...], wdn[:, cols])
        acc1[...] += nt(b1[...], wup[:, cols])
        gffn[1, :, cols] = tn(cot[...], b0[...]).astype(BF)
        gffn[0, :, cols] = tn(hid_c[...], b1[...]).astype(BF)
        for m in range(2):
            ffn.core_copy(m, tile).start()

    def back_norm(at, scale, grad_src, stream_src, base_src, want_out):
        sums = [jnp.zeros((1, D), F), jnp.zeros((1, D), F)]
        for i in range(ROWS // 32):
            rs = slice(i * 32, i * 32 + 32)
            back, ds, db = norm_back(grad_src[rs, :], stream_src[rs, :], scale)
            total = base_src[rs, :].astype(F) + back
            in_grad[rs, :] = total
            gbf[rs, :] = total.astype(BF)
            sums = [sums[0] + ds, sums[1] + db]
            if want_out:
                out_ref[rs, :] = (stream_c[rs, :] + acc0[rs, :]).astype(BF)
        mgrad[at : at + 1, :] = sums[0]
        mgrad[at + 1 : at + 2, :] = sums[1]

    leave(0)
    back_norm(4, sf, acc1, stream_c, cot, True)

    gatt[7] = tn(gbf[...], mixb[...]).astype(BF)
    mgr[...] = (nn(gbf[...], watt[7]) * linv_b[...]).astype(BF)
    leave(1)

    @pl.loop(0, 4)
    def _(hp):
        lanes = pl.ds(pl.multiple_of(hp * 128, 128), 128)
        prod = mgr[:, lanes].astype(F) * mixb[:, lanes].astype(F)
        dqs, dks, dvs = [], [], []
        for half in range(2):
            h = hp * 2 + half
            inner = jnp.sum(keep(prod, half), axis=-1, keepdims=True)
            mg = keep(mgr[:, lanes], half)
            dp = nt(mg, venc[:, lanes])
            b0[...] = (pe[h].astype(F) * (dp - inner)).astype(BF)
            dqs.append(nn(b0[...], kenc[:, lanes]))
            dks.append(tn(b0[...], keep(qb[:, lanes], half)))
            dvs.append(tn(pe[h], mg))
        dq[:, lanes] = (jnp.where(half_lanes(dqs[0].shape, 0), dqs[0], dqs[1]) * 0.125).astype(BF)
        kenc[:, lanes] = (dks[0] + dks[1]).astype(BF)
        venc[:, lanes] = (dvs[0] + dvs[1]).astype(BF)

    gatt[4] = tn(hid_b[...], dq[...]).astype(BF)
    gatt[5] = tn(enc[...], kenc[...]).astype(BF)
    gatt[6] = tn(enc[...], venc[...]).astype(BF)
    egrad[...] = (nt(kenc[...], watt[5]) + nt(venc[...], watt[6])).astype(BF)
    leave(2)
    acc1[...] = nt(dq[...], watt[4])
    back_norm(2, sb, acc1, stream_b, in_grad, False)

    gatt[3] = tn(gbf[...], mixa[...]).astype(BF)
    mgr[...] = (nn(gbf[...], watt[3]) * linv_a[...]).astype(BF)
    leave(3)

    @pl.when(odd == 0)
    def _():
        for h in range(8):
            ps[h, ROWS:LOC, :] = jnp.zeros((LOC - ROWS, 256), BF)
        spec_o[:, ROWS:LOC, :] = jnp.zeros((2, LOC - ROWS, 128), F)

    @pl.when(odd == 1)
    def _():
        for h in range(8):
            ps[h, 0:64, :] = jnp.zeros((64, 256), BF)
        spec_o[:, 0:64, :] = jnp.zeros((2, 64, 128), F)

    @pl.loop(0, 4)
    def _(turn):
        side = jnp.where(turn < 2, 1 - c, c)
        band = jnp.where(turn < 2, turn, jnp.where(turn == 2, 1 - y, y))
        hp = band * 2 + side
        lanes = pl.ds(pl.multiple_of(hp * 128, 128), 128)
        prod = mgr[:, lanes].astype(F) * mixa[:, lanes].astype(F)
        dqs, dks, dvs = [], [], []
        dks_s = [[], [], []]
        dvs_s = [[], [], []]
        for half in range(2):
            h = hp * 2 + half
            inner = jnp.sum(keep(prod, half), axis=-1, keepdims=True)
            mg = keep(mgr[:, lanes], half)
            qm = keep(qbuf[own, lanes], half)
            dp = nt(mg, vbuf[0:TRK, lanes])
            ds = (pt[h].astype(F) * (dp - inner)).astype(BF)
            spec_o[0, own, :] = mg.astype(F)
            spec_o[1, own, :] = jnp.broadcast_to(inner, (ROWS, 128))
            dq_s = []
            for lb in range(3):
                r = slice(lb * BLK, (lb + 1) * BLK)
                k_rows = slice(TRK + lb * 256, TRK + (lb + 1) * 256)
                mgl = spec_o[0, r, :].astype(BF)
                dpl = nt(mgl, vbuf[k_rows, lanes])
                inner_l = spec_o[1, r, 0:1]
                dsl = (ps[h, r, :].astype(F) * (dpl - inner_l)).astype(BF)
                ss[r, 0:128] = nn(dsl, kbuf[k_rows, lanes])
                dks_s[lb].append(tn(dsl, keep(qbuf[r, lanes], half)))
                dvs_s[lb].append(tn(ps[h, r, :], mgl))
            dqs.append(nn(ds, kbuf[0:TRK, lanes]) + ss[own, 0:128])
            dks.append(tn(ds, qm))
            dvs.append(tn(pt[h], mg))
        dq[:, lanes] = (jnp.where(half_lanes(dqs[0].shape, 0), dqs[0], dqs[1]) * 0.125).astype(BF)
        kbuf[0:TRK, lanes] = (dks[0] + dks[1]).astype(BF)
        vbuf[0:TRK, lanes] = (dvs[0] + dvs[1]).astype(BF)
        for lb in range(3):
            k_rows = slice(TRK + lb * 256, TRK + (lb + 1) * 256)
            kbuf[k_rows, lanes] = (dks_s[lb][0] + dks_s[lb][1]).astype(BF)
            vbuf[k_rows, lanes] = (dvs_s[lb][0] + dvs_s[lb][1]).astype(BF)

        total = None
        for at in range(0, KV, KV // 2):
            rs = slice(at, at + KV // 2)
            both = jnp.concatenate([kbuf[rs, lanes], vbuf[rs, lanes]], axis=1)
            part = tn(both, hid[rs, :])
            total = part if total is None else total + part
        kv_grad = jnp.transpose(total)
        gatt[1, :, lanes] = kv_grad[:, 0:128].astype(BF)
        gatt[2, :, lanes] = kv_grad[:, 128:256].astype(BF)
        gatt[0, :, lanes] = tn(hloc[own, :], dq[:, lanes]).astype(BF)

        @pl.when(turn < 2)
        def _():
            for m in range(2):
                for xx in range(2):
                    att[0].core_copy(m, band * 2 + xx).start()

        @pl.when(turn == 0)
        def _():
            leave(4)

        @pl.when(turn == 2)
        def _():
            leave(5)

    def key_grad(rs):
        return (nt(kbuf[rs, :], watt[1]) + nt(vbuf[rs, :], watt[2])).astype(BF)

    for lb in range(3):
        pe[lb, 0:256, :] = key_grad(slice(TRK + lb * 256, TRK + (lb + 1) * 256))

    def trunk_grad(rs):
        tok[rs, :] = key_grad(rs)

    row_loop(TRK, 256, trunk_grad)

    for b in range(BRANCHES):
        hits = [is_parent(lb, b) for lb in range(3)]
        for piece in range(4):
            total = jnp.zeros((32, D), F)
            for lb in range(3):
                at = piece * 32
                total += jnp.where(hits[lb], pe[lb, at : at + 32, :].astype(F), 0.0)
            at = TRK + b * BLK + piece * 32
            tok[at : at + 32, :] = total.astype(BF)
    for lb in range(3):
        spec_g[lb * BLK : (lb + 1) * BLK, :] = pe[lb, BLK : 2 * BLK, :]

    leave(6)
    acc1[...] = nt(dq[...], watt[0])

    def own_sum(rs):
        extra = spec_g[pl.ds(pl.multiple_of(rs.start + off, 32), 32), :].astype(F)
        acc1[rs, :] += extra

    row_loop(ROWS, 32, own_sum, 5)
    leave(7)
    leave(8)

    wire.arrived(halo, s_halo, to_y, y == 0)

    @pl.when(y == 0)
    def _():
        acc1[ROWS - 64 : ROWS, :] += halo[...].astype(F)

    @pl.when(x == 0)
    def _():
        def body(rs):
            mine = tok[pl.ds(pl.multiple_of(ci * ROWS + rs.start, 32), 32), :].astype(F)
            acc1[rs, :] += mine + rx_g[1, rs, :].astype(F)

        row_loop(ROWS, 32, body)

    @pl.when(ci == 4)
    def _():
        def body(rs):
            mine = tok[pl.ds(pl.multiple_of(4 * ROWS + rs.start, 32), 32), :].astype(F)
            acc1[rs, :] += mine + rx_g[1, rs, :].astype(F)

        row_loop(256, 32, body)

    mgrad[6:8, :] = jnp.zeros((2, D), F)
    sums = [jnp.zeros((1, D), F), jnp.zeros((1, D), F)]
    for i in range(ROWS // 32):
        rs = slice(i * 32, i * 32 + 32)
        back, ds, db = norm_back(acc1[rs, :], tok_own[rs, :].astype(F), sa)
        in_grad[rs, :] += back
        sums = [sums[0] + ds, sums[1] + db]
    mgrad[0:1, :] = sums[0]
    mgrad[1:2, :] = sums[1]
    leave(9)

    for i in range(5):
        result(i).wait()
    wire.drain()
    for family in (ffn, *att):
        family.drain()
    tree_peers(lambda k, to, _: mod_1(k, to).wait_send())
    peers(lambda k, to, _: mod_2(k, to).wait_send())
    peers(
        lambda k, to, _: wire.copy(
            cond_parts.at[to], cond_all.at[fs], s_cond + k, {"fsdp": to}
        ).wait_send()
    )
    peers(
        lambda k, to, _: wire.copy(
            part_out.at[to], part_in.at[fs], s_part + k, {"fsdp": to}
        ).wait_send()
    )
    for g in range(6):
        peers(
            lambda k, to, _, g=g: wire.copy(
                groups[g][0], place(g, my_rows, y, x, c), s_z[g] + k, {"fsdp": to}
            ).wait_send()
        )


def layer_call(n, parents, cond_parts, w_mod, tokens, enc, cot, weights):
    vm = pl.BlockSpec(memory_space=pltpu.VMEM)
    hbm = pl.BlockSpec(memory_space=pl.ANY)
    sds = jax.ShapeDtypeStruct
    rows = w_mod.shape[0]
    return pl.pallas_call(
        functools.partial(layer_kernel, n),
        out_shape=(
            sds((ROWS, D), BF),
            sds((ROWS, D), F),
            sds((ENC // 4, D), F),
            sds((n, 8, D), F),
            sds(cond_parts.shape, F),
            sds((2, 4, 2, rows, 128), BF),
            sds((4, 2, rows, 256), BF),
        ),
        in_specs=[pl.BlockSpec(memory_space=pltpu.SMEM), vm, vm, hbm, hbm, vm] + [hbm] * 6,
        out_specs=(vm, vm, vm, hbm, hbm, hbm, hbm),
        scratch_shapes=[
            pltpu.VMEM((8, D, D), BF),
            pltpu.VMEM((D, FF), BF),
            pltpu.VMEM((D, FF), BF),
            pltpu.VMEM((8 * ROWS + 64, D), BF),
            pltpu.VMEM((ENC, D), BF),
            pltpu.VMEM((n, 8, D), F),
            pltpu.VMEM((n, 8, D), F),
            pltpu.VMEM((8, D), F),
            pltpu.VMEM((*cond_parts.shape,), F),
            pltpu.VMEM((ROWS, D), BF),
            pltpu.VMEM((8, D), F),
            pltpu.VMEM((KV, D), BF),
            pltpu.VMEM((LOC, D), BF),
            pltpu.VMEM((KV, D), BF),
            pltpu.VMEM((KV, D), BF),
            pltpu.VMEM((LOC, D), BF),
            pltpu.VMEM((8, ROWS, TRK), BF),
            pltpu.VMEM((8, LOC, 256), BF),
            pltpu.VMEM((ROWS, TRK), BF),
            pltpu.VMEM((LOC, 256), BF),
            pltpu.VMEM((ROWS, TRK), F),
            pltpu.VMEM((LOC, 256), F),
            pltpu.VMEM((2, LOC, 128), F),
            pltpu.VMEM((ROWS, D), BF),
            pltpu.VMEM((ROWS, D), F),
            pltpu.VMEM((ROWS, D), F),
            pltpu.VMEM((ROWS, D), BF),
            pltpu.VMEM((ROWS, D), BF),
            pltpu.VMEM((ENC, D), BF),
            pltpu.VMEM((ENC, D), BF),
            pltpu.VMEM((ROWS, D), BF),
            pltpu.VMEM((8, ROWS, ENC), BF),
            pltpu.VMEM((ROWS, D), BF),
            pltpu.VMEM((ROWS, D), BF),
            pltpu.VMEM((ROWS, D), BF),
            pltpu.VMEM((ROWS, D), F),
            pltpu.VMEM((ROWS, D), F),
            pltpu.VMEM((ROWS, D), BF),
            pltpu.VMEM((ROWS, D), BF),
            pltpu.VMEM((ROWS, D), BF),
            pltpu.VMEM((D, D), F),
            pltpu.VMEM((ROWS, D), F),
            pltpu.VMEM((8, D, D), BF),
            pltpu.VMEM((2, D, FF), BF),
            pltpu.VMEM((8, D, 256), BF),
            pltpu.VMEM((2, 6, D, 128), BF),
            pltpu.VMEM((2, n, 2, rows, 128), BF),
            pltpu.VMEM((2, 4, 2, rows, 128), BF),
            pltpu.VMEM((n, 2, 4, rows, 128), BF),
            pltpu.VMEM((2, 4, rows, 128), BF),
            pltpu.VMEM((n, 2, rows, 256), BF),
            pltpu.VMEM((4, 2, rows, 256), BF),
            pltpu.VMEM((896, D), BF),
            pltpu.VMEM((2, ROWS, D), BF),
            pltpu.VMEM((64, D), BF),
            pltpu.VMEM((2, 128, D), BF),
            pltpu.VMEM((4, 128, D), BF),
            pltpu.VMEM((8, 8, D), F),
            pltpu.VMEM((n, 8, D), F),
            pltpu.SemaphoreType.DMA((16 * n + 160,)),
            pltpu.SemaphoreType.DMA((16 * n + 160,)),
            pltpu.SemaphoreType.DMA((9,)),
            pltpu.SemaphoreType.REGULAR((2,)),
        ],
        compiler_params=pltpu.CompilerParams(
            vmem_limit_bytes=VMEM_LIMIT, collective_id=0, has_side_effects=True
        ),
        name="layer",
    )(parents, cond_parts, w_mod, tokens, enc, cot, *weights)


def finish_kernel(
    n, rows, out, grad, enc, mod, cond, att, ffn, o_out, o_grad, o_enc, o_mod, qkv, so, cqkv, co, up, dn
):
    o_out[...] = out[...]
    o_grad[...] = grad[...]
    o_enc[...] = enc[...]
    for v in range(6):
        o_mod[:, v * D : (v + 1) * D] = lax.dot_general(
            cond[:, 0, 0:rows],
            mod[:, v, :],
            (((0,), (0,)), ((), ())),
            precision=lax.Precision.HIGHEST,
            preferred_element_type=F,
        )
    for q in range(4):
        up[:, q * 256 : (q + 1) * 256] = ffn[q, 0].astype(F)
        dn[:, q * 256 : (q + 1) * 256] = ffn[q, 1].astype(F)
        cols = slice((q % 2) * 128, (q % 2) * 128 + 128)
        for a, (stack, single) in enumerate(((qkv, so), (cqkv, co))):
            for m in range(2):
                value = att[a, q, m].astype(F)
                at = 2 * (q // 2) + m
                if at < 3:
                    stack[at, :, cols] = value
                else:
                    single[:, cols] = value


def finish_call(n, rows, *parts):
    vm = pl.BlockSpec(memory_space=pltpu.VMEM)
    sds = jax.ShapeDtypeStruct
    return pl.pallas_call(
        functools.partial(finish_kernel, n, rows),
        out_shape=(
            sds((ROWS, D), BF),
            sds((ROWS, D), F),
            sds((ENC // 4, D), F),
            sds((rows, 6 * D), F),
            sds((3, rows, 256), F),
            sds((rows, 256), F),
            sds((3, rows, 256), F),
            sds((rows, 256), F),
            sds((rows, 1024), F),
            sds((rows, 1024), F),
        ),
        in_specs=[vm] * 7,
        out_specs=(vm,) * 10,
        name="finish",
    )(*parts)


def timestep_code(timesteps, width):
    half = width // 2
    frequency = jnp.exp(-math.log(10000.0) * jnp.arange(half, dtype=F) / half)
    angles = timesteps.astype(F)[:, None] * frequency[None, :]
    return jnp.concatenate([jnp.sin(angles), jnp.cos(angles)], axis=-1)


def per_device(
    tokens,
    encoder_states,
    timesteps,
    parents,
    w_mod,
    w_self_qkv,
    w_self_out,
    w_cross_qkv,
    w_cross_out,
    w_up,
    w_down,
    cotangent,
):
    rows = w_mod.shape[0]
    condition = jax.nn.silu(timestep_code(timesteps, D)).astype(BF)
    n = lax.axis_size("fsdp")
    padded_cond = jnp.pad(condition.astype(F).reshape(n, 1, rows), ((0, 0), (0, 7), (0, max(128 - rows, 0))))
    parts = layer_call(
        n,
        parents,
        padded_cond,
        w_mod,
        tokens,
        encoder_states,
        cotangent[0],
        (w_self_qkv, w_self_out, w_cross_qkv, w_cross_out, w_up, w_down),
    )
    out, in_grad, enc_grad, grad_mod, *weights = finish_call(n, rows, *parts)
    return (out[None], in_grad[None], enc_grad[None], grad_mod, *weights)


def solution(mesh):
    rows = P("fsdp", ("ctx", "tp"), None)
    return jax.shard_map(
        per_device,
        mesh=mesh,
        in_specs=(
            rows,
            P("fsdp", "ctx", None),
            P("fsdp"),
            P("fsdp", None),
            P("fsdp", None),
            P(None, "fsdp", "tp"),
            P("fsdp", "tp"),
            P(None, "fsdp", "tp"),
            P("fsdp", "tp"),
            P("fsdp", "tp"),
            P("fsdp", "tp"),
            rows,
        ),
        out_specs=(
            rows,
            rows,
            P("fsdp", "ctx", None),
            P("fsdp", None),
            P(None, "fsdp", "tp"),
            P("fsdp", "tp"),
            P(None, "fsdp", "tp"),
            P("fsdp", "tp"),
            P("fsdp", "tp"),
            P("fsdp", "tp"),
        ),
        check_vma=False,
    )
```

```python
import functools
import math

import jax
import jax.numpy as jnp
from jax import lax
from jax.experimental import pallas as pl
from jax.experimental.pallas import tpu as pltpu
from jax.sharding import PartitionSpec as P

BF = jnp.bfloat16
F = jnp.float32
D = 512
FF = 2048
HD = 64
ROWS = 320
LOC = 384
BLK = 128
TRUNK = 8
BRANCHES = 4
TRK = TRUNK * BLK
SHARED = (TRUNK + BRANCHES) * BLK
SPEC = 2 * LOC
KV = TRK + SPEC
ENC = 512
EPS = 1e-05
NEG = -1e30
VMEM_LIMIT = 67043328


def nn(a, b):
    return lax.dot_general(a, b, (((1,), (0,)), ((), ())), preferred_element_type=F)


def nt(a, b):
    return lax.dot_general(a, b, (((1,), (1,)), ((), ())), preferred_element_type=F)


def tn(a, b):
    return lax.dot_general(a, b, (((0,), (0,)), ((), ())), preferred_element_type=F)


def normed(v):
    center = v - jnp.mean(v, axis=-1, keepdims=True)
    rstd = lax.rsqrt(jnp.mean(center * center, axis=-1, keepdims=True) + EPS)
    return center * rstd, rstd


def norm_back(grad, stream, scale):
    n, rstd = normed(stream)
    gn = grad * (1.0 + scale)
    back = rstd * (
        gn
        - jnp.mean(gn, axis=-1, keepdims=True)
        - n * jnp.mean(gn * n, axis=-1, keepdims=True)
    )
    return back, jnp.sum(grad * n, axis=0, keepdims=True), jnp.sum(grad, axis=0, keepdims=True)


def row_loop(total, step, body, unroll=1):
    if unroll == 0:
        for i in range(total // step):
            body(pl.ds(i * step, step))
        return

    @pl.loop(0, total // (step * unroll))
    def _(i):
        for j in range(unroll):
            body(pl.ds(pl.multiple_of((i * unroll + j) * step, step), step))


def half_lanes(shape, half):
    lane = lax.broadcasted_iota(jnp.int32, shape, len(shape) - 1)
    return (lane // HD) == half


def keep(value, half):
    return jnp.where(half_lanes(value.shape, half), value, jnp.zeros_like(value))


MESH = pl.DeviceIdType.MESH


class Wire:
    def __init__(self, send, recv):
        self.send, self.recv, self.used, self.sent = send, recv, 0, []

    def slot(self, count=1):
        self.used += count
        return self.used - count

    def copy(self, src, dst, at, to):
        return pltpu.make_async_remote_copy(
            src_ref=src,
            dst_ref=dst,
            send_sem=self.send.at[at],
            recv_sem=self.recv.at[at],
            device_id=to,
            device_id_type=MESH,
        )

    def push(self, dst, at, to, when=None, src=None):
        src = src or dst
        if when is None:
            self.copy(src(), dst(), at, to).start()
        else:

            @pl.when(when)
            def _():
                self.copy(src(), dst(), at, to).start()

        self.sent.append((src, dst, at, to, when))

    def arrived(self, dst, at, to, when=None):
        if when is None:
            self.copy(dst, dst, at, to).wait_recv()
        else:

            @pl.when(when)
            def _():
                self.copy(dst, dst, at, to).wait_recv()

    def drain(self):
        for src, dst, at, to, when in self.sent:
            if when is None:
                self.copy(src(), dst(), at, to).wait_send()
            else:

                @pl.when(when)
                def _(src=src, dst=dst, at=at, to=to):
                    self.copy(src(), dst(), at, to).wait_send()

        self.sent = []


def layer_kernel(
    n,
    parents_ref,
    cond_parts,
    w_mod,
    tok_in,
    enc_in,
    cot,
    w_sqkv,
    w_so,
    w_cqkv,
    w_co,
    w_up,
    w_dn,
    out_ref,
    in_grad,
    enc_out,
    mod_out,
    cond_out,
    att_out,
    ffn_out,
    watt,
    wup,
    wdn,
    tok,
    enc,
    part_out,
    part_in,
    mod,
    cond_all,
    tok_own,
    mgrad,
    hid,
    hloc,
    kbuf,
    vbuf,
    qbuf,
    pt,
    ps,
    bias_t,
    bias_s,
    st,
    ss,
    spec_o,
    mixa,
    stream_b,
    stream_c,
    hid_b,
    hid_c,
    kenc,
    venc,
    qb,
    pe,
    mixb,
    b0,
    b1,
    acc0,
    acc1,
    gbf,
    mgr,
    dq,
    wk_acc,
    wv_acc,
    gatt,
    gffn,
    rc_att,
    rx_att,
    zr_att,
    rg_att,
    zl_att,
    zs_att,
    zr_ffn,
    rg_ffn,
    rc_g,
    rx_g,
    halo,
    rc_e,
    rx_e,
    mod1,
    mod2,
    send,
    recv,
    local,
    ready,
):
    t0, t1 = st.at[:, 0:D], st.at[:, D : 2 * D]
    egrad = enc
    fs = lax.axis_index("fsdp")
    cx = lax.axis_index("ctx")
    y = lax.axis_index("tp")
    x, c = cx // 2, lax.rem(cx, 2)
    ci = cx * 2 + y
    odd = y
    off = pl.multiple_of(odd * 64, 64)
    own = pl.ds(off, ROWS)
    base = (ci * 5) // 2
    rows = w_mod.shape[0]
    to_y = {"tp": 1 - y}
    to_c = {"ctx": 2 * x + 1 - c}
    to_x = {"ctx": 2 * (1 - x) + c}
    wire = Wire(send, recv)

    my_rows = pl.ds(pl.multiple_of(fs * rows, rows), rows)

    def att_cols(yy, cc):
        return pl.ds(pl.multiple_of(yy * 256 + cc * 128, 128), 128)

    def ffn_cols(yy, xx, cc):
        return pl.ds(pl.multiple_of(yy * 1024 + xx * 512 + cc * 256, 256), 256)

    half = pl.ds(pl.multiple_of(c * 128, 128), 128)
    quarter = pl.ds(pl.multiple_of(cx * 256, 256), 256)
    groups = (
        (w_sqkv.at[:, :, half], watt, slice(0, 3), 0),
        (w_so.at[:, half], watt, 3, 0),
        (w_cqkv.at[:, :, half], watt, slice(4, 7), 0),
        (w_co.at[:, half], watt, 7, 0),
        (w_up.at[:, quarter], wup, None, 1),
        (w_dn.at[:, quarter], wdn, None, 1),
    )

    def place(g, row_at, yy, xx, cc):
        _, buf, index, wide = groups[g]
        if wide:
            return buf.at[row_at, ffn_cols(yy, xx, cc)]
        return buf.at[index, row_at, att_cols(yy, cc)]

    def chunk(i):
        return tok.at[pl.ds(pl.multiple_of(i * ROWS, ROWS), ROWS), :]

    def enc_part(i):
        return enc.at[pl.ds(pl.multiple_of(i * 128, 128), 128), :]

    all_rows = pl.ds(0, D)

    local_copies = [
        pltpu.make_async_copy(tok_in.at[0], chunk(ci), local.at[0]),
        pltpu.make_async_copy(enc_in.at[0], enc_part(cx), local.at[1]),
    ] + [
        pltpu.make_async_copy(groups[g][0], place(g, my_rows, y, x, c), local.at[2 + g])
        for g in range(6)
    ]
    local_copies.append(pltpu.make_async_copy(tok_in.at[0], tok_own, local.at[8]))
    for copy in local_copies:
        copy.start()

    barrier = pltpu.get_barrier_semaphore()

    @pl.loop(1, n)
    def _(k):
        pl.semaphore_signal(
            barrier, inc=1, device_id={"fsdp": lax.rem(fs + k, n)}, device_id_type=MESH
        )

    @pl.loop(1, 8)
    def _(k):
        other = lax.rem(ci + k, 8)
        pl.semaphore_signal(
            barrier,
            inc=1,
            device_id={"ctx": other // 2, "tp": lax.rem(other, 2)},
            device_id_type=MESH,
        )

    pl.semaphore_wait(barrier, n - 1 + 7)

    def peers(make):
        @pl.loop(1, n)
        def _(k):
            make(k, lax.rem(fs + k, n), lax.rem(fs + n - k, n))

    s_cond = wire.slot(n)
    s_part = wire.slot(n)
    s_z = [wire.slot(n) for _ in range(6)]
    s_y = [wire.slot() for _ in range(6)]
    s_c0 = [wire.slot() for _ in range(6)]
    s_c1 = [wire.slot() for _ in range(6)]
    s_x0 = [wire.slot() for _ in range(6)]
    s_x1 = [wire.slot() for _ in range(6)]
    s_c2 = [wire.slot() for _ in range(6)]
    s_c3 = [wire.slot() for _ in range(6)]
    s_ty, s_tx, s_txy, s_tc0, s_tc1, s_tc2, s_tc3, s_ty2 = (
        wire.slot() for _ in range(8)
    )
    s_ex, s_ec0, s_ec1 = (wire.slot() for _ in range(3))

    peers(
        lambda k, to, _: wire.copy(
            cond_parts.at[to], cond_all.at[fs], s_cond + k, {"fsdp": to}
        ).start()
    )
    left = x == 0

    def tail_rows(i):
        return tok.at[pl.ds(pl.multiple_of(i * ROWS + ROWS - 64, 64), 64), :]

    wire.push(
        lambda: chunk(ci), s_ty, to_y, jnp.logical_or(left, ci == 4), lambda: tok_in.at[0]
    )
    wire.push(
        lambda: tail_rows(ci), s_ty2, to_y, ci == 6, lambda: tok_in.at[0, ROWS - 64 : ROWS, :]
    )
    wire.push(lambda: chunk(ci), s_tx, to_x, x == 0, lambda: tok_in.at[0])
    wire.push(
        lambda: chunk(ci), s_tc0, to_c, jnp.logical_or(left, ci == 4), lambda: tok_in.at[0]
    )

    def z_start(g):
        peers(
            lambda k, to, _: wire.copy(
                groups[g][0], place(g, my_rows, y, x, c), s_z[g] + k, {"fsdp": to}
            ).start()
        )

    z_start(0)

    def mask_trunk(rs):
        row = lax.broadcasted_iota(jnp.int32, (32, TRK), 0) + rs.start + ci * ROWS
        col = lax.broadcasted_iota(jnp.int32, (32, TRK), 1)
        bias_t[rs, :] = jnp.where(col <= row, 0.0, NEG).astype(BF)

    row_loop(ROWS, 32, mask_trunk)
    for lb in range(3):
        blk = base + lb
        row = lax.broadcasted_iota(jnp.int32, (BLK, 2 * BLK), 0)
        col = lax.broadcasted_iota(jnp.int32, (BLK, 2 * BLK), 1)
        par_ok = jnp.logical_and(col < BLK, blk >= TRUNK + BRANCHES)
        self_ok = jnp.logical_and(
            jnp.logical_and(col >= BLK, col - BLK <= row), blk >= TRUNK
        )
        bias_s[lb * BLK : (lb + 1) * BLK, :] = jnp.where(
            jnp.logical_or(par_ok, self_ok), 0.0, NEG
        ).astype(BF)

    cond_all[fs] = cond_parts[fs]
    peers(lambda k, _, src: wire.arrived(cond_all.at[src], s_cond + k, {"fsdp": src}))
    for v in range(6):
        part_out[:, v, :] = nn(
            cond_all[:, 0, 0:rows].astype(BF), w_mod[:, v * D : (v + 1) * D]
        )
    part_out[:, 6:8, :] = jnp.zeros((n, 2, D), F)
    peers(
        lambda k, to, _: wire.copy(
            part_out.at[to], part_in.at[fs], s_part + k, {"fsdp": to}
        ).start()
    )
    part_in[fs] = part_out[fs]

    def z_done(g):
        local_copies[2 + g].wait()
        peers(
            lambda k, _, src: wire.arrived(
                place(g, pl.ds(pl.multiple_of(src * rows, rows), rows), y, x, c),
                s_z[g] + k,
                {"fsdp": src},
            )
        )
        slab = lambda: place(g, all_rows, y, x, c)
        wire.push(slab, s_y[g], to_y)
        if groups[g][3]:
            wire.push(slab, s_x0[g], to_x)
        wire.push(slab, s_c0[g], to_c)

    def y_done(g):
        slab = lambda: place(g, all_rows, 1 - y, x, c)
        wire.arrived(slab(), s_y[g], to_y)
        if groups[g][3]:
            wire.push(slab, s_x1[g], to_x)
        wire.push(slab, s_c1[g], to_c)

    def x_done(g, part):
        s_in, s_out = ((s_x0[g], s_c2[g]), (s_x1[g], s_c3[g]))[part]
        slab = lambda: place(g, all_rows, 1 - y if part else y, 1 - x, c)
        wire.arrived(slab(), s_in, to_x)
        wire.push(slab, s_out, to_c)

    def c_part(g, part):
        yy, xx, at = (
            (y, x, s_c0[g]),
            (1 - y, x, s_c1[g]),
            (y, 1 - x, s_c2[g]),
            (1 - y, 1 - x, s_c3[g]),
        )[part]
        wire.arrived(place(g, all_rows, yy, xx, 1 - c), at, to_c)

    def c_done(g):
        wire.arrived(place(g, all_rows, y, x, 1 - c), s_c0[g], to_c)
        wire.arrived(place(g, all_rows, 1 - y, x, 1 - c), s_c1[g], to_c)
    local_copies[0].wait()
    local_copies[1].wait()
    ciy = 4 * x + 2 * c + 1 - y
    cic = 4 * x + 2 * (1 - c) + y
    ciyc = 4 * x + 2 * (1 - c) + 1 - y
    low, lowy, lowc, lowyc = 2 * c + y, 2 * c + 1 - y, 2 * (1 - c) + y, 2 * (1 - c) + 1 - y
    right = x == 1
    local_copies[8].wait()
    wire.arrived(chunk(ciy), s_ty, to_y, jnp.logical_or(left, ci == 5))
    wire.push(lambda: chunk(ciy), s_txy, to_x, left)
    wire.push(lambda: chunk(ciy), s_tc1, to_c, jnp.logical_or(left, ci == 5))
    wire.arrived(tail_rows(ciy), s_ty2, to_y, ci == 7)

    @pl.when(jnp.logical_and(right, y == 0))
    def _():
        tok[pl.ds(pl.multiple_of((ci + 1) * ROWS, 64), 64), :] = jnp.zeros((64, D), BF)

    z_start(1)
    z_start(4)
    wire.arrived(chunk(low), s_tx, to_x, right)
    wire.push(lambda: chunk(low), s_tc2, to_c, right)
    z_done(0)
    z_start(2)
    wire.arrived(chunk(lowy), s_txy, to_x, right)
    wire.push(lambda: chunk(lowy), s_tc3, to_c, right)
    wire.push(lambda: enc_part(cx), s_ex, to_x, None, lambda: enc_in.at[0])
    wire.push(lambda: enc_part(cx), s_ec0, to_c, None, lambda: enc_in.at[0])
    y_done(0)
    z_done(1)
    z_done(4)
    z_start(5)
    z_start(3)

    peers(lambda k, _, src: wire.arrived(part_in.at[src], s_part + k, {"fsdp": src}))
    mod[...] = jnp.sum(part_in[...], axis=0)
    sa, ba = mod[0:1, :], mod[1:2, :]
    sb, bb = mod[2:3, :], mod[3:4, :]
    sf, bf_ = mod[4:5, :], mod[5:6, :]

    wire.arrived(chunk(cic), s_tc0, to_c, jnp.logical_or(left, ci == 6))
    wire.arrived(chunk(ciyc), s_tc1, to_c, jnp.logical_or(left, ci == 7))
    wire.arrived(chunk(lowc), s_tc2, to_c, right)
    wire.arrived(chunk(lowyc), s_tc3, to_c, right)

    def enc_done(step):
        if step == 0:
            wire.arrived(enc_part(2 * (1 - x) + c), s_ex, to_x)
            wire.push(lambda: enc_part(2 * (1 - x) + c), s_ec1, to_c)
        else:
            wire.arrived(enc_part(2 * x + 1 - c), s_ec0, to_c)
            wire.arrived(enc_part(2 * (1 - x) + 1 - c), s_ec1, to_c)

    tok_tb = tok
    tok_loc = tok.at[pl.ds(pl.multiple_of(ci * ROWS - off, 64), LOC), :]

    def relay(step):
        if step == 1:
            y_done(1)
            y_done(4)
            enc_done(0)
        if step == 2:
            z_done(5)
            z_done(3)
        if step == 4:
            c_done(1)
        if step == 5:
            y_done(5)
            y_done(3)
            c_done(3)
        if step == 6:
            x_done(4, 0)
            x_done(5, 0)
        if step == 7:
            y_done(2)
            enc_done(1)
            c_done(2)

    spec_g = qbuf

    def is_parent(lb, branch):
        parent = jnp.full((32, D), parents_ref[0, base + lb], jnp.int32)
        leaf = jnp.full((32, D), base + lb, jnp.int32) >= TRUNK + BRANCHES
        return jnp.logical_and(leaf, parent == TRUNK + branch)

    to_xy = {"ctx": 2 * (1 - x) + c, "tp": 1 - y}
    s_rcg, s_rcg4, s_rcg5, s_halo = (wire.slot() for _ in range(4))
    s_rxy = [wire.slot() for _ in range(2)]
    s_rxx = [wire.slot() for _ in range(2)]
    s_rce = [wire.slot(), wire.slot()]
    s_rxe = [wire.slot() for _ in range(3)]
    s_m1 = wire.slot(8)
    s_m2 = wire.slot(n)
    quad = ((to_y, x, 1 - y), (to_x, 1 - x, y), (to_xy, 1 - x, 1 - y))

    def add_rows(target, terms, total, step=64):
        def body(rs):
            value = terms[0][rs, :].astype(F)
            for term in terms[1:]:
                value += term[rs, :].astype(F)
            target[rs, :] = value.astype(BF)

        row_loop(total, step, body)

    def strip(buf, at):
        return buf.at[:, at * 256 : (at + 1) * 256]

    class Family:
        def __init__(self, unit, core_box, box, landing, held, shape_rows):
            self.unit, self.core_box, self.box = unit, core_box, box
            self.landing, self.held, self.tall = landing, held, shape_rows
            self.s_core = [wire.slot(4) for _ in range(2)]
            self.s_one = [[wire.slot() for _ in range(2)] for _ in range(2)]
            self.s_two = [wire.slot() for _ in range(2)]
            self.s_z = [wire.slot(n) for _ in range(2)]
            self.s_g = wire.slot(4)

        def core_copy(self, m, t):
            return wire.copy(
                self.unit(m, t // 2, lax.rem(t, 2), 1 - c),
                self.core_box(m, t),
                self.s_core[m] + t,
                to_c,
            )

        def core_send(self):
            for m in range(2):
                for t in range(4):
                    self.core_copy(m, t).start()

        def first_send(self):
            for m in range(2):
                for t in range(4):
                    wire.arrived(self.core_box(m, t), self.s_core[m] + t, to_c)
                    mine = self.unit(m, t // 2, t % 2, c)
                    add_rows(mine, (mine, self.core_box(m, t)), D)
            self.one_send()

        def piece(self, m, yy, xx):
            return self.unit(m, yy, xx, c)

        def one_send(self):
            for j in range(2):
                wire.push(
                    lambda j=j: self.box(j),
                    self.s_one[0][j],
                    to_x,
                    None,
                    lambda j=j: self.piece(0, j, 1 - x),
                )
                wire.push(
                    lambda j=j: self.box(2 + j),
                    self.s_one[1][j],
                    to_y,
                    None,
                    lambda j=j: self.piece(1, 1 - y, j),
                )

        def second_send(self):
            for j in range(2):
                wire.arrived(self.box(j), self.s_one[0][j], to_x)
                mine = self.piece(0, j, x)
                add_rows(mine, (mine, self.box(j)), self.tall, min(64, self.tall))
            wire.push(
                lambda: self.box(4),
                self.s_two[0],
                to_y,
                None,
                lambda: self.piece(0, 1 - y, x),
            )
            for j in range(2):
                wire.arrived(self.box(2 + j), self.s_one[1][j], to_y)
                mine = self.piece(1, y, j)
                add_rows(mine, (mine, self.box(2 + j)), self.tall, min(64, self.tall))
            wire.push(
                lambda: self.box(5),
                self.s_two[1],
                to_x,
                None,
                lambda: self.piece(1, y, 1 - x),
            )

        def z_copy(self, m, k, to):
            part = pl.ds(pl.multiple_of(to * rows, rows), rows)
            return wire.copy(
                self.unit(m, y, x, c).at[part, :],
                self.landing.at[fs, m],
                self.s_z[m] + k,
                {"fsdp": to},
            )

        def tree_send(self):
            for m, target in ((0, to_y), (1, to_x)):
                wire.arrived(self.box(4 + m), self.s_two[m], target)
                mine = self.unit(m, y, x, c)
                add_rows(mine, (mine, self.box(4 + m)), D)
                peers(lambda k, to, _, m=m: self.z_copy(m, k, to).start())
                self.landing[fs, m] = self.unit(m, y, x, c)[my_rows, :]

        def g_copy(self, i):
            target, at = ((to_x, cx), (to_c, cx), (to_c, 2 * (1 - x) + c))[i]
            return wire.copy(self.held.at[at], self.held.at[at], self.s_g + i, target)

        def copy_send(self):
            for m in range(2):
                peers(
                    lambda k, _, src, m=m: wire.arrived(
                        self.landing.at[src, m], self.s_z[m] + k, {"fsdp": src}
                    )
                )
            self.held[cx] = jnp.sum(self.landing[...].astype(F), axis=0).astype(BF)
            self.g_copy(0).start()
            self.g_copy(1).start()

        def relay_copy(self):
            wire.arrived(self.held.at[2 * (1 - x) + c], self.s_g, to_x)
            self.g_copy(2).start()

        def collect(self):
            wire.arrived(self.held.at[2 * x + 1 - c], self.s_g + 1, to_c)
            wire.arrived(self.held.at[2 * (1 - x) + 1 - c], self.s_g + 2, to_c)

        def drain(self):
            for m in range(2):
                for t in range(4):
                    self.core_copy(m, t).wait_send()
                peers(lambda k, to, _, m=m: self.z_copy(m, k, to).wait_send())
            for i in range(3):
                self.g_copy(i).wait_send()

    class TreeFirst(Family):
        def piece(self, m, yy, xx):
            return zs_att.at[yy, 2 * xx + m]

        def row_copy(self, yy, k, to):
            part = pl.ds(pl.multiple_of(to * rows, rows), rows)
            return wire.copy(
                gatt.at[4:8, part, att_cols(yy, c)],
                zl_att.at[fs, yy],
                self.s_z[yy] + k,
                {"fsdp": to},
            )

        def one_send(self):
            for yy in range(2):
                peers(lambda k, to, _, yy=yy: self.row_copy(yy, k, to).start())
                zl_att[fs, yy] = gatt[4:8, my_rows, att_cols(yy, c)]

        def sum_trees(self):
            for yy in range(2):
                peers(
                    lambda k, _, src, yy=yy: wire.arrived(
                        zl_att.at[src, yy], self.s_z[yy] + k, {"fsdp": src}
                    )
                )
            zs_att[...] = jnp.sum(zl_att[...].astype(F), axis=0).astype(BF)
            Family.one_send(self)

        def copy_send(self):
            for m, target in ((0, to_y), (1, to_x)):
                wire.arrived(self.box(4 + m), self.s_two[m], target)
                total = self.piece(m, y, x)[...].astype(F) + self.box(4 + m)[...].astype(F)
                self.held[cx, m] = total.astype(BF)
            self.g_copy(0).start()
            self.g_copy(1).start()

        def drain(self):
            for m in range(2):
                for t in range(4):
                    self.core_copy(m, t).wait_send()
                peers(lambda k, to, _, m=m: self.row_copy(m, k, to).wait_send())
            for i in range(3):
                self.g_copy(i).wait_send()

    ffn = Family(
        lambda m, yy, xx, cc: gffn.at[m, :, ffn_cols(yy, xx, cc)],
        lambda m, t: rc_att.at[m * 4 + t],
        lambda i: strip(wdn, i),
        zr_ffn,
        rg_ffn,
        D,
    )

    def attention_family(a):
        kind = (Family, TreeFirst)[a]
        tall = (D, rows)[a]
        return kind(
            lambda m, yy, xx, cc: gatt.at[4 * a + 2 * xx + m, :, att_cols(yy, cc)],
            lambda m, t: rc_att.at[
                4 * a + 2 * m + t // 2, :, pl.ds(pl.multiple_of(lax.rem(t, 2) * 128, 128), 128)
            ],
            lambda i: rx_att.at[a, i, 0:tall],
            zr_att.at[a],
            rg_att.at[a],
            tall,
        )

    att = (attention_family(0), attention_family(1))

    def ffn_free():
        wire.drain()
        for target in (to_y, to_x):
            pl.semaphore_signal(ready.at[0], inc=1, device_id=target, device_id_type=MESH)

    def ffn_chip_send():
        pl.semaphore_wait(ready.at[0], 2)
        ffn.first_send()
        pl.semaphore_signal(ready.at[1], inc=1, device_id=to_c, device_id_type=MESH)

    results = (
        (rg_ffn, ffn_out),
        (rg_att.at[0], att_out.at[0]),
        (rg_att.at[1], att_out.at[1]),
        (mod2, mod_out),
        (cond_all, cond_out),
    )

    def result(i):
        return pltpu.make_async_copy(results[i][0], results[i][1], local.at[i])

    def ffn_finish():
        ffn.collect()
        result(0).start()

    def att_finish(a):
        att[a].collect()
        result(1 + a).start()

    def enc_core_send():
        for xx in range(2):
            wire.push(
                lambda xx=xx: rc_e.at[xx],
                s_rce[xx],
                to_c,
                None,
                lambda xx=xx: egrad.at[pl.ds(pl.multiple_of((2 * xx + 1 - c) * 128, 128), 128), :],
            )

    def enc_rows(xx):
        return egrad.at[pl.ds(pl.multiple_of((2 * xx + c) * 128, 128), 128), :]

    def enc_chip_send():
        for xx in range(2):
            wire.arrived(rc_e.at[xx], s_rce[xx], to_c)
            add_rows(enc_rows(xx), (enc_rows(xx), rc_e.at[xx]), 128)
        for r, (target, xx, _) in enumerate(quad):
            wire.push(
                lambda: rx_e.at[2 * x + y], s_rxe[r], target, None, lambda xx=xx: enc_rows(xx)
            )
        rx_e[2 * x + y] = enc_rows(x)[...]

    def enc_finish():
        for r, (target, xx, yy) in enumerate(quad):
            wire.arrived(rx_e.at[2 * xx + yy], s_rxe[r], target)
        enc_out[...] = jnp.sum(rx_e[...].astype(F), axis=0)

    def shared_core_send():
        to_core = pl.ds(pl.multiple_of(640 * (1 - c), 640), 640)
        wire.push(lambda: rc_g.at[0:640], s_rcg, to_c, None, lambda: tok.at[to_core, :])
        wire.push(
            lambda: rc_g.at[640:896],
            s_rcg4,
            to_c,
            jnp.logical_and(x == 1, c == 1),
            lambda: tok.at[1280:1536, :],
        )
        wire.push(lambda: halo, s_halo, to_y, y == 1, lambda: spec_g.at[0:64, :])

    def part_rows(yy, p):
        return tok.at[pl.ds(pl.multiple_of((2 * c + yy) * ROWS + p * 160, 32), 160), :]

    def core_rows(yy, p):
        return rc_g.at[pl.ds(pl.multiple_of(yy * ROWS + p * 160, 32), 160), :]

    def shared_y_send():
        wire.arrived(rc_g.at[0:640], s_rcg, to_c)
        for p in range(2):
            mine = part_rows(1 - y, p)
            add_rows(mine, (mine, core_rows(1 - y, p)), 160, 32)
            wire.push(
                lambda p=p: rx_g.at[0, p * 160 : p * 160 + 160],
                s_rxy[p],
                to_y,
                None,
                lambda p=p: part_rows(1 - y, p),
            )
        last = jnp.logical_and(x == 1, c == 0)

        @pl.when(last)
        def _():
            wire.arrived(rc_g.at[640:896], s_rcg4, to_c)
            four = tok.at[1280:1536, :]
            add_rows(four, (four, rc_g.at[640:896]), 256)

        wire.push(
            lambda: rx_g.at[1, 0:256],
            s_rcg5,
            to_y,
            jnp.logical_and(last, y == 1),
            lambda: tok.at[1280:1536, :],
        )
        for p in range(2):
            mine = part_rows(y, p)
            add_rows(mine, (mine, core_rows(y, p)), 160, 32)

    def shared_x_send():
        for p in range(2):
            wire.arrived(rx_g.at[0, p * 160 : p * 160 + 160], s_rxy[p], to_y)
            mine = part_rows(y, p)
            add_rows(mine, (mine, rx_g.at[0, p * 160 : p * 160 + 160]), 160, 32)
            wire.push(
                lambda p=p: rx_g.at[1, p * 160 : p * 160 + 160],
                s_rxx[p],
                to_x,
                x == 1,
                lambda p=p: part_rows(y, p),
            )

    def shared_arrived():
        for p in range(2):
            wire.arrived(rx_g.at[1, p * 160 : p * 160 + 160], s_rxx[p], to_x, x == 0)
        wire.arrived(rx_g.at[1, 0:256], s_rcg5, to_y, ci == 4)

    def tree_peers(make):
        @pl.loop(1, 8)
        def _(k):
            make(k, lax.rem(ci + k, 8), lax.rem(ci + 8 - k, 8))

    def device_of(i):
        return {"ctx": i // 2, "tp": lax.rem(i, 2)}

    def mod_1(k, to):
        return wire.copy(mgrad, mod1.at[ci], s_m1 + k, device_of(to))

    def mod_2(k, to):
        return wire.copy(mod2.at[fs], mod2.at[fs], s_m2 + k, {"fsdp": to})

    def mod_tree_send():
        tree_peers(lambda k, to, _: mod_1(k, to).start())
        mod1[ci] = mgrad[...]

    def mod_all_send():
        tree_peers(lambda k, _, src: wire.arrived(mod1.at[src], s_m1 + k, device_of(src)))
        mod2[fs] = jnp.sum(mod1[...], axis=0)
        peers(lambda k, to, _: mod_2(k, to).start())

    def mod_finish():
        peers(lambda k, _, src: wire.arrived(mod2.at[src], s_m2 + k, {"fsdp": src}))
        result(3).start()
        result(4).start()

    def leave(step):
        if step == 0:
            ffn_free()
        if step == 1:
            ffn_chip_send()
        if step == 2:
            pl.semaphore_wait(ready.at[1], 1)
            att[1].core_send()
            enc_core_send()
        if step == 3:
            att[1].first_send()
            enc_chip_send()
        if step == 4:
            ffn.second_send()
        if step == 5:
            ffn.tree_send()
        if step == 6:
            shared_core_send()
        if step == 7:
            shared_y_send()
            att[0].first_send()
            att[1].sum_trees()
            enc_finish()
            shared_x_send()
        if step == 8:
            att[1].second_send()
            att[0].second_send()
            ffn.copy_send()
            shared_arrived()
        if step == 9:
            mod_tree_send()
            att[0].tree_send()
            att[1].copy_send()
            ffn.relay_copy()
            mod_all_send()
            att[0].copy_send()
            att[1].relay_copy()
            ffn_finish()
            mod_finish()
            att[0].relay_copy()
            att_finish(1)
            att_finish(0)

    def hidden(x):
        n, _ = normed(x.astype(F))
        return (n * (1.0 + sa) + ba).astype(BF)

    def hid_trunk(rs):
        hid[rs, :] = hidden(tok_tb[rs, :])

    row_loop(TRK, 32, hid_trunk, 8)

    def hid_loc(rs):
        hloc[rs, :] = hidden(tok_loc[rs, :])

    row_loop(LOC, 32, hid_loc, 6)
    for lb in range(3):
        picks = [is_parent(lb, b) for b in range(1, BRANCHES)]
        for piece in range(4):
            r = piece * 32
            picked = tok_tb[TRK + r : TRK + r + 32, :].astype(F)
            for b in range(1, BRANCHES):
                at = TRK + b * BLK + r
                picked = jnp.where(picks[b - 1], tok_tb[at : at + 32, :].astype(F), picked)
            at = TRK + lb * 256 + r
            hid[at : at + 32, :] = hidden(picked)
        hid[TRK + lb * 256 + BLK : TRK + lb * 256 + 2 * BLK, :] = hloc[
            lb * BLK : (lb + 1) * BLK, :
        ]

    def project(rs):
        kbuf[rs, :] = nn(hid[rs, :], watt[1]).astype(BF)
        vbuf[rs, :] = nn(hid[rs, :], watt[2]).astype(BF)

    z_done(2)
    c_done(0)
    row_loop(KV, 256, project)
    qbuf[...] = (nn(hloc[...], watt[0]) * 0.125).astype(BF)

    linv_a, linv_b = wk_acc.at[0:ROWS, :], wv_acc.at[0:ROWS, :]

    def with_ones(values, half):
        return jnp.where(half_lanes(values.shape, half), values, jnp.ones_like(values))

    def finish_heads(o0, o1, mixed, linv, lanes):
        inv0, inv1 = 1.0 / pltpu.roll(o0, HD, 1), 1.0 / pltpu.roll(o1, HD, 1)
        first = half_lanes(o0.shape, 0)
        mixed[:, lanes] = jnp.where(first, o0 * inv0, o1 * inv1).astype(BF)
        linv[:, lanes] = jnp.where(first, inv0, inv1)

    @pl.loop(0, 4)
    def _(hp):
        for step in (1, 2):

            @pl.when(hp == step)
            def _(step=step):
                relay(step)

        lanes = pl.ds(pl.multiple_of(hp * 128, 128), 128)
        kt = kbuf[0:TRK, lanes]
        vt = vbuf[0:TRK, lanes]
        outs = []
        for half in range(2):
            h = hp * 2 + half
            st[...] = nt(keep(qbuf[own, lanes], half), kt) + bias_t[...].astype(F)
            for lb in range(3):
                r = slice(lb * BLK, (lb + 1) * BLK)
                ks = kbuf[TRK + lb * 256 : TRK + (lb + 1) * 256, lanes]
                ss[r, :] = nt(keep(qbuf[r, lanes], half), ks) + bias_s[r, :].astype(F)
            for i in range(ROWS // 32):
                rs = slice(i * 32, i * 32 + 32)
                ro = pl.ds(pl.multiple_of(i * 32 + off, 32), 32)
                a, b = st[rs, :], ss[ro, :]
                top = jnp.maximum(
                    jnp.max(a, axis=-1, keepdims=True), jnp.max(b, axis=-1, keepdims=True)
                )
                pt[h, rs, :] = jnp.exp(a - top).astype(BF)
                ps[h, ro, :] = jnp.exp(b - top).astype(BF)
            for lb in range(3):
                r = slice(lb * BLK, (lb + 1) * BLK)
                vs = vbuf[TRK + lb * 256 : TRK + (lb + 1) * 256, lanes]
                spec_o[half, r, :] = nn(ps[h, r, :], with_ones(vs, half))
            outs.append(nn(pt[h], with_ones(vt, half)) + spec_o[half, own, :])
        finish_heads(outs[0], outs[1], mixa, linv_a, lanes)

    relay(4)
    t0[...] = nt(mixa[...], watt[3])

    def after_self(rs):
        sbv = tok_own[rs, :].astype(F) + t0[rs, :]
        stream_b[rs, :] = sbv
        n, _ = normed(sbv)
        hid_b[rs, :] = (n * (1.0 + sb) + bb).astype(BF)

    row_loop(ROWS, 32, after_self, 0)

    relay(7)
    kenc[...] = nn(enc[...], watt[5]).astype(BF)
    venc[...] = nn(enc[...], watt[6]).astype(BF)
    qb[...] = (nn(hid_b[...], watt[4]) * 0.125).astype(BF)

    @pl.loop(0, 4)
    def _(hp):
        lanes = pl.ds(pl.multiple_of(hp * 128, 128), 128)
        kt = kenc[:, lanes]
        vt = venc[:, lanes]
        outs = []
        for half in range(2):
            h = hp * 2 + half
            t0[...] = nt(keep(qb[:, lanes], half), kt)
            for i in range(ROWS // 32):
                rs = slice(i * 32, i * 32 + 32)
                a = t0[rs, :]
                pe[h, rs, :] = jnp.exp(a - jnp.max(a, axis=-1, keepdims=True)).astype(BF)
            outs.append(nn(pe[h], with_ones(vt, half)))
        finish_heads(outs[0], outs[1], mixb, linv_b, lanes)

    relay(5)
    t0[...] = nt(mixb[...], watt[7])

    def after_cross(rs):
        scv = stream_b[rs, :] + t0[rs, :]
        stream_c[rs, :] = scv
        n, _ = normed(scv)
        hid_c[rs, :] = (n * (1.0 + sf) + bf_).astype(BF)

    row_loop(ROWS, 32, after_cross, 0)

    relay(6)
    acc0[...] = jnp.zeros_like(acc0)
    acc1[...] = jnp.zeros_like(acc1)

    def flip(v, by):
        return v + by - 2 * v * by

    @pl.loop(0, 4)
    def _(ft):
        @pl.when(ft == 2)
        def _():
            x_done(4, 1)
            x_done(5, 1)

        for part in range(4):

            @pl.when(ft == part)
            def _(part=part):
                c_part(4, part)
                c_part(5, part)

        tile = flip(y, lax.rem(ft, 2)) * 2 + flip(x, ft // 2)
        cols = pl.ds(pl.multiple_of(tile * 512, 512), 512)
        t0[...] = nn(hid_c[...], wup[:, cols])
        t1[...] = nn(cot[...], wdn[:, cols])

        def gelu(rs):
            u = t0[rs, :]
            phi = 0.5 * (1.0 + lax.erf(u * (2.0**-0.5)))
            b0[rs, :] = (u * phi).astype(BF)
            slope = phi + u * (jnp.exp(-0.5 * u * u) * (1.0 / math.sqrt(2.0 * math.pi)))
            b1[rs, :] = (t1[rs, :] * slope).astype(BF)

        row_loop(ROWS, 32, gelu)
        acc0[...] += nt(b0[...], wdn[:, cols])
        acc1[...] += nt(b1[...], wup[:, cols])
        gffn[1, :, cols] = tn(cot[...], b0[...]).astype(BF)
        gffn[0, :, cols] = tn(hid_c[...], b1[...]).astype(BF)
        for m in range(2):
            ffn.core_copy(m, tile).start()

    def back_norm(at, scale, grad_src, stream_src, base_src, want_out):
        sums = [jnp.zeros((1, D), F), jnp.zeros((1, D), F)]
        for i in range(ROWS // 32):
            rs = slice(i * 32, i * 32 + 32)
            back, ds, db = norm_back(grad_src[rs, :], stream_src[rs, :], scale)
            total = base_src[rs, :].astype(F) + back
            in_grad[rs, :] = total
            gbf[rs, :] = total.astype(BF)
            sums = [sums[0] + ds, sums[1] + db]
            if want_out:
                out_ref[rs, :] = (stream_c[rs, :] + acc0[rs, :]).astype(BF)
        mgrad[at : at + 1, :] = sums[0]
        mgrad[at + 1 : at + 2, :] = sums[1]

    leave(0)
    back_norm(4, sf, acc1, stream_c, cot, True)

    gatt[7] = tn(gbf[...], mixb[...]).astype(BF)
    mgr[...] = (nn(gbf[...], watt[7]) * linv_b[...]).astype(BF)
    leave(1)

    @pl.loop(0, 4)
    def _(hp):
        lanes = pl.ds(pl.multiple_of(hp * 128, 128), 128)
        prod = mgr[:, lanes].astype(F) * mixb[:, lanes].astype(F)
        dqs, dks, dvs = [], [], []
        for half in range(2):
            h = hp * 2 + half
            inner = jnp.sum(keep(prod, half), axis=-1, keepdims=True)
            mg = keep(mgr[:, lanes], half)
            dp = nt(mg, venc[:, lanes])
            b0[...] = (pe[h].astype(F) * (dp - inner)).astype(BF)
            dqs.append(nn(b0[...], kenc[:, lanes]))
            dks.append(tn(b0[...], keep(qb[:, lanes], half)))
            dvs.append(tn(pe[h], mg))
        dq[:, lanes] = (jnp.where(half_lanes(dqs[0].shape, 0), dqs[0], dqs[1]) * 0.125).astype(BF)
        kenc[:, lanes] = (dks[0] + dks[1]).astype(BF)
        venc[:, lanes] = (dvs[0] + dvs[1]).astype(BF)

    gatt[4] = tn(hid_b[...], dq[...]).astype(BF)
    gatt[5] = tn(enc[...], kenc[...]).astype(BF)
    gatt[6] = tn(enc[...], venc[...]).astype(BF)
    egrad[...] = (nt(kenc[...], watt[5]) + nt(venc[...], watt[6])).astype(BF)
    leave(2)
    acc1[...] = nt(dq[...], watt[4])
    back_norm(2, sb, acc1, stream_b, in_grad, False)

    gatt[3] = tn(gbf[...], mixa[...]).astype(BF)
    mgr[...] = (nn(gbf[...], watt[3]) * linv_a[...]).astype(BF)
    leave(3)

    @pl.when(odd == 0)
    def _():
        for h in range(8):
            ps[h, ROWS:LOC, :] = jnp.zeros((LOC - ROWS, 256), BF)
        spec_o[:, ROWS:LOC, :] = jnp.zeros((2, LOC - ROWS, 128), F)

    @pl.when(odd == 1)
    def _():
        for h in range(8):
            ps[h, 0:64, :] = jnp.zeros((64, 256), BF)
        spec_o[:, 0:64, :] = jnp.zeros((2, 64, 128), F)

    @pl.loop(0, 4)
    def _(turn):
        side = jnp.where(turn < 2, 1 - c, c)
        band = jnp.where(turn < 2, turn, jnp.where(turn == 2, 1 - y, y))
        hp = band * 2 + side
        lanes = pl.ds(pl.multiple_of(hp * 128, 128), 128)
        prod = mgr[:, lanes].astype(F) * mixa[:, lanes].astype(F)
        dqs, dks, dvs = [], [], []
        dks_s = [[], [], []]
        dvs_s = [[], [], []]
        for half in range(2):
            h = hp * 2 + half
            inner = jnp.sum(keep(prod, half), axis=-1, keepdims=True)
            mg = keep(mgr[:, lanes], half)
            qm = keep(qbuf[own, lanes], half)
            dp = nt(mg, vbuf[0:TRK, lanes])
            ds = (pt[h].astype(F) * (dp - inner)).astype(BF)
            spec_o[0, own, :] = mg.astype(F)
            spec_o[1, own, :] = jnp.broadcast_to(inner, (ROWS, 128))
            dq_s = []
            for lb in range(3):
                r = slice(lb * BLK, (lb + 1) * BLK)
                k_rows = slice(TRK + lb * 256, TRK + (lb + 1) * 256)
                mgl = spec_o[0, r, :].astype(BF)
                dpl = nt(mgl, vbuf[k_rows, lanes])
                inner_l = spec_o[1, r, 0:1]
                dsl = (ps[h, r, :].astype(F) * (dpl - inner_l)).astype(BF)
                ss[r, 0:128] = nn(dsl, kbuf[k_rows, lanes])
                dks_s[lb].append(tn(dsl, keep(qbuf[r, lanes], half)))
                dvs_s[lb].append(tn(ps[h, r, :], mgl))
            dqs.append(nn(ds, kbuf[0:TRK, lanes]) + ss[own, 0:128])
            dks.append(tn(ds, qm))
            dvs.append(tn(pt[h], mg))
        dq[:, lanes] = (jnp.where(half_lanes(dqs[0].shape, 0), dqs[0], dqs[1]) * 0.125).astype(BF)
        kbuf[0:TRK, lanes] = (dks[0] + dks[1]).astype(BF)
        vbuf[0:TRK, lanes] = (dvs[0] + dvs[1]).astype(BF)
        for lb in range(3):
            k_rows = slice(TRK + lb * 256, TRK + (lb + 1) * 256)
            kbuf[k_rows, lanes] = (dks_s[lb][0] + dks_s[lb][1]).astype(BF)
            vbuf[k_rows, lanes] = (dvs_s[lb][0] + dvs_s[lb][1]).astype(BF)

        total = None
        for at in range(0, KV, KV // 2):
            rs = slice(at, at + KV // 2)
            both = jnp.concatenate([kbuf[rs, lanes], vbuf[rs, lanes]], axis=1)
            part = tn(both, hid[rs, :])
            total = part if total is None else total + part
        kv_grad = jnp.transpose(total)
        gatt[1, :, lanes] = kv_grad[:, 0:128].astype(BF)
        gatt[2, :, lanes] = kv_grad[:, 128:256].astype(BF)
        gatt[0, :, lanes] = tn(hloc[own, :], dq[:, lanes]).astype(BF)

        @pl.when(turn < 2)
        def _():
            for m in range(2):
                for xx in range(2):
                    att[0].core_copy(m, band * 2 + xx).start()

        @pl.when(turn == 1)
        def _():
            leave(4)

        @pl.when(turn == 3)
        def _():
            leave(5)

    def key_grad(rs):
        return (nt(kbuf[rs, :], watt[1]) + nt(vbuf[rs, :], watt[2])).astype(BF)

    for lb in range(3):
        pe[lb, 0:256, :] = key_grad(slice(TRK + lb * 256, TRK + (lb + 1) * 256))

    def trunk_grad(rs):
        tok[rs, :] = key_grad(rs)

    row_loop(TRK, 256, trunk_grad)

    for b in range(BRANCHES):
        hits = [is_parent(lb, b) for lb in range(3)]
        for piece in range(4):
            total = jnp.zeros((32, D), F)
            for lb in range(3):
                at = piece * 32
                total += jnp.where(hits[lb], pe[lb, at : at + 32, :].astype(F), 0.0)
            at = TRK + b * BLK + piece * 32
            tok[at : at + 32, :] = total.astype(BF)
    for lb in range(3):
        spec_g[lb * BLK : (lb + 1) * BLK, :] = pe[lb, BLK : 2 * BLK, :]

    leave(6)
    acc1[...] = nt(dq[...], watt[0])

    def own_sum(rs):
        extra = spec_g[pl.ds(pl.multiple_of(rs.start + off, 32), 32), :].astype(F)
        acc1[rs, :] += extra

    row_loop(ROWS, 32, own_sum, 5)
    leave(7)
    leave(8)

    wire.arrived(halo, s_halo, to_y, y == 0)

    @pl.when(y == 0)
    def _():
        acc1[ROWS - 64 : ROWS, :] += halo[...].astype(F)

    @pl.when(x == 0)
    def _():
        def body(rs):
            mine = tok[pl.ds(pl.multiple_of(ci * ROWS + rs.start, 32), 32), :].astype(F)
            acc1[rs, :] += mine + rx_g[1, rs, :].astype(F)

        row_loop(ROWS, 32, body)

    @pl.when(ci == 4)
    def _():
        def body(rs):
            mine = tok[pl.ds(pl.multiple_of(4 * ROWS + rs.start, 32), 32), :].astype(F)
            acc1[rs, :] += mine + rx_g[1, rs, :].astype(F)

        row_loop(256, 32, body)

    mgrad[6:8, :] = jnp.zeros((2, D), F)
    sums = [jnp.zeros((1, D), F), jnp.zeros((1, D), F)]
    for i in range(ROWS // 32):
        rs = slice(i * 32, i * 32 + 32)
        back, ds, db = norm_back(acc1[rs, :], tok_own[rs, :].astype(F), sa)
        in_grad[rs, :] += back
        sums = [sums[0] + ds, sums[1] + db]
    mgrad[0:1, :] = sums[0]
    mgrad[1:2, :] = sums[1]
    leave(9)

    for i in range(5):
        result(i).wait()
    wire.drain()
    for family in (ffn, *att):
        family.drain()
    tree_peers(lambda k, to, _: mod_1(k, to).wait_send())
    peers(lambda k, to, _: mod_2(k, to).wait_send())
    peers(
        lambda k, to, _: wire.copy(
            cond_parts.at[to], cond_all.at[fs], s_cond + k, {"fsdp": to}
        ).wait_send()
    )
    peers(
        lambda k, to, _: wire.copy(
            part_out.at[to], part_in.at[fs], s_part + k, {"fsdp": to}
        ).wait_send()
    )
    for g in range(6):
        peers(
            lambda k, to, _, g=g: wire.copy(
                groups[g][0], place(g, my_rows, y, x, c), s_z[g] + k, {"fsdp": to}
            ).wait_send()
        )


def layer_call(n, parents, cond_parts, w_mod, tokens, enc, cot, weights):
    vm = pl.BlockSpec(memory_space=pltpu.VMEM)
    hbm = pl.BlockSpec(memory_space=pl.ANY)
    sds = jax.ShapeDtypeStruct
    rows = w_mod.shape[0]
    return pl.pallas_call(
        functools.partial(layer_kernel, n),
        out_shape=(
            sds((ROWS, D), BF),
            sds((ROWS, D), F),
            sds((ENC // 4, D), F),
            sds((n, 8, D), F),
            sds(cond_parts.shape, F),
            sds((2, 4, 2, rows, 128), BF),
            sds((4, 2, rows, 256), BF),
        ),
        in_specs=[pl.BlockSpec(memory_space=pltpu.SMEM), vm, vm, hbm, hbm, vm] + [hbm] * 6,
        out_specs=(vm, vm, vm, hbm, hbm, hbm, hbm),
        scratch_shapes=[
            pltpu.VMEM((8, D, D), BF),
            pltpu.VMEM((D, FF), BF),
            pltpu.VMEM((D, FF), BF),
            pltpu.VMEM((8 * ROWS + 64, D), BF),
            pltpu.VMEM((ENC, D), BF),
            pltpu.VMEM((n, 8, D), F),
            pltpu.VMEM((n, 8, D), F),
            pltpu.VMEM((8, D), F),
            pltpu.VMEM((*cond_parts.shape,), F),
            pltpu.VMEM((ROWS, D), BF),
            pltpu.VMEM((8, D), F),
            pltpu.VMEM((KV, D), BF),
            pltpu.VMEM((LOC, D), BF),
            pltpu.VMEM((KV, D), BF),
            pltpu.VMEM((KV, D), BF),
            pltpu.VMEM((LOC, D), BF),
            pltpu.VMEM((8, ROWS, TRK), BF),
            pltpu.VMEM((8, LOC, 256), BF),
            pltpu.VMEM((ROWS, TRK), BF),
            pltpu.VMEM((LOC, 256), BF),
            pltpu.VMEM((ROWS, TRK), F),
            pltpu.VMEM((LOC, 256), F),
            pltpu.VMEM((2, LOC, 128), F),
            pltpu.VMEM((ROWS, D), BF),
            pltpu.VMEM((ROWS, D), F),
            pltpu.VMEM((ROWS, D), F),
            pltpu.VMEM((ROWS, D), BF),
            pltpu.VMEM((ROWS, D), BF),
            pltpu.VMEM((ENC, D), BF),
            pltpu.VMEM((ENC, D), BF),
            pltpu.VMEM((ROWS, D), BF),
            pltpu.VMEM((8, ROWS, ENC), BF),
            pltpu.VMEM((ROWS, D), BF),
            pltpu.VMEM((ROWS, D), BF),
            pltpu.VMEM((ROWS, D), BF),
            pltpu.VMEM((ROWS, D), F),
            pltpu.VMEM((ROWS, D), F),
            pltpu.VMEM((ROWS, D), BF),
            pltpu.VMEM((ROWS, D), BF),
            pltpu.VMEM((ROWS, D), BF),
            pltpu.VMEM((D, D), F),
            pltpu.VMEM((ROWS, D), F),
            pltpu.VMEM((8, D, D), BF),
            pltpu.VMEM((2, D, FF), BF),
            pltpu.VMEM((8, D, 256), BF),
            pltpu.VMEM((2, 6, D, 128), BF),
            pltpu.VMEM((2, n, 2, rows, 128), BF),
            pltpu.VMEM((2, 4, 2, rows, 128), BF),
            pltpu.VMEM((n, 2, 4, rows, 128), BF),
            pltpu.VMEM((2, 4, rows, 128), BF),
            pltpu.VMEM((n, 2, rows, 256), BF),
            pltpu.VMEM((4, 2, rows, 256), BF),
            pltpu.VMEM((896, D), BF),
            pltpu.VMEM((2, ROWS, D), BF),
            pltpu.VMEM((64, D), BF),
            pltpu.VMEM((2, 128, D), BF),
            pltpu.VMEM((4, 128, D), BF),
            pltpu.VMEM((8, 8, D), F),
            pltpu.VMEM((n, 8, D), F),
            pltpu.SemaphoreType.DMA((16 * n + 160,)),
            pltpu.SemaphoreType.DMA((16 * n + 160,)),
            pltpu.SemaphoreType.DMA((9,)),
            pltpu.SemaphoreType.REGULAR((2,)),
        ],
        compiler_params=pltpu.CompilerParams(
            vmem_limit_bytes=VMEM_LIMIT, collective_id=0, has_side_effects=True
        ),
        name="layer",
    )(parents, cond_parts, w_mod, tokens, enc, cot, *weights)


def finish_kernel(
    n, rows, out, grad, enc, mod, cond, att, ffn, o_out, o_grad, o_enc, o_mod, qkv, so, cqkv, co, up, dn
):
    o_out[...] = out[...]
    o_grad[...] = grad[...]
    o_enc[...] = enc[...]
    for v in range(6):
        o_mod[:, v * D : (v + 1) * D] = lax.dot_general(
            cond[:, 0, 0:rows],
            mod[:, v, :],
            (((0,), (0,)), ((), ())),
            precision=lax.Precision.HIGHEST,
            preferred_element_type=F,
        )
    for q in range(4):
        up[:, q * 256 : (q + 1) * 256] = ffn[q, 0].astype(F)
        dn[:, q * 256 : (q + 1) * 256] = ffn[q, 1].astype(F)
        cols = slice((q % 2) * 128, (q % 2) * 128 + 128)
        for a, (stack, single) in enumerate(((qkv, so), (cqkv, co))):
            for m in range(2):
                value = att[a, q, m].astype(F)
                at = 2 * (q // 2) + m
                if at < 3:
                    stack[at, :, cols] = value
                else:
                    single[:, cols] = value


def finish_call(n, rows, *parts):
    vm = pl.BlockSpec(memory_space=pltpu.VMEM)
    sds = jax.ShapeDtypeStruct
    return pl.pallas_call(
        functools.partial(finish_kernel, n, rows),
        out_shape=(
            sds((ROWS, D), BF),
            sds((ROWS, D), F),
            sds((ENC // 4, D), F),
            sds((rows, 6 * D), F),
            sds((3, rows, 256), F),
            sds((rows, 256), F),
            sds((3, rows, 256), F),
            sds((rows, 256), F),
            sds((rows, 1024), F),
            sds((rows, 1024), F),
        ),
        in_specs=[vm] * 7,
        out_specs=(vm,) * 10,
        name="finish",
    )(*parts)


def timestep_code(timesteps, width):
    half = width // 2
    frequency = jnp.exp(-math.log(10000.0) * jnp.arange(half, dtype=F) / half)
    angles = timesteps.astype(F)[:, None] * frequency[None, :]
    return jnp.concatenate([jnp.sin(angles), jnp.cos(angles)], axis=-1)


def per_device(
    tokens,
    encoder_states,
    timesteps,
    parents,
    w_mod,
    w_self_qkv,
    w_self_out,
    w_cross_qkv,
    w_cross_out,
    w_up,
    w_down,
    cotangent,
):
    rows = w_mod.shape[0]
    condition = jax.nn.silu(timestep_code(timesteps, D)).astype(BF)
    n = lax.axis_size("fsdp")
    padded_cond = jnp.pad(condition.astype(F).reshape(n, 1, rows), ((0, 0), (0, 7), (0, max(128 - rows, 0))))
    parts = layer_call(
        n,
        parents,
        padded_cond,
        w_mod,
        tokens,
        encoder_states,
        cotangent[0],
        (w_self_qkv, w_self_out, w_cross_qkv, w_cross_out, w_up, w_down),
    )
    out, in_grad, enc_grad, grad_mod, *weights = finish_call(n, rows, *parts)
    return (out[None], in_grad[None], enc_grad[None], grad_mod, *weights)


def solution(mesh):
    rows = P("fsdp", ("ctx", "tp"), None)
    return jax.shard_map(
        per_device,
        mesh=mesh,
        in_specs=(
            rows,
            P("fsdp", "ctx", None),
            P("fsdp"),
            P("fsdp", None),
            P("fsdp", None),
            P(None, "fsdp", "tp"),
            P("fsdp", "tp"),
            P(None, "fsdp", "tp"),
            P("fsdp", "tp"),
            P("fsdp", "tp"),
            P("fsdp", "tp"),
            rows,
        ),
        out_specs=(
            rows,
            rows,
            P("fsdp", "ctx", None),
            P("fsdp", None),
            P(None, "fsdp", "tp"),
            P("fsdp", "tp"),
            P(None, "fsdp", "tp"),
            P("fsdp", "tp"),
            P("fsdp", "tp"),
            P("fsdp", "tp"),
        ),
        check_vma=False,
    )
```

```python
import functools
import math

import jax
import jax.numpy as jnp
from jax import lax
from jax.experimental import pallas as pl
from jax.experimental.pallas import tpu as pltpu
from jax.sharding import PartitionSpec as P

BF = jnp.bfloat16
F = jnp.float32
D = 512
FF = 2048
HD = 64
ROWS = 320
LOC = 384
BLK = 128
TRUNK = 8
BRANCHES = 4
TRK = TRUNK * BLK
SHARED = (TRUNK + BRANCHES) * BLK
SPEC = 2 * LOC
KV = TRK + SPEC
ENC = 512
EPS = 1e-05
NEG = -1e30
VMEM_LIMIT = 67043328


def nn(a, b):
    return lax.dot_general(a, b, (((1,), (0,)), ((), ())), preferred_element_type=F)


def nt(a, b):
    return lax.dot_general(a, b, (((1,), (1,)), ((), ())), preferred_element_type=F)


def tn(a, b):
    return lax.dot_general(a, b, (((0,), (0,)), ((), ())), preferred_element_type=F)


def normed(v):
    center = v - jnp.mean(v, axis=-1, keepdims=True)
    rstd = lax.rsqrt(jnp.mean(center * center, axis=-1, keepdims=True) + EPS)
    return center * rstd, rstd


def norm_back(grad, stream, scale):
    n, rstd = normed(stream)
    gn = grad * (1.0 + scale)
    back = rstd * (
        gn
        - jnp.mean(gn, axis=-1, keepdims=True)
        - n * jnp.mean(gn * n, axis=-1, keepdims=True)
    )
    return back, jnp.sum(grad * n, axis=0, keepdims=True), jnp.sum(grad, axis=0, keepdims=True)


def row_loop(total, step, body, unroll=1):
    if unroll == 0:
        for i in range(total // step):
            body(pl.ds(i * step, step))
        return

    @pl.loop(0, total // (step * unroll))
    def _(i):
        for j in range(unroll):
            body(pl.ds(pl.multiple_of((i * unroll + j) * step, step), step))


def half_lanes(shape, half):
    lane = lax.broadcasted_iota(jnp.int32, shape, len(shape) - 1)
    return (lane // HD) == half


def keep(value, half):
    return jnp.where(half_lanes(value.shape, half), value, jnp.zeros_like(value))


MESH = pl.DeviceIdType.MESH


class Wire:
    def __init__(self, send, recv):
        self.send, self.recv, self.used, self.sent = send, recv, 0, []

    def slot(self, count=1):
        self.used += count
        return self.used - count

    def copy(self, src, dst, at, to):
        return pltpu.make_async_remote_copy(
            src_ref=src,
            dst_ref=dst,
            send_sem=self.send.at[at],
            recv_sem=self.recv.at[at],
            device_id=to,
            device_id_type=MESH,
        )

    def push(self, dst, at, to, when=None, src=None):
        src = src or dst
        if when is None:
            self.copy(src(), dst(), at, to).start()
        else:

            @pl.when(when)
            def _():
                self.copy(src(), dst(), at, to).start()

        self.sent.append((src, dst, at, to, when))

    def arrived(self, dst, at, to, when=None):
        if when is None:
            self.copy(dst, dst, at, to).wait_recv()
        else:

            @pl.when(when)
            def _():
                self.copy(dst, dst, at, to).wait_recv()

    def drain(self):
        for src, dst, at, to, when in self.sent:
            if when is None:
                self.copy(src(), dst(), at, to).wait_send()
            else:

                @pl.when(when)
                def _(src=src, dst=dst, at=at, to=to):
                    self.copy(src(), dst(), at, to).wait_send()

        self.sent = []


def layer_kernel(
    n,
    parents_ref,
    cond_parts,
    w_mod,
    tok_in,
    enc_in,
    cot,
    w_sqkv,
    w_so,
    w_cqkv,
    w_co,
    w_up,
    w_dn,
    out_ref,
    in_grad,
    enc_out,
    mod_out,
    cond_out,
    att_out,
    ffn_out,
    watt,
    wup,
    wdn,
    tok,
    enc,
    part_out,
    part_in,
    mod,
    cond_all,
    tok_own,
    mgrad,
    hid,
    hloc,
    kbuf,
    vbuf,
    qbuf,
    pt,
    ps,
    bias_t,
    bias_s,
    st,
    ss,
    spec_o,
    mixa,
    stream_b,
    stream_c,
    hid_b,
    hid_c,
    kenc,
    venc,
    qb,
    pe,
    mixb,
    b0,
    b1,
    acc0,
    acc1,
    gbf,
    mgr,
    dq,
    wk_acc,
    wv_acc,
    gatt,
    gffn,
    rc_att,
    rx_att,
    zr_att,
    rg_att,
    zl_att,
    zs_att,
    zr_ffn,
    rg_ffn,
    rc_g,
    rx_g,
    halo,
    rc_e,
    rx_e,
    mod1,
    mod2,
    send,
    recv,
    local,
    ready,
):
    t0, t1 = st.at[:, 0:D], st.at[:, D : 2 * D]
    egrad = enc
    fs = lax.axis_index("fsdp")
    cx = lax.axis_index("ctx")
    y = lax.axis_index("tp")
    x, c = cx // 2, lax.rem(cx, 2)
    ci = cx * 2 + y
    odd = y
    off = pl.multiple_of(odd * 64, 64)
    own = pl.ds(off, ROWS)
    base = (ci * 5) // 2
    rows = w_mod.shape[0]
    to_y = {"tp": 1 - y}
    to_c = {"ctx": 2 * x + 1 - c}
    to_x = {"ctx": 2 * (1 - x) + c}
    wire = Wire(send, recv)

    my_rows = pl.ds(pl.multiple_of(fs * rows, rows), rows)

    def att_cols(yy, cc):
        return pl.ds(pl.multiple_of(yy * 256 + cc * 128, 128), 128)

    def ffn_cols(yy, xx, cc):
        return pl.ds(pl.multiple_of(yy * 1024 + xx * 512 + cc * 256, 256), 256)

    half = pl.ds(pl.multiple_of(c * 128, 128), 128)
    quarter = pl.ds(pl.multiple_of(cx * 256, 256), 256)
    groups = (
        (w_sqkv.at[:, :, half], watt, slice(0, 3), 0),
        (w_so.at[:, half], watt, 3, 0),
        (w_cqkv.at[:, :, half], watt, slice(4, 7), 0),
        (w_co.at[:, half], watt, 7, 0),
        (w_up.at[:, quarter], wup, None, 1),
        (w_dn.at[:, quarter], wdn, None, 1),
    )

    def place(g, row_at, yy, xx, cc):
        _, buf, index, wide = groups[g]
        if wide:
            return buf.at[row_at, ffn_cols(yy, xx, cc)]
        return buf.at[index, row_at, att_cols(yy, cc)]

    def chunk(i):
        return tok.at[pl.ds(pl.multiple_of(i * ROWS, ROWS), ROWS), :]

    def enc_part(i):
        return enc.at[pl.ds(pl.multiple_of(i * 128, 128), 128), :]

    all_rows = pl.ds(0, D)

    local_copies = [
        pltpu.make_async_copy(tok_in.at[0], chunk(ci), local.at[0]),
        pltpu.make_async_copy(enc_in.at[0], enc_part(cx), local.at[1]),
    ] + [
        pltpu.make_async_copy(groups[g][0], place(g, my_rows, y, x, c), local.at[2 + g])
        for g in range(6)
    ]
    local_copies.append(pltpu.make_async_copy(tok_in.at[0], tok_own, local.at[8]))
    for copy in local_copies:
        copy.start()

    barrier = pltpu.get_barrier_semaphore()

    @pl.loop(1, n)
    def _(k):
        pl.semaphore_signal(
            barrier, inc=1, device_id={"fsdp": lax.rem(fs + k, n)}, device_id_type=MESH
        )

    @pl.loop(1, 8)
    def _(k):
        other = lax.rem(ci + k, 8)
        pl.semaphore_signal(
            barrier,
            inc=1,
            device_id={"ctx": other // 2, "tp": lax.rem(other, 2)},
            device_id_type=MESH,
        )

    pl.semaphore_wait(barrier, n - 1 + 7)

    def peers(make):
        @pl.loop(1, n)
        def _(k):
            make(k, lax.rem(fs + k, n), lax.rem(fs + n - k, n))

    s_cond = wire.slot(n)
    s_part = wire.slot(n)
    s_z = [wire.slot(n) for _ in range(6)]
    s_y = [wire.slot() for _ in range(6)]
    s_c0 = [wire.slot() for _ in range(6)]
    s_c1 = [wire.slot() for _ in range(6)]
    s_x0 = [wire.slot() for _ in range(6)]
    s_x1 = [wire.slot() for _ in range(6)]
    s_c2 = [wire.slot() for _ in range(6)]
    s_c3 = [wire.slot() for _ in range(6)]
    s_ty, s_tx, s_txy, s_tc0, s_tc1, s_tc2, s_tc3, s_ty2 = (
        wire.slot() for _ in range(8)
    )
    s_ex, s_ec0, s_ec1 = (wire.slot() for _ in range(3))

    peers(
        lambda k, to, _: wire.copy(
            cond_parts.at[to], cond_all.at[fs], s_cond + k, {"fsdp": to}
        ).start()
    )
    left = x == 0

    def tail_rows(i):
        return tok.at[pl.ds(pl.multiple_of(i * ROWS + ROWS - 64, 64), 64), :]

    wire.push(
        lambda: chunk(ci), s_ty, to_y, jnp.logical_or(left, ci == 4), lambda: tok_in.at[0]
    )
    wire.push(
        lambda: tail_rows(ci), s_ty2, to_y, ci == 6, lambda: tok_in.at[0, ROWS - 64 : ROWS, :]
    )
    wire.push(lambda: chunk(ci), s_tx, to_x, x == 0, lambda: tok_in.at[0])
    wire.push(
        lambda: chunk(ci), s_tc0, to_c, jnp.logical_or(left, ci == 4), lambda: tok_in.at[0]
    )

    def z_start(g):
        peers(
            lambda k, to, _: wire.copy(
                groups[g][0], place(g, my_rows, y, x, c), s_z[g] + k, {"fsdp": to}
            ).start()
        )

    z_start(0)

    def mask_trunk(rs):
        row = lax.broadcasted_iota(jnp.int32, (32, TRK), 0) + rs.start + ci * ROWS
        col = lax.broadcasted_iota(jnp.int32, (32, TRK), 1)
        bias_t[rs, :] = jnp.where(col <= row, 0.0, NEG).astype(BF)

    row_loop(ROWS, 32, mask_trunk)
    for lb in range(3):
        blk = base + lb
        row = lax.broadcasted_iota(jnp.int32, (BLK, 2 * BLK), 0)
        col = lax.broadcasted_iota(jnp.int32, (BLK, 2 * BLK), 1)
        par_ok = jnp.logical_and(col < BLK, blk >= TRUNK + BRANCHES)
        self_ok = jnp.logical_and(
            jnp.logical_and(col >= BLK, col - BLK <= row), blk >= TRUNK
        )
        bias_s[lb * BLK : (lb + 1) * BLK, :] = jnp.where(
            jnp.logical_or(par_ok, self_ok), 0.0, NEG
        ).astype(BF)

    cond_all[fs] = cond_parts[fs]
    peers(lambda k, _, src: wire.arrived(cond_all.at[src], s_cond + k, {"fsdp": src}))
    for v in range(6):
        part_out[:, v, :] = nn(
            cond_all[:, 0, 0:rows].astype(BF), w_mod[:, v * D : (v + 1) * D]
        )
    part_out[:, 6:8, :] = jnp.zeros((n, 2, D), F)
    peers(
        lambda k, to, _: wire.copy(
            part_out.at[to], part_in.at[fs], s_part + k, {"fsdp": to}
        ).start()
    )
    part_in[fs] = part_out[fs]

    def z_done(g):
        local_copies[2 + g].wait()
        peers(
            lambda k, _, src: wire.arrived(
                place(g, pl.ds(pl.multiple_of(src * rows, rows), rows), y, x, c),
                s_z[g] + k,
                {"fsdp": src},
            )
        )
        slab = lambda: place(g, all_rows, y, x, c)
        wire.push(slab, s_y[g], to_y)
        if groups[g][3]:
            wire.push(slab, s_x0[g], to_x)
        wire.push(slab, s_c0[g], to_c)

    def y_done(g):
        slab = lambda: place(g, all_rows, 1 - y, x, c)
        wire.arrived(slab(), s_y[g], to_y)
        if groups[g][3]:
            wire.push(slab, s_x1[g], to_x)
        wire.push(slab, s_c1[g], to_c)

    def x_done(g, part):
        s_in, s_out = ((s_x0[g], s_c2[g]), (s_x1[g], s_c3[g]))[part]
        slab = lambda: place(g, all_rows, 1 - y if part else y, 1 - x, c)
        wire.arrived(slab(), s_in, to_x)
        wire.push(slab, s_out, to_c)

    def c_part(g, part):
        yy, xx, at = (
            (y, x, s_c0[g]),
            (1 - y, x, s_c1[g]),
            (y, 1 - x, s_c2[g]),
            (1 - y, 1 - x, s_c3[g]),
        )[part]
        wire.arrived(place(g, all_rows, yy, xx, 1 - c), at, to_c)

    def c_done(g):
        wire.arrived(place(g, all_rows, y, x, 1 - c), s_c0[g], to_c)
        wire.arrived(place(g, all_rows, 1 - y, x, 1 - c), s_c1[g], to_c)
    local_copies[0].wait()
    local_copies[1].wait()
    ciy = 4 * x + 2 * c + 1 - y
    cic = 4 * x + 2 * (1 - c) + y
    ciyc = 4 * x + 2 * (1 - c) + 1 - y
    low, lowy, lowc, lowyc = 2 * c + y, 2 * c + 1 - y, 2 * (1 - c) + y, 2 * (1 - c) + 1 - y
    right = x == 1
    local_copies[8].wait()
    wire.arrived(chunk(ciy), s_ty, to_y, jnp.logical_or(left, ci == 5))
    wire.push(lambda: chunk(ciy), s_txy, to_x, left)
    wire.push(lambda: chunk(ciy), s_tc1, to_c, jnp.logical_or(left, ci == 5))
    wire.arrived(tail_rows(ciy), s_ty2, to_y, ci == 7)

    @pl.when(jnp.logical_and(right, y == 0))
    def _():
        tok[pl.ds(pl.multiple_of((ci + 1) * ROWS, 64), 64), :] = jnp.zeros((64, D), BF)

    z_start(1)
    z_start(4)
    wire.arrived(chunk(low), s_tx, to_x, right)
    wire.push(lambda: chunk(low), s_tc2, to_c, right)
    z_done(0)
    z_start(2)
    wire.arrived(chunk(lowy), s_txy, to_x, right)
    wire.push(lambda: chunk(lowy), s_tc3, to_c, right)
    wire.push(lambda: enc_part(cx), s_ex, to_x, None, lambda: enc_in.at[0])
    wire.push(lambda: enc_part(cx), s_ec0, to_c, None, lambda: enc_in.at[0])
    y_done(0)
    z_done(1)
    z_done(4)
    z_start(5)
    z_start(3)

    peers(lambda k, _, src: wire.arrived(part_in.at[src], s_part + k, {"fsdp": src}))
    mod[...] = jnp.sum(part_in[...], axis=0)
    sa, ba = mod[0:1, :], mod[1:2, :]
    sb, bb = mod[2:3, :], mod[3:4, :]
    sf, bf_ = mod[4:5, :], mod[5:6, :]

    wire.arrived(chunk(cic), s_tc0, to_c, jnp.logical_or(left, ci == 6))
    wire.arrived(chunk(ciyc), s_tc1, to_c, jnp.logical_or(left, ci == 7))
    wire.arrived(chunk(lowc), s_tc2, to_c, right)
    wire.arrived(chunk(lowyc), s_tc3, to_c, right)

    def enc_done(step):
        if step == 0:
            wire.arrived(enc_part(2 * (1 - x) + c), s_ex, to_x)
            wire.push(lambda: enc_part(2 * (1 - x) + c), s_ec1, to_c)
        else:
            wire.arrived(enc_part(2 * x + 1 - c), s_ec0, to_c)
            wire.arrived(enc_part(2 * (1 - x) + 1 - c), s_ec1, to_c)

    tok_tb = tok
    tok_loc = tok.at[pl.ds(pl.multiple_of(ci * ROWS - off, 64), LOC), :]

    def relay(step):
        if step == 1:
            y_done(1)
            y_done(4)
            enc_done(0)
        if step == 2:
            z_done(5)
            z_done(3)
        if step == 4:
            c_done(1)
        if step == 5:
            y_done(5)
            y_done(3)
            c_done(3)
        if step == 6:
            x_done(4, 0)
            x_done(5, 0)
        if step == 7:
            y_done(2)
            enc_done(1)
            c_done(2)

    spec_g = qbuf

    def is_parent(lb, branch):
        parent = jnp.full((32, D), parents_ref[0, base + lb], jnp.int32)
        leaf = jnp.full((32, D), base + lb, jnp.int32) >= TRUNK + BRANCHES
        return jnp.logical_and(leaf, parent == TRUNK + branch)

    to_xy = {"ctx": 2 * (1 - x) + c, "tp": 1 - y}
    s_rcg, s_rcg4, s_rcg5, s_halo = (wire.slot() for _ in range(4))
    s_rxy = [wire.slot() for _ in range(2)]
    s_rxx = [wire.slot() for _ in range(2)]
    s_rce = [wire.slot(), wire.slot()]
    s_rxe = [wire.slot() for _ in range(3)]
    s_m1 = wire.slot(8)
    s_m2 = wire.slot(n)
    quad = ((to_y, x, 1 - y), (to_x, 1 - x, y), (to_xy, 1 - x, 1 - y))

    def add_rows(target, terms, total, step=64):
        def body(rs):
            value = terms[0][rs, :].astype(F)
            for term in terms[1:]:
                value += term[rs, :].astype(F)
            target[rs, :] = value.astype(BF)

        row_loop(total, step, body)

    def strip(buf, at):
        return buf.at[:, at * 256 : (at + 1) * 256]

    class Family:
        def __init__(self, unit, core_box, box, landing, held, shape_rows):
            self.unit, self.core_box, self.box = unit, core_box, box
            self.landing, self.held, self.tall = landing, held, shape_rows
            self.s_core = [wire.slot(4) for _ in range(2)]
            self.s_one = [[wire.slot() for _ in range(2)] for _ in range(2)]
            self.s_two = [wire.slot() for _ in range(2)]
            self.s_z = [wire.slot(n) for _ in range(2)]
            self.s_g = wire.slot(4)

        def core_copy(self, m, t):
            return wire.copy(
                self.unit(m, t // 2, lax.rem(t, 2), 1 - c),
                self.core_box(m, t),
                self.s_core[m] + t,
                to_c,
            )

        def core_send(self):
            for m in range(2):
                for t in range(4):
                    self.core_copy(m, t).start()

        def first_send(self):
            for m in range(2):
                for t in range(4):
                    wire.arrived(self.core_box(m, t), self.s_core[m] + t, to_c)
                    mine = self.unit(m, t // 2, t % 2, c)
                    add_rows(mine, (mine, self.core_box(m, t)), D)
            self.one_send()

        def piece(self, m, yy, xx):
            return self.unit(m, yy, xx, c)

        def one_send(self):
            for j in range(2):
                wire.push(
                    lambda j=j: self.box(j),
                    self.s_one[0][j],
                    to_x,
                    None,
                    lambda j=j: self.piece(0, j, 1 - x),
                )
                wire.push(
                    lambda j=j: self.box(2 + j),
                    self.s_one[1][j],
                    to_y,
                    None,
                    lambda j=j: self.piece(1, 1 - y, j),
                )

        def second_send(self):
            for j in range(2):
                wire.arrived(self.box(j), self.s_one[0][j], to_x)
                mine = self.piece(0, j, x)
                add_rows(mine, (mine, self.box(j)), self.tall, min(64, self.tall))
            wire.push(
                lambda: self.box(4),
                self.s_two[0],
                to_y,
                None,
                lambda: self.piece(0, 1 - y, x),
            )
            for j in range(2):
                wire.arrived(self.box(2 + j), self.s_one[1][j], to_y)
                mine = self.piece(1, y, j)
                add_rows(mine, (mine, self.box(2 + j)), self.tall, min(64, self.tall))
            wire.push(
                lambda: self.box(5),
                self.s_two[1],
                to_x,
                None,
                lambda: self.piece(1, y, 1 - x),
            )

        def z_copy(self, m, k, to):
            part = pl.ds(pl.multiple_of(to * rows, rows), rows)
            return wire.copy(
                self.unit(m, y, x, c).at[part, :],
                self.landing.at[fs, m],
                self.s_z[m] + k,
                {"fsdp": to},
            )

        def tree_send(self):
            for m, target in ((0, to_y), (1, to_x)):
                wire.arrived(self.box(4 + m), self.s_two[m], target)
                mine = self.unit(m, y, x, c)
                add_rows(mine, (mine, self.box(4 + m)), D)
                peers(lambda k, to, _, m=m: self.z_copy(m, k, to).start())
                self.landing[fs, m] = self.unit(m, y, x, c)[my_rows, :]

        def g_copy(self, i):
            target, at = ((to_x, cx), (to_c, cx), (to_c, 2 * (1 - x) + c))[i]
            return wire.copy(self.held.at[at], self.held.at[at], self.s_g + i, target)

        def copy_send(self):
            for m in range(2):
                peers(
                    lambda k, _, src, m=m: wire.arrived(
                        self.landing.at[src, m], self.s_z[m] + k, {"fsdp": src}
                    )
                )
            self.held[cx] = jnp.sum(self.landing[...].astype(F), axis=0).astype(BF)
            self.g_copy(0).start()
            self.g_copy(1).start()

        def relay_copy(self):
            wire.arrived(self.held.at[2 * (1 - x) + c], self.s_g, to_x)
            self.g_copy(2).start()

        def collect(self):
            wire.arrived(self.held.at[2 * x + 1 - c], self.s_g + 1, to_c)
            wire.arrived(self.held.at[2 * (1 - x) + 1 - c], self.s_g + 2, to_c)

        def drain(self):
            for m in range(2):
                for t in range(4):
                    self.core_copy(m, t).wait_send()
                peers(lambda k, to, _, m=m: self.z_copy(m, k, to).wait_send())
            for i in range(3):
                self.g_copy(i).wait_send()

    class TreeFirst(Family):
        def piece(self, m, yy, xx):
            return zs_att.at[yy, 2 * xx + m]

        def row_copy(self, yy, k, to):
            part = pl.ds(pl.multiple_of(to * rows, rows), rows)
            return wire.copy(
                gatt.at[4:8, part, att_cols(yy, c)],
                zl_att.at[fs, yy],
                self.s_z[yy] + k,
                {"fsdp": to},
            )

        def one_send(self):
            for yy in range(2):
                peers(lambda k, to, _, yy=yy: self.row_copy(yy, k, to).start())
                zl_att[fs, yy] = gatt[4:8, my_rows, att_cols(yy, c)]

        def sum_trees(self):
            for yy in range(2):
                peers(
                    lambda k, _, src, yy=yy: wire.arrived(
                        zl_att.at[src, yy], self.s_z[yy] + k, {"fsdp": src}
                    )
                )
            zs_att[...] = jnp.sum(zl_att[...].astype(F), axis=0).astype(BF)
            Family.one_send(self)

        def copy_send(self):
            for m, target in ((0, to_y), (1, to_x)):
                wire.arrived(self.box(4 + m), self.s_two[m], target)
                total = self.piece(m, y, x)[...].astype(F) + self.box(4 + m)[...].astype(F)
                self.held[cx, m] = total.astype(BF)
            self.g_copy(0).start()
            self.g_copy(1).start()

        def drain(self):
            for m in range(2):
                for t in range(4):
                    self.core_copy(m, t).wait_send()
                peers(lambda k, to, _, m=m: self.row_copy(m, k, to).wait_send())
            for i in range(3):
                self.g_copy(i).wait_send()

    ffn = Family(
        lambda m, yy, xx, cc: gffn.at[m, :, ffn_cols(yy, xx, cc)],
        lambda m, t: rc_att.at[m * 4 + t],
        lambda i: strip(wdn, i),
        zr_ffn,
        rg_ffn,
        D,
    )

    def attention_family(a):
        kind = (Family, TreeFirst)[a]
        tall = (D, rows)[a]
        return kind(
            lambda m, yy, xx, cc: gatt.at[4 * a + 2 * xx + m, :, att_cols(yy, cc)],
            lambda m, t: rc_att.at[
                4 * a + 2 * m + t // 2, :, pl.ds(pl.multiple_of(lax.rem(t, 2) * 128, 128), 128)
            ],
            lambda i: rx_att.at[a, i, 0:tall],
            zr_att.at[a],
            rg_att.at[a],
            tall,
        )

    att = (attention_family(0), attention_family(1))

    def ffn_free():
        wire.drain()
        for target in (to_y, to_x):
            pl.semaphore_signal(ready.at[0], inc=1, device_id=target, device_id_type=MESH)

    def ffn_chip_send():
        pl.semaphore_wait(ready.at[0], 2)
        ffn.first_send()
        pl.semaphore_signal(ready.at[1], inc=1, device_id=to_c, device_id_type=MESH)

    results = (
        (rg_ffn, ffn_out),
        (rg_att.at[0], att_out.at[0]),
        (rg_att.at[1], att_out.at[1]),
        (mod2, mod_out),
        (cond_all, cond_out),
    )

    def result(i):
        return pltpu.make_async_copy(results[i][0], results[i][1], local.at[i])

    def ffn_finish():
        ffn.collect()
        result(0).start()

    def att_finish(a):
        att[a].collect()
        result(1 + a).start()

    def enc_core_send():
        for xx in range(2):
            wire.push(
                lambda xx=xx: rc_e.at[xx],
                s_rce[xx],
                to_c,
                None,
                lambda xx=xx: egrad.at[pl.ds(pl.multiple_of((2 * xx + 1 - c) * 128, 128), 128), :],
            )

    def enc_rows(xx):
        return egrad.at[pl.ds(pl.multiple_of((2 * xx + c) * 128, 128), 128), :]

    def enc_chip_send():
        for xx in range(2):
            wire.arrived(rc_e.at[xx], s_rce[xx], to_c)
            add_rows(enc_rows(xx), (enc_rows(xx), rc_e.at[xx]), 128)
        for r, (target, xx, _) in enumerate(quad):
            wire.push(
                lambda: rx_e.at[2 * x + y], s_rxe[r], target, None, lambda xx=xx: enc_rows(xx)
            )
        rx_e[2 * x + y] = enc_rows(x)[...]

    def enc_finish():
        for r, (target, xx, yy) in enumerate(quad):
            wire.arrived(rx_e.at[2 * xx + yy], s_rxe[r], target)
        enc_out[...] = jnp.sum(rx_e[...].astype(F), axis=0)

    def shared_core_send():
        to_core = pl.ds(pl.multiple_of(640 * (1 - c), 640), 640)
        wire.push(lambda: rc_g.at[0:640], s_rcg, to_c, None, lambda: tok.at[to_core, :])
        wire.push(
            lambda: rc_g.at[640:896],
            s_rcg4,
            to_c,
            jnp.logical_and(x == 1, c == 1),
            lambda: tok.at[1280:1536, :],
        )
        wire.push(lambda: halo, s_halo, to_y, y == 1, lambda: spec_g.at[0:64, :])

    def part_rows(yy, p):
        return tok.at[pl.ds(pl.multiple_of((2 * c + yy) * ROWS + p * 160, 32), 160), :]

    def core_rows(yy, p):
        return rc_g.at[pl.ds(pl.multiple_of(yy * ROWS + p * 160, 32), 160), :]

    def shared_y_send():
        wire.arrived(rc_g.at[0:640], s_rcg, to_c)
        for p in range(2):
            mine = part_rows(1 - y, p)
            add_rows(mine, (mine, core_rows(1 - y, p)), 160, 32)
            wire.push(
                lambda p=p: rx_g.at[0, p * 160 : p * 160 + 160],
                s_rxy[p],
                to_y,
                None,
                lambda p=p: part_rows(1 - y, p),
            )
        last = jnp.logical_and(x == 1, c == 0)

        @pl.when(last)
        def _():
            wire.arrived(rc_g.at[640:896], s_rcg4, to_c)
            four = tok.at[1280:1536, :]
            add_rows(four, (four, rc_g.at[640:896]), 256)

        wire.push(
            lambda: rx_g.at[1, 0:256],
            s_rcg5,
            to_y,
            jnp.logical_and(last, y == 1),
            lambda: tok.at[1280:1536, :],
        )
        for p in range(2):
            mine = part_rows(y, p)
            add_rows(mine, (mine, core_rows(y, p)), 160, 32)

    def shared_x_send():
        for p in range(2):
            wire.arrived(rx_g.at[0, p * 160 : p * 160 + 160], s_rxy[p], to_y)
            mine = part_rows(y, p)
            add_rows(mine, (mine, rx_g.at[0, p * 160 : p * 160 + 160]), 160, 32)
            wire.push(
                lambda p=p: rx_g.at[1, p * 160 : p * 160 + 160],
                s_rxx[p],
                to_x,
                x == 1,
                lambda p=p: part_rows(y, p),
            )

    def shared_arrived():
        for p in range(2):
            wire.arrived(rx_g.at[1, p * 160 : p * 160 + 160], s_rxx[p], to_x, x == 0)
        wire.arrived(rx_g.at[1, 0:256], s_rcg5, to_y, ci == 4)

    def tree_peers(make):
        @pl.loop(1, 8)
        def _(k):
            make(k, lax.rem(ci + k, 8), lax.rem(ci + 8 - k, 8))

    def device_of(i):
        return {"ctx": i // 2, "tp": lax.rem(i, 2)}

    def mod_1(k, to):
        return wire.copy(mgrad, mod1.at[ci], s_m1 + k, device_of(to))

    def mod_2(k, to):
        return wire.copy(mod2.at[fs], mod2.at[fs], s_m2 + k, {"fsdp": to})

    def mod_tree_send():
        tree_peers(lambda k, to, _: mod_1(k, to).start())
        mod1[ci] = mgrad[...]

    def mod_all_send():
        tree_peers(lambda k, _, src: wire.arrived(mod1.at[src], s_m1 + k, device_of(src)))
        mod2[fs] = jnp.sum(mod1[...], axis=0)
        peers(lambda k, to, _: mod_2(k, to).start())

    def mod_finish():
        peers(lambda k, _, src: wire.arrived(mod2.at[src], s_m2 + k, {"fsdp": src}))
        result(3).start()
        result(4).start()

    def leave(step):
        if step == 0:
            ffn_free()
        if step == 1:
            ffn_chip_send()
        if step == 2:
            pl.semaphore_wait(ready.at[1], 1)
            att[1].core_send()
            enc_core_send()
        if step == 3:
            att[1].first_send()
            enc_chip_send()
        if step == 4:
            ffn.second_send()
        if step == 5:
            ffn.tree_send()
        if step == 6:
            shared_core_send()
        if step == 7:
            shared_y_send()
            att[0].first_send()
            enc_finish()
            shared_x_send()
        if step == 8:
            att[1].sum_trees()
            att[0].second_send()
            att[1].second_send()
            ffn.copy_send()
            shared_arrived()
        if step == 9:
            mod_tree_send()
            att[0].tree_send()
            att[1].copy_send()
            ffn.relay_copy()
            mod_all_send()
            att[0].copy_send()
            att[1].relay_copy()
            ffn_finish()
            mod_finish()
            att[0].relay_copy()
            att_finish(1)
            att_finish(0)

    def hidden(x):
        n, _ = normed(x.astype(F))
        return (n * (1.0 + sa) + ba).astype(BF)

    def hid_trunk(rs):
        hid[rs, :] = hidden(tok_tb[rs, :])

    row_loop(TRK, 32, hid_trunk, 8)

    def hid_loc(rs):
        hloc[rs, :] = hidden(tok_loc[rs, :])

    row_loop(LOC, 32, hid_loc, 6)
    for lb in range(3):
        picks = [is_parent(lb, b) for b in range(1, BRANCHES)]
        for piece in range(4):
            r = piece * 32
            picked = tok_tb[TRK + r : TRK + r + 32, :].astype(F)
            for b in range(1, BRANCHES):
                at = TRK + b * BLK + r
                picked = jnp.where(picks[b - 1], tok_tb[at : at + 32, :].astype(F), picked)
            at = TRK + lb * 256 + r
            hid[at : at + 32, :] = hidden(picked)
        hid[TRK + lb * 256 + BLK : TRK + lb * 256 + 2 * BLK, :] = hloc[
            lb * BLK : (lb + 1) * BLK, :
        ]

    def project(rs):
        kbuf[rs, :] = nn(hid[rs, :], watt[1]).astype(BF)
        vbuf[rs, :] = nn(hid[rs, :], watt[2]).astype(BF)

    z_done(2)
    c_done(0)
    row_loop(KV, 256, project)
    qbuf[...] = (nn(hloc[...], watt[0]) * 0.125).astype(BF)

    linv_a, linv_b = wk_acc.at[0:ROWS, :], wv_acc.at[0:ROWS, :]

    def with_ones(values, half):
        return jnp.where(half_lanes(values.shape, half), values, jnp.ones_like(values))

    def finish_heads(o0, o1, mixed, linv, lanes):
        inv0, inv1 = 1.0 / pltpu.roll(o0, HD, 1), 1.0 / pltpu.roll(o1, HD, 1)
        first = half_lanes(o0.shape, 0)
        mixed[:, lanes] = jnp.where(first, o0 * inv0, o1 * inv1).astype(BF)
        linv[:, lanes] = jnp.where(first, inv0, inv1)

    @pl.loop(0, 4)
    def _(hp):
        for step in (1, 2):

            @pl.when(hp == step)
            def _(step=step):
                relay(step)

        lanes = pl.ds(pl.multiple_of(hp * 128, 128), 128)
        kt = kbuf[0:TRK, lanes]
        vt = vbuf[0:TRK, lanes]
        outs = []
        for half in range(2):
            h = hp * 2 + half
            st[...] = nt(keep(qbuf[own, lanes], half), kt) + bias_t[...].astype(F)
            for lb in range(3):
                r = slice(lb * BLK, (lb + 1) * BLK)
                ks = kbuf[TRK + lb * 256 : TRK + (lb + 1) * 256, lanes]
                ss[r, :] = nt(keep(qbuf[r, lanes], half), ks) + bias_s[r, :].astype(F)
            for i in range(ROWS // 32):
                rs = slice(i * 32, i * 32 + 32)
                ro = pl.ds(pl.multiple_of(i * 32 + off, 32), 32)
                a, b = st[rs, :], ss[ro, :]
                top = jnp.maximum(
                    jnp.max(a, axis=-1, keepdims=True), jnp.max(b, axis=-1, keepdims=True)
                )
                pt[h, rs, :] = jnp.exp(a - top).astype(BF)
                ps[h, ro, :] = jnp.exp(b - top).astype(BF)
            for lb in range(3):
                r = slice(lb * BLK, (lb + 1) * BLK)
                vs = vbuf[TRK + lb * 256 : TRK + (lb + 1) * 256, lanes]
                spec_o[half, r, :] = nn(ps[h, r, :], with_ones(vs, half))
            outs.append(nn(pt[h], with_ones(vt, half)) + spec_o[half, own, :])
        finish_heads(outs[0], outs[1], mixa, linv_a, lanes)

    relay(4)
    t0[...] = nt(mixa[...], watt[3])

    def after_self(rs):
        sbv = tok_own[rs, :].astype(F) + t0[rs, :]
        stream_b[rs, :] = sbv
        n, _ = normed(sbv)
        hid_b[rs, :] = (n * (1.0 + sb) + bb).astype(BF)

    row_loop(ROWS, 32, after_self, 0)

    relay(7)
    kenc[...] = nn(enc[...], watt[5]).astype(BF)
    venc[...] = nn(enc[...], watt[6]).astype(BF)
    qb[...] = (nn(hid_b[...], watt[4]) * 0.125).astype(BF)

    @pl.loop(0, 4)
    def _(hp):
        lanes = pl.ds(pl.multiple_of(hp * 128, 128), 128)
        kt = kenc[:, lanes]
        vt = venc[:, lanes]
        outs = []
        for half in range(2):
            h = hp * 2 + half
            t0[...] = nt(keep(qb[:, lanes], half), kt)
            for i in range(ROWS // 32):
                rs = slice(i * 32, i * 32 + 32)
                a = t0[rs, :]
                pe[h, rs, :] = jnp.exp(a - jnp.max(a, axis=-1, keepdims=True)).astype(BF)
            outs.append(nn(pe[h], with_ones(vt, half)))
        finish_heads(outs[0], outs[1], mixb, linv_b, lanes)

    relay(5)
    t0[...] = nt(mixb[...], watt[7])

    def after_cross(rs):
        scv = stream_b[rs, :] + t0[rs, :]
        stream_c[rs, :] = scv
        n, _ = normed(scv)
        hid_c[rs, :] = (n * (1.0 + sf) + bf_).astype(BF)

    row_loop(ROWS, 32, after_cross, 0)

    relay(6)
    acc0[...] = jnp.zeros_like(acc0)
    acc1[...] = jnp.zeros_like(acc1)

    def flip(v, by):
        return v + by - 2 * v * by

    @pl.loop(0, 4)
    def _(ft):
        @pl.when(ft == 2)
        def _():
            x_done(4, 1)
            x_done(5, 1)

        for part in range(4):

            @pl.when(ft == part)
            def _(part=part):
                c_part(4, part)
                c_part(5, part)

        tile = flip(y, lax.rem(ft, 2)) * 2 + flip(x, ft // 2)
        cols = pl.ds(pl.multiple_of(tile * 512, 512), 512)
        t0[...] = nn(hid_c[...], wup[:, cols])
        t1[...] = nn(cot[...], wdn[:, cols])

        def gelu(rs):
            u = t0[rs, :]
            phi = 0.5 * (1.0 + lax.erf(u * (2.0**-0.5)))
            b0[rs, :] = (u * phi).astype(BF)
            slope = phi + u * (jnp.exp(-0.5 * u * u) * (1.0 / math.sqrt(2.0 * math.pi)))
            b1[rs, :] = (t1[rs, :] * slope).astype(BF)

        row_loop(ROWS, 32, gelu)
        acc0[...] += nt(b0[...], wdn[:, cols])
        acc1[...] += nt(b1[...], wup[:, cols])
        gffn[1, :, cols] = tn(cot[...], b0[...]).astype(BF)
        gffn[0, :, cols] = tn(hid_c[...], b1[...]).astype(BF)
        for m in range(2):
            ffn.core_copy(m, tile).start()

    def back_norm(at, scale, grad_src, stream_src, base_src, want_out):
        sums = [jnp.zeros((1, D), F), jnp.zeros((1, D), F)]
        for i in range(ROWS // 32):
            rs = slice(i * 32, i * 32 + 32)
            back, ds, db = norm_back(grad_src[rs, :], stream_src[rs, :], scale)
            total = base_src[rs, :].astype(F) + back
            in_grad[rs, :] = total
            gbf[rs, :] = total.astype(BF)
            sums = [sums[0] + ds, sums[1] + db]
            if want_out:
                out_ref[rs, :] = (stream_c[rs, :] + acc0[rs, :]).astype(BF)
        mgrad[at : at + 1, :] = sums[0]
        mgrad[at + 1 : at + 2, :] = sums[1]

    leave(0)
    back_norm(4, sf, acc1, stream_c, cot, True)

    gatt[7] = tn(gbf[...], mixb[...]).astype(BF)
    mgr[...] = (nn(gbf[...], watt[7]) * linv_b[...]).astype(BF)
    leave(1)

    @pl.loop(0, 4)
    def _(hp):
        lanes = pl.ds(pl.multiple_of(hp * 128, 128), 128)
        prod = mgr[:, lanes].astype(F) * mixb[:, lanes].astype(F)
        dqs, dks, dvs = [], [], []
        for half in range(2):
            h = hp * 2 + half
            inner = jnp.sum(keep(prod, half), axis=-1, keepdims=True)
            mg = keep(mgr[:, lanes], half)
            dp = nt(mg, venc[:, lanes])
            b0[...] = (pe[h].astype(F) * (dp - inner)).astype(BF)
            dqs.append(nn(b0[...], kenc[:, lanes]))
            dks.append(tn(b0[...], keep(qb[:, lanes], half)))
            dvs.append(tn(pe[h], mg))
        dq[:, lanes] = (jnp.where(half_lanes(dqs[0].shape, 0), dqs[0], dqs[1]) * 0.125).astype(BF)
        kenc[:, lanes] = (dks[0] + dks[1]).astype(BF)
        venc[:, lanes] = (dvs[0] + dvs[1]).astype(BF)

    gatt[4] = tn(hid_b[...], dq[...]).astype(BF)
    gatt[5] = tn(enc[...], kenc[...]).astype(BF)
    gatt[6] = tn(enc[...], venc[...]).astype(BF)
    egrad[...] = (nt(kenc[...], watt[5]) + nt(venc[...], watt[6])).astype(BF)
    leave(2)
    acc1[...] = nt(dq[...], watt[4])
    back_norm(2, sb, acc1, stream_b, in_grad, False)

    gatt[3] = tn(gbf[...], mixa[...]).astype(BF)
    mgr[...] = (nn(gbf[...], watt[3]) * linv_a[...]).astype(BF)
    leave(3)

    @pl.when(odd == 0)
    def _():
        for h in range(8):
            ps[h, ROWS:LOC, :] = jnp.zeros((LOC - ROWS, 256), BF)
        spec_o[:, ROWS:LOC, :] = jnp.zeros((2, LOC - ROWS, 128), F)

    @pl.when(odd == 1)
    def _():
        for h in range(8):
            ps[h, 0:64, :] = jnp.zeros((64, 256), BF)
        spec_o[:, 0:64, :] = jnp.zeros((2, 64, 128), F)

    @pl.loop(0, 4)
    def _(turn):
        side = jnp.where(turn < 2, 1 - c, c)
        band = jnp.where(turn < 2, turn, jnp.where(turn == 2, 1 - y, y))
        hp = band * 2 + side
        lanes = pl.ds(pl.multiple_of(hp * 128, 128), 128)
        prod = mgr[:, lanes].astype(F) * mixa[:, lanes].astype(F)
        dqs, dks, dvs = [], [], []
        dks_s = [[], [], []]
        dvs_s = [[], [], []]
        for half in range(2):
            h = hp * 2 + half
            inner = jnp.sum(keep(prod, half), axis=-1, keepdims=True)
            mg = keep(mgr[:, lanes], half)
            qm = keep(qbuf[own, lanes], half)
            dp = nt(mg, vbuf[0:TRK, lanes])
            ds = (pt[h].astype(F) * (dp - inner)).astype(BF)
            spec_o[0, own, :] = mg.astype(F)
            spec_o[1, own, :] = jnp.broadcast_to(inner, (ROWS, 128))
            dq_s = []
            for lb in range(3):
                r = slice(lb * BLK, (lb + 1) * BLK)
                k_rows = slice(TRK + lb * 256, TRK + (lb + 1) * 256)
                mgl = spec_o[0, r, :].astype(BF)
                dpl = nt(mgl, vbuf[k_rows, lanes])
                inner_l = spec_o[1, r, 0:1]
                dsl = (ps[h, r, :].astype(F) * (dpl - inner_l)).astype(BF)
                ss[r, 0:128] = nn(dsl, kbuf[k_rows, lanes])
                dks_s[lb].append(tn(dsl, keep(qbuf[r, lanes], half)))
                dvs_s[lb].append(tn(ps[h, r, :], mgl))
            dqs.append(nn(ds, kbuf[0:TRK, lanes]) + ss[own, 0:128])
            dks.append(tn(ds, qm))
            dvs.append(tn(pt[h], mg))
        dq[:, lanes] = (jnp.where(half_lanes(dqs[0].shape, 0), dqs[0], dqs[1]) * 0.125).astype(BF)
        kbuf[0:TRK, lanes] = (dks[0] + dks[1]).astype(BF)
        vbuf[0:TRK, lanes] = (dvs[0] + dvs[1]).astype(BF)
        for lb in range(3):
            k_rows = slice(TRK + lb * 256, TRK + (lb + 1) * 256)
            kbuf[k_rows, lanes] = (dks_s[lb][0] + dks_s[lb][1]).astype(BF)
            vbuf[k_rows, lanes] = (dvs_s[lb][0] + dvs_s[lb][1]).astype(BF)

        total = None
        for at in range(0, KV, KV // 2):
            rs = slice(at, at + KV // 2)
            both = jnp.concatenate([kbuf[rs, lanes], vbuf[rs, lanes]], axis=1)
            part = tn(both, hid[rs, :])
            total = part if total is None else total + part
        kv_grad = jnp.transpose(total)
        gatt[1, :, lanes] = kv_grad[:, 0:128].astype(BF)
        gatt[2, :, lanes] = kv_grad[:, 128:256].astype(BF)
        gatt[0, :, lanes] = tn(hloc[own, :], dq[:, lanes]).astype(BF)

        @pl.when(turn < 2)
        def _():
            for m in range(2):
                for xx in range(2):
                    att[0].core_copy(m, band * 2 + xx).start()

        @pl.when(turn == 1)
        def _():
            leave(4)

        @pl.when(turn == 3)
        def _():
            leave(5)

    def key_grad(rs):
        return (nt(kbuf[rs, :], watt[1]) + nt(vbuf[rs, :], watt[2])).astype(BF)

    for lb in range(3):
        pe[lb, 0:256, :] = key_grad(slice(TRK + lb * 256, TRK + (lb + 1) * 256))

    def trunk_grad(rs):
        tok[rs, :] = key_grad(rs)

    row_loop(TRK, 256, trunk_grad)

    for b in range(BRANCHES):
        hits = [is_parent(lb, b) for lb in range(3)]
        for piece in range(4):
            total = jnp.zeros((32, D), F)
            for lb in range(3):
                at = piece * 32
                total += jnp.where(hits[lb], pe[lb, at : at + 32, :].astype(F), 0.0)
            at = TRK + b * BLK + piece * 32
            tok[at : at + 32, :] = total.astype(BF)
    for lb in range(3):
        spec_g[lb * BLK : (lb + 1) * BLK, :] = pe[lb, BLK : 2 * BLK, :]

    leave(6)
    acc1[...] = nt(dq[...], watt[0])

    def own_sum(rs):
        extra = spec_g[pl.ds(pl.multiple_of(rs.start + off, 32), 32), :].astype(F)
        acc1[rs, :] += extra

    row_loop(ROWS, 32, own_sum, 5)
    leave(7)
    leave(8)

    wire.arrived(halo, s_halo, to_y, y == 0)

    @pl.when(y == 0)
    def _():
        acc1[ROWS - 64 : ROWS, :] += halo[...].astype(F)

    @pl.when(x == 0)
    def _():
        def body(rs):
            mine = tok[pl.ds(pl.multiple_of(ci * ROWS + rs.start, 32), 32), :].astype(F)
            acc1[rs, :] += mine + rx_g[1, rs, :].astype(F)

        row_loop(ROWS, 32, body)

    @pl.when(ci == 4)
    def _():
        def body(rs):
            mine = tok[pl.ds(pl.multiple_of(4 * ROWS + rs.start, 32), 32), :].astype(F)
            acc1[rs, :] += mine + rx_g[1, rs, :].astype(F)

        row_loop(256, 32, body)

    mgrad[6:8, :] = jnp.zeros((2, D), F)
    sums = [jnp.zeros((1, D), F), jnp.zeros((1, D), F)]
    for i in range(ROWS // 32):
        rs = slice(i * 32, i * 32 + 32)
        back, ds, db = norm_back(acc1[rs, :], tok_own[rs, :].astype(F), sa)
        in_grad[rs, :] += back
        sums = [sums[0] + ds, sums[1] + db]
    mgrad[0:1, :] = sums[0]
    mgrad[1:2, :] = sums[1]
    leave(9)

    for i in range(5):
        result(i).wait()
    wire.drain()
    for family in (ffn, *att):
        family.drain()
    tree_peers(lambda k, to, _: mod_1(k, to).wait_send())
    peers(lambda k, to, _: mod_2(k, to).wait_send())
    peers(
        lambda k, to, _: wire.copy(
            cond_parts.at[to], cond_all.at[fs], s_cond + k, {"fsdp": to}
        ).wait_send()
    )
    peers(
        lambda k, to, _: wire.copy(
            part_out.at[to], part_in.at[fs], s_part + k, {"fsdp": to}
        ).wait_send()
    )
    for g in range(6):
        peers(
            lambda k, to, _, g=g: wire.copy(
                groups[g][0], place(g, my_rows, y, x, c), s_z[g] + k, {"fsdp": to}
            ).wait_send()
        )


def layer_call(n, parents, cond_parts, w_mod, tokens, enc, cot, weights):
    vm = pl.BlockSpec(memory_space=pltpu.VMEM)
    hbm = pl.BlockSpec(memory_space=pl.ANY)
    sds = jax.ShapeDtypeStruct
    rows = w_mod.shape[0]
    return pl.pallas_call(
        functools.partial(layer_kernel, n),
        out_shape=(
            sds((ROWS, D), BF),
            sds((ROWS, D), F),
            sds((ENC // 4, D), F),
            sds((n, 8, D), F),
            sds(cond_parts.shape, F),
            sds((2, 4, 2, rows, 128), BF),
            sds((4, 2, rows, 256), BF),
        ),
        in_specs=[pl.BlockSpec(memory_space=pltpu.SMEM), vm, vm, hbm, hbm, vm] + [hbm] * 6,
        out_specs=(vm, vm, vm, hbm, hbm, hbm, hbm),
        scratch_shapes=[
            pltpu.VMEM((8, D, D), BF),
            pltpu.VMEM((D, FF), BF),
            pltpu.VMEM((D, FF), BF),
            pltpu.VMEM((8 * ROWS + 64, D), BF),
            pltpu.VMEM((ENC, D), BF),
            pltpu.VMEM((n, 8, D), F),
            pltpu.VMEM((n, 8, D), F),
            pltpu.VMEM((8, D), F),
            pltpu.VMEM((*cond_parts.shape,), F),
            pltpu.VMEM((ROWS, D), BF),
            pltpu.VMEM((8, D), F),
            pltpu.VMEM((KV, D), BF),
            pltpu.VMEM((LOC, D), BF),
            pltpu.VMEM((KV, D), BF),
            pltpu.VMEM((KV, D), BF),
            pltpu.VMEM((LOC, D), BF),
            pltpu.VMEM((8, ROWS, TRK), BF),
            pltpu.VMEM((8, LOC, 256), BF),
            pltpu.VMEM((ROWS, TRK), BF),
            pltpu.VMEM((LOC, 256), BF),
            pltpu.VMEM((ROWS, TRK), F),
            pltpu.VMEM((LOC, 256), F),
            pltpu.VMEM((2, LOC, 128), F),
            pltpu.VMEM((ROWS, D), BF),
            pltpu.VMEM((ROWS, D), F),
            pltpu.VMEM((ROWS, D), F),
            pltpu.VMEM((ROWS, D), BF),
            pltpu.VMEM((ROWS, D), BF),
            pltpu.VMEM((ENC, D), BF),
            pltpu.VMEM((ENC, D), BF),
            pltpu.VMEM((ROWS, D), BF),
            pltpu.VMEM((8, ROWS, ENC), BF),
            pltpu.VMEM((ROWS, D), BF),
            pltpu.VMEM((ROWS, D), BF),
            pltpu.VMEM((ROWS, D), BF),
            pltpu.VMEM((ROWS, D), F),
            pltpu.VMEM((ROWS, D), F),
            pltpu.VMEM((ROWS, D), BF),
            pltpu.VMEM((ROWS, D), BF),
            pltpu.VMEM((ROWS, D), BF),
            pltpu.VMEM((D, D), F),
            pltpu.VMEM((ROWS, D), F),
            pltpu.VMEM((8, D, D), BF),
            pltpu.VMEM((2, D, FF), BF),
            pltpu.VMEM((8, D, 256), BF),
            pltpu.VMEM((2, 6, D, 128), BF),
            pltpu.VMEM((2, n, 2, rows, 128), BF),
            pltpu.VMEM((2, 4, 2, rows, 128), BF),
            pltpu.VMEM((n, 2, 4, rows, 128), BF),
            pltpu.VMEM((2, 4, rows, 128), BF),
            pltpu.VMEM((n, 2, rows, 256), BF),
            pltpu.VMEM((4, 2, rows, 256), BF),
            pltpu.VMEM((896, D), BF),
            pltpu.VMEM((2, ROWS, D), BF),
            pltpu.VMEM((64, D), BF),
            pltpu.VMEM((2, 128, D), BF),
            pltpu.VMEM((4, 128, D), BF),
            pltpu.VMEM((8, 8, D), F),
            pltpu.VMEM((n, 8, D), F),
            pltpu.SemaphoreType.DMA((16 * n + 160,)),
            pltpu.SemaphoreType.DMA((16 * n + 160,)),
            pltpu.SemaphoreType.DMA((9,)),
            pltpu.SemaphoreType.REGULAR((2,)),
        ],
        compiler_params=pltpu.CompilerParams(
            vmem_limit_bytes=VMEM_LIMIT, collective_id=0, has_side_effects=True
        ),
        name="layer",
    )(parents, cond_parts, w_mod, tokens, enc, cot, *weights)


def finish_kernel(
    n, rows, out, grad, enc, mod, cond, att, ffn, o_out, o_grad, o_enc, o_mod, qkv, so, cqkv, co, up, dn
):
    o_out[...] = out[...]
    o_grad[...] = grad[...]
    o_enc[...] = enc[...]
    for v in range(6):
        o_mod[:, v * D : (v + 1) * D] = lax.dot_general(
            cond[:, 0, 0:rows],
            mod[:, v, :],
            (((0,), (0,)), ((), ())),
            precision=lax.Precision.HIGHEST,
            preferred_element_type=F,
        )
    for q in range(4):
        up[:, q * 256 : (q + 1) * 256] = ffn[q, 0].astype(F)
        dn[:, q * 256 : (q + 1) * 256] = ffn[q, 1].astype(F)
        cols = slice((q % 2) * 128, (q % 2) * 128 + 128)
        for a, (stack, single) in enumerate(((qkv, so), (cqkv, co))):
            for m in range(2):
                value = att[a, q, m].astype(F)
                at = 2 * (q // 2) + m
                if at < 3:
                    stack[at, :, cols] = value
                else:
                    single[:, cols] = value


def finish_call(n, rows, *parts):
    vm = pl.BlockSpec(memory_space=pltpu.VMEM)
    sds = jax.ShapeDtypeStruct
    return pl.pallas_call(
        functools.partial(finish_kernel, n, rows),
        out_shape=(
            sds((ROWS, D), BF),
            sds((ROWS, D), F),
            sds((ENC // 4, D), F),
            sds((rows, 6 * D), F),
            sds((3, rows, 256), F),
            sds((rows, 256), F),
            sds((3, rows, 256), F),
            sds((rows, 256), F),
            sds((rows, 1024), F),
            sds((rows, 1024), F),
        ),
        in_specs=[vm] * 7,
        out_specs=(vm,) * 10,
        name="finish",
    )(*parts)


def timestep_code(timesteps, width):
    half = width // 2
    frequency = jnp.exp(-math.log(10000.0) * jnp.arange(half, dtype=F) / half)
    angles = timesteps.astype(F)[:, None] * frequency[None, :]
    return jnp.concatenate([jnp.sin(angles), jnp.cos(angles)], axis=-1)


def per_device(
    tokens,
    encoder_states,
    timesteps,
    parents,
    w_mod,
    w_self_qkv,
    w_self_out,
    w_cross_qkv,
    w_cross_out,
    w_up,
    w_down,
    cotangent,
):
    rows = w_mod.shape[0]
    condition = jax.nn.silu(timestep_code(timesteps, D)).astype(BF)
    n = lax.axis_size("fsdp")
    padded_cond = jnp.pad(condition.astype(F).reshape(n, 1, rows), ((0, 0), (0, 7), (0, max(128 - rows, 0))))
    parts = layer_call(
        n,
        parents,
        padded_cond,
        w_mod,
        tokens,
        encoder_states,
        cotangent[0],
        (w_self_qkv, w_self_out, w_cross_qkv, w_cross_out, w_up, w_down),
    )
    out, in_grad, enc_grad, grad_mod, *weights = finish_call(n, rows, *parts)
    return (out[None], in_grad[None], enc_grad[None], grad_mod, *weights)


def solution(mesh):
    rows = P("fsdp", ("ctx", "tp"), None)
    return jax.shard_map(
        per_device,
        mesh=mesh,
        in_specs=(
            rows,
            P("fsdp", "ctx", None),
            P("fsdp"),
            P("fsdp", None),
            P("fsdp", None),
            P(None, "fsdp", "tp"),
            P("fsdp", "tp"),
            P(None, "fsdp", "tp"),
            P("fsdp", "tp"),
            P("fsdp", "tp"),
            P("fsdp", "tp"),
            rows,
        ),
        out_specs=(
            rows,
            rows,
            P("fsdp", "ctx", None),
            P("fsdp", None),
            P(None, "fsdp", "tp"),
            P("fsdp", "tp"),
            P(None, "fsdp", "tp"),
            P("fsdp", "tp"),
            P("fsdp", "tp"),
            P("fsdp", "tp"),
        ),
        check_vma=False,
    )
```
